32 devices in a mesh: rows: 16 (over z, y, x), keys: 2 (over core).
Axes of the slice: x: 2, y: 2, z: 4, core: 2. Of those that a mesh axis runs over, the one named last changes fastest.
Arguments:
- tokens: bfloat16 [16, 1024, 768], P('rows', 'keys'), may hold values from -6 to 6
- seg_ids: int32 [16, 1024], P('rows'), may hold values from 0 to 7, as said below
- doc_starts: int32 [16, 1024], P('rows', 'keys'), may hold values from 0 to 1, as said below
- gain_in: float32 [768], replicated, may hold values from 0.1 to 1.9
- shift_in: float32 [768], replicated, may hold values from -3 to 3
- w_query: bfloat16 [768, 768], replicated, may hold values from -0.21875 to 0.21875
- w_key: bfloat16 [768, 768], replicated, may hold values from -0.21875 to 0.21875
- w_value: bfloat16 [768, 768], replicated, may hold values from -0.21875 to 0.21875
- w_out: bfloat16 [768, 768], replicated, may hold values from -0.625 to 0.625
- gain_mid: float32 [768], replicated, may hold values from 0.1 to 1.9
- shift_mid: float32 [768], replicated, may hold values from -3 to 3
- w_up: bfloat16 [768, 3072], replicated, may hold values from -0.21875 to 0.21875
- w_down: bfloat16 [3072, 768], replicated, may hold values from -0.109375 to 0.109375
- out_grad: bfloat16 [16, 1024, 768], P('rows', 'keys'), may hold values from -6 to 6
Outputs:
- output: bfloat16 [16, 1024, 768], P('rows', 'keys')
- input_grad: bfloat16 [16, 1024, 768], P('rows', 'keys')
- key_share: float32 [16, 1024], P('rows', 'keys')
- grad_gain_in: float32 [768], P('rows')
- grad_shift_in: float32 [768], P('rows')
- grad_w_query: float32 [768, 768], P('rows')
- grad_w_key: float32 [768, 768], P('rows')
- grad_w_value: float32 [768, 768], P('rows')
- grad_w_out: float32 [768, 768], P('rows')
- grad_gain_mid: float32 [768], P('rows')
- grad_shift_mid: float32 [768], P('rows')
- grad_w_up: float32 [768, 3072], P('rows')
- grad_w_down: float32 [3072, 768], P('rows')
The draws below stay inside these ranges and needn't reach their ends.
Inputs may be any that keep to these rules, and one draw needn't show every extreme that they name: `seg_ids`: within each row the ids begin at 0 and rise by one at each document's first token; they never fall. Every row holds exactly 8 documents. `doc_starts`: 1 exactly at a row's first token and where seg_ids differs from the previous token's, else 0.
All inputs are finite; a program needn't handle non-finite values.
Results may differ from the reference program's by a relative error of at most 0.019.
Values may be sent and summed in bfloat16 or wider, within the bound.
A program may use at most 192 MiB of HBM per device.

```python
import jax
import jax.numpy as jnp
from jax import lax

D = 768
HEAD = 64
FF = 3072
HEADS = 12
ROW = 1024
ROWS = 16
DOC_RATE = 128


def doc_layout(key):
    row_keys = jax.random.split(jax.random.fold_in(key, 11), ROWS)
    orders = jax.vmap(lambda one_key: jax.random.permutation(one_key, ROW - 1))(row_keys)
    later_starts = (orders < ROW // DOC_RATE - 1).astype(jnp.int32)
    starts = jnp.concatenate([jnp.ones((ROWS, 1), jnp.int32), later_starts], axis=1).astype(jnp.int32)
    return (jnp.cumsum(starts, axis=1).astype(jnp.int32) - 1, starts)


def draw_seg_ids(key, part):
    return doc_layout(key)[0]


def draw_doc_starts(key, part):
    return doc_layout(key)[1]


def steps_of(rng, extent, cuts, least, high):
    def one(position, blocks):
        steps = jax.random.uniform(jax.random.fold_in(jax.random.fold_in(rng, 6), position), (blocks,), jnp.float32, least / len(cuts), high / len(cuts))
        return jnp.repeat(jnp.exp(steps), extent[position] // blocks).reshape((-1,) + (1,) * (len(extent) - position - 1))

    factor_of = one(*cuts[0])
    for cut in cuts[1:]:
        factor_of = factor_of * one(*cut)
    return factor_of


def scatter_about(key, shape, width, limit, pieces=(), held_as=jnp.bfloat16):
    gain = steps_of(key, shape, pieces, -0.22, 0.18) if pieces else 1.0
    entries = jax.random.normal(key, shape, jnp.float32) * width * gain
    return jnp.minimum(jnp.maximum(entries, -limit), limit).astype(held_as)


def setup_inputs(seed: int = 0) -> dict:
    seeds = jax.random.split(jax.random.key(seed), 15)
    return {
        "tokens": scatter_about(seeds[0], (ROWS, ROW, D), 1.0, 6.0, ((0, 16), (1, 2))),
        "seg_ids": draw_seg_ids(jax.random.fold_in(seeds[14], 71), 0),
        "doc_starts": draw_doc_starts(jax.random.fold_in(seeds[14], 71), 0),
        "gain_in": jnp.clip(1.0 + 0.18 * jax.random.normal(seeds[3], (D,), jnp.float32), 0.1, 1.9),
        "shift_in": scatter_about(seeds[4], (D,), 0.5, 3.0, (), jnp.float32),
        "w_query": scatter_about(seeds[5], (D, D), D ** -0.5, 0.21875),
        "w_key": scatter_about(seeds[6], (D, D), D ** -0.5, 0.21875),
        "w_value": scatter_about(seeds[7], (D, D), D ** -0.5, 0.21875),
        "w_out": scatter_about(seeds[8], (D, D), (D // 8) ** -0.5, 0.625),
        "gain_mid": jnp.clip(1.0 + 0.18 * jax.random.normal(seeds[9], (D,), jnp.float32), 0.1, 1.9),
        "shift_mid": scatter_about(seeds[10], (D,), 0.5, 3.0, (), jnp.float32),
        "w_up": scatter_about(seeds[11], (D, FF), D ** -0.5, 0.21875),
        "w_down": scatter_about(seeds[12], (FF, D), FF ** -0.5, 0.109375),
        "out_grad": scatter_about(seeds[13], (ROWS, ROW, D), 1.0, 6.0, ((0, 16), (1, 2))),
    }


EPS = 1e-05
NEGATIVE = -1e+30
HIGHEST = lax.Precision.HIGHEST
SELECT_SHIFT = 4.0

@jax.custom_vjp
def low(v):
    return lax.optimization_barrier(v.astype(jnp.bfloat16)).astype(jnp.float32)

@jax.custom_vjp
def low_back(v):
    return v

def low_keep(v):
    return (low(v), None)

def low_pass(kept, grad):
    return (grad,)

def back_keep(v):
    return (v, None)

def back_low(kept, grad):
    return (low(grad),)
low.defvjp(low_keep, low_pass)
low_back.defvjp(back_keep, back_low)

def layer_norm(field, gain_vec, offset):
    center = field - lax.optimization_barrier(jnp.mean(field, -1, keepdims=True))
    inverse = lax.rsqrt(lax.optimization_barrier(jnp.mean(center * center, -1, keepdims=True)) + EPS)
    return center * inverse * gain_vec + offset

def matmul(left, right):
    return jnp.dot(left, right, precision=HIGHEST)

def one_row(params, row_tokens, row_segs, row_starts):
    gain_in, shift_in, w_query, w_key, w_value, w_out, gain_mid, shift_mid, w_up, w_down = params
    length = row_tokens.shape[0]
    normed = low(layer_norm(row_tokens, gain_in, shift_in))
    queries = low_back(low(matmul(normed, w_query))).reshape(length, HEADS, HEAD)
    key_vecs = low_back(low(matmul(normed, w_key))).reshape(length, HEADS, HEAD)
    values = low_back(low(matmul(normed, w_value))).reshape(length, HEADS, HEAD)
    scores = low_back(jnp.einsum('qhd,khd->hqk', queries, key_vecs, precision=HIGHEST) * HEAD ** (-0.5))
    places = jnp.arange(length)
    same_doc = row_segs[:, None] == row_segs[None, :]
    allowed = same_doc & (places[None, :] <= places[:, None])
    after_key = same_doc & (places[None, :] < places[:, None])
    select = after_key & (row_starts == 0)[None, :]
    chosen = jnp.where(select, jax.nn.softplus(scores[0] - SELECT_SHIFT), 0.0)
    cumulated = jnp.concatenate([jnp.zeros((1, length), jnp.float32), jnp.cumsum(chosen, axis=0)[:-1]], axis=0)
    logits = jnp.where(allowed[None], scores - cumulated[None], NEGATIVE)
    weights = low(jax.nn.softmax(logits, axis=-1))
    heads_out = jnp.einsum('hqk,khd->qhd', weights, values, precision=HIGHEST).reshape(length, -1)
    low_out = low_back(low(heads_out))
    resid = row_tokens + low_back(matmul(low_out, w_out))
    normed_mid = low(layer_norm(resid, gain_mid, shift_mid))
    hidden = low(jax.nn.gelu(low_back(matmul(normed_mid, w_up)), approximate=True))
    result = resid + matmul(hidden, w_down)
    ratios = jnp.where(after_key, jax.nn.sigmoid(cumulated - 2.0), 0.0)
    share = lax.optimization_barrier(jnp.sum(ratios, 0)) / jnp.maximum(lax.optimization_barrier(jnp.sum(after_key.astype(jnp.float32), 0)), 1.0)
    return (result, share)

def reference(tokens, seg_ids, doc_starts, gain_in, shift_in, w_query, w_key, w_value, w_out, gain_mid, shift_mid, w_up, w_down, out_grad):
    params = tuple((member.astype(jnp.float32) for member in (gain_in, shift_in, w_query, w_key, w_value, w_out, gain_mid, shift_mid, w_up, w_down)))

    def forward(params, inputs):

        def per_row(slices):
            return jax.checkpoint(one_row)(params, slices[0], slices[1], slices[2])
        result, share = lax.map(per_row, (inputs, seg_ids, doc_starts))
        return (result, share)
    result, pullback, share = jax.vjp(forward, params, tokens.astype(jnp.float32), has_aux=True)
    grads, grad_tokens = pullback(out_grad.astype(jnp.float32))
    return (result.astype(jnp.bfloat16), grad_tokens.astype(jnp.bfloat16), share, grads[0], grads[1], grads[2], grads[3], grads[4], grads[5], grads[6], grads[7], grads[8], grads[9])
```

```python
import functools

import jax
import jax.numpy as jnp
from jax import lax
from jax.experimental import pallas as pl
from jax.experimental.pallas import tpu as pltpu
from jax.sharding import PartitionSpec as P

HEAD = 64


EPS = 1e-05
NEGATIVE = -1e30
HIGHEST = lax.Precision.HIGHEST
SELECT_SHIFT = 4.0


def joined(value, axis, join):
    pieces = jax.tree.map(lambda part: lax.all_gather(part, axis), value)
    head = jax.tree.map(lambda part: part[0], pieces)
    tail = jax.tree.map(lambda part: part[1:], pieces)
    so_far, _ = lax.scan(lambda so_far, section: (join(so_far, section), None), head, tail)
    return so_far


def layer_norm(field, gain_vec, offset):
    center = field - jnp.mean(field, -1, keepdims=True)
    inverse = lax.rsqrt(jnp.mean(center * center, -1, keepdims=True) + EPS)
    unit_rows = center * inverse
    return (unit_rows * gain_vec + offset, unit_rows, inverse)


def norm_back(gradient, unit_rows, inverse, gain_vec):
    scaled = gradient * gain_vec
    return inverse * (
        scaled
        - jnp.mean(scaled, -1, keepdims=True)
        - unit_rows * jnp.mean(scaled * unit_rows, -1, keepdims=True)
    )


def gelu_tanh(field):
    return jax.nn.gelu(field, approximate=True)


def transpose_dot(left, right):
    return jnp.einsum("ti,to->io", left, right, preferred_element_type=jnp.float32)


def right_dot(left, right):
    return jnp.einsum("ti,oi->to", left, right, preferred_element_type=jnp.float32)


def block_masks(context, seg_block, block_index):
    key_vecs, seg_keys, free_keys, key_pos, block_len, score_scale = context
    query_pos = block_index * block_len + jnp.arange(block_len)
    same_doc = seg_block[:, None] == seg_keys[None, :]
    allowed = same_doc & (key_pos[None, :] <= query_pos[:, None])
    after_key = same_doc & (key_pos[None, :] < query_pos[:, None])
    return (allowed, after_key, after_key & free_keys[None, :])


def block_scores(context, query_blk):
    key_vecs = context[0]
    return (
        jnp.einsum("qhd,khd->hqk", query_blk, key_vecs, preferred_element_type=jnp.float32)
        * context[5]
    )


def recompute(context, query_blk, seg_block, block_index, cumulated_blk):
    allowed, after_key, select = block_masks(context, seg_block, block_index)
    scores = block_scores(context, query_blk)
    logits = jnp.where(allowed[None], scores - cumulated_blk[None], NEGATIVE)
    return (scores, logits, select)


def block_inputs(query_rows, seg_row, block_len):
    blocks = query_rows.shape[0] // block_len
    return (
        query_rows.reshape(blocks, block_len, query_rows.shape[1], query_rows.shape[2]),
        seg_row.reshape(blocks, block_len),
        jnp.arange(blocks),
    )


def head_blocks(stat_rows, block_len):
    return stat_rows.reshape(stat_rows.shape[0], -1, block_len).transpose(1, 0, 2)


def forward_stats(context, query_rows, seg_row):
    block_len = context[4]
    key_len = context[0].shape[0]
    row_len = query_rows.shape[0]
    places = jnp.arange(block_len)
    lower_ones = (places[None, :] < places[:, None]).astype(jnp.float32)

    def scan_step(carried, inputs):
        running, numerator, pair_count = carried
        query_blk, seg_block, block_index = inputs
        allowed, after_key, select = block_masks(context, seg_block, block_index)
        scores = block_scores(context, query_blk)
        chosen = jnp.where(select, jax.nn.softplus(scores[0] - SELECT_SHIFT), 0.0)
        cumulated = running[None, :] + jnp.dot(lower_ones, chosen, precision=HIGHEST)
        logits = jnp.where(allowed[None], scores - cumulated[None], NEGATIVE)
        maxima = jnp.max(logits, -1)
        totals = jnp.sum(jnp.exp(logits - maxima[..., None]), -1)
        numerator = numerator + jnp.sum(
            jnp.where(after_key, jax.nn.sigmoid(cumulated - 2.0), 0.0), 0
        )
        pair_count = pair_count + jnp.sum(after_key.astype(jnp.float32), 0)
        return ((running + jnp.sum(chosen, 0), numerator, pair_count), (cumulated, maxima, totals))

    zeros = jnp.zeros((key_len,), jnp.float32)
    (_, numerator, pair_count), (cumulated, maxima, totals) = lax.scan(
        scan_step, (zeros, zeros, zeros), block_inputs(query_rows, seg_row, block_len)
    )
    head_count = maxima.shape[1]
    maxima = maxima.transpose(1, 0, 2).reshape(head_count, row_len)
    totals = totals.transpose(1, 0, 2).reshape(head_count, row_len)
    share = numerator / jnp.maximum(pair_count, 1.0)
    return (cumulated.reshape(row_len, key_len), maxima, totals, share)


def forward_values(context, values, query_rows, seg_row, cumulated, log_sums):
    block_len = context[4]
    blocks = query_rows.shape[0] // block_len

    def scan_step(carried, inputs):
        query_blk, seg_block, block_index, cumulated_blk, log_blk = inputs
        scores, logits, select = recompute(
            context, query_blk, seg_block, block_index, cumulated_blk
        )
        weights = jnp.exp(logits - log_blk[..., None]).astype(jnp.bfloat16)
        head_sums = jnp.einsum("hqk,khd->qhd", weights, values, preferred_element_type=jnp.float32)
        return (carried, head_sums.reshape(block_len, -1))

    inputs = block_inputs(query_rows, seg_row, block_len) + (
        cumulated.reshape(blocks, block_len, -1),
        head_blocks(log_sums, block_len),
    )
    _, outputs = lax.scan(scan_step, jnp.zeros((), jnp.float32), inputs)
    return outputs.reshape(query_rows.shape[0], -1)


def delta_terms(context, values, query_rows, seg_row, cumulated, log_sums, dout_rows):
    block_len = context[4]
    blocks = query_rows.shape[0] // block_len

    def scan_step(carried, inputs):
        query_blk, seg_block, block_index, cumulated_blk, log_blk, dout_blk = inputs
        scores, logits, select = recompute(
            context, query_blk, seg_block, block_index, cumulated_blk
        )
        weights = jnp.exp(logits - log_blk[..., None])
        grad_weights = jnp.einsum(
            "qhd,khd->hqk", dout_blk, values, preferred_element_type=jnp.float32
        )
        return (carried, jnp.sum(weights * grad_weights, -1))

    inputs = block_inputs(query_rows, seg_row, block_len) + (
        cumulated.reshape(blocks, block_len, -1),
        head_blocks(log_sums, block_len),
        dout_rows.reshape(blocks, block_len, dout_rows.shape[1], dout_rows.shape[2]),
    )
    _, terms = lax.scan(scan_step, jnp.zeros((), jnp.float32), inputs)
    return terms.transpose(1, 0, 2).reshape(terms.shape[1], -1)


def backward_row(context, values, query_rows, seg_row, cumulated, log_sums, dout_rows, deltas):
    key_vecs, block_len, score_scale = (context[0], context[4], context[5])
    blocks = query_rows.shape[0] // block_len
    places = jnp.arange(block_len)
    upper_ones = (places[None, :] > places[:, None]).astype(jnp.float32)

    def scan_step(carried, inputs):
        later_sum, key_grad, value_grad = carried
        query_blk, seg_block, block_index, cumulated_blk, log_blk, dout_blk, delta_blk = inputs
        scores, logits, select = recompute(
            context, query_blk, seg_block, block_index, cumulated_blk
        )
        weights = jnp.exp(logits - log_blk[..., None])
        grad_weights = jnp.einsum(
            "qhd,khd->hqk", dout_blk, values, preferred_element_type=jnp.float32
        )
        grad_logits = weights * (grad_weights - delta_blk[..., None])
        grad_cumulated = -jnp.sum(grad_logits, 0)
        grad_chosen = later_sum[None, :] + jnp.dot(upper_ones, grad_cumulated, precision=HIGHEST)
        extra = jnp.where(select, grad_chosen * jax.nn.sigmoid(scores[0] - SELECT_SHIFT), 0.0)
        grad_scores = grad_logits.at[0].add(extra).astype(jnp.bfloat16)
        query_grad = (
            jnp.einsum("hqk,khd->qhd", grad_scores, key_vecs, preferred_element_type=jnp.float32)
            * score_scale
        )
        key_grad = (
            key_grad
            + jnp.einsum("hqk,qhd->khd", grad_scores, query_blk, preferred_element_type=jnp.float32)
            * score_scale
        )
        value_grad = value_grad + jnp.einsum(
            "hqk,qhd->khd",
            weights.astype(jnp.bfloat16),
            dout_blk,
            preferred_element_type=jnp.float32,
        )
        return (
            (later_sum + jnp.sum(grad_cumulated, 0), key_grad, value_grad),
            query_grad.reshape(block_len, -1),
        )

    inputs = block_inputs(query_rows, seg_row, block_len) + (
        cumulated.reshape(blocks, block_len, -1),
        head_blocks(log_sums, block_len),
        dout_rows.reshape(blocks, block_len, dout_rows.shape[1], dout_rows.shape[2]),
        head_blocks(deltas, block_len),
    )
    zeros = jnp.zeros(key_vecs.shape, jnp.float32)
    start_sum = jnp.zeros((key_vecs.shape[0],), jnp.float32)
    (_, key_grad, value_grad), query_grad = lax.scan(
        scan_step, (start_sum, zeros, zeros), inputs, reverse=True
    )
    return (query_grad.reshape(query_rows.shape[0], -1), key_grad, value_grad)


def combine_stats(first_stats, second_stats):
    maxima = jnp.maximum(first_stats[0], second_stats[0])
    totals = first_stats[1] * jnp.exp(first_stats[0] - maxima) + second_stats[1] * jnp.exp(
        second_stats[0] - maxima
    )
    return (maxima, totals)


MESH = pl.DeviceIdType.MESH


def grid_of(rows):
    short = round((rows / 2) ** (1 / 3))
    return (2 * short, short, short) if 2 * short**3 == rows else (rows, 1, 1)


def place(grid):
    _, wide, deep = grid
    me, core = lax.axis_index("rows"), lax.axis_index("keys")
    slow, mid, fast = me // (wide * deep), (me // deep) % wide, me % deep
    return slow, fast + core * (mid - fast), mid + core * (fast - mid), core


def rank_of(grid, slow, first, second, core):
    mid, fast = second + core * (first - second), first + core * (second - first)
    return (slow * grid[1] + mid) * grid[2] + fast


def reduce_kernel(grid, count, *refs):
    parts, refs = refs[:count], refs[count:]
    outs, refs = refs[:count], refs[count:]
    got1, refs = refs[:count], refs[count:]
    sum1, refs = refs[:count], refs[count:]
    got2, refs = refs[:count], refs[count:]
    sum2, refs = refs[:count], refs[count:]
    got3, refs = refs[:count], refs[count:]
    mine, refs = refs[:count], refs[count:]
    pair, refs = refs[:count], refs[count:]
    send1, recv1, send2, recv2, send3, recv3, send4, recv4 = refs
    long, wide, deep = grid
    slow, first, second, core = place(grid)

    def peers(size, here, target):
        return [target(lax.rem(here + step, size)) for step in range(1, size)]

    near = peers(wide, first, lambda p: (p, rank_of(grid, slow, p, second, core)))
    next_ = peers(deep, second, lambda p: (p, rank_of(grid, slow, first, p, core)))
    far = peers(long, slow, lambda p: (p, rank_of(grid, p, first, second, core)))
    me = rank_of(grid, slow, first, second, core)
    other = 1 - core

    barrier = pltpu.get_barrier_semaphore()
    for _, rank in near + next_ + far:
        pl.semaphore_signal(barrier, inc=1, device_id=(rank, core), device_id_type=MESH)
    pl.semaphore_signal(barrier, inc=1, device_id=(me, other), device_id_type=MESH)
    pl.semaphore_wait(barrier, len(near) + len(next_) + len(far) + 1)

    def copy(source, target, send, recv, device):
        return pltpu.make_async_remote_copy(
            src_ref=source,
            dst_ref=target,
            send_sem=send,
            recv_sem=recv,
            device_id=device,
            device_id_type=MESH,
        )

    first_copies = [
        [
            copy(
                parts[j].at[:, p], got1[j].at[i], send1.at[j, i], recv1.at[j, i], (rank, core)
            )
            for i, (p, rank) in enumerate(near)
        ]
        for j in range(count)
    ]
    for group in first_copies:
        for one in group:
            one.start()
    second_copies = []
    for j in range(count):
        for one in first_copies[j]:
            one.wait_recv()

        @pl.loop(0, long * deep)
        def _(step, j=j):
            a, b = step // deep, step % deep
            total = parts[j][a, first, b].astype(jnp.float32)
            for i in range(len(near)):
                total = total + got1[j][i, a, b].astype(jnp.float32)
            sum1[j][a, b] = total.astype(sum1[j].dtype)

        group = [
            copy(sum1[j].at[:, p], got2[j].at[i], send2.at[j, i], recv2.at[j, i], (rank, core))
            for i, (p, rank) in enumerate(next_)
        ]
        for one in group:
            one.start()
        second_copies.append(group)
    third_copies = []
    for j in range(count):
        for one in second_copies[j]:
            one.wait_recv()

        @pl.loop(0, long)
        def _(a, j=j):
            total = sum1[j][a, second].astype(jnp.float32)
            for i in range(len(next_)):
                total = total + got2[j][i, a].astype(jnp.float32)
            sum2[j][a] = total.astype(sum2[j].dtype)

        group = [
            copy(sum2[j].at[p], got3[j].at[i], send3.at[j, i], recv3.at[j, i], (rank, core))
            for i, (p, rank) in enumerate(far)
        ]
        for one in group:
            one.start()
        third_copies.append(group)
    last_copies = []
    for j in range(count):
        for one in third_copies[j]:
            one.wait_recv()
        total = sum2[j][slow].astype(jnp.float32)
        for i in range(len(far)):
            total = total + got3[j][i].astype(jnp.float32)
        mine[j][...] = total.astype(mine[j].dtype)
        one = copy(mine[j], pair[j], send4.at[j], recv4.at[j], (me, other))
        one.start()
        last_copies.append(one)
    for j in range(count):
        last_copies[j].wait_recv()
        own, their = mine[j][...].astype(jnp.float32), pair[j][...].astype(jnp.float32)
        height, width = own.shape
        if j == count - 1:
            outs[j][...] = own + their
        else:
            outs[j][:, pl.ds(pl.multiple_of(core * width, 128), width)] = own
            outs[j][:, pl.ds(pl.multiple_of(other * width, 128), width)] = their
    for group in first_copies + second_copies + third_copies + [last_copies]:
        for one in group:
            one.wait_send()


def reduce_rows(halves, norm_grads, rows):
    grid = grid_of(rows)
    long, wide, deep = grid
    core = lax.axis_index("keys")
    parts, heights = [], []
    for half in halves:
        height = half.shape[0] // rows
        padded = -(-height // 16) * 16
        part = half.reshape(rows, height, half.shape[1])
        parts.append(jnp.pad(part, ((0, 0), (0, padded - height), (0, 0))))
        heights.append(height)
    vectors = norm_grads.reshape(rows, -1, 4).transpose(0, 2, 1)
    span = vectors.shape[2]
    parts.append(jnp.pad(vectors, ((0, 0), (0, 4), (0, 128 - span))))
    count = len(parts)
    blocks = [part.shape[1:] for part in parts]
    ordered = []
    for part, block in zip(parts, blocks):
        cube = part.reshape((long, wide, deep) + block)
        ordered.append(jnp.where(core == 0, cube.swapaxes(1, 2), cube))
    scratch = []
    dtypes = [part.dtype for part in parts]
    for lead in (
        (max(wide - 1, 1), long, deep),
        (long, deep),
        (max(deep - 1, 1), long),
        (long,),
        (max(long - 1, 1),),
        (),
        (),
    ):
        scratch += [pltpu.VMEM(lead + block, kind) for block, kind in zip(blocks, dtypes)]
    for peers in (wide - 1, deep - 1, long - 1):
        scratch += [pltpu.SemaphoreType.DMA((count, max(peers, 1)))] * 2
    scratch += [pltpu.SemaphoreType.DMA((count,))] * 2
    out_shape = [
        jax.ShapeDtypeStruct((block[0], block[1] * (1 if j == count - 1 else 2)), jnp.float32)
        for j, block in enumerate(blocks)
    ]
    results = pl.pallas_call(
        functools.partial(reduce_kernel, grid, count),
        out_shape=out_shape,
        in_specs=[pl.BlockSpec(memory_space=pltpu.VMEM)] * count,
        out_specs=[pl.BlockSpec(memory_space=pltpu.VMEM)] * count,
        scratch_shapes=scratch,
        compiler_params=pltpu.CompilerParams(
            collective_id=0, has_side_effects=True, vmem_limit_bytes=60 * 1024 * 1024
        ),
        name="reduce_rows",
    )(*ordered)
    summed = [result[:height] for result, height in zip(results, heights)]
    return summed, results[-1][:4, :span].T


def body(
    rows,
    tokens,
    seg_ids,
    doc_starts,
    gain_in,
    shift_in,
    w_query,
    w_key,
    w_value,
    w_out,
    gain_mid,
    shift_mid,
    w_up,
    w_down,
    out_grad,
):
    row_count, key_len, width = tokens.shape
    row_len = seg_ids.shape[1]
    head_count = width // HEAD
    score_scale = HEAD ** (-0.5)
    block_len = min(512, row_len)
    key_first = lax.axis_index("keys") * key_len
    key_pos = key_first + jnp.arange(key_len)
    seg_keys = lax.dynamic_slice_in_dim(seg_ids, key_first, key_len, 1)
    free_keys = doc_starts == 0
    token_count = row_count * key_len
    flat_in = tokens.reshape(token_count, width).astype(jnp.float32)
    normed_in, unit_in, inverse_in = layer_norm(flat_in, gain_in, shift_in)
    low_in = normed_in.astype(jnp.bfloat16)
    queries = jnp.dot(low_in, w_query, preferred_element_type=jnp.float32).astype(jnp.bfloat16)
    key_vecs = (
        jnp.dot(low_in, w_key, preferred_element_type=jnp.float32)
        .astype(jnp.bfloat16)
        .reshape(row_count, key_len, head_count, HEAD)
    )
    values = (
        jnp.dot(low_in, w_value, preferred_element_type=jnp.float32)
        .astype(jnp.bfloat16)
        .reshape(row_count, key_len, head_count, HEAD)
    )
    query_all = lax.all_gather(
        queries.reshape(row_count, key_len, width), "keys", axis=1, tiled=True
    ).reshape(row_count, row_len, head_count, HEAD)
    row_index = 0
    context = (
        key_vecs[row_index],
        seg_keys[row_index],
        free_keys[row_index],
        key_pos,
        block_len,
        score_scale,
    )
    contexts = [context]
    cumulated, maxima, totals, share = forward_stats(
        context, query_all[row_index], seg_ids[row_index]
    )
    cumulated_list = [cumulated]
    maxima_list = [maxima]
    totals_list = [totals]
    share_list = [share]
    maxima, totals = joined((jnp.stack(maxima_list), jnp.stack(totals_list)), "keys", combine_stats)
    log_sums = maxima + jnp.log(totals)
    head_parts = jnp.stack(
        [
            forward_values(
                contexts[0], values[0], query_all[0], seg_ids[0], cumulated_list[0], log_sums[0]
            )
        ]
    )
    head_out = lax.psum_scatter(
        head_parts.astype(jnp.bfloat16), "keys", scatter_dimension=1, tiled=True
    ).astype(jnp.float32)
    low_out = head_out.reshape(token_count, width).astype(jnp.bfloat16)
    resid = flat_in + jnp.dot(low_out, w_out, preferred_element_type=jnp.float32)
    normed_mid, unit_mid, inverse_mid = layer_norm(resid, gain_mid, shift_mid)
    low_mid = normed_mid.astype(jnp.bfloat16)
    upward = jnp.dot(low_mid, w_up, preferred_element_type=jnp.float32)
    hidden = gelu_tanh(upward).astype(jnp.bfloat16)
    output = (resid + jnp.dot(hidden, w_down, preferred_element_type=jnp.float32)).astype(
        jnp.bfloat16
    )
    cotangent = out_grad.reshape(token_count, width)
    grad_down = transpose_dot(hidden, cotangent)
    grad_hidden = right_dot(cotangent, w_down)
    _, pullback = jax.vjp(gelu_tanh, upward)
    grad_upward = pullback(grad_hidden)[0].astype(jnp.bfloat16)
    grad_up = transpose_dot(low_mid, grad_upward)
    grad_mid = right_dot(grad_upward, w_up)
    grad_resid = cotangent.astype(jnp.float32) + norm_back(
        grad_mid, unit_mid, inverse_mid, gain_mid
    )
    low_resid = grad_resid.astype(jnp.bfloat16)
    grad_outproj = transpose_dot(low_out, low_resid)
    grad_heads = right_dot(low_resid, w_out).astype(jnp.bfloat16)
    dout_all = lax.all_gather(
        grad_heads.reshape(row_count, key_len, width), "keys", axis=1, tiled=True
    ).reshape(row_count, row_len, head_count, HEAD)
    delta_parts = jnp.stack(
        [
            delta_terms(
                contexts[0],
                values[0],
                query_all[0],
                seg_ids[0],
                cumulated_list[0],
                log_sums[0],
                dout_all[0],
            )
        ]
    )
    deltas = lax.psum(delta_parts, "keys")
    row_index = 0
    query_grad, key_grad, value_grad = backward_row(
        contexts[row_index],
        values[row_index],
        query_all[row_index],
        seg_ids[row_index],
        cumulated_list[row_index],
        log_sums[row_index],
        dout_all[row_index],
        deltas[row_index],
    )
    query_parts = [query_grad]
    key_grads = [key_grad]
    value_grads = [value_grad]
    query_own = lax.psum_scatter(
        jnp.stack(query_parts).astype(jnp.bfloat16), "keys", scatter_dimension=1, tiled=True
    ).astype(jnp.float32)
    low_query_grad = query_own.reshape(token_count, width).astype(jnp.bfloat16)
    low_key_grad = jnp.stack(key_grads).reshape(token_count, width).astype(jnp.bfloat16)
    low_value_grad = jnp.stack(value_grads).reshape(token_count, width).astype(jnp.bfloat16)
    grad_query = transpose_dot(low_in, low_query_grad)
    grad_key = transpose_dot(low_in, low_key_grad)
    grad_value = transpose_dot(low_in, low_value_grad)
    grad_norm = (
        right_dot(low_query_grad, w_query)
        + right_dot(low_key_grad, w_key)
        + right_dot(low_value_grad, w_value)
    )
    grad_tokens = (
        (grad_resid + norm_back(grad_norm, unit_in, inverse_in, gain_in))
        .astype(jnp.bfloat16)
        .reshape(row_count, key_len, width)
    )
    norm_grads = jnp.stack(
        [
            jnp.sum(grad_norm * unit_in, 0),
            jnp.sum(grad_norm, 0),
            jnp.sum(grad_mid * unit_mid, 0),
            jnp.sum(grad_mid, 0),
        ],
        1,
    )
    halves = (
        lax.psum_scatter(
            grad_query.astype(jnp.bfloat16), "keys", scatter_dimension=1, tiled=True
        ),
        lax.psum_scatter(grad_key.astype(jnp.bfloat16), "keys", scatter_dimension=1, tiled=True),
        lax.psum_scatter(
            grad_value.astype(jnp.bfloat16), "keys", scatter_dimension=1, tiled=True
        ),
        lax.psum_scatter(
            grad_outproj.astype(jnp.bfloat16), "keys", scatter_dimension=1, tiled=True
        ),
        lax.psum_scatter(grad_up.astype(jnp.bfloat16), "keys", scatter_dimension=1, tiled=True),
        lax.psum_scatter(grad_down.astype(jnp.bfloat16), "keys", scatter_dimension=1, tiled=True),
    )
    summed, norm_sums = reduce_rows(halves, norm_grads, rows)
    key_share = jnp.stack(share_list)
    return (
        output.reshape(row_count, key_len, width),
        grad_tokens,
        key_share,
        norm_sums[:, 0],
        norm_sums[:, 1],
        summed[0],
        summed[1],
        summed[2],
        summed[3],
        norm_sums[:, 2],
        norm_sums[:, 3],
        summed[4],
        summed[5],
    )


def solution(mesh):
    in_specs = (
        P("rows", "keys", None),
        P("rows", None),
        P("rows", "keys"),
        P(),
        P(),
        P(),
        P(),
        P(),
        P(),
        P(),
        P(),
        P(),
        P(),
        P("rows", "keys", None),
    )
    out_specs = (
        P("rows", "keys", None),
        P("rows", "keys", None),
        P("rows", "keys"),
        P("rows"),
        P("rows"),
        P("rows", None),
        P("rows", None),
        P("rows", None),
        P("rows", None),
        P("rows"),
        P("rows"),
        P("rows", None),
        P("rows", None),
    )
    return jax.shard_map(
        functools.partial(body, mesh.shape["rows"]), mesh=mesh, in_specs=in_specs, out_specs=out_specs, check_vma=False
    )
```

```python
import functools

import jax
import jax.numpy as jnp
from jax import lax
from jax.experimental import pallas as pl
from jax.experimental.pallas import tpu as pltpu
from jax.sharding import PartitionSpec as P

HEAD = 64
PAIR = 2 * HEAD
TILE = 256
EPS = 1e-05
MASKED = 1e30
SELECT_SHIFT = 4.0
LOW = jnp.bfloat16
FULL = jnp.float32
MESH = pl.DeviceIdType.MESH
VMEM_LIMIT = 62 * 1024 * 1024


def contract(left, right, left_dim, right_dim):
    return lax.dot_general(
        left, right, (((left_dim,), (right_dim,)), ((), ())), preferred_element_type=FULL
    )


def layer_norm(field):
    center = field - jnp.mean(field, -1, keepdims=True)
    inverse = lax.rsqrt(jnp.mean(center * center, -1, keepdims=True) + EPS)
    return center * inverse, inverse


def remote(source, target, send, recv, device):
    return pltpu.make_async_remote_copy(
        src_ref=source,
        dst_ref=target,
        send_sem=send,
        recv_sem=recv,
        device_id=device,
        device_id_type=MESH,
    )


def lanes_below(shape, bound):
    return lax.broadcasted_iota(jnp.int32, shape, len(shape) - 1) < bound


def rows_of(start, size):
    return pl.ds(pl.multiple_of(start, size), size)


def attend_kernel(
    tokens,
    seg,
    gain,
    shift,
    w_query,
    w_key,
    w_value,
    low_in_out,
    query_out,
    key_out,
    value_out,
    prob_outs,
    slope_outs,
    heads_out,
    other_out,
    share_out,
    far_tokens,
    low_in,
    weights,
    queries,
    keys,
    values,
    lead_query,
    lead_key,
    probs,
    slopes,
    penalty,
    heads,
    seg_cols,
    free_cols,
    running,
    numerator,
    pairs_seen,
    far_send,
    far_recv,
    head_send,
    head_recv,
    weight_sems,
    out_sems,
    prob_sems,
):
    core = lax.axis_index("keys")
    row = lax.axis_index("rows")
    other = 1 - core
    partner = (row, other)
    half, width = tokens.shape
    length = 2 * half
    mine = width // 2
    pair_count = mine // PAIR
    tiles = length // TILE

    columns = pl.ds(pl.multiple_of(core * mine, 128), mine)
    loads = []
    for place, source in enumerate((w_query, w_key, w_value)):
        loads.append((source.at[:, columns], weights.at[:, pl.ds(place * mine, mine)]))
    for place, source in enumerate((w_query, w_key)):
        loads.append(
            (source.at[:, pl.ds(0, PAIR)], weights.at[:, pl.ds(3 * mine + place * PAIR, PAIR)])
        )
    loads = [
        pltpu.make_async_copy(source, target, weight_sems.at[i])
        for i, (source, target) in enumerate(loads)
    ]
    for one in loads:
        one.start()

    barrier = pltpu.get_barrier_semaphore()
    pl.semaphore_signal(barrier, inc=1, device_id=partner, device_id_type=MESH)
    pl.semaphore_wait(barrier, 1)
    exchange = remote(tokens, far_tokens, far_send, far_recv, partner)
    exchange.start()

    seg_row = seg[...]
    seg_wide = jnp.broadcast_to(seg_row.astype(FULL), (128, length))
    spot = lax.broadcasted_iota(jnp.int32, (128, length), 1)
    before = pltpu.roll(seg_wide, 1, 1)
    free_wide = jnp.where((spot > 0) & (before == seg_wide), 1.0, 0.0)
    seg_cols[...] = seg_wide.T
    free_cols[...] = free_wide.T

    def normalize(source, place):
        for step in range(half // TILE):
            unit, _ = layer_norm(source[pl.ds(step * TILE, TILE), :].astype(FULL))
            low_in[rows_of(place + step * TILE, TILE), :] = (
                unit * gain[...] + shift[...]
            ).astype(LOW)

    def project(place):
        for step in range(half // TILE):
            here = rows_of(place + step * TILE, TILE)
            result = contract(low_in[here, :], weights[...], 1, 0).astype(LOW)
            for p in range(pair_count):
                queries[p, here, :] = result[:, p * PAIR : (p + 1) * PAIR] * LOW(0.125)
                keys[p, here, :] = result[:, mine + p * PAIR : mine + (p + 1) * PAIR]
                values[p, here, :] = result[:, 2 * mine + p * PAIR : 2 * mine + (p + 1) * PAIR]
            keep = lanes_below((TILE, PAIR), HEAD)
            first = result[:, 3 * mine : 3 * mine + PAIR]
            lead_query[here, :] = jnp.where(keep, first, LOW(0.0)) * LOW(0.125)
            lead_key[here, :] = result[:, 3 * mine + PAIR :]

    normalize(tokens, core * half)
    for one in loads:
        one.wait()
    project(core * half)
    exchange.wait_recv()
    normalize(far_tokens, other * half)
    project(other * half)

    puts = [
        pltpu.make_async_copy(low_in, low_in_out, out_sems.at[0]),
        pltpu.make_async_copy(queries, query_out, out_sems.at[1]),
        pltpu.make_async_copy(keys, key_out, out_sems.at[2]),
        pltpu.make_async_copy(values, value_out, out_sems.at[3]),
    ]
    for one in puts:
        one.start()

    spots = (
        lax.broadcasted_iota(jnp.int32, (TILE, TILE), 0),
        lax.broadcasted_iota(jnp.int32, (TILE, TILE), 1),
    )
    earlier = jnp.where(spots[0] < spots[1], 1.0, 0.0).astype(LOW)
    running[...] = jnp.zeros_like(running)
    numerator[...] = jnp.zeros_like(numerator)
    pairs_seen[...] = jnp.zeros_like(pairs_seen)
    for t in range(tiles):
        count = (t + 1) * TILE
        span = pl.ds(t * TILE, TILE)
        shape = (count, TILE)
        scores = contract(lead_key[pl.ds(0, count), :], lead_query[span, :], 1, 1)
        same = seg_cols[pl.ds(0, count), 0:1] == seg[:, span].astype(FULL)
        key_spot = lax.broadcasted_iota(jnp.int32, shape, 0)
        query_spot = lax.broadcasted_iota(jnp.int32, shape, 1) + t * TILE
        later = same & (key_spot < query_spot)
        allowed = same & (key_spot <= query_spot)
        select = jnp.where(later, free_cols[pl.ds(0, count), 0:1], 0.0)
        level = scores - SELECT_SHIFT
        small = jnp.exp(-jnp.abs(level))
        chosen = select * (jnp.maximum(level, 0.0) + jnp.log1p(small))
        slopes[t][...] = (
            select * jnp.where(level >= 0.0, 1.0, small) / (1.0 + small)
        ).astype(LOW)
        high = chosen.astype(LOW)
        rest = (chosen - high.astype(FULL)).astype(LOW)
        total = (
            running[pl.ds(0, count), :]
            + contract(high, earlier, 1, 0)
            + contract(rest, earlier, 1, 0)
        )
        penalty[pl.ds(0, count), span] = jnp.where(allowed, total, MASKED)
        running[pl.ds(0, count), :] += jnp.sum(chosen, -1, keepdims=True)
        share = 1.0 / (1.0 + jnp.exp(2.0 - total))
        numerator[pl.ds(0, count), :] += jnp.sum(jnp.where(later, share, 0.0), -1, keepdims=True)
        pairs_seen[pl.ds(0, count), :] += jnp.sum(jnp.where(later, 1.0, 0.0), -1, keepdims=True)
    slope_puts = [
        pltpu.make_async_copy(slopes[t], slope_outs[t], out_sems.at[4 + t]) for t in range(tiles)
    ]
    for one in slope_puts:
        one.start()

    own = rows_of(core * half, half)
    shares = numerator[own, :] / jnp.maximum(pairs_seen[own, :], 1.0)
    share_out[...] = jnp.broadcast_to(shares, (half, 128)).T[0:8, :]

    def put_probs(p, t):
        return pltpu.make_async_copy(
            probs[t].at[p], prob_outs[t].at[p], prob_sems.at[p, t]
        )

    def send_heads(p):
        return remote(
            heads.at[p, rows_of(other * half, half)],
            other_out.at[p],
            head_send.at[p],
            head_recv.at[p],
            partner,
        )

    @pl.loop(0, pair_count)
    def _(p):
        for t in range(tiles):
            count = (t + 1) * TILE
            span = pl.ds(t * TILE, TILE)
            query = queries[p, span, :]
            keep = lanes_below((TILE, PAIR), HEAD)
            outs = []
            for h in range(2):
                masked = jnp.where(keep == (h == 0), query, LOW(0.0))
                logits = (
                    contract(keys[p, pl.ds(0, count), :], masked, 1, 1)
                    - penalty[pl.ds(0, count), span]
                )
                scaled = jnp.exp(logits - jnp.max(logits, 0, keepdims=True))
                prob = (scaled * (1.0 / jnp.sum(scaled, 0, keepdims=True))).astype(LOW)
                probs[t][p, :, pl.ds(h * TILE, TILE)] = prob
                out = contract(values[p, pl.ds(0, count), :], prob, 0, 0)
                outs.append(out[h * HEAD : (h + 1) * HEAD, :])
            heads[p, span, :] = jnp.concatenate(outs, 0).T.astype(LOW)
            put_probs(p, t).start()
        send_heads(p).start()

    last = pltpu.make_async_copy(heads, heads_out, out_sems.at[4 + tiles])
    last.start()
    for p in range(pair_count):
        send_heads(p).wait()
        for t in range(tiles):
            put_probs(p, t).wait()
    for one in puts + slope_puts + [last]:
        one.wait()
    exchange.wait_send()


def attend(tokens, seg, gain, shift, w_query, w_key, w_value):
    half, width = tokens.shape
    length, mine = 2 * half, width // 2
    pairs, tiles = mine // PAIR, 2 * half // TILE
    spans = [(t + 1) * TILE for t in range(tiles)]
    outs = [
        jax.ShapeDtypeStruct((length, width), LOW),
        jax.ShapeDtypeStruct((pairs, length, PAIR), LOW),
        jax.ShapeDtypeStruct((pairs, length, PAIR), LOW),
        jax.ShapeDtypeStruct((pairs, length, PAIR), LOW),
        [jax.ShapeDtypeStruct((pairs, span, 2 * TILE), LOW) for span in spans],
        [jax.ShapeDtypeStruct((span, TILE), LOW) for span in spans],
        jax.ShapeDtypeStruct((pairs, length, PAIR), LOW),
        jax.ShapeDtypeStruct((pairs, half, PAIR), LOW),
        jax.ShapeDtypeStruct((8, half), FULL),
    ]
    anywhere = pl.BlockSpec(memory_space=pl.ANY)
    local = pl.BlockSpec(memory_space=pltpu.VMEM)
    out_specs = [anywhere] * 4 + [[anywhere] * tiles, [anywhere] * tiles, anywhere, anywhere, local]
    scratch = [
        pltpu.VMEM((half, width), LOW),
        pltpu.VMEM((length, width), LOW),
        pltpu.VMEM((width, 3 * mine + 2 * PAIR), LOW),
        pltpu.VMEM((pairs, length, PAIR), LOW),
        pltpu.VMEM((pairs, length, PAIR), LOW),
        pltpu.VMEM((pairs, length, PAIR), LOW),
        pltpu.VMEM((length, PAIR), LOW),
        pltpu.VMEM((length, PAIR), LOW),
        [pltpu.VMEM((pairs, span, 2 * TILE), LOW) for span in spans],
        [pltpu.VMEM((span, TILE), LOW) for span in spans],
        pltpu.VMEM((length, length), FULL),
        pltpu.VMEM((pairs, length, PAIR), LOW),
        pltpu.VMEM((length, 128), FULL),
        pltpu.VMEM((length, 128), FULL),
        pltpu.VMEM((length, 1), FULL),
        pltpu.VMEM((length, 1), FULL),
        pltpu.VMEM((length, 1), FULL),
        pltpu.SemaphoreType.DMA,
        pltpu.SemaphoreType.DMA,
        pltpu.SemaphoreType.DMA((pairs,)),
        pltpu.SemaphoreType.DMA((pairs,)),
        pltpu.SemaphoreType.DMA((5,)),
        pltpu.SemaphoreType.DMA((5 + tiles,)),
        pltpu.SemaphoreType.DMA((pairs, tiles)),
    ]
    return pl.pallas_call(
        attend_kernel,
        out_shape=outs,
        in_specs=[local] * 4 + [anywhere] * 3,
        out_specs=out_specs,
        scratch_shapes=scratch,
        compiler_params=pltpu.CompilerParams(
            collective_id=1, has_side_effects=True, vmem_limit_bytes=VMEM_LIMIT
        ),
        name="attend",
    )(tokens, seg, gain, shift, w_query, w_key, w_value)

def gelu_parts(field):
    scale = 0.7978845608028654
    square = field * field
    inner = jnp.tanh(scale * field * (1.0 + 0.044715 * square))
    half_sum = 0.5 * (1.0 + inner)
    slope = half_sum + 0.5 * field * (1.0 - inner * inner) * (
        scale * (1.0 + 3.0 * 0.044715 * square)
    )
    return field * half_sum, slope


GRID = (4, 2, 2)
COUNT = GRID[0] * GRID[1] * GRID[2]
KINDS = ("down", "up", "out", "attn", "vec")
FAN = {"down": 1, "up": 2, "out": 1, "attn": 3, "vec": 1}


def block_shapes(width, hidden):
    mine = width // 2
    tall = width // COUNT
    return {
        "down": ((hidden // COUNT, mine), LOW),
        "up": ((tall, mine * 2), LOW),
        "out": ((tall, mine), LOW),
        "attn": ((tall, mine), LOW),
        "vec": ((8, 128), FULL),
    }


def finish_kernel(fused, *refs):
    refs = list(refs)

    def take(count):
        taken = refs[:count]
        del refs[:count]
        return taken if count > 1 else taken[0]

    tokens, cotangent, gain_in, gain_mid, shift_mid = take(5)
    low_in_hbm, query_hbm, key_hbm, value_hbm = take(4)
    prob_hbm, slope_hbm = take(4), take(4)
    heads_hbm, other_hbm = take(2)
    w_query, w_key, w_value, w_out, w_up, w_down = take(6)
    output, input_grad = take(2)
    results = dict(zip(KINDS, take(len(KINDS))))
    (
        grads_all,
        weight_out,
        heads,
        heads_far,
        resid,
        low_mid,
        grad_resid,
        low_resid,
        grad_heads,
        low_in,
        queries,
        keys,
        values,
    ) = take(13)
    probs = take(4)
    share_send, share_recv = take(4), take(4)
    stage, catch_mid, catch_out = take(3)
    stage_down, stage_out = take(2)
    vec_sums = take(1)
    parts = dict(zip(KINDS, take(len(KINDS))))
    if fused:
        got1 = dict(zip(KINDS, take(len(KINDS))))
        got2 = dict(zip(KINDS, take(len(KINDS))))
        got3 = dict(zip(KINDS, take(len(KINDS))))
        pair = dict(zip(KINDS, take(len(KINDS))))
        sems = {
            name: take(2) for name in ("down1", "down2", "down3", "down4")
        }
        for kind in KINDS[1:]:
            for stage_name in "1234":
                sems[kind + stage_name] = take(2)
    (load_sems, g_sems, mid_sems, dz_sems, a_sems, b_sems, c_sems, pd_sems, po_sems, df_sems, prob_sems) = take(11)

    long, wide, deep = GRID
    core = lax.axis_index("keys")
    row = lax.axis_index("rows")
    other = 1 - core
    partner = (row, other)
    half, width = tokens.shape
    length, mine = 2 * half, width // 2
    pair_count = mine // PAIR
    tiles = length // TILE
    hidden = w_down.shape[0]
    block = hidden // 4
    own_start, far_start = core * half, other * half

    if fused:
        slow, mid, fast = row // (wide * deep), (row // deep) % wide, row % deep
    else:
        slow, mid, fast = 0, 0, 0

    def spot_of(rank, whose):
        z, y, x = rank // (wide * deep), (rank // deep) % wide, rank % deep
        if not fused:
            return z, y, x
        return z, x + whose * (y - x), y + whose * (x - y)

    first, second = fast + core * (mid - fast), mid + core * (fast - mid)
    near, next_ = 1 - first, 1 - second

    def rank_of(z, a, b):
        y, x = b + core * (a - b), a + core * (b - a)
        return (z * wide + y) * deep + x

    near_device = (rank_of(slow, near, second), core)
    next_device = (rank_of(slow, first, next_), core)
    far_places = [lax.rem(slow + step, long) for step in range(1, long)]

    def add_into(target, index, terms):
        total = target[index].astype(FULL)
        for term in terms:
            total = total + term.astype(FULL)
        target[index] = total.astype(target.dtype)

    class Job:
        def __init__(self, kind, k, z=None):
            self.kind, self.k, self.z = kind, k, z

        def first_copy(self):
            kind, k, z = self.kind, self.k, self.z
            part, got = parts[kind].at[k], got1[kind].at[k]
            send, recv = sems[kind + "1"]
            if z is None:
                return remote(part.at[:, near], got, send.at[k], recv.at[k], near_device)
            return remote(part.at[z, near], got.at[z], send.at[z], recv.at[z], near_device)

        def second_copy(self):
            kind, k, z = self.kind, self.k, self.z
            part, got = parts[kind].at[k], got2[kind].at[k]
            send, recv = sems[kind + "2"]
            if z is None:
                return remote(part.at[:, first, next_], got, send.at[k], recv.at[k], next_device)
            return remote(
                part.at[z, first, next_], got.at[z], send.at[z], recv.at[z], next_device
            )

        def third_copies(self):
            kind, k = self.kind, self.k
            send, recv = sems[kind + "3"]
            return [
                remote(
                    parts[kind].at[k, z, first, second],
                    got3[kind].at[k, step],
                    send.at[k, step],
                    recv.at[k, step],
                    (rank_of(z, first, second), core),
                )
                for step, z in enumerate(far_places)
            ]

        def last_copy(self):
            kind, k = self.kind, self.k
            send, recv = sems[kind + "4"]
            return remote(
                parts[kind].at[k, slow, first, second],
                pair[kind].at[k],
                send.at[k],
                recv.at[k],
                partner,
            )

        def start(self):
            self.first_copy().start()

        def turn(self):
            self.first_copy().wait_recv()
            kind, k = self.kind, self.k
            if self.z is None:

                @pl.loop(0, long * deep)
                def _(step):
                    z, b = step // deep, lax.rem(step, deep)
                    add_into(parts[kind], (k, z, first, b), [got1[kind][k, z, b]])

            else:

                @pl.loop(0, deep)
                def _(b):
                    add_into(parts[kind], (k, self.z, first, b), [got1[kind][k, self.z, b]])

            self.second_copy().start()

        def gather(self):
            self.second_copy().wait_recv()
            kind, k = self.kind, self.k
            if self.z is None:

                @pl.loop(0, long)
                def _(z):
                    add_into(parts[kind], (k, z, first, second), [got2[kind][k, z]])

            else:
                add_into(parts[kind], (k, self.z, first, second), [got2[kind][k, self.z]])

        def spread(self):
            for one in self.third_copies():
                one.start()

        def close(self):
            for one in self.third_copies():
                one.wait_recv()
            kind, k = self.kind, self.k
            add_into(
                parts[kind],
                (k, slow, first, second),
                [got3[kind][k, step] for step in range(long - 1)],
            )
            self.last_copy().start()

        def store(self):
            self.last_copy().wait_recv()
            kind, k = self.kind, self.k
            results[kind][k, core] = parts[kind][k, slow, first, second]
            results[kind][k, other] = pair[kind][k]

        def drain(self, early=True, late=True):
            if early:
                self.first_copy().wait_send()
                self.second_copy().wait_send()
            if late:
                for one in self.third_copies():
                    one.wait_send()
                self.last_copy().wait_send()

    def steps(job, *names):
        if fused:
            for name in names:
                getattr(job, name)()

    down_jobs = [Job("down", 0, z) for z in range(long)]
    down = Job("down", 0)
    up_jobs = [Job("up", k) for k in range(2)]
    out_job = Job("out", 0)
    attn_jobs = [Job("attn", k) for k in range(pair_count)]
    vec_job = Job("vec", 0)

    def local(source, target, index):
        return pltpu.make_async_copy(source, target, load_sems.at[index])

    own, far = rows_of(own_start, half), rows_of(far_start, half)
    g_load = local(cotangent, grads_all.at[own], 0)
    out_loads = [
        local(w_out.at[rows_of(core * mine, mine)], weight_out.at[pl.ds(0, mine)], 1),
        local(w_out.at[rows_of(other * mine, mine)], weight_out.at[pl.ds(mine, mine)], 2),
        local(heads_hbm, heads, 3),
        local(other_hbm, heads_far, 4),
    ]
    late_loads = [
        local(low_in_hbm, low_in, 5),
        local(query_hbm, queries, 6),
        local(key_hbm, keys, 7),
        local(value_hbm, values, 8),
    ]
    for one in out_loads + [g_load]:
        one.start()

    peers = [partner]
    if fused:
        peers += [near_device, next_device]
        peers += [(rank_of(z, first, second), core) for z in far_places]
    barrier = pltpu.get_barrier_semaphore()
    for peer in peers:
        pl.semaphore_signal(barrier, inc=1, device_id=peer, device_id_type=MESH)
    pl.semaphore_wait(barrier, len(peers))

    def two(source_of, target_of, pair_sems):
        return [
            remote(source_of(i), target_of(i), pair_sems.at[0, i], pair_sems.at[1, i], partner)
            for i in range(2)
        ]

    def own_rows(i):
        return rows_of(own_start + i * TILE, TILE)

    def far_rows(i):
        return rows_of(far_start + i * TILE, TILE)

    g_far = remote(cotangent, grads_all.at[own], g_sems.at[0], g_sems.at[1], partner)
    g_far.start()
    mid_far = two(lambda i: low_mid.at[own_rows(i)], lambda i: low_mid.at[own_rows(i)], mid_sems)
    dz_far = two(
        lambda i: low_resid.at[own_rows(i)], lambda i: low_resid.at[own_rows(i)], dz_sems
    )

    def spans(i):
        return pl.ds(i * TILE, TILE)

    mid_back = two(lambda i: stage.at[spans(i)], lambda i: catch_mid.at[spans(i)], a_sems)
    out_back = two(lambda i: stage.at[spans(i)], lambda i: catch_out.at[spans(i)], c_sems)
    in_back = two(lambda i: stage.at[spans(i)], lambda i: catch_mid.at[spans(i)], b_sems)

    def feed_forward(weight_up, weight_down, hidden_low, grad_up):
        up_loads = [
            local(
                w_up.at[:, pl.ds(pl.multiple_of((core * 2 + b) * block, 128), block)],
                weight_up.at[b],
                9 + b,
            )
            for b in range(2)
        ]
        down_loads = [
            local(w_down.at[rows_of((core * 2 + b) * block, block)], weight_down.at[b], 11 + b)
            for b in range(2)
        ]
        for b in range(2):
            up_loads[b].start()
            down_loads[b].start()
        for one in out_loads:
            one.wait()

        for i in range(2):
            here = spans(i)
            joined = jnp.concatenate(
                [heads[p, own_rows(i), :] for p in range(pair_count)]
                + [heads_far[p, here, :] for p in range(pair_count)],
                1,
            )
            field = tokens[here, :].astype(FULL) + contract(joined, weight_out[...], 1, 0)
            resid[here, :] = field
            unit, _ = layer_norm(field)
            low_mid[own_rows(i), :] = (unit * gain_mid[...] + shift_mid[...]).astype(LOW)
            mid_far[i].start()

        for one in up_loads + down_loads + [g_load]:
            one.wait()
        for one in late_loads:
            one.start()

        @pl.loop(0, 2)
        def _(b):
            @pl.loop(0, tiles)
            def _(i):
                @pl.when((b == 0) & (i == 2))
                def _():
                    for one in mid_far:
                        one.wait_recv()
                    g_far.wait_recv()

                here = rows_of(lax.rem(core * 2 + i, tiles) * TILE, TILE)
                field = contract(low_mid[here, :], weight_up[b], 1, 0)
                value, slope = gelu_parts(field)
                hidden_low[b, here, :] = value.astype(LOW)
                back = contract(grads_all[here, :], weight_down[b], 1, 1)
                grad_up[b, here, :] = (back * slope).astype(LOW)

            tall = hidden // COUNT
            per = mine // tall
            for m in range(2):
                grad = contract(
                    hidden_low[b, :, pl.ds(m * mine, mine)], grads_all[...], 0, 0
                ).astype(LOW)
                kept = jnp.where(core == 0, grad[:, :mine], grad[:, mine:])
                given = jnp.where(core == 0, grad[:, mine:], grad[:, :mine])
                for i in range(per):
                    rank = (core * 2 + b) * (COUNT // 4) + m * per + i
                    z, a, s = spot_of(rank, core)
                    parts["down"][0, z, a, s] = kept[i * tall : (i + 1) * tall]
                    _, a, s = spot_of(rank, other)
                    stage_down[b, a, s] = given[i * tall : (i + 1) * tall]
            give_down(b).start()
            tall = width // COUNT
            per = mine // tall
            for m in range(2):
                grad = contract(
                    low_mid[:, pl.ds(m * mine, mine)], grad_up[b], 0, 0
                ).astype(LOW)
                for i in range(per):
                    z, a, s = spot_of(m * per + i, core)
                    parts["up"][b, z, a, s] = grad[i * tall : (i + 1) * tall]
            give_down(b).wait_recv()
            if fused:
                Job("down", 0, core * 2 + b).start()
                Job("down", 0, other * 2 + b).start()
                Job("up", b).start()

        for i in range(2):
            here = far_rows(i)
            stage[spans(i), :] = (
                contract(grad_up[0, here, :], weight_up[0], 1, 1)
                + contract(grad_up[1, here, :], weight_up[1], 1, 1)
            ).astype(LOW)
            mid_back[i].start()
        for i in range(2):
            here = own_rows(i)
            grad_resid[spans(i), :] = contract(grad_up[0, here, :], weight_up[0], 1, 1) + contract(
                grad_up[1, here, :], weight_up[1], 1, 1
            )
        if fused:
            down_jobs_turn(0)
        gain_sum = jnp.zeros((1, width), FULL)
        shift_sum = jnp.zeros((1, width), FULL)
        for i in range(2):
            here = spans(i)
            mid_back[i].wait_recv()
            grad = grad_resid[here, :] + catch_mid[here, :].astype(FULL)
            unit, inverse = layer_norm(resid[here, :])
            gain_sum = gain_sum + jnp.sum(grad * unit, 0, keepdims=True)
            shift_sum = shift_sum + jnp.sum(grad, 0, keepdims=True)
            scaled = grad * gain_mid[...]
            total = grads_all[own_rows(i), :].astype(FULL) + inverse * (
                scaled
                - jnp.mean(scaled, -1, keepdims=True)
                - unit * jnp.mean(scaled * unit, -1, keepdims=True)
            )
            grad_resid[here, :] = total
            low_resid[own_rows(i), :] = total.astype(LOW)
            dz_far[i].start()
        vec_sums[2:3, :] = gain_sum
        vec_sums[3:4, :] = shift_sum

        for i in range(2):
            mid_back[i].wait_send()
            here = far_rows(i)
            stage[spans(i), :] = (
                contract(hidden_low[0, here, :], weight_down[0], 1, 0)
                + contract(hidden_low[1, here, :], weight_down[1], 1, 0)
            ).astype(LOW)
            out_back[i].start()
        for i in range(2):
            here = own_rows(i)
            resid[spans(i), :] += contract(hidden_low[0, here, :], weight_down[0], 1, 0) + contract(
                hidden_low[1, here, :], weight_down[1], 1, 0
            )
        for i in range(2):
            here = spans(i)
            out_back[i].wait_recv()
            output[here, :] = (resid[here, :] + catch_out[here, :].astype(FULL)).astype(LOW)

    def give_down(b):
        return remote(
            stage_down.at[b],
            parts["down"].at[0, core * 2 + b],
            pd_sems.at[0, b],
            pd_sems.at[1, b],
            partner,
        )

    def down_jobs_turn(b):
        Job("down", 0, core * 2 + b).turn()
        Job("down", 0, other * 2 + b).turn()

    give_out = remote(
        stage_out,
        parts["out"].at[0, pl.ds(core * 2, 2)],
        po_sems.at[0],
        po_sems.at[1],
        partner,
    )

    vec_sums[...] = jnp.zeros_like(vec_sums)
    pl.run_scoped(
        feed_forward,
        pltpu.VMEM((2, width, block), LOW),
        pltpu.VMEM((2, block, width), LOW),
        pltpu.VMEM((2, length, block), LOW),
        pltpu.VMEM((2, length, block), LOW),
    )

    def prob_load(p, t):
        return pltpu.make_async_copy(prob_hbm[t].at[p], probs[t], prob_sems.at[t])

    def attention(slopes, fades, key_sum, value_sum, carry, grad_qkv, weight_in):
        for t in range(tiles):
            prob_load(pair_count - 1, t).start()
        slope_loads = [local(slope_hbm[t], slopes[t], 13 + t) for t in range(tiles)]
        weight_loads = []
        for place, source in enumerate((w_query, w_key, w_value)):
            for p in range(pair_count):
                weight_loads.append(
                    local(
                        source.at[:, pl.ds(pl.multiple_of(core * mine + p * PAIR, 128), PAIR)],
                        weight_in.at[:, pl.ds(p * mine + place * PAIR, PAIR)],
                        17 + place * pair_count + p,
                    )
                )
        for one in slope_loads + weight_loads:
            one.start()

        def head_grads(here):
            result = contract(low_resid[here, :], weight_out[pl.ds(0, mine), :], 1, 1).astype(LOW)
            for p in range(pair_count):
                grad_heads[p, here, :] = result[:, p * PAIR : (p + 1) * PAIR]

        for i in range(2):
            head_grads(own_rows(i))
        for i in range(2):
            dz_far[i].wait_recv()
            head_grads(far_rows(i))

        joined = jnp.concatenate([heads[p] for p in range(pair_count)], 1)
        grad = contract(joined, low_resid[...], 0, 0).astype(LOW)
        kept = jnp.where(core == 0, grad[:, :mine], grad[:, mine:])
        given = jnp.where(core == 0, grad[:, mine:], grad[:, :mine])
        tall = width // COUNT
        for i in range(mine // tall):
            rank = core * (COUNT // 2) + i
            z, a, s = spot_of(rank, core)
            parts["out"][0, z, a, s] = kept[i * tall : (i + 1) * tall]
            _, a, s = spot_of(rank, other)
            stage_out[i // (wide * deep), a, s] = given[i * tall : (i + 1) * tall]
        give_out.start()
        for one in late_loads:
            one.wait()
        give_out.wait_recv()
        steps(out_job, "start")

        keep = lanes_below((TILE, PAIR), HEAD)
        spots = (
            lax.broadcasted_iota(jnp.int32, (TILE, TILE), 0),
            lax.broadcasted_iota(jnp.int32, (TILE, TILE), 1),
        )
        after = jnp.where(spots[0] > spots[1], 1.0, 0.0).astype(LOW)

        def fade_send(t):
            return remote(
                share_send[t], share_recv[t], df_sems.at[0, t], df_sems.at[1, t], partner
            )

        def pair_step(step, p):
            for t in reversed(range(tiles)):
                count = (t + 1) * TILE
                span, rows = pl.ds(t * TILE, TILE), pl.ds(0, count)
                prob_load(p, t).wait()
                grad_tile = grad_heads[p, span, :]
                product = (grad_tile.astype(FULL) * heads[p, span, :].astype(FULL)).T
                query = queries[p, span, :]
                grads, masked_q, masked_g = [], [], []
                fade = None
                for h in range(2):
                    mask = keep == (h == 0)
                    masked_g.append(jnp.where(mask, grad_tile, LOW(0.0)))
                    masked_q.append(jnp.where(mask, query, LOW(0.0)))
                    delta = jnp.sum(product[h * HEAD : (h + 1) * HEAD, :], 0, keepdims=True)
                    change = probs[t][:, pl.ds(h * TILE, TILE)].astype(FULL) * (
                        contract(values[p, rows, :], masked_g[h], 1, 1) - delta
                    )
                    fade = change if fade is None else fade + change
                    grads.append(change.astype(LOW))

                @pl.when(step == 0)
                def _():
                    fades[rows, span] = fade

                @pl.when(step > 0)
                def _():
                    fades[rows, span] += fade

                both = jnp.concatenate(grads, 1)
                key_part = contract(both, jnp.concatenate(masked_q, 0), 1, 0)
                value_part = contract(probs[t][...], jnp.concatenate(masked_g, 0), 1, 0)
                if t == tiles - 1:
                    key_sum[...] = key_part
                    value_sum[...] = value_part
                else:
                    key_sum[rows, :] += key_part
                    value_sum[rows, :] += value_part
                query_part = contract(keys[p, rows, :], both, 0, 0)
                query_part = jnp.concatenate(
                    [query_part[:HEAD, :TILE], query_part[HEAD:, TILE:]], 0
                )
                grad_qkv[p, span, pl.ds(0, PAIR)] = (query_part.T * 0.125).astype(LOW)

                @pl.when(step < pair_count - 1)
                def _():
                    prob_load(p - 1, t).start()

                @pl.when((step == pair_count - 1) & (core == 1))
                def _():
                    share_send[t][...] = fades[rows, span].astype(LOW)
                    fade_send(t).start()

        def lead_head():
            @pl.when(core == 0)
            def _():
                carry[...] = jnp.zeros_like(carry)
                for t in reversed(range(tiles)):
                    count = (t + 1) * TILE
                    span, rows = pl.ds(t * TILE, TILE), pl.ds(0, count)
                    fade_send(t).wait_recv()
                    total = fades[rows, span] + share_recv[t][...].astype(FULL)
                    low_total = total.astype(LOW)
                    later = contract(low_total, after, 1, 0) + carry[rows, :]
                    carry[rows, :] += jnp.sum(total, -1, keepdims=True)
                    extra = (-later * slopes[t][...].astype(FULL)).astype(LOW)
                    query = jnp.where(keep, queries[0, span, :], LOW(0.0))
                    key_sum[rows, :] += contract(extra, query, 1, 0)
                    part = contract(keys[0, rows, :], extra, 0, 0)
                    part = jnp.where(
                        lax.broadcasted_iota(jnp.int32, part.shape, 0) < HEAD, part, 0.0
                    )
                    grad_qkv[0, span, pl.ds(0, PAIR)] = (
                        grad_qkv[0, span, pl.ds(0, PAIR)].astype(FULL) + part.T * 0.125
                    ).astype(LOW)

            @pl.when(core == 1)
            def _():
                for t in range(tiles):
                    fade_send(t).wait_send()

        def pair_weights(p):
            grad_qkv[p, :, pl.ds(PAIR, PAIR)] = key_sum[...].astype(LOW)
            grad_qkv[p, :, pl.ds(2 * PAIR, PAIR)] = value_sum[...].astype(LOW)
            for m in range(2):
                grad = contract(low_in[:, pl.ds(m * mine, mine)], grad_qkv[p], 0, 0).astype(LOW)
                for i in range(mine // tall):
                    z, a, s = spot_of(m * (mine // tall) + i, core)
                    parts["attn"][p, z, a, s] = grad[i * tall : (i + 1) * tall]
            steps(Job("attn", p), "start")

        @pl.loop(0, pair_count)
        def _(step):
            p = pair_count - 1 - step
            pair_step(step, p)

            @pl.when(step == pair_count - 1)
            def _():
                for one in slope_loads:
                    one.wait()
                lead_head()

            pair_weights(p)
            if fused:

                @pl.when(step == 0)
                def _():
                    up_jobs[0].turn()
                    Job("down", 0, core * 2).gather()
                    Job("down", 0, other * 2).gather()
                    down_jobs_turn(1)

                @pl.when(step == 1)
                def _():
                    up_jobs[0].gather()
                    up_jobs[0].spread()
                    up_jobs[1].turn()
                    Job("down", 0, core * 2 + 1).gather()
                    Job("down", 0, other * 2 + 1).gather()
                    down.spread()

        for one in weight_loads:
            one.wait()
        for i in range(2):
            out_back[i].wait_send()
            here = far_rows(i)
            joined = jnp.concatenate([grad_qkv[p, here, :] for p in range(pair_count)], 1)
            stage[spans(i), :] = contract(joined, weight_in[...], 1, 1).astype(LOW)
            in_back[i].start()
        gain_sum = jnp.zeros((1, width), FULL)
        shift_sum = jnp.zeros((1, width), FULL)
        for i in range(2):
            joined = jnp.concatenate([grad_qkv[p, own_rows(i), :] for p in range(pair_count)], 1)
            resid[spans(i), :] = contract(joined, weight_in[...], 1, 1)
        steps(out_job, "turn")
        for i in range(2):
            here = spans(i)
            in_back[i].wait_recv()
            grad = resid[here, :] + catch_mid[here, :].astype(FULL)
            unit, inverse = layer_norm(tokens[here, :].astype(FULL))
            gain_sum = gain_sum + jnp.sum(grad * unit, 0, keepdims=True)
            shift_sum = shift_sum + jnp.sum(grad, 0, keepdims=True)
            scaled = grad * gain_in[...]
            input_grad[here, :] = (
                grad_resid[here, :]
                + inverse
                * (
                    scaled
                    - jnp.mean(scaled, -1, keepdims=True)
                    - unit * jnp.mean(scaled * unit, -1, keepdims=True)
                )
            ).astype(LOW)
        vec_sums[0:1, :] = gain_sum
        vec_sums[1:2, :] = shift_sum
        for i in range(2):
            in_back[i].wait_send()

    pl.run_scoped(
        attention,
        [pltpu.VMEM(((t + 1) * TILE, TILE), LOW) for t in range(tiles)],
        pltpu.VMEM((length, length), FULL),
        pltpu.VMEM((length, PAIR), FULL),
        pltpu.VMEM((length, PAIR), FULL),
        pltpu.VMEM((length, 1), FULL),
        pltpu.VMEM((pair_count, length, mine), LOW),
        pltpu.VMEM((width, 3 * mine), LOW),
    )

    if not fused:
        for kind in KINDS[:-1]:
            one = pltpu.make_async_copy(parts[kind], results[kind], load_sems.at[0])
            one.start()
            one.wait()
        one = pltpu.make_async_copy(vec_sums, results["vec"], load_sems.at[0])
        one.start()
        one.wait()
    else:
        sums = vec_sums[...]
        tall = width // COUNT
        for rank in range(COUNT):
            z, a, s = spot_of(rank, core)
            shifted = pltpu.roll(sums, width - rank * tall, 1) if rank else sums
            parts["vec"][0, z, a, s] = shifted[:, :128]
        vec_job.start()
        for job in attn_jobs[:0:-1]:
            job.turn()
        up_jobs[1].gather()
        up_jobs[1].spread()
        out_job.gather()
        out_job.spread()
        attn_jobs[0].turn()
        vec_job.turn()
        down.close()
        up_jobs[0].close()
        for job in attn_jobs[::-1] + [vec_job]:
            job.gather()
            job.spread()
        everything = [down] + up_jobs + [out_job] + attn_jobs[::-1] + [vec_job]
        for job in everything[2:]:
            job.close()
        for job in everything:
            job.store()
        for job in down_jobs:
            job.drain(late=False)
        down.drain(early=False)
        for job in everything[1:]:
            job.drain()
    g_far.wait_send()
    give_out.wait_send()
    for b in range(2):
        give_down(b).wait_send()
    for one in mid_far + dz_far:
        one.wait_send()


def finish(fused, tokens, cotangent, gain_in, gain_mid, shift_mid, forward, weights):
    low_in, queries, keys, values, probs, slopes, heads, heads_far = forward
    half, width = tokens.shape
    length, mine = 2 * half, width // 2
    hidden = weights[-1].shape[0]
    pairs, tiles = mine // PAIR, length // TILE
    shapes = block_shapes(width, hidden)
    long, wide, deep = GRID
    anywhere = pl.BlockSpec(memory_space=pl.ANY)
    local = pl.BlockSpec(memory_space=pltpu.VMEM)
    outs = [jax.ShapeDtypeStruct((half, width), LOW)] * 2
    out_specs = [local] * 2
    for kind in KINDS:
        shape, kept = shapes[kind]
        if fused:
            outs.append(jax.ShapeDtypeStruct((FAN[kind], 2) + shape, kept))
            out_specs.append(local)
        elif kind == "vec":
            outs.append(jax.ShapeDtypeStruct((8, width), FULL))
            out_specs.append(anywhere)
        else:
            outs.append(jax.ShapeDtypeStruct((FAN[kind],) + GRID + shape, kept))
            out_specs.append(anywhere)
    scratch = [
        pltpu.VMEM((length, width), LOW),
        pltpu.VMEM((width, width), LOW),
        pltpu.VMEM((pairs, length, PAIR), LOW),
        pltpu.VMEM((pairs, half, PAIR), LOW),
        pltpu.VMEM((half, width), FULL),
        pltpu.VMEM((length, width), LOW),
        pltpu.VMEM((half, width), FULL),
        pltpu.VMEM((length, width), LOW),
        pltpu.VMEM((pairs, length, PAIR), LOW),
        pltpu.VMEM((length, width), LOW),
        pltpu.VMEM((pairs, length, PAIR), LOW),
        pltpu.VMEM((pairs, length, PAIR), LOW),
        pltpu.VMEM((pairs, length, PAIR), LOW),
    ]
    scratch += [pltpu.VMEM(((t + 1) * TILE, 2 * TILE), LOW) for t in range(tiles)]
    scratch += [pltpu.VMEM(((t + 1) * TILE, TILE), LOW) for t in range(tiles)] * 2
    scratch += [pltpu.VMEM((half, width), LOW)] * 3
    scratch += [
        pltpu.VMEM((2, wide, deep) + shapes["down"][0], LOW),
        pltpu.VMEM((2, wide, deep) + shapes["out"][0], LOW),
        pltpu.VMEM((8, width), FULL),
    ]
    scratch += [pltpu.VMEM((FAN[kind],) + GRID + shapes[kind][0], shapes[kind][1]) for kind in KINDS]
    dma = pltpu.SemaphoreType.DMA
    if fused:
        for lead in ((long, deep), (long,), (long - 1,), ()):
            scratch += [
                pltpu.VMEM((FAN[kind],) + lead + shapes[kind][0], shapes[kind][1])
                for kind in KINDS
            ]
        scratch += [dma((long,))] * 4 + [dma((1, long - 1))] * 2 + [dma((1,))] * 2
        for kind in KINDS[1:]:
            fan = FAN[kind]
            scratch += [dma((fan,))] * 4 + [dma((fan, long - 1))] * 2 + [dma((fan,))] * 2
    scratch += [dma((17 + 3 * pairs,)), dma((2,))]
    scratch += [dma((2, 2))] * 6
    scratch += [dma((2,)), dma((2, tiles)), dma((tiles,))]
    return pl.pallas_call(
        functools.partial(finish_kernel, fused),
        out_shape=outs,
        in_specs=[local] + [anywhere] + [local] * 3 + [anywhere] * (4 + 2 * tiles + 2 + 6),
        out_specs=out_specs,
        scratch_shapes=scratch,
        compiler_params=pltpu.CompilerParams(
            collective_id=0, has_side_effects=True, vmem_limit_bytes=VMEM_LIMIT
        ),
        name="finish",
    )(
        tokens,
        cotangent,
        gain_in,
        gain_mid,
        shift_mid,
        low_in,
        queries,
        keys,
        values,
        *probs,
        *slopes,
        heads,
        heads_far,
        *weights,
    )

def deliver_kernel(output_in, grad_in, down, up, out, attn, vec, output, input_grad, *grads):
    output[...] = output_in[...]
    input_grad[...] = grad_in[...]
    g_query, g_key, g_value, g_out, g_up, g_down, g_vec = grads
    tall, mine = out.shape[2:]
    for k in range(2):
        g_down[:, k * mine : (k + 1) * mine] = down[0, k].astype(FULL)
        g_out[:, k * mine : (k + 1) * mine] = out[0, k].astype(FULL)
        for b in range(2):
            g_up[:, (2 * k + b) * 2 * mine : (2 * k + b + 1) * 2 * mine] = up[b, k].astype(FULL)
        for p in range(attn.shape[0]):
            for place, target in enumerate((g_query, g_key, g_value)):
                target[:, k * mine + p * PAIR : k * mine + (p + 1) * PAIR] = attn[
                    p, k, :, place * PAIR : (place + 1) * PAIR
                ].astype(FULL)
    g_vec[...] = vec[0, 0] + vec[0, 1]


def deliver(output, input_grad, down, up, out, attn, vec):
    tall, mine = out.shape[2:]
    width = 2 * mine
    shapes = [(tall, width)] * 4 + [(tall, 2 * up.shape[3] * 2), (down.shape[2], width), (8, 128)]
    return pl.pallas_call(
        deliver_kernel,
        out_shape=[
            jax.ShapeDtypeStruct(output.shape, output.dtype),
            jax.ShapeDtypeStruct(input_grad.shape, input_grad.dtype),
        ]
        + [jax.ShapeDtypeStruct(shape, FULL) for shape in shapes],
        compiler_params=pltpu.CompilerParams(vmem_limit_bytes=VMEM_LIMIT),
        name="deliver",
    )(output, input_grad, down, up, out, attn, vec)


def reduce_plain(parts, rows):
    down, up, out, attn, vec = parts
    width = vec.shape[1]

    def scattered(part):
        summed = lax.psum_scatter(part.astype(FULL), "rows", scatter_dimension=0, tiled=True)
        return summed.astype(LOW)

    def joined(part):
        return lax.all_gather(part, "keys", axis=1, tiled=True).astype(FULL)

    def flat(part):
        return part.reshape(-1, part.shape[-1])

    attn_sums = [scattered(flat(attn[p])) for p in range(attn.shape[0])]
    halves = [
        jnp.concatenate([one[:, i * PAIR : (i + 1) * PAIR] for one in attn_sums], 1)
        for i in range(3)
    ]
    halves.append(scattered(flat(out[0])))
    halves.append(jnp.concatenate([scattered(flat(up[b])) for b in range(2)], 1))
    halves.append(scattered(flat(down[0])))
    sums = lax.psum_scatter(
        lax.psum(vec[:4].T, "keys"), "rows", scatter_dimension=0, tiled=True
    )
    return [joined(one) for one in halves], [sums[:, i] for i in range(4)]


def body(
    rows,
    tokens,
    seg_ids,
    doc_starts,
    gain_in,
    shift_in,
    w_query,
    w_key,
    w_value,
    w_out,
    gain_mid,
    shift_mid,
    w_up,
    w_down,
    out_grad,
):
    fused = rows == COUNT
    own_tokens, own_grad = tokens[0], out_grad[0]
    width = own_tokens.shape[1]
    low_in, queries, keys, values, probs, slopes, heads, heads_far, shares = attend(
        own_tokens, seg_ids, gain_in[None], shift_in[None], w_query, w_key, w_value
    )
    output, input_grad, *parts = finish(
        fused,
        own_tokens,
        own_grad,
        gain_in[None],
        gain_mid[None],
        shift_mid[None],
        (low_in, queries, keys, values, probs, slopes, heads, heads_far),
        (w_query, w_key, w_value, w_out, w_up, w_down),
    )
    if fused:
        output, input_grad, *grads, vec = deliver(output, input_grad, *parts)
        vectors = [vec[i, : width // rows] for i in range(4)]
    else:
        grads, vectors = reduce_plain(parts, rows)
    g_query, g_key, g_value, g_out, g_up, g_down = grads
    return (
        output[None],
        input_grad[None],
        shares[:1],
        vectors[0],
        vectors[1],
        g_query,
        g_key,
        g_value,
        g_out,
        vectors[2],
        vectors[3],
        g_up,
        g_down,
    )


def solution(mesh):
    in_specs = (
        P("rows", "keys", None),
        P("rows", None),
        P("rows", "keys"),
        P(),
        P(),
        P(),
        P(),
        P(),
        P(),
        P(),
        P(),
        P(),
        P(),
        P("rows", "keys", None),
    )
    out_specs = (
        P("rows", "keys", None),
        P("rows", "keys", None),
        P("rows", "keys"),
        P("rows"),
        P("rows"),
        P("rows", None),
        P("rows", None),
        P("rows", None),
        P("rows", None),
        P("rows"),
        P("rows"),
        P("rows", None),
        P("rows", None),
    )
    return jax.shard_map(
        functools.partial(body, mesh.shape["rows"]),
        mesh=mesh,
        in_specs=in_specs,
        out_specs=out_specs,
        check_vma=False,
    )
```

```python
import functools

import jax
import jax.numpy as jnp
from jax import lax
from jax.experimental import pallas as pl
from jax.experimental.pallas import tpu as pltpu
from jax.sharding import PartitionSpec as P

HEAD = 64
PAIR = 2 * HEAD
TILE = 256
EPS = 1e-05
MASKED = 1e30
SELECT_SHIFT = 4.0
LOW = jnp.bfloat16
FULL = jnp.float32
MESH = pl.DeviceIdType.MESH
VMEM_LIMIT = 67_000_000


def contract(left, right, left_dim, right_dim):
    return lax.dot_general(
        left, right, (((left_dim,), (right_dim,)), ((), ())), preferred_element_type=FULL
    )


def layer_norm(field):
    center = field - jnp.mean(field, -1, keepdims=True)
    inverse = lax.rsqrt(jnp.mean(center * center, -1, keepdims=True) + EPS)
    return center * inverse, inverse


def remote(source, target, send, recv, device):
    return pltpu.make_async_remote_copy(
        src_ref=source,
        dst_ref=target,
        send_sem=send,
        recv_sem=recv,
        device_id=device,
        device_id_type=MESH,
    )


def lanes_below(shape, bound):
    return lax.broadcasted_iota(jnp.int32, shape, len(shape) - 1) < bound


def flat(ref):
    return ref[...].reshape(1, ref.shape[0])


def corner(step, tiles):
    t = sum((step >= n * (n + 1) // 2).astype(jnp.int32) for n in range(1, tiles))
    return t, step - t * (t + 1) // 2


def rows_of(start, size):
    return pl.ds(pl.multiple_of(start, size), size)


def attend_kernel(
    tokens,
    seg,
    gain,
    shift,
    w_query,
    w_key,
    w_value,
    low_in_out,
    query_out,
    key_out,
    value_out,
    prob_outs,
    slopes_out,
    heads_out,
    other_out,
    share_out,
    all_tokens,
    low_in,
    weights,
    queries,
    keys,
    values,
    lead_query,
    lead_key,
    probs,
    slopes,
    penalty,
    heads,
    seg_cols,
    free_cols,
    running,
    numerator,
    pairs_seen,
    far_send,
    far_recv,
    head_send,
    head_recv,
    weight_sems,
    out_sems,
    prob_sems,
):
    core = lax.axis_index("keys")
    row = lax.axis_index("rows")
    other = 1 - core
    partner = (row, other)
    half, width = tokens.shape
    length = 2 * half
    mine = width // 2
    pair_count = mine // PAIR
    tiles = length // TILE

    columns = pl.ds(pl.multiple_of(core * mine, 128), mine)
    loads = []
    for place, source in enumerate((w_query, w_key, w_value)):
        loads.append((source.at[:, columns], weights.at[:, pl.ds(place * mine, mine)]))
    for place, source in enumerate((w_query, w_key)):
        loads.append(
            (source.at[:, pl.ds(0, PAIR)], weights.at[:, pl.ds(3 * mine + place * PAIR, PAIR)])
        )
    own = rows_of(core * half, half)
    loads = [
        pltpu.make_async_copy(source, target, weight_sems.at[i])
        for i, (source, target) in enumerate(loads)
    ]
    own_load = pltpu.make_async_copy(tokens, all_tokens.at[own], weight_sems.at[5])
    own_load.start()
    for one in loads:
        one.start()

    barrier = pltpu.get_barrier_semaphore()
    pl.semaphore_signal(barrier, inc=1, device_id=partner, device_id_type=MESH)
    pl.semaphore_wait(barrier, 1)
    exchange = remote(tokens, all_tokens.at[own], far_send, far_recv, partner)
    exchange.start()

    seg_row = seg[...]
    seg_wide = jnp.broadcast_to(seg_row.astype(FULL), (128, length))
    spot = lax.broadcasted_iota(jnp.int32, (128, length), 1)
    before = pltpu.roll(seg_wide, 1, 1)
    free_wide = jnp.where((spot > 0) & (before == seg_wide), 1.0, 0.0)
    seg_cols[...] = seg_wide.T
    free_cols[...] = free_wide.T
    own_load.wait()

    keep = lanes_below((TILE, PAIR), HEAD)

    @pl.loop(0, tiles)
    def _(i):
        @pl.when(i == half // TILE)
        def _():
            exchange.wait_recv()

        here = rows_of(lax.rem(core * (half // TILE) + i, tiles) * TILE, TILE)
        unit, _ = layer_norm(all_tokens[here, :].astype(FULL))
        low_in[here, :] = (unit * flat(gain) + flat(shift)).astype(LOW)

        @pl.when(i == 0)
        def _():
            for one in loads:
                one.wait()

        result = contract(low_in[here, :], weights[...], 1, 0).astype(LOW)
        for p in range(pair_count):
            queries[p, here, :] = result[:, p * PAIR : (p + 1) * PAIR] * LOW(0.125)
            keys[p, here, :] = result[:, mine + p * PAIR : mine + (p + 1) * PAIR]
            values[p, here, :] = result[:, 2 * mine + p * PAIR : 2 * mine + (p + 1) * PAIR]
        first = result[:, 3 * mine : 3 * mine + PAIR]
        lead_query[here, :] = jnp.where(keep, first, LOW(0.0)) * LOW(0.125)
        lead_key[here, :] = result[:, 3 * mine + PAIR :]

    puts = [
        pltpu.make_async_copy(low_in, low_in_out, out_sems.at[0]),
        pltpu.make_async_copy(queries, query_out, out_sems.at[1]),
        pltpu.make_async_copy(keys, key_out, out_sems.at[2]),
        pltpu.make_async_copy(values, value_out, out_sems.at[3]),
    ]
    for one in puts:
        one.start()

    spots = (
        lax.broadcasted_iota(jnp.int32, (TILE, 2 * TILE), 0),
        lax.broadcasted_iota(jnp.int32, (TILE, 2 * TILE), 1),
    )
    pairs = (
        lax.broadcasted_iota(jnp.int32, (2 * TILE, 2 * TILE), 0),
        lax.broadcasted_iota(jnp.int32, (2 * TILE, 2 * TILE), 1),
    )
    earlier = jnp.where(pairs[0] < pairs[1], 1.0, 0.0).astype(LOW)
    running[...] = jnp.zeros_like(running)
    numerator[...] = jnp.zeros_like(numerator)
    pairs_seen[...] = jnp.zeros_like(pairs_seen)

    @pl.loop(0, (tiles // 2) * (tiles // 2 + 1))
    def _(step):
        wide = sum((step >= n * (n + 1)).astype(jnp.int32) for n in range(1, tiles // 2))
        k = step - wide * (wide + 1)
        rows, span = rows_of(k * TILE, TILE), rows_of(wide * 2 * TILE, 2 * TILE)
        scores = contract(lead_key[rows, :], lead_query[span, :], 1, 1)
        repeat = 2 * TILE // 128
        same = jnp.concatenate([seg_cols[rows, :]] * repeat, 1) == seg[:, span].astype(FULL)
        ahead = spots[1] - spots[0] + (2 * wide - k) * TILE
        later = same & (ahead > 0)
        allowed = same & (ahead >= 0)
        select = jnp.where(later, jnp.concatenate([free_cols[rows, :]] * repeat, 1), 0.0)
        level = scores - SELECT_SHIFT
        chosen = select * (jnp.maximum(level, 0.0) + jnp.log(1.0 + jnp.exp(-jnp.abs(level))))
        slope = (select * (0.5 + 0.5 * jnp.tanh(0.5 * level))).astype(LOW)

        @pl.when(k <= 2 * wide)
        def _():
            slopes[wide * (2 * wide + 1) + k] = slope[:, :TILE]

        slopes[(2 * wide + 1) * (wide + 1) + k] = slope[:, TILE:]
        high = chosen.astype(LOW)
        rest = (chosen - high.astype(FULL)).astype(LOW)
        total = (
            running[rows, :] + contract(high, earlier, 1, 0) + contract(rest, earlier, 1, 0)
        )
        penalty[rows, span] = jnp.where(allowed, total, MASKED)
        running[rows, :] += jnp.sum(chosen, -1, keepdims=True)
        share = jnp.where(later, 0.5 + 0.5 * jnp.tanh(0.5 * total - 1.0), 0.0)
        numerator[rows, :] += jnp.sum(share, -1, keepdims=True)
        pairs_seen[rows, :] += jnp.sum(jnp.where(later, 1.0, 0.0), -1, keepdims=True)

    slope_put = pltpu.make_async_copy(slopes, slopes_out, out_sems.at[4])
    slope_put.start()

    shares = numerator[own, :] / jnp.maximum(pairs_seen[own, :], 1.0)
    share_out[...] = jnp.broadcast_to(shares, (half, 128)).T[0:8, :]

    def put_probs(p, t):
        return pltpu.make_async_copy(
            probs[t].at[p], prob_outs[t].at[p], prob_sems.at[p, t]
        )

    def send_heads(p):
        return remote(
            heads.at[p, rows_of(other * half, half)],
            other_out.at[p],
            head_send.at[p],
            head_recv.at[p],
            partner,
        )

    @pl.loop(0, pair_count)
    def _(p):
        for t in range(tiles):
            count = (t + 1) * TILE
            span = pl.ds(t * TILE, TILE)
            query = queries[p, span, :]
            outs = []
            for h in range(2):
                masked = jnp.where(keep == (h == 0), query, LOW(0.0))
                logits = (
                    contract(keys[p, pl.ds(0, count), :], masked, 1, 1)
                    - penalty[pl.ds(0, count), span]
                )
                scaled = jnp.exp(logits - jnp.max(logits, 0, keepdims=True))
                prob = (scaled * (1.0 / jnp.sum(scaled, 0, keepdims=True))).astype(LOW)
                probs[t][p, :, pl.ds(h * TILE, TILE)] = prob
                out = contract(values[p, pl.ds(0, count), :], prob, 0, 0)
                outs.append(out[h * HEAD : (h + 1) * HEAD, :])
            heads[p, span, :] = jnp.concatenate(outs, 0).T.astype(LOW)
            put_probs(p, t).start()
        send_heads(p).start()

    last = pltpu.make_async_copy(heads, heads_out, out_sems.at[5])
    last.start()
    for p in range(pair_count):
        send_heads(p).wait()
        for t in range(tiles):
            put_probs(p, t).wait()
    for one in puts + [slope_put, last]:
        one.wait()
    exchange.wait_send()


def attend(tokens, seg, gain, shift, w_query, w_key, w_value):
    half, width = tokens.shape
    length, mine = 2 * half, width // 2
    pairs, tiles = mine // PAIR, 2 * half // TILE
    spans = [(t + 1) * TILE for t in range(tiles)]
    corners = tiles * (tiles + 1) // 2
    outs = [
        jax.ShapeDtypeStruct((length, width), LOW),
        jax.ShapeDtypeStruct((pairs, length, PAIR), LOW),
        jax.ShapeDtypeStruct((pairs, length, PAIR), LOW),
        jax.ShapeDtypeStruct((pairs, length, PAIR), LOW),
        [jax.ShapeDtypeStruct((pairs, span, 2 * TILE), LOW) for span in spans],
        jax.ShapeDtypeStruct((corners, TILE, TILE), LOW),
        jax.ShapeDtypeStruct((pairs, length, PAIR), LOW),
        jax.ShapeDtypeStruct((pairs, half, PAIR), LOW),
        jax.ShapeDtypeStruct((8, half), FULL),
    ]
    anywhere = pl.BlockSpec(memory_space=pl.ANY)
    local = pl.BlockSpec(memory_space=pltpu.VMEM)
    out_specs = [anywhere] * 4 + [[anywhere] * tiles, anywhere, anywhere, anywhere, local]
    scratch = [
        pltpu.VMEM((length, width), LOW),
        pltpu.VMEM((length, width), LOW),
        pltpu.VMEM((width, 3 * mine + 2 * PAIR), LOW),
        pltpu.VMEM((pairs, length, PAIR), LOW),
        pltpu.VMEM((pairs, length, PAIR), LOW),
        pltpu.VMEM((pairs, length, PAIR), LOW),
        pltpu.VMEM((length, PAIR), LOW),
        pltpu.VMEM((length, PAIR), LOW),
        [pltpu.VMEM((pairs, span, 2 * TILE), LOW) for span in spans],
        pltpu.VMEM((corners, TILE, TILE), LOW),
        pltpu.VMEM((length, length), FULL),
        pltpu.VMEM((pairs, length, PAIR), LOW),
        pltpu.VMEM((length, 128), FULL),
        pltpu.VMEM((length, 128), FULL),
        pltpu.VMEM((length, 1), FULL),
        pltpu.VMEM((length, 1), FULL),
        pltpu.VMEM((length, 1), FULL),
        pltpu.SemaphoreType.DMA,
        pltpu.SemaphoreType.DMA,
        pltpu.SemaphoreType.DMA((pairs,)),
        pltpu.SemaphoreType.DMA((pairs,)),
        pltpu.SemaphoreType.DMA((6,)),
        pltpu.SemaphoreType.DMA((6,)),
        pltpu.SemaphoreType.DMA((pairs, tiles)),
    ]
    return pl.pallas_call(
        attend_kernel,
        out_shape=outs,
        in_specs=[anywhere] + [local] * 3 + [anywhere] * 3,
        out_specs=out_specs,
        scratch_shapes=scratch,
        compiler_params=pltpu.CompilerParams(
            collective_id=1, has_side_effects=True, vmem_limit_bytes=VMEM_LIMIT
        ),
        name="attend",
    )(tokens, seg, gain, shift, w_query, w_key, w_value)

def gelu_parts(field):
    scale = 0.7978845608028654
    square = field * field
    inner = jnp.tanh(scale * field * (1.0 + 0.044715 * square))
    half_sum = 0.5 * (1.0 + inner)
    slope = half_sum + 0.5 * field * (1.0 - inner * inner) * (
        scale * (1.0 + 3.0 * 0.044715 * square)
    )
    return field * half_sum, slope


GRID = (4, 2, 2)
COUNT = GRID[0] * GRID[1] * GRID[2]
KINDS = ("down", "up", "out", "attn", "early", "lead", "vec")
FAN = {"down": 1, "up": 2, "out": 1, "attn": 2, "early": 1, "lead": 1, "vec": 1}


def block_shapes(width, hidden):
    mine = width // 2
    tall = width // COUNT
    return {
        "down": ((hidden // COUNT, mine), LOW),
        "up": ((tall, mine * 2), LOW),
        "out": ((tall, mine), LOW),
        "attn": ((tall, mine), LOW),
        "early": ((tall, 2 * PAIR), LOW),
        "lead": ((tall, PAIR), LOW),
        "vec": ((8, 128), FULL),
    }


def finish_kernel(fused, *refs):
    refs = list(refs)

    def take(count):
        taken = refs[:count]
        del refs[:count]
        return taken if count > 1 else taken[0]

    tokens, cotangent, gain_in, gain_mid, shift_mid = take(5)
    low_in_hbm, query_hbm, key_hbm, value_hbm = take(4)
    prob_hbm, slope_hbm = take(4), take(1)
    heads_hbm, other_hbm = take(2)
    w_query, w_key, w_value, w_out, w_up, w_down = take(6)
    output, input_grad = take(2)
    results = dict(zip(KINDS, take(len(KINDS))))
    (
        grads_all,
        weight_out,
        heads,
        heads_far,
        resid,
        low_mid,
        grad_resid,
        low_resid,
        grad_heads,
        low_in,
        queries,
        keys,
        values,
    ) = take(13)
    probs = take(4)
    share_send, share_recv = take(2)
    stage, stage_far, catch_mid, catch_out = take(4)
    weight_down, hidden_low = take(2)
    stage_down, stage_out = take(2)
    vec_sums = take(1)
    parts = dict(zip(KINDS, take(len(KINDS))))
    if fused:
        got1 = dict(zip(KINDS, take(len(KINDS))))
        got2 = dict(zip(KINDS, take(len(KINDS))))
        got3 = dict(zip(KINDS, take(len(KINDS))))
        pair = dict(zip(KINDS, take(len(KINDS))))
        sems = {
            name: take(2) for name in ("down1", "down2", "down3", "down4")
        }
        for kind in KINDS[1:]:
            for stage_name in "1234":
                sems[kind + stage_name] = take(2)
    (load_sems, g_sems, mid_sems, dz_sems, a_sems, b_sems, c_sems, pd_sems, po_sems, df_sems, prob_sems) = take(11)

    long, wide, deep = GRID
    core = lax.axis_index("keys")
    row = lax.axis_index("rows")
    other = 1 - core
    partner = (row, other)
    half, width = tokens.shape
    length, mine = 2 * half, width // 2
    pair_count = mine // PAIR
    tiles = length // TILE
    hidden = w_down.shape[0]
    block = hidden // 4
    own_start, far_start = core * half, other * half

    if fused:
        slow, mid, fast = row // (wide * deep), (row // deep) % wide, row % deep
    else:
        slow, mid, fast = 0, 0, 0

    def spot_of(rank, whose):
        z, y, x = rank // (wide * deep), (rank // deep) % wide, rank % deep
        if not fused:
            return z, y, x
        return z, x + whose * (y - x), y + whose * (x - y)

    first, second = fast + core * (mid - fast), mid + core * (fast - mid)
    near, next_ = 1 - first, 1 - second

    def rank_of(z, a, b):
        y, x = b + core * (a - b), a + core * (b - a)
        return (z * wide + y) * deep + x

    near_device = (rank_of(slow, near, second), core)
    next_device = (rank_of(slow, first, next_), core)
    far_places = [lax.rem(slow + step, long) for step in range(1, long)]

    def add_into(target, index, terms):
        total = target[index].astype(FULL)
        for term in terms:
            total = total + term.astype(FULL)
        target[index] = total.astype(target.dtype)

    class Job:
        def __init__(self, kind, k):
            self.kind, self.k = kind, k

        def first_copy(self):
            kind, k = self.kind, self.k
            part, got = parts[kind].at[k], got1[kind].at[k]
            send, recv = sems[kind + "1"]
            return remote(part.at[:, near], got, send.at[k], recv.at[k], near_device)

        def second_copy(self):
            kind, k = self.kind, self.k
            part, got = parts[kind].at[k], got2[kind].at[k]
            send, recv = sems[kind + "2"]
            return remote(part.at[:, first, next_], got, send.at[k], recv.at[k], next_device)

        def third_copies(self):
            kind, k = self.kind, self.k
            send, recv = sems[kind + "3"]
            return [
                remote(
                    parts[kind].at[k, z, first, second],
                    got3[kind].at[k, step],
                    send.at[k, step],
                    recv.at[k, step],
                    (rank_of(z, first, second), core),
                )
                for step, z in enumerate(far_places)
            ]

        def last_copy(self):
            kind, k = self.kind, self.k
            send, recv = sems[kind + "4"]
            return remote(
                parts[kind].at[k, slow, first, second],
                pair[kind].at[k],
                send.at[k],
                recv.at[k],
                partner,
            )

        def start(self):
            self.first_copy().start()

        def turn(self):
            self.first_copy().wait_recv()
            kind, k = self.kind, self.k

            @pl.loop(0, long * deep)
            def _(step):
                z, b = step // deep, lax.rem(step, deep)
                add_into(parts[kind], (k, z, first, b), [got1[kind][k, z, b]])

            self.second_copy().start()

        def gather(self):
            self.second_copy().wait_recv()
            kind, k = self.kind, self.k

            @pl.loop(0, long)
            def _(z):
                add_into(parts[kind], (k, z, first, second), [got2[kind][k, z]])

            for one in self.third_copies():
                one.start()

        def close(self):
            for one in self.third_copies():
                one.wait_recv()
            kind, k = self.kind, self.k
            add_into(
                parts[kind],
                (k, slow, first, second),
                [got3[kind][k, step] for step in range(long - 1)],
            )
            self.last_copy().start()

        def store(self):
            self.last_copy().wait_recv()
            kind, k = self.kind, self.k
            results[kind][k, core] = parts[kind][k, slow, first, second]
            results[kind][k, other] = pair[kind][k]

        def drain(self):
            self.first_copy().wait_send()
            self.second_copy().wait_send()
            for one in self.third_copies():
                one.wait_send()
            self.last_copy().wait_send()

    class Down(Job):
        def near_copy(self, z):
            send, recv = sems["down1"]
            return remote(
                parts["down"].at[0, z, near],
                got1["down"].at[0, z],
                send.at[z],
                recv.at[z],
                near_device,
            )

        def slow_copy(self, step):
            z = lax.rem(slow + step, long)
            send, recv = sems["down2"]
            return remote(
                parts["down"].at[0, z, first],
                got2["down"].at[0, step - 1],
                send.at[step - 1],
                recv.at[step - 1],
                (rank_of(z, first, second), core),
            )

        def next_copy(self):
            send, recv = sems["down3"]
            return remote(
                parts["down"].at[0, slow, first, next_],
                got3["down"].at[0],
                send.at[0],
                recv.at[0],
                next_device,
            )

        def start_at(self, z):
            self.near_copy(z).start()

        def turn_at(self, z):
            self.near_copy(z).wait_recv()

            @pl.loop(0, deep)
            def _(b):
                add_into(parts["down"], (0, z, first, b), [got1["down"][0, z, b]])

            step = lax.rem(z - slow + long, long)

            @pl.when(step > 0)
            def _():
                self.slow_copy(step).start()

        def cross(self):
            for step in range(1, long):
                self.slow_copy(step).wait_recv()

            @pl.loop(0, deep)
            def _(b):
                add_into(
                    parts["down"],
                    (0, slow, first, b),
                    [got2["down"][0, step, b] for step in range(long - 1)],
                )

            self.next_copy().start()

        def close(self):
            self.next_copy().wait_recv()
            add_into(parts["down"], (0, slow, first, second), [got3["down"][0]])
            self.last_copy().start()

        def drain(self):
            for z in range(long):
                self.near_copy(z).wait_send()
            for step in range(1, long):
                self.slow_copy(step).wait_send()
            self.next_copy().wait_send()
            self.last_copy().wait_send()

    class Vectors(Job):
        def first_copies(self):
            send, recv = sems["vec1"]
            places = ((near, second), (first, next_), (near, next_))
            return [
                remote(
                    parts["vec"].at[0, :, a, b],
                    got1["vec"].at[0, i],
                    send.at[i],
                    recv.at[i],
                    (rank_of(slow, a, b), core),
                )
                for i, (a, b) in enumerate(places)
            ]

        def start(self):
            for one in self.first_copies():
                one.start()

        def gather(self):
            for one in self.first_copies():
                one.wait_recv()

            @pl.loop(0, long)
            def _(z):
                add_into(
                    parts["vec"], (0, z, first, second), [got1["vec"][0, i, z] for i in range(3)]
                )

            for one in self.third_copies():
                one.start()

        def drain(self):
            for one in self.first_copies() + self.third_copies():
                one.wait_send()
            self.last_copy().wait_send()

    def steps(*names):
        if fused:
            for name in names:
                job, step = name.split()
                getattr(jobs[job], step)()

    def steps_when(condition, *names):
        if fused:
            pl.when(condition)(lambda: steps(*names))

    down = Down("down", 0)
    jobs = {"down": down, "vec": Vectors("vec", 0)}
    jobs |= {kind: Job(kind, 0) for kind in ("out", "early", "lead")}
    jobs |= {f"up{k}": Job("up", k) for k in range(2)}
    jobs |= {f"attn{k + 1}": Job("attn", k) for k in range(pair_count - 1)}

    def local(source, target, index):
        return pltpu.make_async_copy(source, target, load_sems.at[index])

    own = rows_of(own_start, half)
    in_put = local(low_mid.at[pl.ds(0, half)], input_grad, 0)
    out_put = local(low_mid.at[pl.ds(half, half)], output, 1)
    g_load = local(cotangent, grads_all.at[own], 0)
    out_loads = [
        local(w_out.at[rows_of(core * mine, mine)], weight_out.at[pl.ds(0, mine)], 1),
        local(w_out.at[rows_of(other * mine, mine)], weight_out.at[pl.ds(mine, mine)], 2),
        local(heads_hbm, heads, 3),
        local(other_hbm, heads_far, 4),
    ]
    late_loads = [
        local(low_in_hbm, low_in, 5),
        local(query_hbm, queries, 6),
        local(key_hbm, keys, 7),
        local(value_hbm, values, 8),
    ]
    for one in out_loads + [g_load]:
        one.start()

    peers = [partner]
    if fused:
        peers += [near_device, next_device, (rank_of(slow, near, next_), core)]
        peers += [(rank_of(z, first, second), core) for z in far_places]
    barrier = pltpu.get_barrier_semaphore()
    for peer in peers:
        pl.semaphore_signal(barrier, inc=1, device_id=peer, device_id_type=MESH)

    def own_rows(i):
        return rows_of(own_start + i * TILE, TILE)

    def far_rows(i):
        return rows_of(far_start + i * TILE, TILE)

    def tile_rows(i):
        return rows_of(i * TILE, TILE)

    def to_partner(source, target, pair_sems):
        def one(i):
            return remote(
                source(i), target(i), pair_sems.at[0, i], pair_sems.at[1, i], partner
            )

        return one

    g_far = remote(cotangent, grads_all.at[own], g_sems.at[0], g_sems.at[1], partner)
    mid_far = to_partner(
        lambda i: low_mid.at[own_rows(i)], lambda i: low_mid.at[own_rows(i)], mid_sems
    )
    dz_far = to_partner(
        lambda i: low_resid.at[own_rows(i)], lambda i: low_resid.at[own_rows(i)], dz_sems
    )
    mid_back = to_partner(
        lambda i: stage.at[tile_rows(i)], lambda i: catch_mid.at[tile_rows(i)], a_sems
    )
    in_back = to_partner(
        lambda i: stage.at[tile_rows(i)], lambda i: catch_mid.at[tile_rows(i)], b_sems
    )
    out_back = to_partner(
        lambda i: stage_far.at[tile_rows(i)], lambda i: catch_out.at[tile_rows(i)], c_sems
    )

    def feed_forward(weight_up, grad_up):
        up_loads = [
            local(
                w_up.at[:, pl.ds(pl.multiple_of((core * 2 + b) * block, 128), block)],
                weight_up.at[b],
                9 + b,
            )
            for b in range(2)
        ]
        down_loads = [
            local(w_down.at[rows_of((core * 2 + b) * block, block)], weight_down.at[b], 11 + b)
            for b in range(2)
        ]
        for b in range(2):
            up_loads[b].start()
            down_loads[b].start()
        for one in out_loads:
            one.wait()

        @pl.loop(0, 2)
        def _(i):
            here, place = tile_rows(i), own_rows(i)
            joined = jnp.concatenate(
                [heads[p, place, :] for p in range(pair_count)]
                + [heads_far[p, here, :] for p in range(pair_count)],
                1,
            )
            field = tokens[here, :].astype(FULL) + contract(joined, weight_out[...], 1, 0)
            resid[here, :] = field
            unit, _ = layer_norm(field)
            low_mid[place, :] = (unit * flat(gain_mid) + flat(shift_mid)).astype(LOW)

        pl.semaphore_wait(barrier, len(peers))
        g_far.start()
        for i in range(2):
            mid_far(i).start()

        for one in up_loads + down_loads + [g_load]:
            one.wait()
        for one in late_loads:
            one.start()

        @pl.loop(0, 2)
        def _(b):
            @pl.loop(0, tiles)
            def _(i):
                @pl.when((b == 0) & (i == 2))
                def _():
                    for j in range(2):
                        mid_far(j).wait_recv()

                here = rows_of(lax.rem(core * 2 + i, tiles) * TILE, TILE)
                value, slope = gelu_parts(contract(low_mid[here, :], weight_up[b], 1, 0))
                hidden_low[b, here, :] = value.astype(LOW)
                grad_up[b, here, :] = slope.astype(LOW)
                if fused:

                    @pl.when((b == 1) & (i == 0))
                    def _():
                        down.turn_at(core * 2)

                    @pl.when((b == 1) & (i == 2))
                    def _():
                        down.turn_at(other * 2)

            @pl.when(b == 0)
            def _():
                g_far.wait_recv()

            tall = hidden // COUNT
            per = mine // tall
            @pl.loop(0, 2)
            def _(m):
                place = pl.ds(pl.multiple_of(m * mine, 128), mine)
                grad = contract(hidden_low[b, :, place], grads_all[...], 0, 0).astype(LOW)
                kept = jnp.where(core == 0, grad[:, :mine], grad[:, mine:])
                given = jnp.where(core == 0, grad[:, mine:], grad[:, :mine])
                for i in range(per):
                    rank = (core * 2 + b) * (COUNT // 4) + m * per + i
                    z, a, s = spot_of(rank, core)
                    parts["down"][0, z, a, s] = kept[i * tall : (i + 1) * tall]
                    _, a, s = spot_of(rank, other)
                    stage_down[b, a, s] = given[i * tall : (i + 1) * tall]
            give_down(b).start()
            if fused:
                down.start_at(core * 2 + b)

            @pl.loop(0, tiles)
            def _(i):
                here = rows_of(i * TILE, TILE)
                back = contract(grads_all[here, :], weight_down[b], 1, 1)
                grad_up[b, here, :] = (back * grad_up[b, here, :].astype(FULL)).astype(LOW)

                @pl.when(i == 1)
                def _():
                    give_down(b).wait_recv()
                    if fused:
                        down.start_at(other * 2 + b)

                steps_when((b == 1) & (i == 2), "up0 turn")

            @pl.loop(0, 2)
            def _(m):
                tall = width // COUNT
                per = mine // tall
                place = pl.ds(pl.multiple_of(m * mine, 128), mine)
                grad = contract(low_mid[:, place], grad_up[b], 0, 0).astype(LOW)
                for i in range(per):
                    z, a, s = spot_of(m * per + i, core)
                    parts["up"][b, z, a, s] = grad[i * tall : (i + 1) * tall]

            if fused:
                Job("up", b).start()

        def mid_part(here):
            return contract(grad_up[0, here, :], weight_up[0], 1, 1) + contract(
                grad_up[1, here, :], weight_up[1], 1, 1
            )

        @pl.loop(0, tiles)
        def _(i):
            part = mid_part(rows_of(lax.rem(other * 2 + i, tiles) * TILE, TILE))

            @pl.when(i < 2)
            def _():
                stage[tile_rows(i), :] = part.astype(LOW)
                mid_back(i).start()

            @pl.when(i >= 2)
            def _():
                grad_resid[tile_rows(i - 2), :] = part

            if fused:

                @pl.when(i == 1)
                def _():
                    down.turn_at(core * 2 + 1)

        if fused:
            down.turn_at(other * 2 + 1)
        steps("up0 gather")

        @pl.loop(0, 2)
        def _(i):
            here = tile_rows(i)
            mid_back(i).wait_recv()
            grad = grad_resid[here, :] + catch_mid[here, :].astype(FULL)
            unit, inverse = layer_norm(resid[here, :])
            vec_sums[2:3, :] += jnp.sum(grad * unit, 0, keepdims=True)
            vec_sums[3:4, :] += jnp.sum(grad, 0, keepdims=True)
            scaled = grad * flat(gain_mid)
            total = grads_all[own_rows(i), :].astype(FULL) + inverse * (
                scaled
                - jnp.mean(scaled, -1, keepdims=True)
                - unit * jnp.mean(scaled * unit, -1, keepdims=True)
            )
            grad_resid[here, :] = total
            low_resid[own_rows(i), :] = total.astype(LOW)
            dz_far(i).start()

        for i in range(2):
            mid_back(i).wait_send()

    def give_down(b):
        return remote(
            stage_down.at[b],
            parts["down"].at[0, core * 2 + b],
            pd_sems.at[0, b],
            pd_sems.at[1, b],
            partner,
        )

    give_out = remote(
        stage_out,
        parts["out"].at[0, pl.ds(core * 2, 2)],
        po_sems.at[0],
        po_sems.at[1],
        partner,
    )

    vec_sums[...] = jnp.zeros_like(vec_sums)
    pl.run_scoped(
        feed_forward,
        pltpu.VMEM((2, width, block), LOW),
        pltpu.VMEM((2, length, block), LOW),
    )

    def prob_load(p, t):
        return pltpu.make_async_copy(prob_hbm[t].at[p], probs[t], prob_sems.at[t])

    def attention(slopes, fades, key_sum, value_sum, carry, grad_qkv, weight_in):
        for t in range(tiles):
            prob_load(pair_count - 1, t).start()
        slope_load = local(slope_hbm, slopes, 13)
        weight_loads = []
        for place, source in enumerate((w_query, w_key, w_value)):
            for p in range(pair_count):
                weight_loads.append(
                    local(
                        source.at[:, pl.ds(pl.multiple_of(core * mine + p * PAIR, 128), PAIR)],
                        weight_in.at[:, pl.ds(p * mine + place * PAIR, PAIR)],
                        17 + place * pair_count + p,
                    )
                )
        for one in [slope_load] + weight_loads:
            one.start()

        def head_grads(here):
            result = contract(low_resid[here, :], weight_out[pl.ds(0, mine), :], 1, 1).astype(LOW)
            for p in range(pair_count):
                grad_heads[p, here, :] = result[:, p * PAIR : (p + 1) * PAIR]

        @pl.loop(0, tiles)
        def _(i):
            @pl.when(i > 1)
            def _():
                dz_far(i - 2).wait_recv()

            head_grads(rows_of(lax.rem(core * 2 + i, tiles) * TILE, TILE))

        joined = jnp.concatenate([heads[p] for p in range(pair_count)], 1)
        grad = contract(joined, low_resid[...], 0, 0).astype(LOW)
        kept = jnp.where(core == 0, grad[:, :mine], grad[:, mine:])
        given = jnp.where(core == 0, grad[:, mine:], grad[:, :mine])
        tall = width // COUNT
        for i in range(mine // tall):
            rank = core * (COUNT // 2) + i
            z, a, s = spot_of(rank, core)
            parts["out"][0, z, a, s] = kept[i * tall : (i + 1) * tall]
            _, a, s = spot_of(rank, other)
            stage_out[i // (wide * deep), a, s] = given[i * tall : (i + 1) * tall]
        give_out.start()
        for one in late_loads:
            one.wait()
        give_out.wait_recv()
        steps("out start", "up1 turn")

        keep = lanes_below((TILE, PAIR), HEAD)
        spots = (
            lax.broadcasted_iota(jnp.int32, (TILE, TILE), 0),
            lax.broadcasted_iota(jnp.int32, (TILE, TILE), 1),
        )
        after = jnp.where(spots[0] > spots[1], 1.0, 0.0).astype(LOW)

        def fade_send(t):
            part = pl.ds(t * (t + 1) // 2, t + 1)
            return remote(
                share_send.at[part],
                share_recv.at[part],
                df_sems.at[0, t],
                df_sems.at[1, t],
                partner,
            )

        def pair_step(step, p):
            for t in reversed(range(tiles)):
                count = (t + 1) * TILE
                span, rows = pl.ds(t * TILE, TILE), pl.ds(0, count)
                prob_load(p, t).wait()
                grad_tile = grad_heads[p, span, :]
                product = (grad_tile.astype(FULL) * heads[p, span, :].astype(FULL)).T
                query = queries[p, span, :]
                grads, masked_q, masked_g = [], [], []
                fade = None
                for h in range(2):
                    mask = keep == (h == 0)
                    masked_g.append(jnp.where(mask, grad_tile, LOW(0.0)))
                    masked_q.append(jnp.where(mask, query, LOW(0.0)))
                    delta = jnp.sum(product[h * HEAD : (h + 1) * HEAD, :], 0, keepdims=True)
                    change = probs[t][:, pl.ds(h * TILE, TILE)].astype(FULL) * (
                        contract(values[p, rows, :], masked_g[h], 1, 1) - delta
                    )
                    fade = change if fade is None else fade + change
                    grads.append(change.astype(LOW))

                @pl.when(step == 0)
                def _():
                    fades[rows, span] = fade

                @pl.when(step > 0)
                def _():
                    fades[rows, span] += fade

                both = jnp.concatenate(grads, 1)
                key_part = contract(both, jnp.concatenate(masked_q, 0), 1, 0)
                value_part = contract(probs[t][...], jnp.concatenate(masked_g, 0), 1, 0)
                if t == tiles - 1:
                    key_sum[...] = key_part
                    value_sum[...] = value_part
                else:
                    key_sum[rows, :] += key_part
                    value_sum[rows, :] += value_part
                query_part = contract(keys[p, rows, :], both, 0, 0)
                query_part = jnp.concatenate(
                    [query_part[:HEAD, :TILE], query_part[HEAD:, TILE:]], 0
                )
                grad_qkv[p, span, pl.ds(0, PAIR)] = (query_part.T * 0.125).astype(LOW)

                @pl.when(step < pair_count - 1)
                def _():
                    prob_load(p - 1, t).start()

                @pl.when((step == pair_count - 1) & (core == 1))
                def _():
                    share_send[pl.ds(t * (t + 1) // 2, t + 1)] = (
                        fades[rows, span].astype(LOW).reshape(t + 1, TILE, TILE)
                    )
                    fade_send(t).start()

        def lead_head():
            @pl.when(core == 0)
            def _():
                carry[...] = jnp.zeros_like(carry)
                for t in reversed(range(tiles)):
                    count = (t + 1) * TILE
                    span, rows = pl.ds(t * TILE, TILE), pl.ds(0, count)
                    part = pl.ds(t * (t + 1) // 2, t + 1)
                    fade_send(t).wait_recv()
                    total = fades[rows, span] + share_recv[part].astype(FULL).reshape(count, TILE)
                    later = contract(total.astype(LOW), after, 1, 0) + carry[rows, :]
                    if t:
                        carry[rows, :] += jnp.sum(total, -1, keepdims=True)
                    slope = slopes[part].astype(FULL).reshape(count, TILE)
                    extra = (-later * slope).astype(LOW)
                    query = jnp.where(keep, queries[0, span, :], LOW(0.0))
                    key_sum[rows, :] += contract(extra, query, 1, 0)
                    whole = contract(keys[0, rows, :], extra, 0, 0).T * 0.125
                    grad_qkv[0, span, pl.ds(0, PAIR)] = (
                        grad_qkv[0, span, pl.ds(0, PAIR)].astype(FULL)
                        + jnp.where(keep, whole, 0.0)
                    ).astype(LOW)

            @pl.when(core == 1)
            def _():
                for t in range(tiles):
                    fade_send(t).wait_send()

        def weights_into(kind, k, right):
            @pl.loop(0, 2)
            def _(m):
                place = pl.ds(pl.multiple_of(m * mine, 128), mine)
                grad = contract(low_in[:, place], right, 0, 0).astype(LOW)
                for i in range(mine // tall):
                    z, a, s = spot_of(m * (mine // tall) + i, core)
                    parts[kind][k, z, a, s] = grad[i * tall : (i + 1) * tall]

            if fused:
                Job(kind, k).start()

        @pl.loop(0, pair_count)
        def _(step):
            p = pair_count - 1 - step
            pair_step(step, p)
            grad_qkv[p, :, pl.ds(2 * PAIR, PAIR)] = value_sum[...].astype(LOW)

            @pl.when(p > 0)
            def _():
                grad_qkv[p, :, pl.ds(PAIR, PAIR)] = key_sum[...].astype(LOW)
                weights_into("attn", p - 1, grad_qkv[p])

            steps_when(step == 0, "up1 gather", "out turn", "down cross")
            steps_when(step == 1, "attn2 turn", "out gather", "up0 close")

        keep_all = lanes_below((length, PAIR), HEAD)
        second_head = jnp.where(
            keep_all,
            pltpu.roll(grad_qkv[0, :, pl.ds(0, PAIR)].astype(FULL), HEAD, 1),
            key_sum[...],
        )
        weights_into(
            "early",
            0,
            jnp.concatenate(
                [second_head.astype(LOW), grad_qkv[0, :, pl.ds(2 * PAIR, PAIR)]], 1
            ),
        )
        slope_load.wait()
        lead_head()
        grad_qkv[0, :, pl.ds(PAIR, PAIR)] = key_sum[...].astype(LOW)
        first_head = jnp.where(
            keep_all,
            grad_qkv[0, :, pl.ds(0, PAIR)].astype(FULL),
            pltpu.roll(key_sum[...], HEAD, 1),
        )
        weights_into("lead", 0, first_head.astype(LOW))

        for one in weight_loads:
            one.wait()

        def in_part(here):
            joined = jnp.concatenate([grad_qkv[p, here, :] for p in range(pair_count)], 1)
            return contract(joined, weight_in[...], 1, 1)

        @pl.loop(0, tiles)
        def _(i):
            part = in_part(rows_of(lax.rem(other * 2 + i, tiles) * TILE, TILE))

            @pl.when(i < 2)
            def _():
                stage[tile_rows(i), :] = part.astype(LOW)
                in_back(i).start()

            @pl.when(i >= 2)
            def _():
                fades[tile_rows(i - 2), pl.ds(0, width)] = part

            steps_when(i == 1, "attn1 turn", "attn2 gather")
            steps_when(i == 3, "early turn", "attn1 gather", "down close")

        steps("lead turn")
        for i in range(2):
            mid_far(i).wait_send()

        @pl.loop(0, 2)
        def _(i):
            here = tile_rows(i)
            in_back(i).wait_recv()
            grad = fades[here, pl.ds(0, width)] + catch_mid[here, :].astype(FULL)
            unit, inverse = layer_norm(tokens[here, :].astype(FULL))
            vec_sums[0:1, :] += jnp.sum(grad * unit, 0, keepdims=True)
            vec_sums[1:2, :] += jnp.sum(grad, 0, keepdims=True)
            scaled = grad * flat(gain_in)
            low_mid[here, :] = (
                grad_resid[here, :]
                + inverse
                * (
                    scaled
                    - jnp.mean(scaled, -1, keepdims=True)
                    - unit * jnp.mean(scaled * unit, -1, keepdims=True)
                )
            ).astype(LOW)

        in_put.start()
        for i in range(2):
            in_back(i).wait_send()

    pl.run_scoped(
        attention,
        pltpu.VMEM((tiles * (tiles + 1) // 2, TILE, TILE), LOW),
        pltpu.VMEM((length, length), FULL),
        pltpu.VMEM((length, PAIR), FULL),
        pltpu.VMEM((length, PAIR), FULL),
        pltpu.VMEM((length, 1), FULL),
        pltpu.VMEM((pair_count, length, mine), LOW),
        pltpu.VMEM((width, 3 * mine), LOW),
    )

    if not fused:
        for kind in KINDS[:-1]:
            one = pltpu.make_async_copy(parts[kind], results[kind], load_sems.at[0])
            one.start()
            one.wait()
        one = pltpu.make_async_copy(vec_sums, results["vec"], load_sems.at[0])
        one.start()
        one.wait()
    else:
        sums = vec_sums[...]
        tall = width // COUNT
        for rank in range(COUNT):
            z, a, s = spot_of(rank, core)
            shifted = pltpu.roll(sums, width - rank * tall, 1) if rank else sums
            parts["vec"][0, z, a, s] = shifted[:, :128]
    steps("vec start", "early gather")

    def out_part(here):
        return contract(hidden_low[0, here, :], weight_down[0], 1, 0) + contract(
            hidden_low[1, here, :], weight_down[1], 1, 0
        )

    @pl.loop(0, tiles)
    def _(i):
        part = out_part(rows_of(lax.rem(other * 2 + i, tiles) * TILE, TILE))

        @pl.when(i < 2)
        def _():
            stage_far[tile_rows(i), :] = part.astype(LOW)
            out_back(i).start()

        @pl.when(i >= 2)
        def _():
            resid[tile_rows(i - 2), :] += part

        steps_when(i == 0, "lead gather", "up1 close")
        steps_when(i == 1, "vec gather", "out close", "attn2 close")
        steps_when(i == 2, "attn1 close")

    steps("early close", "lead close", "down store", "up0 store", "up1 store")

    @pl.loop(0, 2)
    def _(i):
        here = tile_rows(i)
        out_back(i).wait_recv()
        low_mid[rows_of(half + i * TILE, TILE), :] = (
            resid[here, :] + catch_out[here, :].astype(FULL)
        ).astype(LOW)

    out_put.start()
    steps("out store", "attn2 store", "attn1 store", "early store", "vec close")
    steps("lead store", "vec store")
    if fused:
        for job in jobs.values():
            job.drain()
    in_put.wait()
    out_put.wait()
    g_far.wait_send()
    give_out.wait_send()
    for i in range(2):
        give_down(i).wait_send()
        for one in (dz_far, out_back):
            one(i).wait_send()


def finish(fused, tokens, cotangent, gain_in, gain_mid, shift_mid, forward, weights):
    low_in, queries, keys, values, probs, slopes, heads, heads_far = forward
    half, width = tokens.shape
    length, mine = 2 * half, width // 2
    hidden = weights[-1].shape[0]
    pairs, tiles = mine // PAIR, length // TILE
    shapes = block_shapes(width, hidden)
    long, wide, deep = GRID
    anywhere = pl.BlockSpec(memory_space=pl.ANY)
    local = pl.BlockSpec(memory_space=pltpu.VMEM)
    outs = [jax.ShapeDtypeStruct((half, width), LOW)] * 2
    out_specs = [anywhere] * 2
    for kind in KINDS:
        shape, kept = shapes[kind]
        if fused:
            outs.append(jax.ShapeDtypeStruct((FAN[kind], 2) + shape, kept))
            out_specs.append(local)
        elif kind == "vec":
            outs.append(jax.ShapeDtypeStruct((8, width), FULL))
            out_specs.append(anywhere)
        else:
            outs.append(jax.ShapeDtypeStruct((FAN[kind],) + GRID + shape, kept))
            out_specs.append(anywhere)
    scratch = [
        pltpu.VMEM((length, width), LOW),
        pltpu.VMEM((width, width), LOW),
        pltpu.VMEM((pairs, length, PAIR), LOW),
        pltpu.VMEM((pairs, half, PAIR), LOW),
        pltpu.VMEM((half, width), FULL),
        pltpu.VMEM((length, width), LOW),
        pltpu.VMEM((half, width), FULL),
        pltpu.VMEM((length, width), LOW),
        pltpu.VMEM((pairs, length, PAIR), LOW),
        pltpu.VMEM((length, width), LOW),
        pltpu.VMEM((pairs, length, PAIR), LOW),
        pltpu.VMEM((pairs, length, PAIR), LOW),
        pltpu.VMEM((pairs, length, PAIR), LOW),
    ]
    scratch += [pltpu.VMEM(((t + 1) * TILE, 2 * TILE), LOW) for t in range(tiles)]
    corners = tiles * (tiles + 1) // 2
    scratch += [pltpu.VMEM((corners, TILE, TILE), LOW)] * 2
    scratch += [pltpu.VMEM((half, width), LOW)] * 4
    block = hidden // 4
    scratch += [pltpu.VMEM((2, block, width), LOW), pltpu.VMEM((2, length, block), LOW)]
    scratch += [
        pltpu.VMEM((2, wide, deep) + shapes["down"][0], LOW),
        pltpu.VMEM((2, wide, deep) + shapes["out"][0], LOW),
        pltpu.VMEM((8, width), FULL),
    ]
    scratch += [pltpu.VMEM((FAN[kind],) + GRID + shapes[kind][0], shapes[kind][1]) for kind in KINDS]
    dma = pltpu.SemaphoreType.DMA
    if fused:
        leads = {kind: ((long, deep), (long,), (long - 1,), ()) for kind in KINDS}
        leads["down"] = ((long, deep), (long - 1, deep), (), ())
        leads["vec"] = ((3, long), (), (long - 1,), ())
        for step in range(4):
            scratch += [
                pltpu.VMEM((FAN[kind],) + leads[kind][step] + shapes[kind][0], shapes[kind][1])
                for kind in KINDS
            ]
        scratch += [dma((long,))] * 2 + [dma((long - 1,))] * 2 + [dma((1,))] * 4
        for kind in KINDS[1:]:
            fan = FAN[kind]
            count = 3 if kind == "vec" else fan
            scratch += [dma((count,))] * 4 + [dma((fan, long - 1))] * 2 + [dma((fan,))] * 2
    scratch += [dma((17 + 3 * pairs,)), dma((2,))]
    scratch += [dma((2, 2))] * 6
    scratch += [dma((2,)), dma((2, tiles)), dma((tiles,))]
    return pl.pallas_call(
        functools.partial(finish_kernel, fused),
        out_shape=outs,
        in_specs=[local] + [anywhere] + [local] * 3 + [anywhere] * (4 + tiles + 1 + 2 + 6),
        out_specs=out_specs,
        scratch_shapes=scratch,
        compiler_params=pltpu.CompilerParams(
            collective_id=0, has_side_effects=True, vmem_limit_bytes=VMEM_LIMIT
        ),
        name="finish",
    )(
        tokens,
        cotangent,
        gain_in,
        gain_mid,
        shift_mid,
        low_in,
        queries,
        keys,
        values,
        *probs,
        slopes,
        heads,
        heads_far,
        *weights,
    )

def deliver_kernel(
    output_in,
    grad_in,
    share_in,
    down,
    up,
    out,
    attn,
    early,
    lead,
    vec,
    output,
    input_grad,
    share,
    *grads,
):
    output[...] = output_in[...]
    input_grad[...] = grad_in[...]
    share[...] = share_in[0:1, :]
    g_query, g_key, g_value, g_out, g_up, g_down, *g_vecs = grads
    tall, mine = out.shape[2:]
    for k in range(2):
        g_down[:, k * mine : (k + 1) * mine] = down[0, k].astype(FULL)
        g_out[:, k * mine : (k + 1) * mine] = out[0, k].astype(FULL)
        for b in range(2):
            g_up[:, (2 * k + b) * 2 * mine : (2 * k + b + 1) * 2 * mine] = up[b, k].astype(FULL)
        for p in range(attn.shape[0]):
            for place, target in enumerate((g_query, g_key, g_value)):
                target[:, k * mine + (p + 1) * PAIR : k * mine + (p + 2) * PAIR] = attn[
                    p, k, :, place * PAIR : (place + 1) * PAIR
                ].astype(FULL)
        start = k * mine
        ones, twos = lead[0, k].astype(FULL), early[0, k].astype(FULL)
        keep = lanes_below(ones.shape, HEAD)
        seconds = twos[:, :PAIR]
        g_query[:, start : start + PAIR] = jnp.where(keep, ones, pltpu.roll(seconds, HEAD, 1))
        g_key[:, start : start + PAIR] = jnp.where(keep, pltpu.roll(ones, HEAD, 1), seconds)
        g_value[:, start : start + PAIR] = twos[:, PAIR:]
    sums = vec[0, 0] + vec[0, 1]
    for i, target in enumerate(g_vecs):
        target[...] = sums[i, :tall]


def deliver(output, input_grad, shares, down, up, out, attn, early, lead, vec):
    tall, mine = out.shape[2:]
    width = 2 * mine
    shapes = [(tall, width)] * 4 + [(tall, 2 * up.shape[3] * 2), (down.shape[2], width)]
    shapes += [(tall,)] * 4
    return pl.pallas_call(
        deliver_kernel,
        out_shape=[
            jax.ShapeDtypeStruct(output.shape, output.dtype),
            jax.ShapeDtypeStruct(input_grad.shape, input_grad.dtype),
            jax.ShapeDtypeStruct((1, shares.shape[1]), FULL),
        ]
        + [jax.ShapeDtypeStruct(shape, FULL) for shape in shapes],
        compiler_params=pltpu.CompilerParams(vmem_limit_bytes=VMEM_LIMIT),
        name="deliver",
    )(output, input_grad, shares, down, up, out, attn, early, lead, vec)


def reduce_plain(parts, rows):
    down, up, out, attn, early, lead, vec = parts
    width = vec.shape[1]

    def scattered(part):
        summed = lax.psum_scatter(part.astype(FULL), "rows", scatter_dimension=0, tiled=True)
        return summed.astype(LOW)

    def joined(part):
        return lax.all_gather(part, "keys", axis=1, tiled=True).astype(FULL)

    def flat_part(part):
        return part.reshape(-1, part.shape[-1])

    ones, twos = scattered(flat_part(lead[0])), scattered(flat_part(early[0]))
    first = [
        jnp.concatenate([ones[:, :HEAD], twos[:, :HEAD]], 1),
        jnp.concatenate([ones[:, HEAD:], twos[:, HEAD:PAIR]], 1),
        twos[:, PAIR:],
    ]
    rest = [scattered(flat_part(attn[p])) for p in range(attn.shape[0])]
    halves = [
        jnp.concatenate([first[i]] + [one[:, i * PAIR : (i + 1) * PAIR] for one in rest], 1)
        for i in range(3)
    ]
    halves.append(scattered(flat_part(out[0])))
    halves.append(jnp.concatenate([scattered(flat_part(up[b])) for b in range(2)], 1))
    halves.append(scattered(flat_part(down[0])))
    sums = lax.psum_scatter(
        lax.psum(vec[:4].T, "keys"), "rows", scatter_dimension=0, tiled=True
    )
    return [joined(one) for one in halves], [sums[:, i] for i in range(4)]


def body(
    rows,
    tokens,
    seg_ids,
    doc_starts,
    gain_in,
    shift_in,
    w_query,
    w_key,
    w_value,
    w_out,
    gain_mid,
    shift_mid,
    w_up,
    w_down,
    out_grad,
):
    fused = rows == COUNT
    own_tokens, own_grad = tokens[0], out_grad[0]
    low_in, queries, keys, values, probs, slopes, heads, heads_far, shares = attend(
        own_tokens, seg_ids, gain_in, shift_in, w_query, w_key, w_value
    )
    output, input_grad, *parts = finish(
        fused,
        own_tokens,
        own_grad,
        gain_in,
        gain_mid,
        shift_mid,
        (low_in, queries, keys, values, probs, slopes, heads, heads_far),
        (w_query, w_key, w_value, w_out, w_up, w_down),
    )
    if fused:
        output, input_grad, shares, *grads = deliver(output, input_grad, shares, *parts)
        grads, vectors = grads[:6], grads[6:]
    else:
        grads, vectors = reduce_plain(parts, rows)
    g_query, g_key, g_value, g_out, g_up, g_down = grads
    return (
        output[None],
        input_grad[None],
        shares[:1],
        vectors[0],
        vectors[1],
        g_query,
        g_key,
        g_value,
        g_out,
        vectors[2],
        vectors[3],
        g_up,
        g_down,
    )


def solution(mesh):
    in_specs = (
        P("rows", "keys", None),
        P("rows", None),
        P("rows", "keys"),
        P(),
        P(),
        P(),
        P(),
        P(),
        P(),
        P(),
        P(),
        P(),
        P(),
        P("rows", "keys", None),
    )
    out_specs = (
        P("rows", "keys", None),
        P("rows", "keys", None),
        P("rows", "keys"),
        P("rows"),
        P("rows"),
        P("rows", None),
        P("rows", None),
        P("rows", None),
        P("rows", None),
        P("rows"),
        P("rows"),
        P("rows", None),
        P("rows", None),
    )
    return jax.shard_map(
        functools.partial(body, mesh.shape["rows"]),
        mesh=mesh,
        in_specs=in_specs,
        out_specs=out_specs,
        check_vma=False,
    )
```

```python
import functools

import jax
import jax.numpy as jnp
from jax import lax
from jax.experimental import pallas as pl
from jax.experimental.pallas import tpu as pltpu
from jax.sharding import PartitionSpec as P

HEAD = 64
PAIR = 2 * HEAD
TILE = 256
EPS = 1e-05
MASKED = 1e30
SELECT_SHIFT = 4.0
LOW = jnp.bfloat16
FULL = jnp.float32
MESH = pl.DeviceIdType.MESH
VMEM_LIMIT = 67_000_000


def contract(left, right, left_dim, right_dim):
    return lax.dot_general(
        left, right, (((left_dim,), (right_dim,)), ((), ())), preferred_element_type=FULL
    )


def layer_norm(field):
    center = field - jnp.mean(field, -1, keepdims=True)
    inverse = lax.rsqrt(jnp.mean(center * center, -1, keepdims=True) + EPS)
    return center * inverse, inverse


def remote(source, target, send, recv, device):
    return pltpu.make_async_remote_copy(
        src_ref=source,
        dst_ref=target,
        send_sem=send,
        recv_sem=recv,
        device_id=device,
        device_id_type=MESH,
    )


def lanes_below(shape, bound):
    return lax.broadcasted_iota(jnp.int32, shape, len(shape) - 1) < bound


def flat(ref):
    return ref[...].reshape(1, ref.shape[0])


def corner(step, tiles):
    t = sum((step >= n * (n + 1) // 2).astype(jnp.int32) for n in range(1, tiles))
    return t, step - t * (t + 1) // 2


def rows_of(start, size):
    return pl.ds(pl.multiple_of(start, size), size)


def attend_kernel(
    tokens,
    seg,
    gain,
    shift,
    w_query,
    w_key,
    w_value,
    low_in_out,
    query_out,
    key_out,
    value_out,
    prob_outs,
    slopes_out,
    heads_out,
    other_out,
    share_out,
    all_tokens,
    low_in,
    weights,
    queries,
    keys,
    values,
    lead_query,
    lead_key,
    probs,
    slopes,
    penalty,
    heads,
    seg_cols,
    free_cols,
    running,
    numerator,
    pairs_seen,
    far_send,
    far_recv,
    head_send,
    head_recv,
    weight_sems,
    out_sems,
    prob_sems,
):
    core = lax.axis_index("keys")
    row = lax.axis_index("rows")
    other = 1 - core
    partner = (row, other)
    half, width = tokens.shape
    length = 2 * half
    mine = width // 2
    pair_count = mine // PAIR
    tiles = length // TILE

    columns = pl.ds(pl.multiple_of(core * mine, 128), mine)
    loads = []
    for place, source in enumerate((w_query, w_key, w_value)):
        loads.append((source.at[:, columns], weights.at[:, pl.ds(place * mine, mine)]))
    for place, source in enumerate((w_query, w_key)):
        loads.append(
            (source.at[:, pl.ds(0, PAIR)], weights.at[:, pl.ds(3 * mine + place * PAIR, PAIR)])
        )
    own = rows_of(core * half, half)
    loads = [
        pltpu.make_async_copy(source, target, weight_sems.at[i])
        for i, (source, target) in enumerate(loads)
    ]
    own_load = pltpu.make_async_copy(tokens, all_tokens.at[own], weight_sems.at[5])
    own_load.start()
    for one in loads:
        one.start()

    barrier = pltpu.get_barrier_semaphore()
    pl.semaphore_signal(barrier, inc=1, device_id=partner, device_id_type=MESH)
    pl.semaphore_wait(barrier, 1)
    exchange = remote(tokens, all_tokens.at[own], far_send, far_recv, partner)
    exchange.start()

    seg_row = seg[...]
    seg_wide = jnp.broadcast_to(seg_row.astype(FULL), (128, length))
    spot = lax.broadcasted_iota(jnp.int32, (128, length), 1)
    before = pltpu.roll(seg_wide, 1, 1)
    free_wide = jnp.where((spot > 0) & (before == seg_wide), 1.0, 0.0)
    seg_cols[...] = seg_wide.T
    free_cols[...] = free_wide.T
    own_load.wait()

    keep = lanes_below((TILE, PAIR), HEAD)

    @pl.loop(0, tiles)
    def _(i):
        @pl.when(i == half // TILE)
        def _():
            exchange.wait_recv()

        here = rows_of(lax.rem(core * (half // TILE) + i, tiles) * TILE, TILE)
        unit, _ = layer_norm(all_tokens[here, :].astype(FULL))
        low_in[here, :] = (unit * flat(gain) + flat(shift)).astype(LOW)

        @pl.when(i == 0)
        def _():
            for one in loads:
                one.wait()

        result = contract(low_in[here, :], weights[...], 1, 0).astype(LOW)
        for p in range(pair_count):
            queries[p, here, :] = result[:, p * PAIR : (p + 1) * PAIR] * LOW(0.125)
            keys[p, here, :] = result[:, mine + p * PAIR : mine + (p + 1) * PAIR]
            values[p, here, :] = result[:, 2 * mine + p * PAIR : 2 * mine + (p + 1) * PAIR]
        first = result[:, 3 * mine : 3 * mine + PAIR]
        lead_query[here, :] = jnp.where(keep, first, LOW(0.0)) * LOW(0.125)
        lead_key[here, :] = result[:, 3 * mine + PAIR :]

    puts = [
        pltpu.make_async_copy(low_in, low_in_out, out_sems.at[0]),
        pltpu.make_async_copy(queries, query_out, out_sems.at[1]),
        pltpu.make_async_copy(keys, key_out, out_sems.at[2]),
        pltpu.make_async_copy(values, value_out, out_sems.at[3]),
    ]
    for one in puts:
        one.start()

    spots = (
        lax.broadcasted_iota(jnp.int32, (2 * TILE, 2 * TILE), 0),
        lax.broadcasted_iota(jnp.int32, (2 * TILE, 2 * TILE), 1),
    )
    earlier = jnp.where(spots[0] < spots[1], 1.0, 0.0).astype(LOW)
    running[...] = jnp.zeros_like(running)
    numerator[...] = jnp.zeros_like(numerator)
    pairs_seen[...] = jnp.zeros_like(pairs_seen)

    @pl.loop(0, (tiles // 2) * (tiles // 2 + 1) // 2)
    def _(step):
        wide, k = corner(step, tiles // 2)
        rows, span = rows_of(k * 2 * TILE, 2 * TILE), rows_of(wide * 2 * TILE, 2 * TILE)
        scores = contract(lead_key[rows, :], lead_query[span, :], 1, 1)
        repeat = 2 * TILE // 128
        same = jnp.concatenate([seg_cols[rows, :]] * repeat, 1) == seg[:, span].astype(FULL)
        ahead = spots[1] - spots[0] + (wide - k) * 2 * TILE
        later = same & (ahead > 0)
        allowed = same & (ahead >= 0)
        select = jnp.where(later, jnp.concatenate([free_cols[rows, :]] * repeat, 1), 0.0)
        level = scores - SELECT_SHIFT
        chosen = select * (jnp.maximum(level, 0.0) + jnp.log(1.0 + jnp.exp(-jnp.abs(level))))
        slope = (select * (0.5 + 0.5 * jnp.tanh(0.5 * level))).astype(LOW)

        slopes[wide * (2 * wide + 1) + 2 * k] = slope[:TILE, :TILE]

        @pl.when(k < wide)
        def _():
            slopes[wide * (2 * wide + 1) + 2 * k + 1] = slope[TILE:, :TILE]

        slopes[(2 * wide + 1) * (wide + 1) + 2 * k] = slope[:TILE, TILE:]
        slopes[(2 * wide + 1) * (wide + 1) + 2 * k + 1] = slope[TILE:, TILE:]
        high = chosen.astype(LOW)
        rest = (chosen - high.astype(FULL)).astype(LOW)
        total = (
            running[rows, :] + contract(high, earlier, 1, 0) + contract(rest, earlier, 1, 0)
        )
        penalty[rows, span] = jnp.where(allowed, total, MASKED)
        running[rows, :] += jnp.sum(chosen, -1, keepdims=True)
        share = jnp.where(later, 0.5 + 0.5 * jnp.tanh(0.5 * total - 1.0), 0.0)
        numerator[rows, :] += jnp.sum(share, -1, keepdims=True)
        pairs_seen[rows, :] += jnp.sum(jnp.where(later, 1.0, 0.0), -1, keepdims=True)

    slope_put = pltpu.make_async_copy(slopes, slopes_out, out_sems.at[4])
    slope_put.start()

    shares = numerator[own, :] / jnp.maximum(pairs_seen[own, :], 1.0)
    share_out[...] = jnp.broadcast_to(shares, (half, 128)).T[0:8, :]

    def put_probs(p, t):
        return pltpu.make_async_copy(
            probs[t].at[p], prob_outs[t].at[p], prob_sems.at[p, t]
        )

    def send_heads(p):
        return remote(
            heads.at[p, rows_of(other * half, half)],
            other_out.at[p],
            head_send.at[p],
            head_recv.at[p],
            partner,
        )

    @pl.loop(0, pair_count)
    def _(p):
        for t in range(tiles):
            count = (t + 1) * TILE
            span = pl.ds(t * TILE, TILE)
            query = queries[p, span, :]
            outs = []
            for h in range(2):
                masked = jnp.where(keep == (h == 0), query, LOW(0.0))
                logits = (
                    contract(keys[p, pl.ds(0, count), :], masked, 1, 1)
                    - penalty[pl.ds(0, count), span]
                )
                scaled = jnp.exp(logits - jnp.max(logits, 0, keepdims=True))
                prob = (scaled * (1.0 / jnp.sum(scaled, 0, keepdims=True))).astype(LOW)
                probs[t][p, :, pl.ds(h * TILE, TILE)] = prob
                out = contract(values[p, pl.ds(0, count), :], prob, 0, 0)
                outs.append(out[h * HEAD : (h + 1) * HEAD, :])
            heads[p, span, :] = jnp.concatenate(outs, 0).T.astype(LOW)
            put_probs(p, t).start()
        send_heads(p).start()

    last = pltpu.make_async_copy(heads, heads_out, out_sems.at[5])
    last.start()
    for p in range(pair_count):
        send_heads(p).wait()
        for t in range(tiles):
            put_probs(p, t).wait()
    for one in puts + [slope_put, last]:
        one.wait()
    exchange.wait_send()


def attend(tokens, seg, gain, shift, w_query, w_key, w_value):
    half, width = tokens.shape
    length, mine = 2 * half, width // 2
    pairs, tiles = mine // PAIR, 2 * half // TILE
    spans = [(t + 1) * TILE for t in range(tiles)]
    corners = tiles * (tiles + 1) // 2
    outs = [
        jax.ShapeDtypeStruct((length, width), LOW),
        jax.ShapeDtypeStruct((pairs, length, PAIR), LOW),
        jax.ShapeDtypeStruct((pairs, length, PAIR), LOW),
        jax.ShapeDtypeStruct((pairs, length, PAIR), LOW),
        [jax.ShapeDtypeStruct((pairs, span, 2 * TILE), LOW) for span in spans],
        jax.ShapeDtypeStruct((corners, TILE, TILE), LOW),
        jax.ShapeDtypeStruct((pairs, length, PAIR), LOW),
        jax.ShapeDtypeStruct((pairs, half, PAIR), LOW),
        jax.ShapeDtypeStruct((8, half), FULL),
    ]
    anywhere = pl.BlockSpec(memory_space=pl.ANY)
    local = pl.BlockSpec(memory_space=pltpu.VMEM)
    out_specs = [anywhere] * 4 + [[anywhere] * tiles, anywhere, anywhere, anywhere, local]
    scratch = [
        pltpu.VMEM((length, width), LOW),
        pltpu.VMEM((length, width), LOW),
        pltpu.VMEM((width, 3 * mine + 2 * PAIR), LOW),
        pltpu.VMEM((pairs, length, PAIR), LOW),
        pltpu.VMEM((pairs, length, PAIR), LOW),
        pltpu.VMEM((pairs, length, PAIR), LOW),
        pltpu.VMEM((length, PAIR), LOW),
        pltpu.VMEM((length, PAIR), LOW),
        [pltpu.VMEM((pairs, span, 2 * TILE), LOW) for span in spans],
        pltpu.VMEM((corners, TILE, TILE), LOW),
        pltpu.VMEM((length, length), FULL),
        pltpu.VMEM((pairs, length, PAIR), LOW),
        pltpu.VMEM((length, 128), FULL),
        pltpu.VMEM((length, 128), FULL),
        pltpu.VMEM((length, 1), FULL),
        pltpu.VMEM((length, 1), FULL),
        pltpu.VMEM((length, 1), FULL),
        pltpu.SemaphoreType.DMA,
        pltpu.SemaphoreType.DMA,
        pltpu.SemaphoreType.DMA((pairs,)),
        pltpu.SemaphoreType.DMA((pairs,)),
        pltpu.SemaphoreType.DMA((6,)),
        pltpu.SemaphoreType.DMA((6,)),
        pltpu.SemaphoreType.DMA((pairs, tiles)),
    ]
    return pl.pallas_call(
        attend_kernel,
        out_shape=outs,
        in_specs=[anywhere] + [local] * 3 + [anywhere] * 3,
        out_specs=out_specs,
        scratch_shapes=scratch,
        compiler_params=pltpu.CompilerParams(
            collective_id=1, has_side_effects=True, vmem_limit_bytes=VMEM_LIMIT
        ),
        name="attend",
    )(tokens, seg, gain, shift, w_query, w_key, w_value)

def gelu_parts(field):
    scale = 0.7978845608028654
    square = field * field
    inner = jnp.tanh(scale * field * (1.0 + 0.044715 * square))
    half_sum = 0.5 * (1.0 + inner)
    slope = half_sum + 0.5 * field * (1.0 - inner * inner) * (
        scale * (1.0 + 3.0 * 0.044715 * square)
    )
    return field * half_sum, slope


GRID = (4, 2, 2)
COUNT = GRID[0] * GRID[1] * GRID[2]
KINDS = ("down", "up", "out", "attn", "early", "lead", "vec")
FAN = {"down": 1, "up": 2, "out": 1, "attn": 2, "early": 1, "lead": 1, "vec": 1}


def block_shapes(width, hidden):
    mine = width // 2
    tall = width // COUNT
    return {
        "down": ((hidden // COUNT, mine), LOW),
        "up": ((tall, mine * 2), LOW),
        "out": ((tall, mine), LOW),
        "attn": ((tall, mine), LOW),
        "early": ((tall, 2 * PAIR), LOW),
        "lead": ((tall, PAIR), LOW),
        "vec": ((8, 128), FULL),
    }


def finish_kernel(fused, *refs):
    refs = list(refs)

    def take(count):
        taken = refs[:count]
        del refs[:count]
        return taken if count > 1 else taken[0]

    tokens, cotangent, gain_in, gain_mid, shift_mid = take(5)
    low_in_hbm, query_hbm, key_hbm, value_hbm = take(4)
    prob_hbm, slope_hbm = take(4), take(1)
    heads_hbm, other_hbm = take(2)
    w_query, w_key, w_value, w_out, w_up, w_down = take(6)
    output, input_grad = take(2)
    results = dict(zip(KINDS, take(len(KINDS))))
    (
        grads_all,
        weight_out,
        heads,
        heads_far,
        resid,
        low_mid,
        grad_resid,
        low_resid,
        grad_heads,
        low_in,
        queries,
        keys,
        values,
    ) = take(13)
    probs = take(4)
    share_send, share_recv = take(2)
    stage, stage_far, catch_mid, catch_out = take(4)
    weight_down, hidden_low = take(2)
    stage_down, stage_out = take(2)
    vec_sums = take(1)
    parts = dict(zip(KINDS, take(len(KINDS))))
    if fused:
        got1 = dict(zip(KINDS, take(len(KINDS))))
        got2 = dict(zip(KINDS, take(len(KINDS))))
        got3 = dict(zip(KINDS, take(len(KINDS))))
        pair = dict(zip(KINDS, take(len(KINDS))))
        sems = {
            name: take(2) for name in ("down1", "down2", "down3", "down4")
        }
        for kind in KINDS[1:]:
            for stage_name in "1234":
                sems[kind + stage_name] = take(2)
        for kind in KINDS:
            sems[kind + "5"] = take(1)
    (load_sems, g_sems, mid_sems, dz_sems, a_sems, b_sems, c_sems, pd_sems, po_sems, df_sems, prob_sems) = take(11)

    long, wide, deep = GRID
    core = lax.axis_index("keys")
    row = lax.axis_index("rows")
    other = 1 - core
    partner = (row, other)
    half, width = tokens.shape
    length, mine = 2 * half, width // 2
    pair_count = mine // PAIR
    tiles = length // TILE
    hidden = w_down.shape[0]
    block = hidden // 4
    own_start, far_start = core * half, other * half

    if fused:
        slow, mid, fast = row // (wide * deep), (row // deep) % wide, row % deep
    else:
        slow, mid, fast = 0, 0, 0

    def spot_of(rank, whose):
        z, y, x = rank // (wide * deep), (rank // deep) % wide, rank % deep
        if not fused:
            return z, y, x
        return z, x + whose * (y - x), y + whose * (x - y)

    first, second = fast + core * (mid - fast), mid + core * (fast - mid)
    near, next_ = 1 - first, 1 - second

    def rank_of(z, a, b):
        y, x = b + core * (a - b), a + core * (b - a)
        return (z * wide + y) * deep + x

    near_device = (rank_of(slow, near, second), core)
    next_device = (rank_of(slow, first, next_), core)
    far_places = [lax.rem(slow + step, long) for step in range(1, long)]

    def add_into(target, index, terms):
        total = target[index].astype(FULL)
        for term in terms:
            total = total + term.astype(FULL)
        target[index] = total.astype(target.dtype)

    class Job:
        def __init__(self, kind, k):
            self.kind, self.k = kind, k

        def first_copy(self):
            kind, k = self.kind, self.k
            part, got = parts[kind].at[k], got1[kind].at[k]
            send, recv = sems[kind + "1"]
            return remote(part.at[:, near], got, send.at[k], recv.at[k], near_device)

        def second_copy(self):
            kind, k = self.kind, self.k
            part, got = parts[kind].at[k], got2[kind].at[k]
            send, recv = sems[kind + "2"]
            return remote(part.at[:, first, next_], got, send.at[k], recv.at[k], next_device)

        def third_copies(self):
            kind, k = self.kind, self.k
            send, recv = sems[kind + "3"]
            return [
                remote(
                    parts[kind].at[k, z, first, second],
                    got3[kind].at[k, step],
                    send.at[k, step],
                    recv.at[k, step],
                    (rank_of(z, first, second), core),
                )
                for step, z in enumerate(far_places)
            ]

        def last_copy(self):
            kind, k = self.kind, self.k
            send, recv = sems[kind + "4"]
            return remote(
                parts[kind].at[k, slow, first, second],
                pair[kind].at[k],
                send.at[k],
                recv.at[k],
                partner,
            )

        def start(self):
            self.first_copy().start()

        def turn(self):
            self.first_copy().wait_recv()
            kind, k = self.kind, self.k

            @pl.loop(0, long * deep)
            def _(step):
                z, b = step // deep, lax.rem(step, deep)
                add_into(parts[kind], (k, z, first, b), [got1[kind][k, z, b]])

            self.second_copy().start()

        def gather(self):
            self.second_copy().wait_recv()
            kind, k = self.kind, self.k

            @pl.loop(0, long)
            def _(z):
                add_into(parts[kind], (k, z, first, second), [got2[kind][k, z]])

            for one in self.third_copies():
                one.start()

        def close(self):
            for one in self.third_copies():
                one.wait_recv()
            kind, k = self.kind, self.k
            add_into(
                parts[kind],
                (k, slow, first, second),
                [got3[kind][k, step] for step in range(long - 1)],
            )
            self.last_copy().start()

        def puts(self):
            kind, k = self.kind, self.k
            own_part = parts[kind].at[k, slow, first, second]
            sem = sems[kind + "5"]
            return [
                pltpu.make_async_copy(own_part, results[kind].at[k, core], sem.at[k, 0]),
                pltpu.make_async_copy(pair[kind].at[k], results[kind].at[k, other], sem.at[k, 1]),
            ]

        def store(self):
            self.last_copy().wait_recv()
            for one in self.puts():
                one.start()

        def drain(self):
            self.first_copy().wait_send()
            self.second_copy().wait_send()
            for one in self.third_copies():
                one.wait_send()
            self.last_copy().wait_send()
            for one in self.puts():
                one.wait()

    class Down(Job):
        def near_copy(self, z):
            send, recv = sems["down1"]
            return remote(
                parts["down"].at[0, z, near],
                got1["down"].at[0, z],
                send.at[z],
                recv.at[z],
                near_device,
            )

        def slow_copy(self, step):
            z = lax.rem(slow + step, long)
            send, recv = sems["down2"]
            return remote(
                parts["down"].at[0, z, first],
                got2["down"].at[0, step - 1],
                send.at[step - 1],
                recv.at[step - 1],
                (rank_of(z, first, second), core),
            )

        def next_copy(self):
            send, recv = sems["down3"]
            return remote(
                parts["down"].at[0, slow, first, next_],
                got3["down"].at[0],
                send.at[0],
                recv.at[0],
                next_device,
            )

        def start_at(self, z):
            self.near_copy(z).start()

        def turn_at(self, z):
            self.near_copy(z).wait_recv()

            @pl.loop(0, deep)
            def _(b):
                add_into(parts["down"], (0, z, first, b), [got1["down"][0, z, b]])

            step = lax.rem(z - slow + long, long)

            @pl.when(step > 0)
            def _():
                self.slow_copy(step).start()

        def cross(self):
            for step in range(1, long):
                self.slow_copy(step).wait_recv()

            @pl.loop(0, deep)
            def _(b):
                add_into(
                    parts["down"],
                    (0, slow, first, b),
                    [got2["down"][0, step, b] for step in range(long - 1)],
                )

            self.next_copy().start()

        def close(self):
            self.next_copy().wait_recv()
            add_into(parts["down"], (0, slow, first, second), [got3["down"][0]])
            self.last_copy().start()

        def drain(self):
            for z in range(long):
                self.near_copy(z).wait_send()
            for step in range(1, long):
                self.slow_copy(step).wait_send()
            self.next_copy().wait_send()
            self.last_copy().wait_send()
            for one in self.puts():
                one.wait()

    class Vectors(Job):
        def first_copies(self):
            send, recv = sems["vec1"]
            places = ((near, second), (first, next_), (near, next_))
            return [
                remote(
                    parts["vec"].at[0, :, a, b],
                    got1["vec"].at[0, i],
                    send.at[i],
                    recv.at[i],
                    (rank_of(slow, a, b), core),
                )
                for i, (a, b) in enumerate(places)
            ]

        def start(self):
            for one in self.first_copies():
                one.start()

        def gather(self):
            for one in self.first_copies():
                one.wait_recv()

            @pl.loop(0, long)
            def _(z):
                add_into(
                    parts["vec"], (0, z, first, second), [got1["vec"][0, i, z] for i in range(3)]
                )

            for one in self.third_copies():
                one.start()

        def drain(self):
            for one in self.first_copies() + self.third_copies():
                one.wait_send()
            self.last_copy().wait_send()
            for one in self.puts():
                one.wait()

    def steps(*names):
        if fused:
            for name in names:
                job, step = name.split()
                getattr(jobs[job], step)()

    def steps_when(condition, *names):
        if fused:
            pl.when(condition)(lambda: steps(*names))

    down = Down("down", 0)
    jobs = {"down": down, "vec": Vectors("vec", 0)}
    jobs |= {kind: Job(kind, 0) for kind in ("out", "early", "lead")}
    jobs |= {f"up{k}": Job("up", k) for k in range(2)}
    jobs |= {f"attn{k + 1}": Job("attn", k) for k in range(pair_count - 1)}

    def local(source, target, index):
        return pltpu.make_async_copy(source, target, load_sems.at[index])

    own = rows_of(own_start, half)
    in_put = local(low_mid.at[pl.ds(0, half)], input_grad, 0)
    out_put = local(low_mid.at[pl.ds(half, half)], output, 1)
    g_load = local(cotangent, grads_all.at[own], 0)
    out_loads = [
        local(w_out.at[rows_of(core * mine, mine)], weight_out.at[pl.ds(0, mine)], 1),
        local(w_out.at[rows_of(other * mine, mine)], weight_out.at[pl.ds(mine, mine)], 2),
        local(heads_hbm, heads, 3),
        local(other_hbm, heads_far, 4),
    ]
    late_loads = [
        local(low_in_hbm, low_in, 5),
        local(query_hbm, queries, 6),
        local(key_hbm, keys, 7),
        local(value_hbm, values, 8),
    ]
    for one in out_loads + [g_load]:
        one.start()

    peers = [partner]
    if fused:
        peers += [near_device, next_device, (rank_of(slow, near, next_), core)]
        peers += [(rank_of(z, first, second), core) for z in far_places]
    barrier = pltpu.get_barrier_semaphore()
    for peer in peers:
        pl.semaphore_signal(barrier, inc=1, device_id=peer, device_id_type=MESH)

    def own_rows(i):
        return rows_of(own_start + i * TILE, TILE)

    def far_rows(i):
        return rows_of(far_start + i * TILE, TILE)

    def tile_rows(i):
        return rows_of(i * TILE, TILE)

    def to_partner(source, target, pair_sems):
        def one(i):
            return remote(
                source(i), target(i), pair_sems.at[0, i], pair_sems.at[1, i], partner
            )

        return one

    g_far = remote(cotangent, grads_all.at[own], g_sems.at[0], g_sems.at[1], partner)
    mid_far = to_partner(
        lambda i: low_mid.at[own_rows(i)], lambda i: low_mid.at[own_rows(i)], mid_sems
    )
    dz_far = to_partner(
        lambda i: low_resid.at[own_rows(i)], lambda i: low_resid.at[own_rows(i)], dz_sems
    )
    mid_back = to_partner(
        lambda i: stage.at[tile_rows(i)], lambda i: catch_mid.at[tile_rows(i)], a_sems
    )
    in_back = to_partner(
        lambda i: stage.at[tile_rows(i)], lambda i: catch_mid.at[tile_rows(i)], b_sems
    )
    out_back = to_partner(
        lambda i: stage_far.at[tile_rows(i)], lambda i: catch_out.at[tile_rows(i)], c_sems
    )

    def feed_forward(weight_up, grad_up):
        up_loads = [
            local(
                w_up.at[:, pl.ds(pl.multiple_of((core * 2 + b) * block, 128), block)],
                weight_up.at[b],
                9 + b,
            )
            for b in range(2)
        ]
        down_loads = [
            local(w_down.at[rows_of((core * 2 + b) * block, block)], weight_down.at[b], 11 + b)
            for b in range(2)
        ]
        for b in range(2):
            up_loads[b].start()
            down_loads[b].start()
        for one in out_loads:
            one.wait()

        @pl.loop(0, 2)
        def _(i):
            here, place = tile_rows(i), own_rows(i)
            joined = jnp.concatenate(
                [heads[p, place, :] for p in range(pair_count)]
                + [heads_far[p, here, :] for p in range(pair_count)],
                1,
            )
            field = tokens[here, :].astype(FULL) + contract(joined, weight_out[...], 1, 0)
            resid[here, :] = field
            unit, _ = layer_norm(field)
            low_mid[place, :] = (unit * flat(gain_mid) + flat(shift_mid)).astype(LOW)

        pl.semaphore_wait(barrier, len(peers))
        for i in range(2):
            mid_far(i).start()
        g_far.start()

        for one in up_loads + down_loads + [g_load]:
            one.wait()
        for one in late_loads:
            one.start()

        @pl.loop(0, 2)
        def _(b):
            @pl.loop(0, tiles)
            def _(i):
                @pl.when((b == 0) & (i == 2))
                def _():
                    for j in range(2):
                        mid_far(j).wait_recv()

                here = rows_of(lax.rem(core * 2 + i, tiles) * TILE, TILE)
                value, slope = gelu_parts(contract(low_mid[here, :], weight_up[b], 1, 0))
                hidden_low[b, here, :] = value.astype(LOW)
                grad_up[b, here, :] = slope.astype(LOW)
                if fused:

                    @pl.when((b == 1) & (i == 3))
                    def _():
                        down.turn_at(core * 2)

            @pl.when(b == 0)
            def _():
                g_far.wait_recv()

            tall = hidden // COUNT
            per = mine // tall
            @pl.loop(0, 2)
            def _(m):
                place = pl.ds(pl.multiple_of(m * mine, 128), mine)
                grad = contract(hidden_low[b, :, place], grads_all[...], 0, 0).astype(LOW)
                kept = jnp.where(core == 0, grad[:, :mine], grad[:, mine:])
                given = jnp.where(core == 0, grad[:, mine:], grad[:, :mine])
                for i in range(per):
                    rank = (core * 2 + b) * (COUNT // 4) + m * per + i
                    z, a, s = spot_of(rank, core)
                    parts["down"][0, z, a, s] = kept[i * tall : (i + 1) * tall]
                    _, a, s = spot_of(rank, other)
                    stage_down[b, a, s] = given[i * tall : (i + 1) * tall]
            give_down(b).start()
            if fused:
                down.start_at(core * 2 + b)

            @pl.loop(0, tiles)
            def _(i):
                here = rows_of(i * TILE, TILE)
                back = contract(grads_all[here, :], weight_down[b], 1, 1)
                grad_up[b, here, :] = (back * grad_up[b, here, :].astype(FULL)).astype(LOW)

                @pl.when(i == 3)
                def _():
                    give_down(b).wait_recv()
                    if fused:
                        down.start_at(other * 2 + b)

                if fused:

                    @pl.when((b == 1) & (i == 1))
                    def _():
                        down.turn_at(other * 2)

            @pl.loop(0, 2)
            def _(m):
                tall = width // COUNT
                per = mine // tall
                place = pl.ds(pl.multiple_of(m * mine, 128), mine)
                grad = contract(low_mid[:, place], grad_up[b], 0, 0).astype(LOW)
                for i in range(per):
                    z, a, s = spot_of(m * per + i, core)
                    parts["up"][b, z, a, s] = grad[i * tall : (i + 1) * tall]

            if fused:
                Job("up", b).start()

        def mid_part(here):
            return contract(grad_up[0, here, :], weight_up[0], 1, 1) + contract(
                grad_up[1, here, :], weight_up[1], 1, 1
            )

        @pl.loop(0, tiles)
        def _(i):
            part = mid_part(rows_of(lax.rem(other * 2 + i, tiles) * TILE, TILE))

            @pl.when(i < 2)
            def _():
                stage[tile_rows(i), :] = part.astype(LOW)
                mid_back(i).start()

            @pl.when(i >= 2)
            def _():
                grad_resid[tile_rows(i - 2), :] = part

            steps_when(i == 1, "up0 turn")

        @pl.loop(0, 2)
        def _(i):
            here = tile_rows(i)
            mid_back(i).wait_recv()
            grad = grad_resid[here, :] + catch_mid[here, :].astype(FULL)
            unit, inverse = layer_norm(resid[here, :])
            vec_sums[2:3, :] += jnp.sum(grad * unit, 0, keepdims=True)
            vec_sums[3:4, :] += jnp.sum(grad, 0, keepdims=True)
            scaled = grad * flat(gain_mid)
            total = grads_all[own_rows(i), :].astype(FULL) + inverse * (
                scaled
                - jnp.mean(scaled, -1, keepdims=True)
                - unit * jnp.mean(scaled * unit, -1, keepdims=True)
            )
            grad_resid[here, :] = total
            low_resid[own_rows(i), :] = total.astype(LOW)
            dz_far(i).start()

        for i in range(2):
            mid_back(i).wait_send()
        if fused:
            down.turn_at(core * 2 + 1)

    def give_down(b):
        return remote(
            stage_down.at[b],
            parts["down"].at[0, core * 2 + b],
            pd_sems.at[0, b],
            pd_sems.at[1, b],
            partner,
        )

    give_out = remote(
        stage_out,
        parts["out"].at[0, pl.ds(core * 2, 2)],
        po_sems.at[0],
        po_sems.at[1],
        partner,
    )

    vec_sums[...] = jnp.zeros_like(vec_sums)
    pl.run_scoped(
        feed_forward,
        pltpu.VMEM((2, width, block), LOW),
        pltpu.VMEM((2, length, block), LOW),
    )

    def prob_load(p, t):
        return pltpu.make_async_copy(prob_hbm[t].at[p], probs[t], prob_sems.at[t])

    def attention(slopes, fades, key_sum, value_sum, carry, grad_qkv, weight_in):
        for t in range(tiles):
            prob_load(pair_count - 1, t).start()
        slope_load = local(slope_hbm, slopes, 13)
        weight_loads = []
        for place, source in enumerate((w_query, w_key, w_value)):
            for p in range(pair_count):
                weight_loads.append(
                    local(
                        source.at[:, pl.ds(pl.multiple_of(core * mine + p * PAIR, 128), PAIR)],
                        weight_in.at[:, pl.ds(p * mine + place * PAIR, PAIR)],
                        17 + place * pair_count + p,
                    )
                )
        for one in [slope_load] + weight_loads:
            one.start()

        def head_grads(here):
            result = contract(low_resid[here, :], weight_out[pl.ds(0, mine), :], 1, 1).astype(LOW)
            for p in range(pair_count):
                grad_heads[p, here, :] = result[:, p * PAIR : (p + 1) * PAIR]

        @pl.loop(0, tiles)
        def _(i):
            @pl.when(i > 1)
            def _():
                dz_far(i - 2).wait_recv()

            head_grads(rows_of(lax.rem(core * 2 + i, tiles) * TILE, TILE))

        joined = jnp.concatenate([heads[p] for p in range(pair_count)], 1)
        grad = contract(joined, low_resid[...], 0, 0).astype(LOW)
        kept = jnp.where(core == 0, grad[:, :mine], grad[:, mine:])
        given = jnp.where(core == 0, grad[:, mine:], grad[:, :mine])
        tall = width // COUNT
        for i in range(mine // tall):
            rank = core * (COUNT // 2) + i
            z, a, s = spot_of(rank, core)
            parts["out"][0, z, a, s] = kept[i * tall : (i + 1) * tall]
            _, a, s = spot_of(rank, other)
            stage_out[i // (wide * deep), a, s] = given[i * tall : (i + 1) * tall]
        give_out.start()
        for one in late_loads:
            one.wait()
        if fused:
            down.turn_at(other * 2 + 1)

        keep = lanes_below((TILE, PAIR), HEAD)
        spots = (
            lax.broadcasted_iota(jnp.int32, (TILE, TILE), 0),
            lax.broadcasted_iota(jnp.int32, (TILE, TILE), 1),
        )
        after = jnp.where(spots[0] > spots[1], 1.0, 0.0).astype(LOW)

        def fade_send(t):
            part = pl.ds(t * (t + 1) // 2, t + 1)
            return remote(
                share_send.at[part],
                share_recv.at[part],
                df_sems.at[0, t],
                df_sems.at[1, t],
                partner,
            )

        def pair_step(step, p):
            for t in reversed(range(tiles)):
                count = (t + 1) * TILE
                span, rows = pl.ds(t * TILE, TILE), pl.ds(0, count)
                prob_load(p, t).wait()
                grad_tile = grad_heads[p, span, :]
                product = (grad_tile.astype(FULL) * heads[p, span, :].astype(FULL)).T
                query = queries[p, span, :]
                grads, masked_q, masked_g = [], [], []
                fade = None
                for h in range(2):
                    mask = keep == (h == 0)
                    masked_g.append(jnp.where(mask, grad_tile, LOW(0.0)))
                    masked_q.append(jnp.where(mask, query, LOW(0.0)))
                    delta = jnp.sum(product[h * HEAD : (h + 1) * HEAD, :], 0, keepdims=True)
                    change = probs[t][:, pl.ds(h * TILE, TILE)].astype(FULL) * (
                        contract(values[p, rows, :], masked_g[h], 1, 1) - delta
                    )
                    fade = change if fade is None else fade + change
                    grads.append(change.astype(LOW))

                @pl.when(step == 0)
                def _():
                    fades[rows, span] = fade

                @pl.when(step > 0)
                def _():
                    fades[rows, span] += fade

                both = jnp.concatenate(grads, 1)
                key_part = contract(both, jnp.concatenate(masked_q, 0), 1, 0)
                value_part = contract(probs[t][...], jnp.concatenate(masked_g, 0), 1, 0)
                if t == tiles - 1:
                    key_sum[...] = key_part
                    value_sum[...] = value_part
                else:
                    key_sum[rows, :] += key_part
                    value_sum[rows, :] += value_part
                query_part = contract(keys[p, rows, :], both, 0, 0)
                query_part = jnp.concatenate(
                    [query_part[:HEAD, :TILE], query_part[HEAD:, TILE:]], 0
                )
                grad_qkv[p, span, pl.ds(0, PAIR)] = (query_part.T * 0.125).astype(LOW)

                @pl.when(step < pair_count - 1)
                def _():
                    prob_load(p - 1, t).start()

                if t == tiles - 1:
                    steps_when(step == 1, "up1 turn")
                    steps_when(step == 2, "out turn", "down cross", "up1 gather")

                @pl.when((step == pair_count - 1) & (core == 1))
                def _():
                    share_send[pl.ds(t * (t + 1) // 2, t + 1)] = (
                        fades[rows, span].astype(LOW).reshape(t + 1, TILE, TILE)
                    )
                    fade_send(t).start()

        def lead_head():
            @pl.when(core == 0)
            def _():
                carry[...] = jnp.zeros_like(carry)
                for t in reversed(range(tiles)):
                    count = (t + 1) * TILE
                    span, rows = pl.ds(t * TILE, TILE), pl.ds(0, count)
                    part = pl.ds(t * (t + 1) // 2, t + 1)
                    fade_send(t).wait_recv()
                    total = fades[rows, span] + share_recv[part].astype(FULL).reshape(count, TILE)
                    later = contract(total.astype(LOW), after, 1, 0) + carry[rows, :]
                    if t:
                        carry[rows, :] += jnp.sum(total, -1, keepdims=True)
                    slope = slopes[part].astype(FULL).reshape(count, TILE)
                    extra = (-later * slope).astype(LOW)
                    query = jnp.where(keep, queries[0, span, :], LOW(0.0))
                    key_sum[rows, :] += contract(extra, query, 1, 0)
                    whole = contract(keys[0, rows, :], extra, 0, 0).T * 0.125
                    grad_qkv[0, span, pl.ds(0, PAIR)] = (
                        grad_qkv[0, span, pl.ds(0, PAIR)].astype(FULL)
                        + jnp.where(keep, whole, 0.0)
                    ).astype(LOW)

            @pl.when(core == 1)
            def _():
                for t in range(tiles):
                    fade_send(t).wait_send()

        def weights_into(kind, k, right):
            @pl.loop(0, 2)
            def _(m):
                place = pl.ds(pl.multiple_of(m * mine, 128), mine)
                grad = contract(low_in[:, place], right, 0, 0).astype(LOW)
                for i in range(mine // tall):
                    z, a, s = spot_of(m * (mine // tall) + i, core)
                    parts[kind][k, z, a, s] = grad[i * tall : (i + 1) * tall]

            if fused:
                Job(kind, k).start()

        @pl.loop(0, pair_count)
        def _(step):
            p = pair_count - 1 - step
            pair_step(step, p)
            grad_qkv[p, :, pl.ds(2 * PAIR, PAIR)] = value_sum[...].astype(LOW)

            @pl.when(p > 0)
            def _():
                grad_qkv[p, :, pl.ds(PAIR, PAIR)] = key_sum[...].astype(LOW)
                weights_into("attn", p - 1, grad_qkv[p])

            @pl.when(step == 0)
            def _():
                give_out.wait_recv()
                steps("out start", "up0 gather")


        keep_all = lanes_below((length, PAIR), HEAD)
        second_head = jnp.where(
            keep_all,
            pltpu.roll(grad_qkv[0, :, pl.ds(0, PAIR)].astype(FULL), HEAD, 1),
            key_sum[...],
        )
        weights_into(
            "early",
            0,
            jnp.concatenate(
                [second_head.astype(LOW), grad_qkv[0, :, pl.ds(2 * PAIR, PAIR)]], 1
            ),
        )
        slope_load.wait()
        steps("attn2 turn", "up0 close")
        lead_head()
        grad_qkv[0, :, pl.ds(PAIR, PAIR)] = key_sum[...].astype(LOW)
        first_head = jnp.where(
            keep_all,
            grad_qkv[0, :, pl.ds(0, PAIR)].astype(FULL),
            pltpu.roll(key_sum[...], HEAD, 1),
        )
        weights_into("lead", 0, first_head.astype(LOW))

        for one in weight_loads:
            one.wait()

        def in_part(here):
            joined = jnp.concatenate([grad_qkv[p, here, :] for p in range(pair_count)], 1)
            return contract(joined, weight_in[...], 1, 1)

        @pl.loop(0, tiles)
        def _(i):
            part = in_part(rows_of(lax.rem(other * 2 + i, tiles) * TILE, TILE))

            @pl.when(i < 2)
            def _():
                stage[tile_rows(i), :] = part.astype(LOW)
                in_back(i).start()

            @pl.when(i >= 2)
            def _():
                fades[tile_rows(i - 2), pl.ds(0, width)] = part

            steps_when(i == 1, "attn2 gather", "out gather")
            steps_when(i == 3, "attn1 turn", "down close")

        for i in range(2):
            mid_far(i).wait_send()

        @pl.loop(0, 2)
        def _(i):
            here = tile_rows(i)
            in_back(i).wait_recv()
            grad = fades[here, pl.ds(0, width)] + catch_mid[here, :].astype(FULL)
            unit, inverse = layer_norm(tokens[here, :].astype(FULL))
            vec_sums[0:1, :] += jnp.sum(grad * unit, 0, keepdims=True)
            vec_sums[1:2, :] += jnp.sum(grad, 0, keepdims=True)
            scaled = grad * flat(gain_in)
            low_mid[here, :] = (
                grad_resid[here, :]
                + inverse
                * (
                    scaled
                    - jnp.mean(scaled, -1, keepdims=True)
                    - unit * jnp.mean(scaled * unit, -1, keepdims=True)
                )
            ).astype(LOW)

        in_put.start()
        for i in range(2):
            in_back(i).wait_send()

    pl.run_scoped(
        attention,
        pltpu.VMEM((tiles * (tiles + 1) // 2, TILE, TILE), LOW),
        pltpu.VMEM((length, length), FULL),
        pltpu.VMEM((length, PAIR), FULL),
        pltpu.VMEM((length, PAIR), FULL),
        pltpu.VMEM((length, 1), FULL),
        pltpu.VMEM((pair_count, length, mine), LOW),
        pltpu.VMEM((width, 3 * mine), LOW),
    )

    if not fused:
        for kind in KINDS[:-1]:
            one = pltpu.make_async_copy(parts[kind], results[kind], load_sems.at[0])
            one.start()
            one.wait()
        one = pltpu.make_async_copy(vec_sums, results["vec"], load_sems.at[0])
        one.start()
        one.wait()
    else:
        sums = vec_sums[...]
        tall = width // COUNT
        for rank in range(COUNT):
            z, a, s = spot_of(rank, core)
            shifted = pltpu.roll(sums, width - rank * tall, 1) if rank else sums
            parts["vec"][0, z, a, s] = shifted[:, :128]
    steps("vec start", "early turn")

    def out_part(here):
        return contract(hidden_low[0, here, :], weight_down[0], 1, 0) + contract(
            hidden_low[1, here, :], weight_down[1], 1, 0
        )

    @pl.loop(0, tiles)
    def _(i):
        part = out_part(rows_of(lax.rem(other * 2 + i, tiles) * TILE, TILE))

        @pl.when(i < 2)
        def _():
            stage_far[tile_rows(i), :] = part.astype(LOW)
            out_back(i).start()

        @pl.when(i >= 2)
        def _():
            resid[tile_rows(i - 2), :] += part

        steps_when(i == 0, "lead turn", "attn1 gather", "up1 close")
        steps_when(i == 1, "early gather")
        steps_when(i == 2, "vec gather", "out close")
        steps_when(i == 3, "lead gather", "attn2 close")

    steps("down store", "up0 store", "up1 store")

    @pl.loop(0, 2)
    def _(i):
        here = tile_rows(i)
        out_back(i).wait_recv()
        low_mid[rows_of(half + i * TILE, TILE), :] = (
            resid[here, :] + catch_out[here, :].astype(FULL)
        ).astype(LOW)

    out_put.start()
    steps("attn1 close", "early close", "vec close", "lead close")
    steps("out store", "attn2 store", "attn1 store", "early store", "vec store", "lead store")
    if fused:
        for job in jobs.values():
            job.drain()
    in_put.wait()
    out_put.wait()
    g_far.wait_send()
    give_out.wait_send()
    for i in range(2):
        give_down(i).wait_send()
        for one in (dz_far, out_back):
            one(i).wait_send()


def finish(fused, tokens, cotangent, gain_in, gain_mid, shift_mid, forward, weights):
    low_in, queries, keys, values, probs, slopes, heads, heads_far = forward
    half, width = tokens.shape
    length, mine = 2 * half, width // 2
    hidden = weights[-1].shape[0]
    pairs, tiles = mine // PAIR, length // TILE
    shapes = block_shapes(width, hidden)
    long, wide, deep = GRID
    anywhere = pl.BlockSpec(memory_space=pl.ANY)
    local = pl.BlockSpec(memory_space=pltpu.VMEM)
    outs = [jax.ShapeDtypeStruct((half, width), LOW)] * 2
    out_specs = [anywhere] * 2
    for kind in KINDS:
        shape, kept = shapes[kind]
        if fused:
            outs.append(jax.ShapeDtypeStruct((FAN[kind], 2) + shape, kept))
            out_specs.append(anywhere)
        elif kind == "vec":
            outs.append(jax.ShapeDtypeStruct((8, width), FULL))
            out_specs.append(anywhere)
        else:
            outs.append(jax.ShapeDtypeStruct((FAN[kind],) + GRID + shape, kept))
            out_specs.append(anywhere)
    scratch = [
        pltpu.VMEM((length, width), LOW),
        pltpu.VMEM((width, width), LOW),
        pltpu.VMEM((pairs, length, PAIR), LOW),
        pltpu.VMEM((pairs, half, PAIR), LOW),
        pltpu.VMEM((half, width), FULL),
        pltpu.VMEM((length, width), LOW),
        pltpu.VMEM((half, width), FULL),
        pltpu.VMEM((length, width), LOW),
        pltpu.VMEM((pairs, length, PAIR), LOW),
        pltpu.VMEM((length, width), LOW),
        pltpu.VMEM((pairs, length, PAIR), LOW),
        pltpu.VMEM((pairs, length, PAIR), LOW),
        pltpu.VMEM((pairs, length, PAIR), LOW),
    ]
    scratch += [pltpu.VMEM(((t + 1) * TILE, 2 * TILE), LOW) for t in range(tiles)]
    corners = tiles * (tiles + 1) // 2
    scratch += [pltpu.VMEM((corners, TILE, TILE), LOW)] * 2
    scratch += [pltpu.VMEM((half, width), LOW)] * 4
    block = hidden // 4
    scratch += [pltpu.VMEM((2, block, width), LOW), pltpu.VMEM((2, length, block), LOW)]
    scratch += [
        pltpu.VMEM((2, wide, deep) + shapes["down"][0], LOW),
        pltpu.VMEM((2, wide, deep) + shapes["out"][0], LOW),
        pltpu.VMEM((8, width), FULL),
    ]
    scratch += [pltpu.VMEM((FAN[kind],) + GRID + shapes[kind][0], shapes[kind][1]) for kind in KINDS]
    dma = pltpu.SemaphoreType.DMA
    if fused:
        leads = {kind: ((long, deep), (long,), (long - 1,), ()) for kind in KINDS}
        leads["down"] = ((long, deep), (long - 1, deep), (), ())
        leads["vec"] = ((3, long), (), (long - 1,), ())
        for step in range(4):
            scratch += [
                pltpu.VMEM((FAN[kind],) + leads[kind][step] + shapes[kind][0], shapes[kind][1])
                for kind in KINDS
            ]
        scratch += [dma((long,))] * 2 + [dma((long - 1,))] * 2 + [dma((1,))] * 4
        for kind in KINDS[1:]:
            fan = FAN[kind]
            count = 3 if kind == "vec" else fan
            scratch += [dma((count,))] * 4 + [dma((fan, long - 1))] * 2 + [dma((fan,))] * 2
        scratch += [dma((FAN[kind], 2)) for kind in KINDS]
    scratch += [dma((17 + 3 * pairs,)), dma((2,))]
    scratch += [dma((2, 2))] * 6
    scratch += [dma((2,)), dma((2, tiles)), dma((tiles,))]
    return pl.pallas_call(
        functools.partial(finish_kernel, fused),
        out_shape=outs,
        in_specs=[local] + [anywhere] + [local] * 3 + [anywhere] * (4 + tiles + 1 + 2 + 6),
        out_specs=out_specs,
        scratch_shapes=scratch,
        compiler_params=pltpu.CompilerParams(
            collective_id=0, has_side_effects=True, vmem_limit_bytes=VMEM_LIMIT
        ),
        name="finish",
    )(
        tokens,
        cotangent,
        gain_in,
        gain_mid,
        shift_mid,
        low_in,
        queries,
        keys,
        values,
        *probs,
        slopes,
        heads,
        heads_far,
        *weights,
    )

def deliver_kernel(count, *refs):
    refs, (load_sems, put_sems) = refs[:-2], refs[-2:]
    targets = refs[count : (len(refs) - 2 * count + 2) // 2 + count]
    sources, held = refs[:count], refs[count + len(targets) : 2 * count + len(targets)]
    made = refs[2 * count + len(targets) :]
    loads = [
        pltpu.make_async_copy(source, target, load_sems.at[i])
        for i, (source, target) in enumerate(zip(sources, held))
    ]
    for one in loads[2:] + loads[:2]:
        one.start()
    puts = [
        pltpu.make_async_copy(source, target, put_sems.at[i])
        for i, (source, target) in enumerate(zip(held[:2] + made, targets))
    ]
    for one in loads[2:]:
        one.wait()
    share_in, down, up, out, attn, early, lead, vec = held[2:]
    share, g_query, g_key, g_value, g_out, g_up, g_down, *g_vecs = made
    tall, mine = out.shape[2:]
    for k in range(2):
        for b in range(2):
            g_up[:, (2 * k + b) * 2 * mine : (2 * k + b + 1) * 2 * mine] = up[b, k].astype(FULL)
    puts[7].start()
    for k in range(2):
        g_down[:, k * mine : (k + 1) * mine] = down[0, k].astype(FULL)
    puts[8].start()
    for i in range(2):
        loads[i].wait()
        puts[i].start()
    for k in range(2):
        start = k * mine
        g_out[:, start : start + mine] = out[0, k].astype(FULL)
        for p in range(attn.shape[0]):
            for place, target in enumerate((g_query, g_key, g_value)):
                target[:, start + (p + 1) * PAIR : start + (p + 2) * PAIR] = attn[
                    p, k, :, place * PAIR : (place + 1) * PAIR
                ].astype(FULL)
        ones, twos = lead[0, k].astype(FULL), early[0, k].astype(FULL)
        keep = lanes_below(ones.shape, HEAD)
        seconds = twos[:, :PAIR]
        g_query[:, start : start + PAIR] = jnp.where(keep, ones, pltpu.roll(seconds, HEAD, 1))
        g_key[:, start : start + PAIR] = jnp.where(keep, pltpu.roll(ones, HEAD, 1), seconds)
        g_value[:, start : start + PAIR] = twos[:, PAIR:]
    share[...] = share_in[0:1, :]
    sums = vec[0, 0] + vec[0, 1]
    for i, target in enumerate(g_vecs):
        target[...] = sums[i, :tall]
    for one in puts[2:7] + puts[9:]:
        one.start()
    for one in puts:
        one.wait()


def deliver(*arrays):
    output, _, shares, down, up, out = arrays[:6]
    tall, mine = out.shape[2:]
    width = 2 * mine
    shapes = [(1, shares.shape[1])] + [(tall, width)] * 4
    shapes += [(tall, 2 * up.shape[3] * 2), (down.shape[2], width)] + [(tall,)] * 4
    anywhere = pl.BlockSpec(memory_space=pl.ANY)
    return pl.pallas_call(
        functools.partial(deliver_kernel, len(arrays)),
        out_shape=[jax.ShapeDtypeStruct(output.shape, output.dtype)] * 2
        + [jax.ShapeDtypeStruct(shape, FULL) for shape in shapes],
        in_specs=[anywhere] * len(arrays),
        out_specs=[anywhere] * (2 + len(shapes)),
        scratch_shapes=[pltpu.VMEM(one.shape, one.dtype) for one in arrays]
        + [pltpu.VMEM(shape, FULL) for shape in shapes]
        + [pltpu.SemaphoreType.DMA((len(arrays),)), pltpu.SemaphoreType.DMA((2 + len(shapes),))],
        compiler_params=pltpu.CompilerParams(vmem_limit_bytes=VMEM_LIMIT),
        name="deliver",
    )(*arrays)


def reduce_plain(parts, rows):
    down, up, out, attn, early, lead, vec = parts
    width = vec.shape[1]

    def scattered(part):
        summed = lax.psum_scatter(part.astype(FULL), "rows", scatter_dimension=0, tiled=True)
        return summed.astype(LOW)

    def joined(part):
        return lax.all_gather(part, "keys", axis=1, tiled=True).astype(FULL)

    def flat_part(part):
        return part.reshape(-1, part.shape[-1])

    ones, twos = scattered(flat_part(lead[0])), scattered(flat_part(early[0]))
    first = [
        jnp.concatenate([ones[:, :HEAD], twos[:, :HEAD]], 1),
        jnp.concatenate([ones[:, HEAD:], twos[:, HEAD:PAIR]], 1),
        twos[:, PAIR:],
    ]
    rest = [scattered(flat_part(attn[p])) for p in range(attn.shape[0])]
    halves = [
        jnp.concatenate([first[i]] + [one[:, i * PAIR : (i + 1) * PAIR] for one in rest], 1)
        for i in range(3)
    ]
    halves.append(scattered(flat_part(out[0])))
    halves.append(jnp.concatenate([scattered(flat_part(up[b])) for b in range(2)], 1))
    halves.append(scattered(flat_part(down[0])))
    sums = lax.psum_scatter(
        lax.psum(vec[:4].T, "keys"), "rows", scatter_dimension=0, tiled=True
    )
    return [joined(one) for one in halves], [sums[:, i] for i in range(4)]


def body(
    rows,
    tokens,
    seg_ids,
    doc_starts,
    gain_in,
    shift_in,
    w_query,
    w_key,
    w_value,
    w_out,
    gain_mid,
    shift_mid,
    w_up,
    w_down,
    out_grad,
):
    fused = rows == COUNT
    own_tokens, own_grad = tokens[0], out_grad[0]
    low_in, queries, keys, values, probs, slopes, heads, heads_far, shares = attend(
        own_tokens, seg_ids, gain_in, shift_in, w_query, w_key, w_value
    )
    output, input_grad, *parts = finish(
        fused,
        own_tokens,
        own_grad,
        gain_in,
        gain_mid,
        shift_mid,
        (low_in, queries, keys, values, probs, slopes, heads, heads_far),
        (w_query, w_key, w_value, w_out, w_up, w_down),
    )
    if fused:
        output, input_grad, shares, *grads = deliver(output, input_grad, shares, *parts)
        grads, vectors = grads[:6], grads[6:]
    else:
        grads, vectors = reduce_plain(parts, rows)
    g_query, g_key, g_value, g_out, g_up, g_down = grads
    return (
        output[None],
        input_grad[None],
        shares[:1],
        vectors[0],
        vectors[1],
        g_query,
        g_key,
        g_value,
        g_out,
        vectors[2],
        vectors[3],
        g_up,
        g_down,
    )


def solution(mesh):
    in_specs = (
        P("rows", "keys", None),
        P("rows", None),
        P("rows", "keys"),
        P(),
        P(),
        P(),
        P(),
        P(),
        P(),
        P(),
        P(),
        P(),
        P(),
        P("rows", "keys", None),
    )
    out_specs = (
        P("rows", "keys", None),
        P("rows", "keys", None),
        P("rows", "keys"),
        P("rows"),
        P("rows"),
        P("rows", None),
        P("rows", None),
        P("rows", None),
        P("rows", None),
        P("rows"),
        P("rows"),
        P("rows", None),
        P("rows", None),
    )
    return jax.shard_map(
        functools.partial(body, mesh.shape["rows"]),
        mesh=mesh,
        in_specs=in_specs,
        out_specs=out_specs,
        check_vma=False,
    )
```

```python
import functools

import jax
import jax.numpy as jnp
from jax import lax
from jax.experimental import pallas as pl
from jax.experimental.pallas import tpu as pltpu
from jax.sharding import PartitionSpec as P

HEAD = 64
PAIR = 2 * HEAD
TILE = 256
EPS = 1e-05
MASKED = 1e30
SELECT_SHIFT = 4.0
LOW = jnp.bfloat16
FULL = jnp.float32
MESH = pl.DeviceIdType.MESH
VMEM_LIMIT = 67_000_000


def contract(left, right, left_dim, right_dim):
    return lax.dot_general(
        left, right, (((left_dim,), (right_dim,)), ((), ())), preferred_element_type=FULL
    )


def layer_norm(field):
    center = field - jnp.mean(field, -1, keepdims=True)
    inverse = lax.rsqrt(jnp.mean(center * center, -1, keepdims=True) + EPS)
    return center * inverse, inverse


def remote(source, target, send, recv, device):
    return pltpu.make_async_remote_copy(
        src_ref=source,
        dst_ref=target,
        send_sem=send,
        recv_sem=recv,
        device_id=device,
        device_id_type=MESH,
    )


def lanes_below(shape, bound):
    return lax.broadcasted_iota(jnp.int32, shape, len(shape) - 1) < bound


def flat(ref):
    return ref[...].reshape(1, ref.shape[0])


def corner(step, tiles):
    t = sum((step >= n * (n + 1) // 2).astype(jnp.int32) for n in range(1, tiles))
    return t, step - t * (t + 1) // 2


def rows_of(start, size):
    return pl.ds(pl.multiple_of(start, size), size)


def attend_kernel(
    tokens,
    seg,
    gain,
    shift,
    w_query,
    w_key,
    w_value,
    low_in_out,
    query_out,
    key_out,
    value_out,
    prob_outs,
    slopes_out,
    heads_out,
    other_out,
    scales_out,
    share_out,
    all_tokens,
    low_in,
    weights,
    queries,
    keys,
    values,
    lead_query,
    lead_key,
    probs,
    slopes,
    penalty,
    heads,
    scales,
    scale_cols,
    seg_cols,
    free_cols,
    running,
    numerator,
    pairs_seen,
    far_send,
    far_recv,
    head_send,
    head_recv,
    weight_sems,
    out_sems,
    prob_sems,
):
    core = lax.axis_index("keys")
    row = lax.axis_index("rows")
    other = 1 - core
    partner = (row, other)
    half, width = tokens.shape
    length = 2 * half
    mine = width // 2
    pair_count = mine // PAIR
    tiles = length // TILE

    columns = pl.ds(pl.multiple_of(core * mine, 128), mine)
    loads = []
    for place, source in enumerate((w_query, w_key, w_value)):
        loads.append((source.at[:, columns], weights.at[:, pl.ds(place * mine, mine)]))
    for place, source in enumerate((w_query, w_key)):
        loads.append(
            (source.at[:, pl.ds(0, PAIR)], weights.at[:, pl.ds(3 * mine + place * PAIR, PAIR)])
        )
    own = rows_of(core * half, half)
    loads = [
        pltpu.make_async_copy(source, target, weight_sems.at[i])
        for i, (source, target) in enumerate(loads)
    ]
    own_load = pltpu.make_async_copy(tokens, all_tokens.at[own], weight_sems.at[5])
    own_load.start()
    for one in loads:
        one.start()

    barrier = pltpu.get_barrier_semaphore()
    pl.semaphore_signal(barrier, inc=1, device_id=partner, device_id_type=MESH)
    pl.semaphore_wait(barrier, 1)
    exchange = remote(tokens, all_tokens.at[own], far_send, far_recv, partner)
    exchange.start()

    seg_row = seg[...]
    seg_wide = jnp.broadcast_to(seg_row.astype(FULL), (128, length))
    spot = lax.broadcasted_iota(jnp.int32, (128, length), 1)
    before = pltpu.roll(seg_wide, 1, 1)
    free_wide = jnp.where((spot > 0) & (before == seg_wide), 1.0, 0.0)
    seg_cols[...] = seg_wide.T
    free_cols[...] = free_wide.T
    own_load.wait()

    keep = lanes_below((TILE, PAIR), HEAD)

    @pl.loop(0, tiles)
    def _(i):
        @pl.when(i == half // TILE)
        def _():
            exchange.wait_recv()

        here = rows_of(lax.rem(core * (half // TILE) + i, tiles) * TILE, TILE)
        unit, _ = layer_norm(all_tokens[here, :].astype(FULL))
        low_in[here, :] = (unit * flat(gain) + flat(shift)).astype(LOW)

        @pl.when(i == 0)
        def _():
            for one in loads:
                one.wait()

        result = contract(low_in[here, :], weights[...], 1, 0).astype(LOW)
        for p in range(pair_count):
            queries[p, here, :] = result[:, p * PAIR : (p + 1) * PAIR] * LOW(0.125)
            keys[p, here, :] = result[:, mine + p * PAIR : mine + (p + 1) * PAIR]
            values[p, here, :] = result[:, 2 * mine + p * PAIR : 2 * mine + (p + 1) * PAIR]
        first = result[:, 3 * mine : 3 * mine + PAIR]
        lead_query[here, :] = jnp.where(keep, first, LOW(0.0)) * LOW(0.125)
        lead_key[here, :] = result[:, 3 * mine + PAIR :]

    puts = [
        pltpu.make_async_copy(low_in, low_in_out, out_sems.at[0]),
        pltpu.make_async_copy(queries, query_out, out_sems.at[1]),
        pltpu.make_async_copy(keys, key_out, out_sems.at[2]),
        pltpu.make_async_copy(values, value_out, out_sems.at[3]),
    ]
    for one in puts:
        one.start()

    spots = (
        lax.broadcasted_iota(jnp.int32, (2 * TILE, 2 * TILE), 0),
        lax.broadcasted_iota(jnp.int32, (2 * TILE, 2 * TILE), 1),
    )
    earlier = jnp.where(spots[0] < spots[1], 1.0, 0.0).astype(LOW)
    scales[...] = jnp.zeros_like(scales)
    running[...] = jnp.zeros_like(running)
    numerator[...] = jnp.zeros_like(numerator)
    pairs_seen[...] = jnp.zeros_like(pairs_seen)

    @pl.loop(0, (tiles // 2) * (tiles // 2 + 1) // 2)
    def _(step):
        wide, k = corner(step, tiles // 2)
        rows, span = rows_of(k * 2 * TILE, 2 * TILE), rows_of(wide * 2 * TILE, 2 * TILE)
        scores = contract(lead_key[rows, :], lead_query[span, :], 1, 1)
        repeat = 2 * TILE // 128
        same = jnp.concatenate([seg_cols[rows, :]] * repeat, 1) == seg[:, span].astype(FULL)
        ahead = spots[1] - spots[0] + (wide - k) * 2 * TILE
        later = same & (ahead > 0)
        allowed = same & (ahead >= 0)
        select = jnp.where(later, jnp.concatenate([free_cols[rows, :]] * repeat, 1), 0.0)
        level = scores - SELECT_SHIFT
        chosen = select * (jnp.maximum(level, 0.0) + jnp.log(1.0 + jnp.exp(-jnp.abs(level))))
        slope = (select * (0.5 + 0.5 * jnp.tanh(0.5 * level))).astype(LOW)

        slopes[wide * (2 * wide + 1) + 2 * k] = slope[:TILE, :TILE]

        @pl.when(k < wide)
        def _():
            slopes[wide * (2 * wide + 1) + 2 * k + 1] = slope[TILE:, :TILE]

        slopes[(2 * wide + 1) * (wide + 1) + 2 * k] = slope[:TILE, TILE:]
        slopes[(2 * wide + 1) * (wide + 1) + 2 * k + 1] = slope[TILE:, TILE:]
        high = chosen.astype(LOW)
        rest = (chosen - high.astype(FULL)).astype(LOW)
        total = (
            running[rows, :] + contract(high, earlier, 1, 0) + contract(rest, earlier, 1, 0)
        )
        penalty[rows, span] = jnp.where(allowed, total, MASKED)
        running[rows, :] += jnp.sum(chosen, -1, keepdims=True)
        share = jnp.where(later, 0.5 + 0.5 * jnp.tanh(0.5 * total - 1.0), 0.0)
        numerator[rows, :] += jnp.sum(share, -1, keepdims=True)
        pairs_seen[rows, :] += jnp.sum(jnp.where(later, 1.0, 0.0), -1, keepdims=True)

    slope_put = pltpu.make_async_copy(slopes, slopes_out, out_sems.at[4])
    slope_put.start()

    shares = numerator[own, :] / jnp.maximum(pairs_seen[own, :], 1.0)
    share_out[...] = jnp.broadcast_to(shares, (half, 128)).T[0:8, :]

    def put_probs(p, t):
        return pltpu.make_async_copy(
            probs[t].at[p], prob_outs[t].at[p], prob_sems.at[p, t]
        )

    def send_heads(p):
        return remote(
            heads.at[p, rows_of(other * half, half)],
            other_out.at[p],
            head_send.at[p],
            head_recv.at[p],
            partner,
        )

    @pl.loop(0, pair_count)
    def _(p):
        for t in range(tiles):
            count = (t + 1) * TILE
            span = pl.ds(t * TILE, TILE)
            query = queries[p, span, :]
            both = jnp.concatenate(
                [jnp.where(keep, query, LOW(0.0)), jnp.where(keep, LOW(0.0), query)], 0
            )
            fine = penalty[pl.ds(0, count), span]
            logits = contract(keys[p, pl.ds(0, count), :], both, 1, 1) - jnp.concatenate(
                [fine, fine], 1
            )
            scaled = jnp.exp(logits - jnp.max(logits, 0, keepdims=True))
            prob = scaled.astype(LOW)
            probs[t][p] = prob
            scale = 1.0 / jnp.sum(scaled, 0, keepdims=True)
            scales[pl.ds(2 * p, 1), span] = scale[:, :TILE]
            scales[pl.ds(2 * p + 1, 1), span] = scale[:, TILE:]
            out = contract(values[p, pl.ds(0, count), :], prob, 0, 0) * scale
            out = jnp.concatenate([out[:HEAD, :TILE], out[HEAD:, TILE:]], 0)
            heads[p, span, :] = out.T.astype(LOW)
        for t in range(tiles):
            put_probs(p, t).start()
        send_heads(p).start()

    scale_cols[...] = scales[...].T
    scale_put = pltpu.make_async_copy(scale_cols, scales_out, out_sems.at[6])
    scale_put.start()
    last = pltpu.make_async_copy(heads, heads_out, out_sems.at[5])
    last.start()
    for p in range(pair_count):
        send_heads(p).wait()
        for t in range(tiles):
            put_probs(p, t).wait()
    for one in puts + [slope_put, scale_put, last]:
        one.wait()
    exchange.wait_send()


def attend(tokens, seg, gain, shift, w_query, w_key, w_value):
    half, width = tokens.shape
    length, mine = 2 * half, width // 2
    pairs, tiles = mine // PAIR, 2 * half // TILE
    spans = [(t + 1) * TILE for t in range(tiles)]
    corners = tiles * (tiles + 1) // 2
    outs = [
        jax.ShapeDtypeStruct((length, width), LOW),
        jax.ShapeDtypeStruct((pairs, length, PAIR), LOW),
        jax.ShapeDtypeStruct((pairs, length, PAIR), LOW),
        jax.ShapeDtypeStruct((pairs, length, PAIR), LOW),
        [jax.ShapeDtypeStruct((pairs, span, 2 * TILE), LOW) for span in spans],
        jax.ShapeDtypeStruct((corners, TILE, TILE), LOW),
        jax.ShapeDtypeStruct((pairs, length, PAIR), LOW),
        jax.ShapeDtypeStruct((pairs, half, PAIR), LOW),
        jax.ShapeDtypeStruct((length, 128), FULL),
        jax.ShapeDtypeStruct((8, half), FULL),
    ]
    anywhere = pl.BlockSpec(memory_space=pl.ANY)
    local = pl.BlockSpec(memory_space=pltpu.VMEM)
    out_specs = [anywhere] * 4 + [[anywhere] * tiles, anywhere, anywhere, anywhere, anywhere, local]
    scratch = [
        pltpu.VMEM((length, width), LOW),
        pltpu.VMEM((length, width), LOW),
        pltpu.VMEM((width, 3 * mine + 2 * PAIR), LOW),
        pltpu.VMEM((pairs, length, PAIR), LOW),
        pltpu.VMEM((pairs, length, PAIR), LOW),
        pltpu.VMEM((pairs, length, PAIR), LOW),
        pltpu.VMEM((length, PAIR), LOW),
        pltpu.VMEM((length, PAIR), LOW),
        [pltpu.VMEM((pairs, span, 2 * TILE), LOW) for span in spans],
        pltpu.VMEM((corners, TILE, TILE), LOW),
        pltpu.VMEM((length, length), FULL),
        pltpu.VMEM((pairs, length, PAIR), LOW),
        pltpu.VMEM((128, length), FULL),
        pltpu.VMEM((length, 128), FULL),
        pltpu.VMEM((length, 128), FULL),
        pltpu.VMEM((length, 128), FULL),
        pltpu.VMEM((length, 1), FULL),
        pltpu.VMEM((length, 1), FULL),
        pltpu.VMEM((length, 1), FULL),
        pltpu.SemaphoreType.DMA,
        pltpu.SemaphoreType.DMA,
        pltpu.SemaphoreType.DMA((pairs,)),
        pltpu.SemaphoreType.DMA((pairs,)),
        pltpu.SemaphoreType.DMA((6,)),
        pltpu.SemaphoreType.DMA((7,)),
        pltpu.SemaphoreType.DMA((pairs, tiles)),
    ]
    return pl.pallas_call(
        attend_kernel,
        out_shape=outs,
        in_specs=[anywhere] + [local] * 3 + [anywhere] * 3,
        out_specs=out_specs,
        scratch_shapes=scratch,
        compiler_params=pltpu.CompilerParams(
            collective_id=1, has_side_effects=True, vmem_limit_bytes=VMEM_LIMIT
        ),
        name="attend",
    )(tokens, seg, gain, shift, w_query, w_key, w_value)

def gelu_parts(field):
    scale = 0.7978845608028654
    square = field * field
    inner = jnp.tanh(scale * field * (1.0 + 0.044715 * square))
    half_sum = 0.5 * (1.0 + inner)
    slope = half_sum + 0.5 * field * (1.0 - inner * inner) * (
        scale * (1.0 + 3.0 * 0.044715 * square)
    )
    return field * half_sum, slope


GRID = (4, 2, 2)
COUNT = GRID[0] * GRID[1] * GRID[2]
KINDS = ("down", "up", "out", "attn", "early", "lead", "vec")
FAN = {"down": 1, "up": 2, "out": 1, "attn": 2, "early": 1, "lead": 1, "vec": 1}


def block_shapes(width, hidden):
    mine = width // 2
    tall = width // COUNT
    return {
        "down": ((hidden // COUNT, mine), LOW),
        "up": ((tall, mine * 2), LOW),
        "out": ((tall, mine), LOW),
        "attn": ((tall, mine), LOW),
        "early": ((tall, 2 * PAIR), LOW),
        "lead": ((tall, PAIR), LOW),
        "vec": ((8, 128), FULL),
    }


def finish_kernel(fused, *refs):
    refs = list(refs)

    def take(count):
        taken = refs[:count]
        del refs[:count]
        return taken if count > 1 else taken[0]

    tokens, cotangent, gain_in, gain_mid, shift_mid = take(5)
    low_in_hbm, query_hbm, key_hbm, value_hbm = take(4)
    prob_hbm, slope_hbm = take(4), take(1)
    heads_hbm, other_hbm, scales_hbm = take(3)
    w_query, w_key, w_value, w_out, w_up, w_down = take(6)
    output, input_grad = take(2)
    results = dict(zip(KINDS, take(len(KINDS))))
    (
        grads_all,
        weight_out,
        heads,
        heads_far,
        resid,
        low_mid,
        grad_resid,
        low_resid,
        grad_heads,
        low_in,
        queries,
        keys,
        values,
        scales,
    ) = take(14)
    probs = take(4)
    share_send, share_recv = take(2)
    stage, stage_far, catch_mid, catch_out = take(4)
    weight_down, hidden_low = take(2)
    stage_down, stage_out = take(2)
    vec_sums = take(1)
    parts = dict(zip(KINDS, take(len(KINDS))))
    if fused:
        got1 = dict(zip(KINDS, take(len(KINDS))))
        got2 = dict(zip(KINDS, take(len(KINDS))))
        got3 = dict(zip(KINDS, take(len(KINDS))))
        pair = dict(zip(KINDS, take(len(KINDS))))
        sems = {
            name: take(2) for name in ("down1", "down2", "down3", "down4")
        }
        for kind in KINDS[1:]:
            for stage_name in "1234":
                sems[kind + stage_name] = take(2)
        for kind in KINDS:
            sems[kind + "5"] = take(1)
    (load_sems, g_sems, mid_sems, dz_sems, a_sems, b_sems, c_sems, pd_sems, po_sems, df_sems, prob_sems) = take(11)

    long, wide, deep = GRID
    core = lax.axis_index("keys")
    row = lax.axis_index("rows")
    other = 1 - core
    partner = (row, other)
    half, width = tokens.shape
    length, mine = 2 * half, width // 2
    pair_count = mine // PAIR
    tiles = length // TILE
    hidden = w_down.shape[0]
    block = hidden // 4
    own_start, far_start = core * half, other * half

    if fused:
        slow, mid, fast = row // (wide * deep), (row // deep) % wide, row % deep
    else:
        slow, mid, fast = 0, 0, 0

    def spot_of(rank, whose):
        z, y, x = rank // (wide * deep), (rank // deep) % wide, rank % deep
        if not fused:
            return z, y, x
        return z, x + whose * (y - x), y + whose * (x - y)

    first, second = fast + core * (mid - fast), mid + core * (fast - mid)
    near, next_ = 1 - first, 1 - second

    def rank_of(z, a, b):
        y, x = b + core * (a - b), a + core * (b - a)
        return (z * wide + y) * deep + x

    near_device = (rank_of(slow, near, second), core)
    next_device = (rank_of(slow, first, next_), core)
    far_places = [lax.rem(slow + step, long) for step in range(1, long)]

    def add_into(target, index, terms):
        total = target[index].astype(FULL)
        for term in terms:
            total = total + term.astype(FULL)
        target[index] = total.astype(target.dtype)

    class Job:
        def __init__(self, kind, k):
            self.kind, self.k = kind, k

        def first_copy(self):
            kind, k = self.kind, self.k
            part, got = parts[kind].at[k], got1[kind].at[k]
            send, recv = sems[kind + "1"]
            return remote(part.at[:, near], got, send.at[k], recv.at[k], near_device)

        def second_copy(self):
            kind, k = self.kind, self.k
            part, got = parts[kind].at[k], got2[kind].at[k]
            send, recv = sems[kind + "2"]
            return remote(part.at[:, first, next_], got, send.at[k], recv.at[k], next_device)

        def third_copies(self):
            kind, k = self.kind, self.k
            send, recv = sems[kind + "3"]
            return [
                remote(
                    parts[kind].at[k, z, first, second],
                    got3[kind].at[k, step],
                    send.at[k, step],
                    recv.at[k, step],
                    (rank_of(z, first, second), core),
                )
                for step, z in enumerate(far_places)
            ]

        def last_copy(self):
            kind, k = self.kind, self.k
            send, recv = sems[kind + "4"]
            return remote(
                parts[kind].at[k, slow, first, second],
                pair[kind].at[k],
                send.at[k],
                recv.at[k],
                partner,
            )

        def start(self):
            self.first_copy().start()

        def turn(self):
            self.first_copy().wait_recv()
            kind, k = self.kind, self.k

            @pl.loop(0, long * deep)
            def _(step):
                z, b = step // deep, lax.rem(step, deep)
                add_into(parts[kind], (k, z, first, b), [got1[kind][k, z, b]])

            self.second_copy().start()

        def gather(self):
            self.second_copy().wait_recv()
            kind, k = self.kind, self.k

            @pl.loop(0, long)
            def _(z):
                add_into(parts[kind], (k, z, first, second), [got2[kind][k, z]])

            for one in self.third_copies():
                one.start()

        def close(self):
            for one in self.third_copies():
                one.wait_recv()
            kind, k = self.kind, self.k
            add_into(
                parts[kind],
                (k, slow, first, second),
                [got3[kind][k, step] for step in range(long - 1)],
            )
            self.last_copy().start()

        def puts(self):
            kind, k = self.kind, self.k
            own_part = parts[kind].at[k, slow, first, second]
            sem = sems[kind + "5"]
            return [
                pltpu.make_async_copy(own_part, results[kind].at[k, core], sem.at[k, 0]),
                pltpu.make_async_copy(pair[kind].at[k], results[kind].at[k, other], sem.at[k, 1]),
            ]

        def store(self):
            self.last_copy().wait_recv()
            for one in self.puts():
                one.start()

        def drain(self):
            self.first_copy().wait_send()
            self.second_copy().wait_send()
            for one in self.third_copies():
                one.wait_send()
            self.last_copy().wait_send()
            for one in self.puts():
                one.wait()

    class Down(Job):
        def near_copy(self, z):
            send, recv = sems["down1"]
            return remote(
                parts["down"].at[0, z, near],
                got1["down"].at[0, z],
                send.at[z],
                recv.at[z],
                near_device,
            )

        def slow_copy(self, step):
            z = lax.rem(slow + step, long)
            send, recv = sems["down2"]
            return remote(
                parts["down"].at[0, z, first],
                got2["down"].at[0, step - 1],
                send.at[step - 1],
                recv.at[step - 1],
                (rank_of(z, first, second), core),
            )

        def next_copy(self):
            send, recv = sems["down3"]
            return remote(
                parts["down"].at[0, slow, first, next_],
                got3["down"].at[0],
                send.at[0],
                recv.at[0],
                next_device,
            )

        def start_at(self, z):
            self.near_copy(z).start()

        def turn_at(self, z):
            self.near_copy(z).wait_recv()

            @pl.loop(0, deep)
            def _(b):
                add_into(parts["down"], (0, z, first, b), [got1["down"][0, z, b]])

            step = lax.rem(z - slow + long, long)

            @pl.when(step > 0)
            def _():
                self.slow_copy(step).start()

        def cross(self):
            for step in range(1, long):
                self.slow_copy(step).wait_recv()

            @pl.loop(0, deep)
            def _(b):
                add_into(
                    parts["down"],
                    (0, slow, first, b),
                    [got2["down"][0, step, b] for step in range(long - 1)],
                )

            self.next_copy().start()

        def close(self):
            self.next_copy().wait_recv()
            add_into(parts["down"], (0, slow, first, second), [got3["down"][0]])
            self.last_copy().start()

        def drain(self):
            for z in range(long):
                self.near_copy(z).wait_send()
            for step in range(1, long):
                self.slow_copy(step).wait_send()
            self.next_copy().wait_send()
            self.last_copy().wait_send()
            for one in self.puts():
                one.wait()

    class Vectors(Job):
        def first_copies(self):
            send, recv = sems["vec1"]
            places = ((near, second), (first, next_), (near, next_))
            return [
                remote(
                    parts["vec"].at[0, :, a, b],
                    got1["vec"].at[0, i],
                    send.at[i],
                    recv.at[i],
                    (rank_of(slow, a, b), core),
                )
                for i, (a, b) in enumerate(places)
            ]

        def start(self):
            for one in self.first_copies():
                one.start()

        def gather(self):
            for one in self.first_copies():
                one.wait_recv()

            @pl.loop(0, long)
            def _(z):
                add_into(
                    parts["vec"], (0, z, first, second), [got1["vec"][0, i, z] for i in range(3)]
                )

            for one in self.third_copies():
                one.start()

        def drain(self):
            for one in self.first_copies() + self.third_copies():
                one.wait_send()
            self.last_copy().wait_send()
            for one in self.puts():
                one.wait()

    def steps(*names):
        if fused:
            for name in names:
                job, step = name.split()
                getattr(jobs[job], step)()

    def steps_when(condition, *names):
        if fused:
            pl.when(condition)(lambda: steps(*names))

    down = Down("down", 0)
    jobs = {"down": down, "vec": Vectors("vec", 0)}
    jobs |= {kind: Job(kind, 0) for kind in ("out", "early", "lead")}
    jobs |= {f"up{k}": Job("up", k) for k in range(2)}
    jobs |= {f"attn{k + 1}": Job("attn", k) for k in range(pair_count - 1)}

    def local(source, target, index):
        return pltpu.make_async_copy(source, target, load_sems.at[index])

    own = rows_of(own_start, half)
    in_put = local(low_mid.at[pl.ds(0, half)], input_grad, 0)
    out_put = local(low_mid.at[pl.ds(half, half)], output, 1)
    g_load = local(cotangent, grads_all.at[own], 0)
    out_loads = [
        local(w_out.at[rows_of(core * mine, mine)], weight_out.at[pl.ds(0, mine)], 1),
        local(w_out.at[rows_of(other * mine, mine)], weight_out.at[pl.ds(mine, mine)], 2),
        local(heads_hbm, heads, 3),
        local(other_hbm, heads_far, 4),
    ]
    late_loads = [
        local(low_in_hbm, low_in, 5),
        local(query_hbm, queries, 6),
        local(key_hbm, keys, 7),
        local(value_hbm, values, 8),
        local(scales_hbm, scales, 14),
    ]
    for one in out_loads:
        one.start()

    peers = [partner]
    if fused:
        peers += [near_device, next_device, (rank_of(slow, near, next_), core)]
        peers += [(rank_of(z, first, second), core) for z in far_places]
    barrier = pltpu.get_barrier_semaphore()
    for peer in peers:
        pl.semaphore_signal(barrier, inc=1, device_id=peer, device_id_type=MESH)

    def own_rows(i):
        return rows_of(own_start + i * TILE, TILE)

    def far_rows(i):
        return rows_of(far_start + i * TILE, TILE)

    def tile_rows(i):
        return rows_of(i * TILE, TILE)

    def to_partner(source, target, pair_sems):
        def one(i):
            return remote(
                source(i), target(i), pair_sems.at[0, i], pair_sems.at[1, i], partner
            )

        return one

    g_far = remote(cotangent, grads_all.at[own], g_sems.at[0], g_sems.at[1], partner)
    mid_far = to_partner(
        lambda i: low_mid.at[own_rows(i)], lambda i: low_mid.at[own_rows(i)], mid_sems
    )
    dz_far = to_partner(
        lambda i: low_resid.at[own_rows(i)], lambda i: low_resid.at[own_rows(i)], dz_sems
    )
    mid_back = to_partner(
        lambda i: stage.at[tile_rows(i)], lambda i: catch_mid.at[tile_rows(i)], a_sems
    )
    in_back = to_partner(
        lambda i: stage.at[tile_rows(i)], lambda i: catch_mid.at[tile_rows(i)], b_sems
    )
    out_back = to_partner(
        lambda i: stage_far.at[tile_rows(i)], lambda i: catch_out.at[tile_rows(i)], c_sems
    )

    def feed_forward(weight_up, grad_up):
        up_loads = [
            local(
                w_up.at[:, pl.ds(pl.multiple_of((core * 2 + b) * block, 128), block)],
                weight_up.at[b],
                9 + b,
            )
            for b in range(2)
        ]
        down_loads = [
            local(w_down.at[rows_of((core * 2 + b) * block, block)], weight_down.at[b], 11 + b)
            for b in range(2)
        ]
        for one in out_loads:
            one.wait()
        for one in up_loads + [g_load] + down_loads:
            one.start()

        @pl.loop(0, 2)
        def _(i):
            here, place = tile_rows(i), own_rows(i)
            joined = jnp.concatenate(
                [heads[p, place, :] for p in range(pair_count)]
                + [heads_far[p, here, :] for p in range(pair_count)],
                1,
            )
            field = tokens[here, :].astype(FULL) + contract(joined, weight_out[...], 1, 0)
            resid[here, :] = field
            unit, _ = layer_norm(field)
            low_mid[place, :] = (unit * flat(gain_mid) + flat(shift_mid)).astype(LOW)

            @pl.when(i == 0)
            def _():
                pl.semaphore_wait(barrier, len(peers))

            mid_far(i).start()

        g_far.start()

        for one in up_loads:
            one.wait()
        for one in late_loads:
            one.start()

        @pl.loop(0, 2)
        def _(b):
            @pl.loop(0, tiles)
            def _(i):
                @pl.when((b == 0) & (i >= 2))
                def _():
                    mid_far(i - 2).wait_recv()

                here = rows_of(lax.rem(core * 2 + i, tiles) * TILE, TILE)
                value, slope = gelu_parts(contract(low_mid[here, :], weight_up[b], 1, 0))
                hidden_low[b, here, :] = value.astype(LOW)
                grad_up[b, here, :] = slope.astype(LOW)
                if fused:

                    @pl.when((b == 1) & (i == 3))
                    def _():
                        down.turn_at(core * 2)

            @pl.when(b == 0)
            def _():
                for one in [g_load] + down_loads:
                    one.wait()
                g_far.wait_recv()

            tall = hidden // COUNT
            per = mine // tall
            @pl.loop(0, 2)
            def _(m):
                place = pl.ds(pl.multiple_of(m * mine, 128), mine)
                grad = contract(hidden_low[b, :, place], grads_all[...], 0, 0).astype(LOW)
                kept = jnp.where(core == 0, grad[:, :mine], grad[:, mine:])
                given = jnp.where(core == 0, grad[:, mine:], grad[:, :mine])
                for i in range(per):
                    rank = (core * 2 + b) * (COUNT // 4) + m * per + i
                    z, a, s = spot_of(rank, core)
                    parts["down"][0, z, a, s] = kept[i * tall : (i + 1) * tall]
                    _, a, s = spot_of(rank, other)
                    stage_down[b, a, s] = given[i * tall : (i + 1) * tall]
            give_down(b).start()
            if fused:
                down.start_at(core * 2 + b)

            @pl.loop(0, tiles)
            def _(i):
                here = rows_of(i * TILE, TILE)
                back = contract(grads_all[here, :], weight_down[b], 1, 1)
                grad_up[b, here, :] = (back * grad_up[b, here, :].astype(FULL)).astype(LOW)

                @pl.when(i == 3)
                def _():
                    give_down(b).wait_recv()
                    if fused:
                        down.start_at(other * 2 + b)

                if fused:

                    @pl.when((b == 1) & (i == 1))
                    def _():
                        down.turn_at(other * 2)

            @pl.loop(0, 2)
            def _(m):
                tall = width // COUNT
                per = mine // tall
                place = pl.ds(pl.multiple_of(m * mine, 128), mine)
                grad = contract(low_mid[:, place], grad_up[b], 0, 0).astype(LOW)
                for i in range(per):
                    z, a, s = spot_of(m * per + i, core)
                    parts["up"][b, z, a, s] = grad[i * tall : (i + 1) * tall]

            if fused:
                Job("up", b).start()

        def mid_part(here):
            return contract(grad_up[0, here, :], weight_up[0], 1, 1) + contract(
                grad_up[1, here, :], weight_up[1], 1, 1
            )

        @pl.loop(0, tiles)
        def _(i):
            part = mid_part(rows_of(lax.rem(other * 2 + i, tiles) * TILE, TILE))

            @pl.when(i < 2)
            def _():
                stage[tile_rows(i), :] = part.astype(LOW)
                mid_back(i).start()

            @pl.when(i >= 2)
            def _():
                grad_resid[tile_rows(i - 2), :] = part

            steps_when(i == 1, "up0 turn")

        @pl.loop(0, 2)
        def _(i):
            here = tile_rows(i)
            mid_back(i).wait_recv()
            grad = grad_resid[here, :] + catch_mid[here, :].astype(FULL)
            unit, inverse = layer_norm(resid[here, :])
            vec_sums[2:3, :] += jnp.sum(grad * unit, 0, keepdims=True)
            vec_sums[3:4, :] += jnp.sum(grad, 0, keepdims=True)
            scaled = grad * flat(gain_mid)
            total = grads_all[own_rows(i), :].astype(FULL) + inverse * (
                scaled
                - jnp.mean(scaled, -1, keepdims=True)
                - unit * jnp.mean(scaled * unit, -1, keepdims=True)
            )
            grad_resid[here, :] = total
            low_resid[own_rows(i), :] = total.astype(LOW)
            dz_far(i).start()

        for i in range(2):
            mid_back(i).wait_send()
        if fused:
            down.turn_at(core * 2 + 1)

    def give_down(b):
        return remote(
            stage_down.at[b],
            parts["down"].at[0, core * 2 + b],
            pd_sems.at[0, b],
            pd_sems.at[1, b],
            partner,
        )

    give_out = remote(
        stage_out,
        parts["out"].at[0, pl.ds(core * 2, 2)],
        po_sems.at[0],
        po_sems.at[1],
        partner,
    )

    vec_sums[...] = jnp.zeros_like(vec_sums)
    pl.run_scoped(
        feed_forward,
        pltpu.VMEM((2, width, block), LOW),
        pltpu.VMEM((2, length, block), LOW),
    )

    def prob_load(p, t, slot):
        return pltpu.make_async_copy(prob_hbm[t].at[p], probs[t].at[slot], prob_sems.at[t, slot])

    def attention(slopes, fades, key_sum, value_sum, carry, grad_qkv, weight_in):
        for t in range(tiles):
            prob_load(pair_count - 1, t, 0).start()
        slope_load = local(slope_hbm, slopes, 13)
        weight_loads = []
        for place, source in enumerate((w_query, w_key, w_value)):
            for p in range(pair_count):
                weight_loads.append(
                    local(
                        source.at[:, pl.ds(pl.multiple_of(core * mine + p * PAIR, 128), PAIR)],
                        weight_in.at[:, pl.ds(p * mine + place * PAIR, PAIR)],
                        17 + place * pair_count + p,
                    )
                )
        for one in [slope_load] + weight_loads:
            one.start()

        keep = lanes_below((TILE, PAIR), HEAD)
        for one in late_loads:
            one.wait()

        def head_grads(here):
            result = contract(low_resid[here, :], weight_out[pl.ds(0, mine), :], 1, 1)
            for p in range(pair_count):
                scale = jnp.where(
                    keep, scales[here, 2 * p : 2 * p + 1], scales[here, 2 * p + 1 : 2 * p + 2]
                )
                grad_heads[p, here, :] = (result[:, p * PAIR : (p + 1) * PAIR] * scale).astype(LOW)

        @pl.loop(0, tiles)
        def _(i):
            @pl.when(i > 1)
            def _():
                dz_far(i - 2).wait_recv()

            head_grads(rows_of(lax.rem(core * 2 + i, tiles) * TILE, TILE))

        joined = jnp.concatenate([heads[p] for p in range(pair_count)], 1)
        grad = contract(joined, low_resid[...], 0, 0).astype(LOW)
        kept = jnp.where(core == 0, grad[:, :mine], grad[:, mine:])
        given = jnp.where(core == 0, grad[:, mine:], grad[:, :mine])
        tall = width // COUNT
        for i in range(mine // tall):
            rank = core * (COUNT // 2) + i
            z, a, s = spot_of(rank, core)
            parts["out"][0, z, a, s] = kept[i * tall : (i + 1) * tall]
            _, a, s = spot_of(rank, other)
            stage_out[i // (wide * deep), a, s] = given[i * tall : (i + 1) * tall]
        give_out.start()
        if fused:
            down.turn_at(other * 2 + 1)

        spots = (
            lax.broadcasted_iota(jnp.int32, (TILE, TILE), 0),
            lax.broadcasted_iota(jnp.int32, (TILE, TILE), 1),
        )
        after = jnp.where(spots[0] > spots[1], 1.0, 0.0).astype(LOW)

        def fade_send(t):
            part = pl.ds(t * (t + 1) // 2, t + 1)
            return remote(
                share_send.at[part],
                share_recv.at[part],
                df_sems.at[0, t],
                df_sems.at[1, t],
                partner,
            )

        def pair_step(step, p):
            slot = lax.rem(step, 2)
            for t in range(tiles):
                prob_load(p, t, slot).wait()

            @pl.when(step < pair_count - 1)
            def _():
                for t in range(tiles):
                    prob_load(p - 1, t, 1 - slot).start()

            for t in reversed(range(tiles)):
                count = (t + 1) * TILE
                span, rows = pl.ds(t * TILE, TILE), pl.ds(0, count)
                grad_tile = grad_heads[p, span, :]
                product = (grad_tile.astype(FULL) * heads[p, span, :].astype(FULL)).T
                query = queries[p, span, :]
                sides_q = jnp.concatenate(
                    [jnp.where(keep, query, LOW(0.0)), jnp.where(keep, LOW(0.0), query)], 0
                )
                sides_g = jnp.concatenate(
                    [jnp.where(keep, grad_tile, LOW(0.0)), jnp.where(keep, LOW(0.0), grad_tile)], 0
                )
                delta = jnp.concatenate(
                    [
                        jnp.sum(product[:HEAD, :], 0, keepdims=True),
                        jnp.sum(product[HEAD:, :], 0, keepdims=True),
                    ],
                    1,
                )
                change = probs[t][slot].astype(FULL) * (
                    contract(values[p, rows, :], sides_g, 1, 1) - delta
                )
                fade = change[:, :TILE] + change[:, TILE:]
                both = change.astype(LOW)
                fades[rows, span] = jnp.where(step == 0, 0.0, fades[rows, span]) + fade

                key_part = contract(both, sides_q, 1, 0)
                value_part = contract(probs[t][slot], sides_g, 1, 0)
                if t == tiles - 1:
                    key_sum[...] = key_part
                    value_sum[...] = value_part
                else:
                    key_sum[rows, :] += key_part
                    value_sum[rows, :] += value_part
                query_part = contract(keys[p, rows, :], both, 0, 0)
                query_part = jnp.concatenate(
                    [query_part[:HEAD, :TILE], query_part[HEAD:, TILE:]], 0
                )
                grad_qkv[p, span, pl.ds(0, PAIR)] = (query_part.T * 0.125).astype(LOW)

                if t == tiles - 1:
                    steps_when(step == 1, "up1 turn")
                    steps_when(step == 2, "attn2 turn", "up1 gather")

        def lead_head():
            @pl.when(core == 0)
            def _():
                carry[...] = jnp.zeros_like(carry)
                for t in reversed(range(tiles)):
                    count = (t + 1) * TILE
                    span, rows = pl.ds(t * TILE, TILE), pl.ds(0, count)
                    part = pl.ds(t * (t + 1) // 2, t + 1)
                    fade_send(t).wait_recv()
                    total = fades[rows, span] + share_recv[part].astype(FULL).reshape(count, TILE)
                    later = contract(total.astype(LOW), after, 1, 0) + carry[rows, :]
                    if t:
                        carry[rows, :] += jnp.sum(total, -1, keepdims=True)
                    slope = slopes[part].astype(FULL).reshape(count, TILE)
                    extra = (-later * slope).astype(LOW)
                    query = jnp.where(keep, queries[0, span, :], LOW(0.0))
                    key_sum[rows, :] += contract(extra, query, 1, 0)
                    whole = contract(keys[0, rows, :], extra, 0, 0).T * 0.125
                    grad_qkv[0, span, pl.ds(0, PAIR)] = (
                        grad_qkv[0, span, pl.ds(0, PAIR)].astype(FULL)
                        + jnp.where(keep, whole, 0.0)
                    ).astype(LOW)

            @pl.when(core == 1)
            def _():
                for t in range(tiles):
                    fade_send(t).wait_send()

        def weights_into(kind, k, right):
            @pl.loop(0, 2)
            def _(m):
                place = pl.ds(pl.multiple_of(m * mine, 128), mine)
                grad = contract(low_in[:, place], right, 0, 0).astype(LOW)
                for i in range(mine // tall):
                    z, a, s = spot_of(m * (mine // tall) + i, core)
                    parts[kind][k, z, a, s] = grad[i * tall : (i + 1) * tall]

            if fused:
                Job(kind, k).start()

        @pl.loop(0, pair_count)
        def _(step):
            p = pair_count - 1 - step
            pair_step(step, p)
            grad_qkv[p, :, pl.ds(2 * PAIR, PAIR)] = value_sum[...].astype(LOW)

            @pl.when(p > 0)
            def _():
                grad_qkv[p, :, pl.ds(PAIR, PAIR)] = key_sum[...].astype(LOW)
                weights_into("attn", p - 1, grad_qkv[p])

            @pl.when(step == 0)
            def _():
                give_out.wait_recv()
                steps("out start", "up0 gather")


        @pl.when(core == 1)
        def _():
            for t in reversed(range(tiles)):
                count = (t + 1) * TILE
                share_send[pl.ds(t * (t + 1) // 2, t + 1)] = (
                    fades[pl.ds(0, count), pl.ds(t * TILE, TILE)]
                    .astype(LOW)
                    .reshape(t + 1, TILE, TILE)
                )
                fade_send(t).start()

        keep_all = lanes_below((length, PAIR), HEAD)
        second_head = jnp.where(
            keep_all,
            pltpu.roll(grad_qkv[0, :, pl.ds(0, PAIR)].astype(FULL), HEAD, 1),
            key_sum[...],
        )
        weights_into(
            "early",
            0,
            jnp.concatenate(
                [second_head.astype(LOW), grad_qkv[0, :, pl.ds(2 * PAIR, PAIR)]], 1
            ),
        )
        slope_load.wait()
        steps("down cross", "out turn", "attn2 gather", "attn1 turn", "up0 close")
        lead_head()
        grad_qkv[0, :, pl.ds(PAIR, PAIR)] = key_sum[...].astype(LOW)
        first_head = jnp.where(
            keep_all,
            grad_qkv[0, :, pl.ds(0, PAIR)].astype(FULL),
            pltpu.roll(key_sum[...], HEAD, 1),
        )
        weights_into("lead", 0, first_head.astype(LOW))

        for one in weight_loads:
            one.wait()

        def in_part(here):
            joined = jnp.concatenate([grad_qkv[p, here, :] for p in range(pair_count)], 1)
            return contract(joined, weight_in[...], 1, 1)

        @pl.loop(0, tiles)
        def _(i):
            part = in_part(rows_of(lax.rem(other * 2 + i, tiles) * TILE, TILE))

            @pl.when(i < 2)
            def _():
                stage[tile_rows(i), :] = part.astype(LOW)
                in_back(i).start()

            @pl.when(i >= 2)
            def _():
                fades[tile_rows(i - 2), pl.ds(0, width)] = part

            steps_when(i == 1, "out gather", "early turn", "attn1 gather")
            steps_when(i == 3, "lead turn")

        for i in range(2):
            mid_far(i).wait_send()

        @pl.loop(0, 2)
        def _(i):
            here = tile_rows(i)
            in_back(i).wait_recv()
            grad = fades[here, pl.ds(0, width)] + catch_mid[here, :].astype(FULL)
            unit, inverse = layer_norm(tokens[here, :].astype(FULL))
            vec_sums[0:1, :] += jnp.sum(grad * unit, 0, keepdims=True)
            vec_sums[1:2, :] += jnp.sum(grad, 0, keepdims=True)
            scaled = grad * flat(gain_in)
            low_mid[here, :] = (
                grad_resid[here, :]
                + inverse
                * (
                    scaled
                    - jnp.mean(scaled, -1, keepdims=True)
                    - unit * jnp.mean(scaled * unit, -1, keepdims=True)
                )
            ).astype(LOW)

        in_put.start()
        for i in range(2):
            in_back(i).wait_send()

    pl.run_scoped(
        attention,
        pltpu.VMEM((tiles * (tiles + 1) // 2, TILE, TILE), LOW),
        pltpu.VMEM((length, length), FULL),
        pltpu.VMEM((length, PAIR), FULL),
        pltpu.VMEM((length, PAIR), FULL),
        pltpu.VMEM((length, 1), FULL),
        pltpu.VMEM((pair_count, length, mine), LOW),
        pltpu.VMEM((width, 3 * mine), LOW),
    )

    if not fused:
        for kind in KINDS[:-1]:
            one = pltpu.make_async_copy(parts[kind], results[kind], load_sems.at[0])
            one.start()
            one.wait()
        one = pltpu.make_async_copy(vec_sums, results["vec"], load_sems.at[0])
        one.start()
        one.wait()
    else:
        sums = vec_sums[...]
        tall = width // COUNT
        for rank in range(COUNT):
            z, a, s = spot_of(rank, core)
            shifted = pltpu.roll(sums, width - rank * tall, 1) if rank else sums
            parts["vec"][0, z, a, s] = shifted[:, :128]
    steps("vec start", "early gather", "down close")

    def out_part(here):
        return contract(hidden_low[0, here, :], weight_down[0], 1, 0) + contract(
            hidden_low[1, here, :], weight_down[1], 1, 0
        )

    @pl.loop(0, tiles)
    def _(i):
        part = out_part(rows_of(lax.rem(other * 2 + i, tiles) * TILE, TILE))

        @pl.when(i < 2)
        def _():
            stage_far[tile_rows(i), :] = part.astype(LOW)
            out_back(i).start()

        @pl.when(i >= 2)
        def _():
            resid[tile_rows(i - 2), :] += part

        steps_when(i == 0, "up1 close", "attn2 close")
        steps_when(i == 1, "lead gather", "out close")
        steps_when(i == 2, "vec gather")
        steps_when(i == 3, "attn1 close")

    steps("down store", "up0 store", "up1 store")

    @pl.loop(0, 2)
    def _(i):
        here = tile_rows(i)
        out_back(i).wait_recv()
        low_mid[rows_of(half + i * TILE, TILE), :] = (
            resid[here, :] + catch_out[here, :].astype(FULL)
        ).astype(LOW)

    out_put.start()
    steps("early close", "lead close", "vec close")
    steps("out store", "attn2 store", "attn1 store", "early store", "vec store", "lead store")
    if fused:
        for job in jobs.values():
            job.drain()
    in_put.wait()
    out_put.wait()
    g_far.wait_send()
    give_out.wait_send()
    for i in range(2):
        give_down(i).wait_send()
        for one in (dz_far, out_back):
            one(i).wait_send()


def finish(fused, tokens, cotangent, gain_in, gain_mid, shift_mid, forward, weights):
    low_in, queries, keys, values, probs, slopes, heads, heads_far, scales = forward
    half, width = tokens.shape
    length, mine = 2 * half, width // 2
    hidden = weights[-1].shape[0]
    pairs, tiles = mine // PAIR, length // TILE
    shapes = block_shapes(width, hidden)
    long, wide, deep = GRID
    anywhere = pl.BlockSpec(memory_space=pl.ANY)
    local = pl.BlockSpec(memory_space=pltpu.VMEM)
    outs = [jax.ShapeDtypeStruct((half, width), LOW)] * 2
    out_specs = [anywhere] * 2
    for kind in KINDS:
        shape, kept = shapes[kind]
        if fused:
            outs.append(jax.ShapeDtypeStruct((FAN[kind], 2) + shape, kept))
            out_specs.append(anywhere)
        elif kind == "vec":
            outs.append(jax.ShapeDtypeStruct((8, width), FULL))
            out_specs.append(anywhere)
        else:
            outs.append(jax.ShapeDtypeStruct((FAN[kind],) + GRID + shape, kept))
            out_specs.append(anywhere)
    scratch = [
        pltpu.VMEM((length, width), LOW),
        pltpu.VMEM((width, width), LOW),
        pltpu.VMEM((pairs, length, PAIR), LOW),
        pltpu.VMEM((pairs, half, PAIR), LOW),
        pltpu.VMEM((half, width), FULL),
        pltpu.VMEM((length, width), LOW),
        pltpu.VMEM((half, width), FULL),
        pltpu.VMEM((length, width), LOW),
        pltpu.VMEM((pairs, length, PAIR), LOW),
        pltpu.VMEM((length, width), LOW),
        pltpu.VMEM((pairs, length, PAIR), LOW),
        pltpu.VMEM((pairs, length, PAIR), LOW),
        pltpu.VMEM((pairs, length, PAIR), LOW),
        pltpu.VMEM((length, 128), FULL),
    ]
    scratch += [pltpu.VMEM((2, (t + 1) * TILE, 2 * TILE), LOW) for t in range(tiles)]
    corners = tiles * (tiles + 1) // 2
    scratch += [pltpu.VMEM((corners, TILE, TILE), LOW)] * 2
    scratch += [pltpu.VMEM((half, width), LOW)] * 4
    block = hidden // 4
    scratch += [pltpu.VMEM((2, block, width), LOW), pltpu.VMEM((2, length, block), LOW)]
    scratch += [
        pltpu.VMEM((2, wide, deep) + shapes["down"][0], LOW),
        pltpu.VMEM((2, wide, deep) + shapes["out"][0], LOW),
        pltpu.VMEM((8, width), FULL),
    ]
    scratch += [pltpu.VMEM((FAN[kind],) + GRID + shapes[kind][0], shapes[kind][1]) for kind in KINDS]
    dma = pltpu.SemaphoreType.DMA
    if fused:
        leads = {kind: ((long, deep), (long,), (long - 1,), ()) for kind in KINDS}
        leads["down"] = ((long, deep), (long - 1, deep), (), ())
        leads["vec"] = ((3, long), (), (long - 1,), ())
        for step in range(4):
            scratch += [
                pltpu.VMEM((FAN[kind],) + leads[kind][step] + shapes[kind][0], shapes[kind][1])
                for kind in KINDS
            ]
        scratch += [dma((long,))] * 2 + [dma((long - 1,))] * 2 + [dma((1,))] * 4
        for kind in KINDS[1:]:
            fan = FAN[kind]
            count = 3 if kind == "vec" else fan
            scratch += [dma((count,))] * 4 + [dma((fan, long - 1))] * 2 + [dma((fan,))] * 2
        scratch += [dma((FAN[kind], 2)) for kind in KINDS]
    scratch += [dma((17 + 3 * pairs,)), dma((2,))]
    scratch += [dma((2, 2))] * 6
    scratch += [dma((2,)), dma((2, tiles)), dma((tiles, 2))]
    return pl.pallas_call(
        functools.partial(finish_kernel, fused),
        out_shape=outs,
        in_specs=[local] + [anywhere] + [local] * 3 + [anywhere] * (4 + tiles + 1 + 3 + 6),
        out_specs=out_specs,
        scratch_shapes=scratch,
        compiler_params=pltpu.CompilerParams(
            collective_id=0, has_side_effects=True, vmem_limit_bytes=VMEM_LIMIT
        ),
        name="finish",
    )(
        tokens,
        cotangent,
        gain_in,
        gain_mid,
        shift_mid,
        low_in,
        queries,
        keys,
        values,
        *probs,
        slopes,
        heads,
        heads_far,
        scales,
        *weights,
    )

def deliver_kernel(count, *refs):
    refs, (load_sems, put_sems) = refs[:-2], refs[-2:]
    targets = refs[count : (len(refs) - 2 * count + 2) // 2 + count]
    sources, held = refs[:count], refs[count + len(targets) : 2 * count + len(targets)]
    made = refs[2 * count + len(targets) :]
    loads = [
        pltpu.make_async_copy(source, target, load_sems.at[i])
        for i, (source, target) in enumerate(zip(sources, held))
    ]
    for one in loads[2:] + loads[:2]:
        one.start()
    puts = [
        pltpu.make_async_copy(source, target, put_sems.at[i])
        for i, (source, target) in enumerate(zip(held[:2] + made, targets))
    ]
    for one in loads[2:]:
        one.wait()
    share_in, down, up, out, attn, early, lead, vec = held[2:]
    share, g_query, g_key, g_value, g_out, g_up, g_down, *g_vecs = made
    tall, mine = out.shape[2:]
    for k in range(2):
        for b in range(2):
            g_up[:, (2 * k + b) * 2 * mine : (2 * k + b + 1) * 2 * mine] = up[b, k].astype(FULL)
    puts[7].start()
    for k in range(2):
        g_down[:, k * mine : (k + 1) * mine] = down[0, k].astype(FULL)
    puts[8].start()
    for i in range(2):
        loads[i].wait()
        puts[i].start()
    for k in range(2):
        start = k * mine
        g_out[:, start : start + mine] = out[0, k].astype(FULL)
        for p in range(attn.shape[0]):
            for place, target in enumerate((g_query, g_key, g_value)):
                target[:, start + (p + 1) * PAIR : start + (p + 2) * PAIR] = attn[
                    p, k, :, place * PAIR : (place + 1) * PAIR
                ].astype(FULL)
        ones, twos = lead[0, k].astype(FULL), early[0, k].astype(FULL)
        keep = lanes_below(ones.shape, HEAD)
        seconds = twos[:, :PAIR]
        g_query[:, start : start + PAIR] = jnp.where(keep, ones, pltpu.roll(seconds, HEAD, 1))
        g_key[:, start : start + PAIR] = jnp.where(keep, pltpu.roll(ones, HEAD, 1), seconds)
        g_value[:, start : start + PAIR] = twos[:, PAIR:]
    share[...] = share_in[0:1, :]
    sums = vec[0, 0] + vec[0, 1]
    for i, target in enumerate(g_vecs):
        target[...] = sums[i, :tall]
    for one in puts[2:7] + puts[9:]:
        one.start()
    for one in puts:
        one.wait()


def deliver(*arrays):
    output, _, shares, down, up, out = arrays[:6]
    tall, mine = out.shape[2:]
    width = 2 * mine
    shapes = [(1, shares.shape[1])] + [(tall, width)] * 4
    shapes += [(tall, 2 * up.shape[3] * 2), (down.shape[2], width)] + [(tall,)] * 4
    anywhere = pl.BlockSpec(memory_space=pl.ANY)
    return pl.pallas_call(
        functools.partial(deliver_kernel, len(arrays)),
        out_shape=[jax.ShapeDtypeStruct(output.shape, output.dtype)] * 2
        + [jax.ShapeDtypeStruct(shape, FULL) for shape in shapes],
        in_specs=[anywhere] * len(arrays),
        out_specs=[anywhere] * (2 + len(shapes)),
        scratch_shapes=[pltpu.VMEM(one.shape, one.dtype) for one in arrays]
        + [pltpu.VMEM(shape, FULL) for shape in shapes]
        + [pltpu.SemaphoreType.DMA((len(arrays),)), pltpu.SemaphoreType.DMA((2 + len(shapes),))],
        compiler_params=pltpu.CompilerParams(vmem_limit_bytes=VMEM_LIMIT),
        name="deliver",
    )(*arrays)


def reduce_plain(parts, rows):
    down, up, out, attn, early, lead, vec = parts
    width = vec.shape[1]

    def scattered(part):
        summed = lax.psum_scatter(part.astype(FULL), "rows", scatter_dimension=0, tiled=True)
        return summed.astype(LOW)

    def joined(part):
        return lax.all_gather(part, "keys", axis=1, tiled=True).astype(FULL)

    def flat_part(part):
        return part.reshape(-1, part.shape[-1])

    ones, twos = scattered(flat_part(lead[0])), scattered(flat_part(early[0]))
    first = [
        jnp.concatenate([ones[:, :HEAD], twos[:, :HEAD]], 1),
        jnp.concatenate([ones[:, HEAD:], twos[:, HEAD:PAIR]], 1),
        twos[:, PAIR:],
    ]
    rest = [scattered(flat_part(attn[p])) for p in range(attn.shape[0])]
    halves = [
        jnp.concatenate([first[i]] + [one[:, i * PAIR : (i + 1) * PAIR] for one in rest], 1)
        for i in range(3)
    ]
    halves.append(scattered(flat_part(out[0])))
    halves.append(jnp.concatenate([scattered(flat_part(up[b])) for b in range(2)], 1))
    halves.append(scattered(flat_part(down[0])))
    sums = lax.psum_scatter(
        lax.psum(vec[:4].T, "keys"), "rows", scatter_dimension=0, tiled=True
    )
    return [joined(one) for one in halves], [sums[:, i] for i in range(4)]


def body(
    rows,
    tokens,
    seg_ids,
    doc_starts,
    gain_in,
    shift_in,
    w_query,
    w_key,
    w_value,
    w_out,
    gain_mid,
    shift_mid,
    w_up,
    w_down,
    out_grad,
):
    fused = rows == COUNT
    own_tokens, own_grad = tokens[0], out_grad[0]
    low_in, queries, keys, values, probs, slopes, heads, heads_far, scales, shares = attend(
        own_tokens, seg_ids, gain_in, shift_in, w_query, w_key, w_value
    )
    output, input_grad, *parts = finish(
        fused,
        own_tokens,
        own_grad,
        gain_in,
        gain_mid,
        shift_mid,
        (low_in, queries, keys, values, probs, slopes, heads, heads_far, scales),
        (w_query, w_key, w_value, w_out, w_up, w_down),
    )
    if fused:
        output, input_grad, shares, *grads = deliver(output, input_grad, shares, *parts)
        grads, vectors = grads[:6], grads[6:]
    else:
        grads, vectors = reduce_plain(parts, rows)
    g_query, g_key, g_value, g_out, g_up, g_down = grads
    return (
        output[None],
        input_grad[None],
        shares[:1],
        vectors[0],
        vectors[1],
        g_query,
        g_key,
        g_value,
        g_out,
        vectors[2],
        vectors[3],
        g_up,
        g_down,
    )


def solution(mesh):
    in_specs = (
        P("rows", "keys", None),
        P("rows", None),
        P("rows", "keys"),
        P(),
        P(),
        P(),
        P(),
        P(),
        P(),
        P(),
        P(),
        P(),
        P(),
        P("rows", "keys", None),
    )
    out_specs = (
        P("rows", "keys", None),
        P("rows", "keys", None),
        P("rows", "keys"),
        P("rows"),
        P("rows"),
        P("rows", None),
        P("rows", None),
        P("rows", None),
        P("rows", None),
        P("rows"),
        P("rows"),
        P("rows", None),
        P("rows", None),
    )
    return jax.shard_map(
        functools.partial(body, mesh.shape["rows"]),
        mesh=mesh,
        in_specs=in_specs,
        out_specs=out_specs,
        check_vma=False,
    )
```

```python
import functools

import jax
import jax.numpy as jnp
from jax import lax
from jax.experimental import pallas as pl
from jax.experimental.pallas import tpu as pltpu
from jax.sharding import PartitionSpec as P

HEAD = 64
PAIR = 2 * HEAD
TILE = 256
EPS = 1e-05
MASKED = 1e30
SELECT_SHIFT = 4.0
LOW = jnp.bfloat16
FULL = jnp.float32
MESH = pl.DeviceIdType.MESH
VMEM_LIMIT = 67_000_000


def contract(left, right, left_dim, right_dim):
    return lax.dot_general(
        left, right, (((left_dim,), (right_dim,)), ((), ())), preferred_element_type=FULL
    )


def layer_norm(field):
    center = field - jnp.mean(field, -1, keepdims=True)
    inverse = lax.rsqrt(jnp.mean(center * center, -1, keepdims=True) + EPS)
    return center * inverse, inverse


def remote(source, target, send, recv, device):
    return pltpu.make_async_remote_copy(
        src_ref=source,
        dst_ref=target,
        send_sem=send,
        recv_sem=recv,
        device_id=device,
        device_id_type=MESH,
    )


def lanes_below(shape, bound):
    return lax.broadcasted_iota(jnp.int32, shape, len(shape) - 1) < bound


def flat(ref):
    return ref[...].reshape(1, ref.shape[0])


def corner(step, tiles):
    t = sum((step >= n * (n + 1) // 2).astype(jnp.int32) for n in range(1, tiles))
    return t, step - t * (t + 1) // 2


def rows_of(start, size):
    return pl.ds(pl.multiple_of(start, size), size)


def gelu_parts(field):
    scale = 0.7978845608028654
    square = field * field
    inner = jnp.tanh(scale * field * (1.0 + 0.044715 * square))
    half_sum = 0.5 * (1.0 + inner)
    slope = half_sum + 0.5 * field * (1.0 - inner * inner) * (
        scale * (1.0 + 3.0 * 0.044715 * square)
    )
    return field * half_sum, slope


GRID = (4, 2, 2)
COUNT = GRID[0] * GRID[1] * GRID[2]
KINDS = ("down", "up", "out", "attn", "early", "lead", "vec")
FAN = {"down": 1, "up": 2, "out": 1, "attn": 2, "early": 1, "lead": 1, "vec": 1}


def block_shapes(width, hidden):
    mine = width // 2
    tall = width // COUNT
    return {
        "down": ((hidden // COUNT, mine), LOW),
        "up": ((tall, mine * 2), LOW),
        "out": ((tall, mine), LOW),
        "attn": ((tall, mine), LOW),
        "early": ((tall, 2 * PAIR), LOW),
        "lead": ((tall, PAIR), LOW),
        "vec": ((8, 128), FULL),
    }


def layer_kernel(fused, *refs):
    refs = list(refs)

    def take(count):
        taken = refs[:count]
        del refs[:count]
        return taken if count > 1 else taken[0]

    tokens_hbm, seg, cotangent, gain, shift, gain_mid, shift_mid = take(7)
    w_query, w_key, w_value, w_out, w_up, w_down = take(6)
    output, input_grad = take(2)
    results = dict(zip(KINDS, take(len(KINDS))))
    prob_hbm, slope_hbm, share_out = take(4), take(1), take(1)
    (
        grads_all,
        weight_out,
        heads,
        heads_far,
        resid,
        low_mid,
        grad_resid,
        low_resid,
        grad_heads,
        low_in,
        queries,
        keys,
        values,
        scales,
        tokens,
    ) = take(15)
    probs = take(4)
    share = take(1)
    stage, catch_mid, catch_out = take(3)
    weight_down, hidden_low = take(2)
    stage_out = take(1)
    vec_sums = take(1)
    parts = dict(zip(KINDS, take(len(KINDS))))
    if fused:
        got1 = dict(zip(KINDS, take(len(KINDS))))
        got2 = dict(zip(KINDS, take(len(KINDS))))
        got3 = dict(zip(KINDS, take(len(KINDS))))
        pair = dict(zip(KINDS, take(len(KINDS))))
        sems = {
            name: take(2) for name in ("down1", "down2", "down3", "down4")
        }
        for kind in KINDS[1:]:
            for stage_name in "1234":
                sems[kind + stage_name] = take(2)
        for kind in KINDS:
            sems[kind + "5"] = take(1)
    (load_sems, g_sems, mid_sems, dz_sems, a_sems, b_sems, c_sems, pd_sems, po_sems, df_sems, prob_sems) = take(11)
    far_sems, head_sems, weight_sems = take(3)

    long, wide, deep = GRID
    core = lax.axis_index("keys")
    row = lax.axis_index("rows")
    other = 1 - core
    partner = (row, other)
    half, width = tokens.shape
    length, mine = 2 * half, width // 2
    pair_count = mine // PAIR
    tiles = length // TILE
    hidden = w_down.shape[0]
    block = hidden // 4
    own_start, far_start = core * half, other * half

    if fused:
        slow, mid, fast = row // (wide * deep), (row // deep) % wide, row % deep
    else:
        slow, mid, fast = 0, 0, 0

    def spot_of(rank, whose):
        z, y, x = rank // (wide * deep), (rank // deep) % wide, rank % deep
        if not fused:
            return z, y, x
        return z, x + whose * (y - x), y + whose * (x - y)

    first, second = fast + core * (mid - fast), mid + core * (fast - mid)
    near, next_ = 1 - first, 1 - second

    def rank_of(z, a, b):
        y, x = b + core * (a - b), a + core * (b - a)
        return (z * wide + y) * deep + x

    near_device = (rank_of(slow, near, second), core)
    next_device = (rank_of(slow, first, next_), core)
    far_places = [lax.rem(slow + step, long) for step in range(1, long)]

    def add_into(target, index, terms):
        total = target[index].astype(FULL)
        for term in terms:
            total = total + term.astype(FULL)
        target[index] = total.astype(target.dtype)

    class Job:
        def __init__(self, kind, k):
            self.kind, self.k = kind, k

        def first_copy(self):
            kind, k = self.kind, self.k
            part, got = parts[kind].at[k], got1[kind].at[k]
            send, recv = sems[kind + "1"]
            return remote(part.at[:, near], got, send.at[k], recv.at[k], near_device)

        def second_copy(self):
            kind, k = self.kind, self.k
            part, got = parts[kind].at[k], got2[kind].at[k]
            send, recv = sems[kind + "2"]
            return remote(part.at[:, first, next_], got, send.at[k], recv.at[k], next_device)

        def third_copies(self):
            kind, k = self.kind, self.k
            send, recv = sems[kind + "3"]
            return [
                remote(
                    parts[kind].at[k, z, first, second],
                    got3[kind].at[k, step],
                    send.at[k, step],
                    recv.at[k, step],
                    (rank_of(z, first, second), core),
                )
                for step, z in enumerate(far_places)
            ]

        def last_copy(self):
            kind, k = self.kind, self.k
            send, recv = sems[kind + "4"]
            return remote(
                parts[kind].at[k, slow, first, second],
                pair[kind].at[k],
                send.at[k],
                recv.at[k],
                partner,
            )

        def start(self):
            self.first_copy().start()

        def turn(self):
            self.first_copy().wait_recv()
            kind, k = self.kind, self.k

            @pl.loop(0, long * deep)
            def _(step):
                z, b = step // deep, lax.rem(step, deep)
                add_into(parts[kind], (k, z, first, b), [got1[kind][k, z, b]])

            self.second_copy().start()

        def gather(self):
            self.second_copy().wait_recv()
            kind, k = self.kind, self.k

            @pl.loop(0, long)
            def _(z):
                add_into(parts[kind], (k, z, first, second), [got2[kind][k, z]])

            for one in self.third_copies():
                one.start()

        def close(self):
            for one in self.third_copies():
                one.wait_recv()
            kind, k = self.kind, self.k
            add_into(
                parts[kind],
                (k, slow, first, second),
                [got3[kind][k, step] for step in range(long - 1)],
            )
            self.last_copy().start()

        def puts(self):
            kind, k = self.kind, self.k
            own_part = parts[kind].at[k, slow, first, second]
            sem = sems[kind + "5"]
            return [
                pltpu.make_async_copy(own_part, results[kind].at[k, core], sem.at[k, 0]),
                pltpu.make_async_copy(pair[kind].at[k], results[kind].at[k, other], sem.at[k, 1]),
            ]

        def store(self):
            self.last_copy().wait_recv()
            for one in self.puts():
                one.start()

        def drain(self):
            self.first_copy().wait_send()
            self.second_copy().wait_send()
            for one in self.third_copies():
                one.wait_send()
            self.last_copy().wait_send()
            for one in self.puts():
                one.wait()

    class Down(Job):
        def near_copy(self, z):
            send, recv = sems["down1"]
            return remote(
                parts["down"].at[0, z, near],
                got1["down"].at[0, z],
                send.at[z],
                recv.at[z],
                near_device,
            )

        def slow_copy(self, step):
            z = lax.rem(slow + step, long)
            send, recv = sems["down2"]
            return remote(
                parts["down"].at[0, z, first],
                got2["down"].at[0, step - 1],
                send.at[step - 1],
                recv.at[step - 1],
                (rank_of(z, first, second), core),
            )

        def next_copy(self):
            send, recv = sems["down3"]
            return remote(
                parts["down"].at[0, slow, first, next_],
                got3["down"].at[0],
                send.at[0],
                recv.at[0],
                next_device,
            )

        def start_at(self, z):
            self.near_copy(z).start()

        def turn_at(self, z):
            self.near_copy(z).wait_recv()

            @pl.loop(0, deep)
            def _(b):
                add_into(parts["down"], (0, z, first, b), [got1["down"][0, z, b]])

            step = lax.rem(z - slow + long, long)

            @pl.when(step > 0)
            def _():
                self.slow_copy(step).start()

        def cross(self):
            for step in range(1, long):
                self.slow_copy(step).wait_recv()

            @pl.loop(0, deep)
            def _(b):
                add_into(
                    parts["down"],
                    (0, slow, first, b),
                    [got2["down"][0, step, b] for step in range(long - 1)],
                )

            self.next_copy().start()

        def close(self):
            self.next_copy().wait_recv()
            add_into(parts["down"], (0, slow, first, second), [got3["down"][0]])
            self.last_copy().start()

        def drain(self):
            for z in range(long):
                self.near_copy(z).wait_send()
            for step in range(1, long):
                self.slow_copy(step).wait_send()
            self.next_copy().wait_send()
            self.last_copy().wait_send()
            for one in self.puts():
                one.wait()

    class Vectors(Job):
        def first_copies(self):
            send, recv = sems["vec1"]
            places = ((near, second), (first, next_), (near, next_))
            return [
                remote(
                    parts["vec"].at[0, :, a, b],
                    got1["vec"].at[0, i],
                    send.at[i],
                    recv.at[i],
                    (rank_of(slow, a, b), core),
                )
                for i, (a, b) in enumerate(places)
            ]

        def start(self):
            for one in self.first_copies():
                one.start()

        def gather(self):
            for one in self.first_copies():
                one.wait_recv()

            @pl.loop(0, long)
            def _(z):
                add_into(
                    parts["vec"], (0, z, first, second), [got1["vec"][0, i, z] for i in range(3)]
                )

            for one in self.third_copies():
                one.start()

        def drain(self):
            for one in self.first_copies() + self.third_copies():
                one.wait_send()
            self.last_copy().wait_send()
            for one in self.puts():
                one.wait()

    def steps(*names):
        if fused:
            for name in names:
                job, step = name.split()
                getattr(jobs[job], step)()

    def steps_when(condition, *names):
        if fused:
            pl.when(condition)(lambda: steps(*names))

    down = Down("down", 0)
    jobs = {"down": down, "vec": Vectors("vec", 0)}
    jobs |= {kind: Job(kind, 0) for kind in ("out", "early", "lead")}
    jobs |= {f"up{k}": Job("up", k) for k in range(2)}
    jobs |= {f"attn{k + 1}": Job("attn", k) for k in range(pair_count - 1)}

    def local(source, target, index):
        return pltpu.make_async_copy(source, target, load_sems.at[index])

    own = rows_of(own_start, half)
    in_put = local(low_mid.at[pl.ds(0, half)], input_grad, 0)
    out_put = local(low_mid.at[pl.ds(half, half)], output, 1)
    g_load = local(cotangent, grads_all.at[own], 0)
    out_loads = [
        local(tokens_hbm, tokens, 15),
        local(w_out.at[rows_of(core * mine, mine)], weight_out.at[pl.ds(0, mine)], 1),
        local(w_out.at[rows_of(other * mine, mine)], weight_out.at[pl.ds(mine, mine)], 2),
    ]
    down_loads = [
        local(w_down.at[rows_of((core * 2 + b) * block, block)], weight_down.at[b], 11 + b)
        for b in range(2)
    ]

    peers = [partner]
    if fused:
        peers += [near_device, next_device, (rank_of(slow, near, next_), core)]
        peers += [(rank_of(z, first, second), core) for z in far_places]
    barrier = pltpu.get_barrier_semaphore()
    for peer in peers:
        pl.semaphore_signal(barrier, inc=1, device_id=peer, device_id_type=MESH)

    exchange = remote(tokens_hbm, low_resid.at[own], far_sems.at[0], far_sems.at[1], partner)

    def send_heads(p):
        return remote(
            heads.at[p, rows_of(far_start, half)],
            heads_far.at[p],
            head_sems.at[0, p],
            head_sems.at[1, p],
            partner,
        )

    def prob_put(t):
        return pltpu.make_async_copy(probs[t].at[0], prob_hbm[t], prob_sems.at[t, 0])

    def prob_load(t):
        return pltpu.make_async_copy(prob_hbm[t], probs[t].at[0], prob_sems.at[t, 1])

    def own_rows(i):
        return rows_of(own_start + i * TILE, TILE)

    def far_rows(i):
        return rows_of(far_start + i * TILE, TILE)

    def tile_rows(i):
        return rows_of(i * TILE, TILE)

    def to_partner(source, target, pair_sems):
        def one(i):
            return remote(
                source(i), target(i), pair_sems.at[0, i], pair_sems.at[1, i], partner
            )

        return one

    g_far = remote(cotangent, grads_all.at[own], g_sems.at[0], g_sems.at[1], partner)
    mid_far = to_partner(
        lambda i: low_mid.at[own_rows(i)], lambda i: low_mid.at[own_rows(i)], mid_sems
    )
    dz_far = to_partner(
        lambda i: low_resid.at[own_rows(i)], lambda i: low_resid.at[own_rows(i)], dz_sems
    )
    mid_back = to_partner(
        lambda i: stage.at[tile_rows(i)], lambda i: catch_mid.at[tile_rows(i)], a_sems
    )
    in_back = to_partner(
        lambda i: stage.at[tile_rows(i)], lambda i: catch_mid.at[tile_rows(i)], b_sems
    )
    out_back = to_partner(
        lambda i: stage.at[tile_rows(i)], lambda i: catch_out.at[tile_rows(i)], c_sems
    )

    def forward(
        weights,
        lead_query,
        lead_key,
        slopes,
        penalty,
        scale_rows,
        seg_cols,
        free_cols,
        sums,
    ):
        def column(rows, i):
            return (rows, pl.ds(i, 1))

        columns = pl.ds(pl.multiple_of(core * mine, 128), mine)
        loads = []
        for place, source in enumerate((w_query, w_key, w_value)):
            loads.append((source.at[:, columns], weights.at[:, pl.ds(place * mine, mine)]))
        for place, source in enumerate((w_query, w_key)):
            loads.append(
                (source.at[:, pl.ds(0, PAIR)], weights.at[:, pl.ds(3 * mine + place * PAIR, PAIR)])
            )
        loads = [
            pltpu.make_async_copy(source, target, weight_sems.at[i])
            for i, (source, target) in enumerate(loads)
        ]
        own_load = pltpu.make_async_copy(tokens_hbm, low_resid.at[own], weight_sems.at[5])
        own_load.start()
        for one in loads:
            one.start()

        pl.semaphore_wait(barrier, len(peers))
        exchange.start()
        g_far.start()
        for one in out_loads + [g_load] + down_loads:
            one.start()

        own_load.wait()

        keep = lanes_below((TILE, PAIR), HEAD)
        keep_half = lanes_below((half, PAIR), HEAD)

        @pl.loop(0, 2)
        def _(i):
            @pl.when(i == 1)
            def _():
                exchange.wait_recv()

            here = rows_of(lax.rem(core + i, 2) * half, half)
            unit, _ = layer_norm(low_resid[here, :].astype(FULL))
            low_in[here, :] = (unit * flat(gain) + flat(shift)).astype(LOW)

            @pl.when(i == 0)
            def _():
                seg_row = seg[...]
                seg_wide = jnp.broadcast_to(seg_row.astype(FULL), (128, length))
                spot = lax.broadcasted_iota(jnp.int32, (128, length), 1)
                before = pltpu.roll(seg_wide, 1, 1)
                free_wide = jnp.where((spot > 0) & (before == seg_wide), 1.0, 0.0)
                seg_cols[...] = seg_wide.T
                free_cols[...] = free_wide.T
                for one in loads:
                    one.wait()

            result = contract(low_in[here, :], weights[...], 1, 0).astype(LOW)
            for p in range(pair_count):
                queries[p, here, :] = result[:, p * PAIR : (p + 1) * PAIR] * LOW(0.125)
                keys[p, here, :] = result[:, mine + p * PAIR : mine + (p + 1) * PAIR]
                values[p, here, :] = result[:, 2 * mine + p * PAIR : 2 * mine + (p + 1) * PAIR]
            first = result[:, 3 * mine : 3 * mine + PAIR]
            lead_query[here, :] = jnp.where(keep_half, first, LOW(0.0)) * LOW(0.125)
            lead_key[here, :] = result[:, 3 * mine + PAIR :]

        spots = (
            lax.broadcasted_iota(jnp.int32, (2 * TILE, 2 * TILE), 0),
            lax.broadcasted_iota(jnp.int32, (2 * TILE, 2 * TILE), 1),
        )
        earlier = jnp.where(spots[0] < spots[1], 1.0, 0.0).astype(LOW)
        scale_rows[...] = jnp.zeros_like(scale_rows)
        sums[...] = jnp.zeros_like(sums)

        @pl.loop(0, (tiles // 2) * (tiles // 2 + 1) // 2)
        def _(step):
            wide, k = corner(step, tiles // 2)
            rows, span = rows_of(k * 2 * TILE, 2 * TILE), rows_of(wide * 2 * TILE, 2 * TILE)
            scores = contract(lead_key[rows, :], lead_query[span, :], 1, 1)
            repeat = 2 * TILE // 128
            same = jnp.concatenate([seg_cols[rows, :]] * repeat, 1) == seg[:, span].astype(FULL)
            ahead = spots[1] - spots[0] + (wide - k) * 2 * TILE
            later = same & (ahead > 0)
            allowed = same & (ahead >= 0)
            select = jnp.where(later, jnp.concatenate([free_cols[rows, :]] * repeat, 1), 0.0)
            level = scores - SELECT_SHIFT
            chosen = select * (jnp.maximum(level, 0.0) + jnp.log(1.0 + jnp.exp(-jnp.abs(level))))
            slope = (select * (0.5 + 0.5 * jnp.tanh(0.5 * level))).astype(LOW)

            slopes[wide * (2 * wide + 1) + 2 * k] = slope[:TILE, :TILE]

            @pl.when(k < wide)
            def _():
                slopes[wide * (2 * wide + 1) + 2 * k + 1] = slope[TILE:, :TILE]

            slopes[(2 * wide + 1) * (wide + 1) + 2 * k] = slope[:TILE, TILE:]
            slopes[(2 * wide + 1) * (wide + 1) + 2 * k + 1] = slope[TILE:, TILE:]
            high = chosen.astype(LOW)
            rest = (chosen - high.astype(FULL)).astype(LOW)
            total = (
                sums[column(rows, 0)] + contract(high, earlier, 1, 0) + contract(rest, earlier, 1, 0)
            )
            penalty[rows, span] = jnp.where(allowed, total, MASKED)
            sums[column(rows, 0)] += jnp.sum(chosen, -1, keepdims=True)
            ratio = jnp.where(later, 0.5 + 0.5 * jnp.tanh(0.5 * total - 1.0), 0.0)
            sums[column(rows, 1)] += jnp.sum(ratio, -1, keepdims=True)
            sums[column(rows, 2)] += jnp.sum(jnp.where(later, 1.0, 0.0), -1, keepdims=True)

        slope_put = pltpu.make_async_copy(slopes, slope_hbm, weight_sems.at[6])
        slope_put.start()

        shares = sums[column(own, 1)] / jnp.maximum(sums[column(own, 2)], 1.0)
        share_out[...] = jnp.broadcast_to(shares, (half, 128)).T[0:8, :]

        @pl.loop(0, pair_count)
        def _(p):
            slot = lax.rem(p, 2)

            @pl.when(p == 2)
            def _():
                for t in range(tiles):
                    prob_put(t).wait()

            for t in range(tiles):
                count = (t + 1) * TILE
                span = pl.ds(t * TILE, TILE)
                query = queries[p, span, :]
                both = jnp.concatenate(
                    [jnp.where(keep, query, LOW(0.0)), jnp.where(keep, LOW(0.0), query)], 0
                )
                fine = penalty[pl.ds(0, count), span]
                logits = contract(keys[p, pl.ds(0, count), :], both, 1, 1) - jnp.concatenate(
                    [fine, fine], 1
                )
                scaled = jnp.exp(logits - jnp.max(logits, 0, keepdims=True))
                prob = scaled.astype(LOW)
                probs[t][slot] = prob
                scale = 1.0 / jnp.sum(scaled, 0, keepdims=True)
                scale_rows[pl.ds(2 * p, 1), span] = scale[:, :TILE]
                scale_rows[pl.ds(2 * p + 1, 1), span] = scale[:, TILE:]
                out = contract(values[p, pl.ds(0, count), :], prob, 0, 0) * scale
                out = jnp.concatenate([out[:HEAD, :TILE], out[HEAD:, TILE:]], 0)
                heads[p, span, :] = out.T.astype(LOW)
            @pl.when(p == 0)
            def _():
                for t in range(tiles):
                    prob_put(t).start()

            send_heads(p).start()

        scales[...] = scale_rows[...].T
        slope_put.wait()
        exchange.wait_send()

    def feed_forward(weight_up, grad_up, stage_down):
        def give_down(b):
            return remote(
                stage_down.at[b],
                parts["down"].at[0, core * 2 + b],
                pd_sems.at[0, b],
                pd_sems.at[1, b],
                partner,
            )

        up_loads = [
            local(
                w_up.at[:, pl.ds(pl.multiple_of((core * 2 + b) * block, 128), block)],
                weight_up.at[b],
                9 + b,
            )
            for b in range(2)
        ]
        for one in up_loads:
            one.start()
        for one in out_loads:
            one.wait()
        for p in range(pair_count):
            send_heads(p).wait_recv()

        @pl.loop(0, 2)
        def _(i):
            here, place = tile_rows(i), own_rows(i)
            joined = jnp.concatenate(
                [heads[p, place, :] for p in range(pair_count)]
                + [heads_far[p, here, :] for p in range(pair_count)],
                1,
            )
            field = tokens[here, :].astype(FULL) + contract(joined, weight_out[...], 1, 0)
            resid[here, :] = field
            unit, _ = layer_norm(field)
            low_mid[place, :] = (unit * flat(gain_mid) + flat(shift_mid)).astype(LOW)

            mid_far(i).start()


        for one in up_loads:
            one.wait()

        @pl.loop(0, 2)
        def _(b):
            @pl.loop(0, tiles)
            def _(i):
                @pl.when((b == 0) & (i >= 2))
                def _():
                    mid_far(i - 2).wait_recv()

                here = rows_of(lax.rem(core * 2 + i, tiles) * TILE, TILE)
                value, slope = gelu_parts(contract(low_mid[here, :], weight_up[b], 1, 0))
                hidden_low[b, here, :] = value.astype(LOW)
                grad_up[b, here, :] = slope.astype(LOW)
                if fused:

                    @pl.when((b == 1) & (i == 3))
                    def _():
                        down.turn_at(core * 2)

            @pl.when(b == 0)
            def _():
                for one in [g_load] + down_loads:
                    one.wait()
                g_far.wait_recv()

            tall = hidden // COUNT
            per = mine // tall
            @pl.loop(0, 2)
            def _(m):
                place = pl.ds(pl.multiple_of(m * mine, 128), mine)
                grad = contract(hidden_low[b, :, place], grads_all[...], 0, 0).astype(LOW)
                kept = jnp.where(core == 0, grad[:, :mine], grad[:, mine:])
                given = jnp.where(core == 0, grad[:, mine:], grad[:, :mine])
                for i in range(per):
                    rank = (core * 2 + b) * (COUNT // 4) + m * per + i
                    z, a, s = spot_of(rank, core)
                    parts["down"][0, z, a, s] = kept[i * tall : (i + 1) * tall]
                    _, a, s = spot_of(rank, other)
                    stage_down[b, a, s] = given[i * tall : (i + 1) * tall]
            give_down(b).start()
            if fused:
                down.start_at(core * 2 + b)

            @pl.loop(0, tiles)
            def _(i):
                here = rows_of(i * TILE, TILE)
                back = contract(grads_all[here, :], weight_down[b], 1, 1)
                grad_up[b, here, :] = (back * grad_up[b, here, :].astype(FULL)).astype(LOW)

                @pl.when(i == 3)
                def _():
                    give_down(b).wait_recv()
                    if fused:
                        down.start_at(other * 2 + b)

                if fused:

                    @pl.when((b == 1) & (i == 1))
                    def _():
                        down.turn_at(other * 2)

            @pl.loop(0, 2)
            def _(m):
                tall = width // COUNT
                per = mine // tall
                place = pl.ds(pl.multiple_of(m * mine, 128), mine)
                grad = contract(low_mid[:, place], grad_up[b], 0, 0).astype(LOW)
                for i in range(per):
                    z, a, s = spot_of(m * per + i, core)
                    parts["up"][b, z, a, s] = grad[i * tall : (i + 1) * tall]

            if fused:
                Job("up", b).start()

        def mid_part(here):
            return contract(grad_up[0, here, :], weight_up[0], 1, 1) + contract(
                grad_up[1, here, :], weight_up[1], 1, 1
            )

        @pl.loop(0, tiles)
        def _(i):
            part = mid_part(rows_of(lax.rem(other * 2 + i, tiles) * TILE, TILE))

            @pl.when(i < 2)
            def _():
                stage[tile_rows(i), :] = part.astype(LOW)
                mid_back(i).start()

            @pl.when(i >= 2)
            def _():
                grad_resid[tile_rows(i - 2), :] = part

            steps_when(i == 1, "up0 turn")

        @pl.loop(0, 2)
        def _(i):
            here = tile_rows(i)
            mid_back(i).wait_recv()
            grad = grad_resid[here, :] + catch_mid[here, :].astype(FULL)
            unit, inverse = layer_norm(resid[here, :])
            vec_sums[2:3, :] += jnp.sum(grad * unit, 0, keepdims=True)
            vec_sums[3:4, :] += jnp.sum(grad, 0, keepdims=True)
            scaled = grad * flat(gain_mid)
            total = grads_all[own_rows(i), :].astype(FULL) + inverse * (
                scaled
                - jnp.mean(scaled, -1, keepdims=True)
                - unit * jnp.mean(scaled * unit, -1, keepdims=True)
            )
            grad_resid[here, :] = total
            low_resid[own_rows(i), :] = total.astype(LOW)
            dz_far(i).start()

        for i in range(2):
            mid_back(i).wait_send()
            give_down(i).wait_send()
        if fused:
            down.turn_at(core * 2 + 1)

    give_out = remote(
        stage_out,
        parts["out"].at[0, pl.ds(core * 2, 2)],
        po_sems.at[0],
        po_sems.at[1],
        partner,
    )

    vec_sums[...] = jnp.zeros_like(vec_sums)
    pl.run_scoped(
        forward,
        pltpu.VMEM((width, 3 * mine + 2 * PAIR), LOW),
        pltpu.VMEM((length, PAIR), LOW),
        pltpu.VMEM((length, PAIR), LOW),
        pltpu.VMEM((tiles * (tiles + 1) // 2, TILE, TILE), LOW),
        pltpu.VMEM((length, length), FULL),
        pltpu.VMEM((128, length), FULL),
        pltpu.VMEM((length, 128), FULL),
        pltpu.VMEM((length, 128), FULL),
        pltpu.VMEM((length, 128), FULL),
    )
    pl.run_scoped(
        feed_forward,
        pltpu.VMEM((2, width, block), LOW),
        pltpu.VMEM((2, length, block), LOW),
        pltpu.VMEM((2, wide, deep) + block_shapes(width, hidden)["down"][0], LOW),
    )

    def attention(slopes, fades, key_sum, value_sum, carry, grad_qkv, weight_in):
        slope_load = local(slope_hbm, slopes, 13)
        weight_loads = []
        for place, source in enumerate((w_query, w_key, w_value)):
            for p in range(pair_count):
                weight_loads.append(
                    local(
                        source.at[:, pl.ds(pl.multiple_of(core * mine + p * PAIR, 128), PAIR)],
                        weight_in.at[:, pl.ds(p * mine + place * PAIR, PAIR)],
                        17 + place * pair_count + p,
                    )
                )
        for one in [slope_load] + weight_loads:
            one.start()

        keep = lanes_below((TILE, PAIR), HEAD)
        def head_grads(here):
            result = contract(low_resid[here, :], weight_out[pl.ds(0, mine), :], 1, 1)
            for p in range(pair_count):
                scale = jnp.where(
                    keep, scales[here, 2 * p : 2 * p + 1], scales[here, 2 * p + 1 : 2 * p + 2]
                )
                grad_heads[p, here, :] = (result[:, p * PAIR : (p + 1) * PAIR] * scale).astype(LOW)

        @pl.loop(0, tiles)
        def _(i):
            @pl.when(i > 1)
            def _():
                dz_far(i - 2).wait_recv()

            head_grads(rows_of(lax.rem(core * 2 + i, tiles) * TILE, TILE))

        joined = jnp.concatenate([heads[p] for p in range(pair_count)], 1)
        grad = contract(joined, low_resid[...], 0, 0).astype(LOW)
        kept = jnp.where(core == 0, grad[:, :mine], grad[:, mine:])
        given = jnp.where(core == 0, grad[:, mine:], grad[:, :mine])
        tall = width // COUNT
        for i in range(mine // tall):
            rank = core * (COUNT // 2) + i
            z, a, s = spot_of(rank, core)
            parts["out"][0, z, a, s] = kept[i * tall : (i + 1) * tall]
            _, a, s = spot_of(rank, other)
            stage_out[i // (wide * deep), a, s] = given[i * tall : (i + 1) * tall]
        give_out.start()
        if fused:
            down.turn_at(other * 2 + 1)

        spots = (
            lax.broadcasted_iota(jnp.int32, (TILE, TILE), 0),
            lax.broadcasted_iota(jnp.int32, (TILE, TILE), 1),
        )
        after = jnp.where(spots[0] > spots[1], 1.0, 0.0).astype(LOW)

        def fade_send(t):
            part = pl.ds(t * (t + 1) // 2, t + 1)
            return remote(
                share.at[part],
                share.at[part],
                df_sems.at[0, t],
                df_sems.at[1, t],
                partner,
            )

        def pair_step(step, p):
            slot = lax.rem(step, 2)
            @pl.when(step == 1)
            def _():
                for t in range(tiles):
                    prob_load(t).start()

            @pl.when(step == 2)
            def _():
                for t in range(tiles):
                    prob_load(t).wait()

            for t in reversed(range(tiles)):
                count = (t + 1) * TILE
                span, rows = pl.ds(t * TILE, TILE), pl.ds(0, count)
                grad_tile = grad_heads[p, span, :]
                product = (grad_tile.astype(FULL) * heads[p, span, :].astype(FULL)).T
                query = queries[p, span, :]
                sides_q = jnp.concatenate(
                    [jnp.where(keep, query, LOW(0.0)), jnp.where(keep, LOW(0.0), query)], 0
                )
                sides_g = jnp.concatenate(
                    [jnp.where(keep, grad_tile, LOW(0.0)), jnp.where(keep, LOW(0.0), grad_tile)], 0
                )
                delta = jnp.concatenate(
                    [
                        jnp.sum(product[:HEAD, :], 0, keepdims=True),
                        jnp.sum(product[HEAD:, :], 0, keepdims=True),
                    ],
                    1,
                )
                change = probs[t][slot].astype(FULL) * (
                    contract(values[p, rows, :], sides_g, 1, 1) - delta
                )
                fade = change[:, :TILE] + change[:, TILE:]
                both = change.astype(LOW)
                fades[rows, span] = jnp.where(step == 0, 0.0, fades[rows, span]) + fade

                key_part = contract(both, sides_q, 1, 0)
                value_part = contract(probs[t][slot], sides_g, 1, 0)
                if t == tiles - 1:
                    key_sum[...] = key_part
                    value_sum[...] = value_part
                else:
                    key_sum[rows, :] += key_part
                    value_sum[rows, :] += value_part
                query_part = contract(keys[p, rows, :], both, 0, 0)
                query_part = jnp.concatenate(
                    [query_part[:HEAD, :TILE], query_part[HEAD:, TILE:]], 0
                )
                grad_qkv[p, span, pl.ds(0, PAIR)] = (query_part.T * 0.125).astype(LOW)

                if t == tiles - 1:
                    @pl.when(step == 0)
                    def _():
                        give_out.wait_recv()
                        steps("out start")

                    steps_when(step == 1, "up1 turn")
                    steps_when(step == 2, "attn2 turn", "up1 gather")

        def lead_head():
            @pl.when(core == 0)
            def _():
                carry[...] = jnp.zeros_like(carry)
                for t in reversed(range(tiles)):
                    count = (t + 1) * TILE
                    span, rows = pl.ds(t * TILE, TILE), pl.ds(0, count)
                    part = pl.ds(t * (t + 1) // 2, t + 1)
                    fade_send(t).wait_recv()
                    total = fades[rows, span] + share[part].astype(FULL).reshape(count, TILE)
                    later = contract(total.astype(LOW), after, 1, 0) + carry[rows, :]
                    if t:
                        carry[rows, :] += jnp.sum(total, -1, keepdims=True)
                    slope = slopes[part].astype(FULL).reshape(count, TILE)
                    extra = (-later * slope).astype(LOW)
                    query = jnp.where(keep, queries[0, span, :], LOW(0.0))
                    key_sum[rows, :] += contract(extra, query, 1, 0)
                    whole = contract(keys[0, rows, :], extra, 0, 0).T * 0.125
                    grad_qkv[0, span, pl.ds(0, PAIR)] = (
                        grad_qkv[0, span, pl.ds(0, PAIR)].astype(FULL)
                        + jnp.where(keep, whole, 0.0)
                    ).astype(LOW)

            @pl.when(core == 1)
            def _():
                for t in range(tiles):
                    fade_send(t).wait_send()

        def weights_into(kind, k, right):
            @pl.loop(0, 2)
            def _(m):
                place = pl.ds(pl.multiple_of(m * mine, 128), mine)
                grad = contract(low_in[:, place], right, 0, 0).astype(LOW)
                for i in range(mine // tall):
                    z, a, s = spot_of(m * (mine // tall) + i, core)
                    parts[kind][k, z, a, s] = grad[i * tall : (i + 1) * tall]

            if fused:
                Job(kind, k).start()

        @pl.loop(0, pair_count)
        def _(step):
            p = pair_count - 1 - step
            pair_step(step, p)
            grad_qkv[p, :, pl.ds(2 * PAIR, PAIR)] = value_sum[...].astype(LOW)

            @pl.when(p > 0)
            def _():
                grad_qkv[p, :, pl.ds(PAIR, PAIR)] = key_sum[...].astype(LOW)
                weights_into("attn", p - 1, grad_qkv[p])

            steps_when(step == 0, "up0 gather")


        @pl.when(core == 1)
        def _():
            for t in reversed(range(tiles)):
                count = (t + 1) * TILE
                share[pl.ds(t * (t + 1) // 2, t + 1)] = (
                    fades[pl.ds(0, count), pl.ds(t * TILE, TILE)]
                    .astype(LOW)
                    .reshape(t + 1, TILE, TILE)
                )
                fade_send(t).start()

        keep_all = lanes_below((length, PAIR), HEAD)
        second_head = jnp.where(
            keep_all,
            pltpu.roll(grad_qkv[0, :, pl.ds(0, PAIR)].astype(FULL), HEAD, 1),
            key_sum[...],
        )
        weights_into(
            "early",
            0,
            jnp.concatenate(
                [second_head.astype(LOW), grad_qkv[0, :, pl.ds(2 * PAIR, PAIR)]], 1
            ),
        )
        slope_load.wait()
        steps("down cross", "out turn", "attn2 gather", "attn1 turn", "up0 close")
        lead_head()
        grad_qkv[0, :, pl.ds(PAIR, PAIR)] = key_sum[...].astype(LOW)
        first_head = jnp.where(
            keep_all,
            grad_qkv[0, :, pl.ds(0, PAIR)].astype(FULL),
            pltpu.roll(key_sum[...], HEAD, 1),
        )
        weights_into("lead", 0, first_head.astype(LOW))

        for one in weight_loads:
            one.wait()

        def in_part(here):
            joined = jnp.concatenate([grad_qkv[p, here, :] for p in range(pair_count)], 1)
            return contract(joined, weight_in[...], 1, 1)

        @pl.loop(0, tiles)
        def _(i):
            part = in_part(rows_of(lax.rem(other * 2 + i, tiles) * TILE, TILE))

            @pl.when(i < 2)
            def _():
                stage[tile_rows(i), :] = part.astype(LOW)
                in_back(i).start()

            @pl.when(i >= 2)
            def _():
                fades[tile_rows(i - 2), pl.ds(0, width)] = part

            steps_when(i == 1, "out gather", "early turn", "attn1 gather")
            steps_when(i == 3, "lead turn")

        for i in range(2):
            mid_far(i).wait_send()

        @pl.loop(0, 2)
        def _(i):
            here = tile_rows(i)
            in_back(i).wait_recv()
            grad = fades[here, pl.ds(0, width)] + catch_mid[here, :].astype(FULL)
            unit, inverse = layer_norm(tokens[here, :].astype(FULL))
            vec_sums[0:1, :] += jnp.sum(grad * unit, 0, keepdims=True)
            vec_sums[1:2, :] += jnp.sum(grad, 0, keepdims=True)
            scaled = grad * flat(gain)
            low_mid[here, :] = (
                grad_resid[here, :]
                + inverse
                * (
                    scaled
                    - jnp.mean(scaled, -1, keepdims=True)
                    - unit * jnp.mean(scaled * unit, -1, keepdims=True)
                )
            ).astype(LOW)

        in_put.start()
        for i in range(2):
            in_back(i).wait_send()

    pl.run_scoped(
        attention,
        pltpu.VMEM((tiles * (tiles + 1) // 2, TILE, TILE), LOW),
        pltpu.VMEM((length, length), FULL),
        pltpu.VMEM((length, PAIR), FULL),
        pltpu.VMEM((length, PAIR), FULL),
        pltpu.VMEM((length, 1), FULL),
        pltpu.VMEM((pair_count, length, mine), LOW),
        pltpu.VMEM((width, 3 * mine), LOW),
    )

    if not fused:
        for kind in KINDS[:-1]:
            one = pltpu.make_async_copy(parts[kind], results[kind], load_sems.at[0])
            one.start()
            one.wait()
        one = pltpu.make_async_copy(vec_sums, results["vec"], load_sems.at[0])
        one.start()
        one.wait()
    else:
        sums = vec_sums[...]
        tall = width // COUNT
        for rank in range(COUNT):
            z, a, s = spot_of(rank, core)
            shifted = pltpu.roll(sums, width - rank * tall, 1) if rank else sums
            parts["vec"][0, z, a, s] = shifted[:, :128]
    steps("vec start", "early gather", "down close")

    def out_part(here):
        return contract(hidden_low[0, here, :], weight_down[0], 1, 0) + contract(
            hidden_low[1, here, :], weight_down[1], 1, 0
        )

    @pl.loop(0, tiles)
    def _(i):
        part = out_part(rows_of(lax.rem(other * 2 + i, tiles) * TILE, TILE))

        @pl.when(i < 2)
        def _():
            stage[tile_rows(i), :] = part.astype(LOW)
            out_back(i).start()

        @pl.when(i >= 2)
        def _():
            resid[tile_rows(i - 2), :] += part

        steps_when(i == 0, "lead gather", "up1 close", "attn2 close")
        steps_when(i == 1, "out close")
        steps_when(i == 2, "vec gather")
        steps_when(i == 3, "attn1 close")

    steps("down store", "up0 store", "up1 store")

    @pl.loop(0, 2)
    def _(i):
        here = tile_rows(i)
        out_back(i).wait_recv()
        low_mid[rows_of(half + i * TILE, TILE), :] = (
            resid[here, :] + catch_out[here, :].astype(FULL)
        ).astype(LOW)

    out_put.start()
    steps("early close", "lead close", "vec close")
    steps("out store", "attn2 store", "attn1 store", "early store", "vec store", "lead store")
    if fused:
        for job in jobs.values():
            job.drain()
    in_put.wait()
    out_put.wait()
    g_far.wait_send()
    give_out.wait_send()
    for i in range(2):
        for one in (dz_far, out_back):
            one(i).wait_send()
    for p in range(pair_count):
        send_heads(p).wait_send()


def layer(fused, tokens, seg, cotangent, gain_in, shift_in, gain_mid, shift_mid, weights):
    half, width = tokens.shape
    length, mine = 2 * half, width // 2
    hidden = weights[-1].shape[0]
    pairs, tiles = mine // PAIR, length // TILE
    shapes = block_shapes(width, hidden)
    long, wide, deep = GRID
    anywhere = pl.BlockSpec(memory_space=pl.ANY)
    local = pl.BlockSpec(memory_space=pltpu.VMEM)
    outs = [jax.ShapeDtypeStruct((half, width), LOW)] * 2
    out_specs = [anywhere] * 2
    for kind in KINDS:
        shape, kept = shapes[kind]
        if fused:
            outs.append(jax.ShapeDtypeStruct((FAN[kind], 2) + shape, kept))
            out_specs.append(anywhere)
        elif kind == "vec":
            outs.append(jax.ShapeDtypeStruct((8, width), FULL))
            out_specs.append(anywhere)
        else:
            outs.append(jax.ShapeDtypeStruct((FAN[kind],) + GRID + shape, kept))
            out_specs.append(anywhere)
    spans = [(t + 1) * TILE for t in range(tiles)]
    outs += [jax.ShapeDtypeStruct((span, 2 * TILE), LOW) for span in spans]
    outs.append(jax.ShapeDtypeStruct((tiles * (tiles + 1) // 2, TILE, TILE), LOW))
    outs.append(jax.ShapeDtypeStruct((8, half), FULL))
    out_specs += [anywhere] * (tiles + 1) + [local]
    scratch = [
        pltpu.VMEM((length, width), LOW),
        pltpu.VMEM((width, width), LOW),
        pltpu.VMEM((pairs, length, PAIR), LOW),
        pltpu.VMEM((pairs, half, PAIR), LOW),
        pltpu.VMEM((half, width), FULL),
        pltpu.VMEM((length, width), LOW),
        pltpu.VMEM((half, width), FULL),
        pltpu.VMEM((length, width), LOW),
        pltpu.VMEM((pairs, length, PAIR), LOW),
        pltpu.VMEM((length, width), LOW),
        pltpu.VMEM((pairs, length, PAIR), LOW),
        pltpu.VMEM((pairs, length, PAIR), LOW),
        pltpu.VMEM((pairs, length, PAIR), LOW),
        pltpu.VMEM((length, 128), FULL),
        pltpu.VMEM((half, width), LOW),
    ]
    scratch += [pltpu.VMEM((2, (t + 1) * TILE, 2 * TILE), LOW) for t in range(tiles)]
    corners = tiles * (tiles + 1) // 2
    scratch += [pltpu.VMEM((corners, TILE, TILE), LOW)]
    scratch += [pltpu.VMEM((half, width), LOW)] * 3
    block = hidden // 4
    scratch += [pltpu.VMEM((2, block, width), LOW), pltpu.VMEM((2, length, block), LOW)]
    scratch += [
        pltpu.VMEM((2, wide, deep) + shapes["out"][0], LOW),
        pltpu.VMEM((8, width), FULL),
    ]
    scratch += [pltpu.VMEM((FAN[kind],) + GRID + shapes[kind][0], shapes[kind][1]) for kind in KINDS]
    dma = pltpu.SemaphoreType.DMA
    if fused:
        leads = {kind: ((long, deep), (long,), (long - 1,), ()) for kind in KINDS}
        leads["down"] = ((long, deep), (long - 1, deep), (), ())
        leads["vec"] = ((3, long), (), (long - 1,), ())
        for step in range(4):
            scratch += [
                pltpu.VMEM((FAN[kind],) + leads[kind][step] + shapes[kind][0], shapes[kind][1])
                for kind in KINDS
            ]
        scratch += [dma((long,))] * 2 + [dma((long - 1,))] * 2 + [dma((1,))] * 4
        for kind in KINDS[1:]:
            fan = FAN[kind]
            count = 3 if kind == "vec" else fan
            scratch += [dma((count,))] * 4 + [dma((fan, long - 1))] * 2 + [dma((fan,))] * 2
        scratch += [dma((FAN[kind], 2)) for kind in KINDS]
    scratch += [dma((17 + 3 * pairs,)), dma((2,))]
    scratch += [dma((2, 2))] * 6
    scratch += [dma((2,)), dma((2, tiles)), dma((tiles, 2))]
    scratch += [dma((2,)), dma((2, pairs)), dma((7,))]
    return pl.pallas_call(
        functools.partial(layer_kernel, fused),
        out_shape=outs,
        in_specs=[anywhere, local, anywhere] + [local] * 4 + [anywhere] * 6,
        out_specs=out_specs,
        scratch_shapes=scratch,
        compiler_params=pltpu.CompilerParams(
            collective_id=0, has_side_effects=True, vmem_limit_bytes=VMEM_LIMIT
        ),
        name="layer",
    )(tokens, seg, cotangent, gain_in, shift_in, gain_mid, shift_mid, *weights)


def deliver_kernel(count, *refs):
    refs, (load_sems, put_sems) = refs[:-2], refs[-2:]
    targets = refs[count : (len(refs) - 2 * count + 2) // 2 + count]
    sources, held = refs[:count], refs[count + len(targets) : 2 * count + len(targets)]
    made = refs[2 * count + len(targets) :]
    loads = [
        pltpu.make_async_copy(source, target, load_sems.at[i])
        for i, (source, target) in enumerate(zip(sources, held))
    ]
    for one in loads[2:] + loads[:2]:
        one.start()
    puts = [
        pltpu.make_async_copy(source, target, put_sems.at[i])
        for i, (source, target) in enumerate(zip(held[:2] + made, targets))
    ]
    for one in loads[2:]:
        one.wait()
    share_in, down, up, out, attn, early, lead, vec = held[2:]
    share, g_query, g_key, g_value, g_out, g_up, g_down, *g_vecs = made
    tall, mine = out.shape[2:]
    for k in range(2):
        for b in range(2):
            g_up[:, (2 * k + b) * 2 * mine : (2 * k + b + 1) * 2 * mine] = up[b, k].astype(FULL)
    puts[7].start()
    for k in range(2):
        g_down[:, k * mine : (k + 1) * mine] = down[0, k].astype(FULL)
    puts[8].start()
    for i in range(2):
        loads[i].wait()
        puts[i].start()
    for k in range(2):
        start = k * mine
        g_out[:, start : start + mine] = out[0, k].astype(FULL)
        for p in range(attn.shape[0]):
            for place, target in enumerate((g_query, g_key, g_value)):
                target[:, start + (p + 1) * PAIR : start + (p + 2) * PAIR] = attn[
                    p, k, :, place * PAIR : (place + 1) * PAIR
                ].astype(FULL)
        ones, twos = lead[0, k].astype(FULL), early[0, k].astype(FULL)
        keep = lanes_below(ones.shape, HEAD)
        seconds = twos[:, :PAIR]
        g_query[:, start : start + PAIR] = jnp.where(keep, ones, pltpu.roll(seconds, HEAD, 1))
        g_key[:, start : start + PAIR] = jnp.where(keep, pltpu.roll(ones, HEAD, 1), seconds)
        g_value[:, start : start + PAIR] = twos[:, PAIR:]
    share[...] = share_in[0:1, :]
    sums = vec[0, 0] + vec[0, 1]
    for i, target in enumerate(g_vecs):
        target[...] = sums[i, :tall]
    for one in puts[2:7] + puts[9:]:
        one.start()
    for one in puts:
        one.wait()


def deliver(*arrays):
    output, _, shares, down, up, out = arrays[:6]
    tall, mine = out.shape[2:]
    width = 2 * mine
    shapes = [(1, shares.shape[1])] + [(tall, width)] * 4
    shapes += [(tall, 2 * up.shape[3] * 2), (down.shape[2], width)] + [(tall,)] * 4
    anywhere = pl.BlockSpec(memory_space=pl.ANY)
    return pl.pallas_call(
        functools.partial(deliver_kernel, len(arrays)),
        out_shape=[jax.ShapeDtypeStruct(output.shape, output.dtype)] * 2
        + [jax.ShapeDtypeStruct(shape, FULL) for shape in shapes],
        in_specs=[anywhere] * len(arrays),
        out_specs=[anywhere] * (2 + len(shapes)),
        scratch_shapes=[pltpu.VMEM(one.shape, one.dtype) for one in arrays]
        + [pltpu.VMEM(shape, FULL) for shape in shapes]
        + [pltpu.SemaphoreType.DMA((len(arrays),)), pltpu.SemaphoreType.DMA((2 + len(shapes),))],
        compiler_params=pltpu.CompilerParams(vmem_limit_bytes=VMEM_LIMIT),
        name="deliver",
    )(*arrays)


def reduce_plain(parts, rows):
    down, up, out, attn, early, lead, vec = parts
    width = vec.shape[1]

    def scattered(part):
        summed = lax.psum_scatter(part.astype(FULL), "rows", scatter_dimension=0, tiled=True)
        return summed.astype(LOW)

    def joined(part):
        return lax.all_gather(part, "keys", axis=1, tiled=True).astype(FULL)

    def flat_part(part):
        return part.reshape(-1, part.shape[-1])

    ones, twos = scattered(flat_part(lead[0])), scattered(flat_part(early[0]))
    first = [
        jnp.concatenate([ones[:, :HEAD], twos[:, :HEAD]], 1),
        jnp.concatenate([ones[:, HEAD:], twos[:, HEAD:PAIR]], 1),
        twos[:, PAIR:],
    ]
    rest = [scattered(flat_part(attn[p])) for p in range(attn.shape[0])]
    halves = [
        jnp.concatenate([first[i]] + [one[:, i * PAIR : (i + 1) * PAIR] for one in rest], 1)
        for i in range(3)
    ]
    halves.append(scattered(flat_part(out[0])))
    halves.append(jnp.concatenate([scattered(flat_part(up[b])) for b in range(2)], 1))
    halves.append(scattered(flat_part(down[0])))
    sums = lax.psum_scatter(
        lax.psum(vec[:4].T, "keys"), "rows", scatter_dimension=0, tiled=True
    )
    return [joined(one) for one in halves], [sums[:, i] for i in range(4)]


def body(
    rows,
    tokens,
    seg_ids,
    doc_starts,
    gain_in,
    shift_in,
    w_query,
    w_key,
    w_value,
    w_out,
    gain_mid,
    shift_mid,
    w_up,
    w_down,
    out_grad,
):
    fused = rows == COUNT
    own_tokens, own_grad = tokens[0], out_grad[0]
    output, input_grad, *parts = layer(
        fused,
        own_tokens,
        seg_ids,
        own_grad,
        gain_in,
        shift_in,
        gain_mid,
        shift_mid,
        (w_query, w_key, w_value, w_out, w_up, w_down),
    )
    parts, shares = parts[: len(KINDS)], parts[-1]
    if fused:
        output, input_grad, shares, *grads = deliver(output, input_grad, shares, *parts)
        grads, vectors = grads[:6], grads[6:]
    else:
        grads, vectors = reduce_plain(parts, rows)
    g_query, g_key, g_value, g_out, g_up, g_down = grads
    return (
        output[None],
        input_grad[None],
        shares[:1],
        vectors[0],
        vectors[1],
        g_query,
        g_key,
        g_value,
        g_out,
        vectors[2],
        vectors[3],
        g_up,
        g_down,
    )


def solution(mesh):
    in_specs = (
        P("rows", "keys", None),
        P("rows", None),
        P("rows", "keys"),
        P(),
        P(),
        P(),
        P(),
        P(),
        P(),
        P(),
        P(),
        P(),
        P(),
        P("rows", "keys", None),
    )
    out_specs = (
        P("rows", "keys", None),
        P("rows", "keys", None),
        P("rows", "keys"),
        P("rows"),
        P("rows"),
        P("rows", None),
        P("rows", None),
        P("rows", None),
        P("rows", None),
        P("rows"),
        P("rows"),
        P("rows", None),
        P("rows", None),
    )
    return jax.shard_map(
        functools.partial(body, mesh.shape["rows"]),
        mesh=mesh,
        in_specs=in_specs,
        out_specs=out_specs,
        check_vma=False,
    )
```

```python
import functools

import jax
import jax.numpy as jnp
from jax import lax
from jax.experimental import pallas as pl
from jax.experimental.pallas import tpu as pltpu
from jax.sharding import PartitionSpec as P

HEAD = 64
PAIR = 2 * HEAD
TILE = 256
EPS = 1e-05
MASKED = 1e30
SELECT_SHIFT = 4.0
LOW = jnp.bfloat16
FULL = jnp.float32
MESH = pl.DeviceIdType.MESH
VMEM_LIMIT = 67_000_000


def contract(left, right, left_dim, right_dim):
    return lax.dot_general(
        left, right, (((left_dim,), (right_dim,)), ((), ())), preferred_element_type=FULL
    )


def layer_norm(field):
    center = field - jnp.mean(field, -1, keepdims=True)
    inverse = lax.rsqrt(jnp.mean(center * center, -1, keepdims=True) + EPS)
    return center * inverse, inverse


def remote(source, target, send, recv, device):
    return pltpu.make_async_remote_copy(
        src_ref=source,
        dst_ref=target,
        send_sem=send,
        recv_sem=recv,
        device_id=device,
        device_id_type=MESH,
    )


def lanes_below(shape, bound):
    return lax.broadcasted_iota(jnp.int32, shape, len(shape) - 1) < bound


def flat(ref):
    return ref[...].reshape(1, ref.shape[0])


def corner(step, tiles):
    t = sum((step >= n * (n + 1) // 2).astype(jnp.int32) for n in range(1, tiles))
    return t, step - t * (t + 1) // 2


def rows_of(start, size):
    return pl.ds(pl.multiple_of(start, size), size)


def gelu_parts(field):
    scale = 0.7978845608028654
    square = field * field
    inner = jnp.tanh(scale * field * (1.0 + 0.044715 * square))
    half_sum = 0.5 * (1.0 + inner)
    slope = half_sum + 0.5 * field * (1.0 - inner * inner) * (
        scale * (1.0 + 3.0 * 0.044715 * square)
    )
    return field * half_sum, slope


GRID = (4, 2, 2)
COUNT = GRID[0] * GRID[1] * GRID[2]
KINDS = ("down", "up", "out", "attn", "early", "lead", "vec")
FAN = {"down": 1, "up": 2, "out": 1, "attn": 2, "early": 1, "lead": 1, "vec": 1}


def block_shapes(width, hidden):
    mine = width // 2
    tall = width // COUNT
    return {
        "down": ((hidden // COUNT, mine), LOW),
        "up": ((tall, mine * 2), LOW),
        "out": ((tall, mine), LOW),
        "attn": ((tall, mine), LOW),
        "early": ((tall, 2 * PAIR), LOW),
        "lead": ((tall, PAIR), LOW),
        "vec": ((8, 128), FULL),
    }


def layer_kernel(fused, *refs):
    refs = list(refs)

    def take(count):
        taken = refs[:count]
        del refs[:count]
        return taken if count > 1 else taken[0]

    tokens_hbm, seg, cotangent, gain, shift, gain_mid, shift_mid = take(7)
    w_query, w_key, w_value, w_out, w_up, w_down = take(6)
    output, input_grad = take(2)
    results = dict(zip(KINDS, take(len(KINDS))))
    prob_hbm, slope_hbm, share_out = take(4), take(1), take(1)
    (
        grads_all,
        weight_out,
        heads,
        heads_far,
        resid,
        low_mid,
        grad_resid,
        low_resid,
        low_in,
        queries,
        keys,
        values,
        scales,
        tokens,
    ) = take(14)
    probs = take(4)
    share = take(1)
    stage, catch_mid, catch_out = take(3)
    weight_down, hidden_low = take(2)
    vec_sums = take(1)
    parts = dict(zip(KINDS, take(len(KINDS))))
    if fused:
        got1 = dict(zip(KINDS, take(len(KINDS))))
        got2 = dict(zip(KINDS, take(len(KINDS))))
        got3 = dict(zip(KINDS, take(len(KINDS))))
        pair = dict(zip(KINDS, take(len(KINDS))))
        sems = {
            name: take(2) for name in ("down1", "down2", "down3", "down4")
        }
        for kind in KINDS[1:]:
            for stage_name in "1234":
                sems[kind + stage_name] = take(2)
        for kind in KINDS:
            sems[kind + "5"] = take(1)
    (load_sems, g_sems, mid_sems, dz_sems, a_sems, b_sems, c_sems, pd_sems, po_sems, df_sems, prob_sems) = take(11)
    far_sems, head_sems, weight_sems = take(3)

    long, wide, deep = GRID
    core = lax.axis_index("keys")
    row = lax.axis_index("rows")
    other = 1 - core
    partner = (row, other)
    half, width = tokens.shape
    length, mine = 2 * half, width // 2
    pair_count = mine // PAIR
    tiles = length // TILE
    hidden = w_down.shape[0]
    block = hidden // 4
    own_start, far_start = core * half, other * half

    if fused:
        slow, mid, fast = row // (wide * deep), (row // deep) % wide, row % deep
    else:
        slow, mid, fast = 0, 0, 0

    def spot_of(rank, whose):
        z, y, x = rank // (wide * deep), (rank // deep) % wide, rank % deep
        if not fused:
            return z, y, x
        return z, x + whose * (y - x), y + whose * (x - y)

    first, second = fast + core * (mid - fast), mid + core * (fast - mid)
    near, next_ = 1 - first, 1 - second

    def rank_of(z, a, b):
        y, x = b + core * (a - b), a + core * (b - a)
        return (z * wide + y) * deep + x

    near_device = (rank_of(slow, near, second), core)
    next_device = (rank_of(slow, first, next_), core)
    far_places = [lax.rem(slow + step, long) for step in range(1, long)]

    def add_into(target, index, terms):
        total = target[index].astype(FULL)
        for term in terms:
            total = total + term.astype(FULL)
        target[index] = total.astype(target.dtype)

    class Job:
        def __init__(self, kind, k):
            self.kind, self.k = kind, k

        def first_copy(self):
            kind, k = self.kind, self.k
            part, got = parts[kind].at[k], got1[kind].at[k]
            send, recv = sems[kind + "1"]
            return remote(part.at[:, near], got, send.at[k], recv.at[k], near_device)

        def second_copy(self):
            kind, k = self.kind, self.k
            part, got = parts[kind].at[k], got2[kind].at[k]
            send, recv = sems[kind + "2"]
            return remote(part.at[:, first, next_], got, send.at[k], recv.at[k], next_device)

        def third_copies(self):
            kind, k = self.kind, self.k
            send, recv = sems[kind + "3"]
            return [
                remote(
                    parts[kind].at[k, z, first, second],
                    got3[kind].at[k, step],
                    send.at[k, step],
                    recv.at[k, step],
                    (rank_of(z, first, second), core),
                )
                for step, z in enumerate(far_places)
            ]

        def last_copy(self):
            kind, k = self.kind, self.k
            send, recv = sems[kind + "4"]
            return remote(
                parts[kind].at[k, slow, first, second],
                pair[kind].at[k],
                send.at[k],
                recv.at[k],
                partner,
            )

        def start(self):
            self.first_copy().start()

        def turn(self):
            self.first_copy().wait_recv()
            kind, k = self.kind, self.k

            @pl.loop(0, long * deep)
            def _(step):
                z, b = step // deep, lax.rem(step, deep)
                add_into(parts[kind], (k, z, first, b), [got1[kind][k, z, b]])

            self.second_copy().start()

        def gather(self):
            self.second_copy().wait_recv()
            kind, k = self.kind, self.k

            @pl.loop(0, long)
            def _(z):
                add_into(parts[kind], (k, z, first, second), [got2[kind][k, z]])

            for one in self.third_copies():
                one.start()

        def close(self):
            for one in self.third_copies():
                one.wait_recv()
            kind, k = self.kind, self.k
            add_into(
                parts[kind],
                (k, slow, first, second),
                [got3[kind][k, step] for step in range(long - 1)],
            )
            self.last_copy().start()

        def puts(self):
            kind, k = self.kind, self.k
            own_part = parts[kind].at[k, slow, first, second]
            sem = sems[kind + "5"]
            return [
                pltpu.make_async_copy(own_part, results[kind].at[k, core], sem.at[k, 0]),
                pltpu.make_async_copy(pair[kind].at[k], results[kind].at[k, other], sem.at[k, 1]),
            ]

        def store(self):
            self.last_copy().wait_recv()
            for one in self.puts():
                one.start()

        def drain(self):
            self.first_copy().wait_send()
            self.second_copy().wait_send()
            for one in self.third_copies():
                one.wait_send()
            self.last_copy().wait_send()
            for one in self.puts():
                one.wait()

    class Down(Job):
        def near_copy(self, z, s):
            send, recv = sems["down1"]
            return remote(
                parts["down"].at[0, z, near, s],
                got1["down"].at[0, z, s],
                send.at[z, s],
                recv.at[z, s],
                near_device,
            )

        def slow_copy(self, step):
            z = lax.rem(slow + step, long)
            send, recv = sems["down2"]
            return remote(
                parts["down"].at[0, z, first],
                got2["down"].at[0, step - 1],
                send.at[step - 1],
                recv.at[step - 1],
                (rank_of(z, first, second), core),
            )

        def next_copy(self):
            send, recv = sems["down3"]
            return remote(
                parts["down"].at[0, slow, first, next_],
                got3["down"].at[0],
                send.at[0],
                recv.at[0],
                next_device,
            )

        def start_at(self, z):
            for s in range(deep):
                self.near_copy(z, s).start()

        def start_part(self, z, m):
            @pl.when(core == 0)
            def _():
                self.near_copy(z, m).start()

            @pl.when((core == 1) & (m == near))
            def _():
                self.start_at(z)

        def turn_at(self, z):
            for s in range(deep):
                self.near_copy(z, s).wait_recv()

            @pl.loop(0, deep)
            def _(b):
                add_into(parts["down"], (0, z, first, b), [got1["down"][0, z, b]])

            step = lax.rem(z - slow + long, long)

            @pl.when(step > 0)
            def _():
                self.slow_copy(step).start()

        def cross(self):
            for step in range(1, long):
                self.slow_copy(step).wait_recv()

            @pl.loop(0, deep)
            def _(b):
                add_into(
                    parts["down"],
                    (0, slow, first, b),
                    [got2["down"][0, step, b] for step in range(long - 1)],
                )

            self.next_copy().start()

        def close(self):
            self.next_copy().wait_recv()
            add_into(parts["down"], (0, slow, first, second), [got3["down"][0]])
            self.last_copy().start()

        def drain(self):
            for z in range(long):
                for s in range(deep):
                    self.near_copy(z, s).wait_send()
            for step in range(1, long):
                self.slow_copy(step).wait_send()
            self.next_copy().wait_send()
            self.last_copy().wait_send()
            for one in self.puts():
                one.wait()

    class Vectors(Job):
        def first_copies(self):
            send, recv = sems["vec1"]
            places = ((near, second), (first, next_), (near, next_))
            return [
                remote(
                    parts["vec"].at[0, :, a, b],
                    got1["vec"].at[0, i],
                    send.at[i],
                    recv.at[i],
                    (rank_of(slow, a, b), core),
                )
                for i, (a, b) in enumerate(places)
            ]

        def start(self):
            for one in self.first_copies():
                one.start()

        def gather(self):
            for one in self.first_copies():
                one.wait_recv()

            @pl.loop(0, long)
            def _(z):
                add_into(
                    parts["vec"], (0, z, first, second), [got1["vec"][0, i, z] for i in range(3)]
                )

            for one in self.third_copies():
                one.start()

        def drain(self):
            for one in self.first_copies() + self.third_copies():
                one.wait_send()
            self.last_copy().wait_send()
            for one in self.puts():
                one.wait()

    def steps(*names):
        if fused:
            for name in names:
                job, step = name.split()
                getattr(jobs[job], step)()

    def steps_when(condition, *names):
        if fused:
            pl.when(condition)(lambda: steps(*names))

    down = Down("down", 0)
    jobs = {"down": down, "vec": Vectors("vec", 0)}
    jobs |= {kind: Job(kind, 0) for kind in ("out", "early", "lead")}
    jobs |= {f"up{k}": Job("up", k) for k in range(2)}
    jobs |= {f"attn{k + 1}": Job("attn", k) for k in range(pair_count - 1)}

    def local(source, target, index):
        return pltpu.make_async_copy(source, target, load_sems.at[index])

    own = rows_of(own_start, half)
    in_put = local(low_mid.at[pl.ds(0, half)], input_grad, 0)
    out_put = local(low_mid.at[pl.ds(half, half)], output, 1)
    g_load = local(cotangent, grads_all.at[own], 0)
    out_loads = [
        local(tokens_hbm, tokens, 15),
        local(w_out.at[rows_of(core * mine, mine)], weight_out.at[pl.ds(0, mine)], 1),
        local(w_out.at[rows_of(other * mine, mine)], weight_out.at[pl.ds(mine, mine)], 2),
    ]
    down_loads = [
        local(w_down.at[rows_of((core * 2 + b) * block, block)], weight_down.at[b], 11 + b)
        for b in range(2)
    ]

    peers = [partner]
    if fused:
        peers += [near_device, next_device, (rank_of(slow, near, next_), core)]
        peers += [(rank_of(z, first, second), core) for z in far_places]
    barrier = pltpu.get_barrier_semaphore()
    for peer in peers:
        pl.semaphore_signal(barrier, inc=1, device_id=peer, device_id_type=MESH)

    exchange = remote(tokens_hbm, low_resid.at[own], far_sems.at[0], far_sems.at[1], partner)

    def send_heads(p):
        return remote(
            heads.at[p, rows_of(far_start, half)],
            heads_far.at[p],
            head_sems.at[0, p],
            head_sems.at[1, p],
            partner,
        )

    def prob_put(t):
        return pltpu.make_async_copy(probs[t].at[0], prob_hbm[t], prob_sems.at[t, 0])

    def prob_load(t):
        return pltpu.make_async_copy(prob_hbm[t], probs[t].at[0], prob_sems.at[t, 1])

    def own_rows(i):
        return rows_of(own_start + i * TILE, TILE)

    def far_rows(i):
        return rows_of(far_start + i * TILE, TILE)

    def tile_rows(i):
        return rows_of(i * TILE, TILE)

    def to_partner(source, target, pair_sems):
        def one(i):
            return remote(
                source(i), target(i), pair_sems.at[0, i], pair_sems.at[1, i], partner
            )

        return one

    g_far = remote(cotangent, grads_all.at[own], g_sems.at[0], g_sems.at[1], partner)
    mid_far = to_partner(
        lambda i: low_mid.at[own_rows(i)], lambda i: low_mid.at[own_rows(i)], mid_sems
    )
    dz_far = to_partner(
        lambda i: low_resid.at[own_rows(i)], lambda i: low_resid.at[own_rows(i)], dz_sems
    )
    mid_back = to_partner(
        lambda i: stage.at[tile_rows(i)], lambda i: catch_mid.at[tile_rows(i)], a_sems
    )
    in_back = to_partner(
        lambda i: stage.at[tile_rows(i)], lambda i: catch_mid.at[tile_rows(i)], b_sems
    )
    out_back = to_partner(
        lambda i: stage.at[tile_rows(i)], lambda i: catch_out.at[tile_rows(i)], c_sems
    )

    def forward(
        weights,
        lead_query,
        lead_key,
        slopes,
        penalty,
        scale_rows,
        seg_cols,
        free_cols,
        sums,
    ):
        def column(rows, i):
            return (rows, pl.ds(i, 1))

        columns = pl.ds(pl.multiple_of(core * mine, 128), mine)
        loads = []
        for place, source in enumerate((w_query, w_key, w_value)):
            loads.append((source.at[:, columns], weights.at[:, pl.ds(place * mine, mine)]))
        for place, source in enumerate((w_query, w_key)):
            loads.append(
                (source.at[:, pl.ds(0, PAIR)], weights.at[:, pl.ds(3 * mine + place * PAIR, PAIR)])
            )
        loads = [
            pltpu.make_async_copy(source, target, weight_sems.at[i])
            for i, (source, target) in enumerate(loads)
        ]
        own_load = pltpu.make_async_copy(tokens_hbm, low_resid.at[own], weight_sems.at[5])
        own_load.start()
        for one in loads:
            one.start()

        pl.semaphore_wait(barrier, len(peers))
        exchange.start()
        g_far.start()
        for one in out_loads + [g_load] + down_loads:
            one.start()

        own_load.wait()

        keep = lanes_below((TILE, PAIR), HEAD)
        keep_half = lanes_below((half, PAIR), HEAD)

        def normalize(whose):
            here = rows_of(whose * half, half)
            unit, _ = layer_norm(low_resid[here, :].astype(FULL))
            low_in[here, :] = (unit * flat(gain) + flat(shift)).astype(LOW)

        def project(whose):
            here = rows_of(whose * half, half)
            result = contract(low_in[here, :], weights[...], 1, 0).astype(LOW)
            for p in range(pair_count):
                queries[p, here, :] = result[:, p * PAIR : (p + 1) * PAIR] * LOW(0.125)
                keys[p, here, :] = result[:, mine + p * PAIR : mine + (p + 1) * PAIR]
                values[p, here, :] = result[:, 2 * mine + p * PAIR : 2 * mine + (p + 1) * PAIR]
            first = result[:, 3 * mine : 3 * mine + PAIR]
            lead_query[here, :] = jnp.where(keep_half, first, LOW(0.0)) * LOW(0.125)
            lead_key[here, :] = result[:, 3 * mine + PAIR :]

        spots = (
            lax.broadcasted_iota(jnp.int32, (2 * TILE, 2 * TILE), 0),
            lax.broadcasted_iota(jnp.int32, (2 * TILE, 2 * TILE), 1),
        )
        earlier = jnp.where(spots[0] < spots[1], 1.0, 0.0).astype(LOW)
        scale_rows[...] = jnp.zeros_like(scale_rows)
        sums[...] = jnp.zeros_like(sums)

        def select_block(wide, k, diagonal=False):
            rows, span = rows_of(k * 2 * TILE, 2 * TILE), rows_of(wide * 2 * TILE, 2 * TILE)
            scores = contract(lead_key[rows, :], lead_query[span, :], 1, 1)
            repeat = 2 * TILE // 128
            same = jnp.concatenate([seg_cols[rows, :]] * repeat, 1) == seg[:, span].astype(FULL)
            ahead = spots[1] - spots[0] + (wide - k) * 2 * TILE
            later = same & (ahead > 0)
            allowed = same & (ahead >= 0)
            select = jnp.where(later, jnp.concatenate([free_cols[rows, :]] * repeat, 1), 0.0)
            level = scores - SELECT_SHIFT
            chosen = select * (jnp.maximum(level, 0.0) + jnp.log(1.0 + jnp.exp(-jnp.abs(level))))
            slope = (select * (0.5 + 0.5 * jnp.tanh(0.5 * level))).astype(LOW)

            slopes[wide * (2 * wide + 1) + 2 * k] = slope[:TILE, :TILE]

            if not diagonal:

                @pl.when(k < wide)
                def _():
                    slopes[wide * (2 * wide + 1) + 2 * k + 1] = slope[TILE:, :TILE]

            slopes[(2 * wide + 1) * (wide + 1) + 2 * k] = slope[:TILE, TILE:]
            slopes[(2 * wide + 1) * (wide + 1) + 2 * k + 1] = slope[TILE:, TILE:]
            high = chosen.astype(LOW)
            rest = (chosen - high.astype(FULL)).astype(LOW)
            total = (
                sums[column(rows, 0)] + contract(high, earlier, 1, 0) + contract(rest, earlier, 1, 0)
            )
            penalty[rows, span] = jnp.where(allowed, total, MASKED)
            sums[column(rows, 0)] += jnp.sum(chosen, -1, keepdims=True)
            ratio = jnp.where(later, 0.5 + 0.5 * jnp.tanh(0.5 * total - 1.0), 0.0)
            sums[column(rows, 1)] += jnp.sum(ratio, -1, keepdims=True)
            sums[column(rows, 2)] += jnp.sum(jnp.where(later, 1.0, 0.0), -1, keepdims=True)

        normalize(core)
        seg_row = seg[...]
        seg_wide = jnp.broadcast_to(seg_row.astype(FULL), (128, length))
        spot = lax.broadcasted_iota(jnp.int32, (128, length), 1)
        before = pltpu.roll(seg_wide, 1, 1)
        free_wide = jnp.where((spot > 0) & (before == seg_wide), 1.0, 0.0)
        seg_cols[...] = seg_wide.T
        free_cols[...] = free_wide.T
        for one in loads:
            one.wait()
        project(core)
        exchange.wait_recv()
        select_block(core, core, True)
        normalize(other)
        project(other)

        @pl.loop(0, 2)
        def _(step):
            select_block(other + step * core, other * (1 - step))

        slope_put = pltpu.make_async_copy(slopes, slope_hbm, weight_sems.at[6])
        slope_put.start()

        shares = sums[column(own, 1)] / jnp.maximum(sums[column(own, 2)], 1.0)
        share_out[...] = jnp.broadcast_to(shares, (half, 128)).T[0:8, :]

        @pl.loop(0, pair_count)
        def _(p):
            slot = lax.rem(p, 2)

            @pl.when(p == 2)
            def _():
                for t in range(tiles):
                    prob_put(t).wait()

            for t in range(tiles):
                count = (t + 1) * TILE
                span = pl.ds(t * TILE, TILE)
                query = queries[p, span, :]
                both = jnp.concatenate(
                    [jnp.where(keep, query, LOW(0.0)), jnp.where(keep, LOW(0.0), query)], 0
                )
                fine = penalty[pl.ds(0, count), span]
                logits = contract(keys[p, pl.ds(0, count), :], both, 1, 1) - jnp.concatenate(
                    [fine, fine], 1
                )
                scaled = jnp.exp(logits - jnp.max(logits, 0, keepdims=True))
                prob = scaled.astype(LOW)
                probs[t][slot] = prob
                scale = 1.0 / jnp.sum(scaled, 0, keepdims=True)
                scale_rows[pl.ds(2 * p, 1), span] = scale[:, :TILE]
                scale_rows[pl.ds(2 * p + 1, 1), span] = scale[:, TILE:]
                out = contract(values[p, pl.ds(0, count), :], prob, 0, 0) * scale
                out = jnp.concatenate([out[:HEAD, :TILE], out[HEAD:, TILE:]], 0)
                heads[p, span, :] = out.T.astype(LOW)
            @pl.when(p == 0)
            def _():
                for t in range(tiles):
                    prob_put(t).start()

            send_heads(p).start()

        scales[...] = scale_rows[...].T
        slope_put.wait()
        exchange.wait_send()

    def feed_forward(weight_up, grad_up, stage_down):
        def give_down(b):
            return remote(
                stage_down.at[b],
                parts["down"].at[0, core * 2 + b],
                pd_sems.at[0, b],
                pd_sems.at[1, b],
                partner,
            )

        up_loads = [
            local(
                w_up.at[:, pl.ds(pl.multiple_of((core * 2 + b) * block, 128), block)],
                weight_up.at[b],
                9 + b,
            )
            for b in range(2)
        ]
        for one in up_loads:
            one.start()
        for one in out_loads:
            one.wait()
        for p in range(pair_count):
            send_heads(p).wait_recv()

        @pl.loop(0, 2)
        def _(i):
            here, place = tile_rows(i), own_rows(i)
            joined = jnp.concatenate(
                [heads[p, place, :] for p in range(pair_count)]
                + [heads_far[p, here, :] for p in range(pair_count)],
                1,
            )
            field = tokens[here, :].astype(FULL) + contract(joined, weight_out[...], 1, 0)
            resid[here, :] = field
            unit, _ = layer_norm(field)
            low_mid[place, :] = (unit * flat(gain_mid) + flat(shift_mid)).astype(LOW)

            mid_far(i).start()


        for one in up_loads:
            one.wait()

        @pl.loop(0, 2)
        def _(b):
            @pl.loop(0, tiles)
            def _(i):
                @pl.when((b == 0) & (i >= 2))
                def _():
                    mid_far(i - 2).wait_recv()

                here = rows_of(lax.rem(core * 2 + i, tiles) * TILE, TILE)
                value, slope = gelu_parts(contract(low_mid[here, :], weight_up[b], 1, 0))
                hidden_low[b, here, :] = value.astype(LOW)
                grad_up[b, here, :] = slope.astype(LOW)
                if fused:

                    @pl.when((b == 1) & (i == 3))
                    def _():
                        down.turn_at(core * 2)

            @pl.when(b == 0)
            def _():
                for one in [g_load] + down_loads:
                    one.wait()
                g_far.wait_recv()

            tall = hidden // COUNT
            per = mine // tall
            @pl.loop(0, 2)
            def _(turn):
                m = lax.rem(turn + core * near, 2)
                place = pl.ds(pl.multiple_of(m * mine, 128), mine)
                grad = contract(hidden_low[b, :, place], grads_all[...], 0, 0).astype(LOW)
                kept = jnp.where(core == 0, grad[:, :mine], grad[:, mine:])
                given = jnp.where(core == 0, grad[:, mine:], grad[:, :mine])
                for i in range(per):
                    rank = (core * 2 + b) * (COUNT // 4) + m * per + i
                    z, a, s = spot_of(rank, core)
                    parts["down"][0, z, a, s] = kept[i * tall : (i + 1) * tall]
                    _, a, s = spot_of(rank, other)
                    stage_down[b, a, s] = given[i * tall : (i + 1) * tall]
                if fused:
                    down.start_part(core * 2 + b, m)

            give_down(b).start()

            @pl.loop(0, tiles)
            def _(i):
                here = rows_of(i * TILE, TILE)
                back = contract(grads_all[here, :], weight_down[b], 1, 1)
                grad_up[b, here, :] = (back * grad_up[b, here, :].astype(FULL)).astype(LOW)

                @pl.when(i == 3)
                def _():
                    give_down(b).wait_recv()
                    if fused:
                        down.start_at(other * 2 + b)

                if fused:

                    @pl.when((b == 1) & (i == 1))
                    def _():
                        down.turn_at(other * 2)

            @pl.loop(0, 2)
            def _(m):
                tall = width // COUNT
                per = mine // tall
                place = pl.ds(pl.multiple_of(m * mine, 128), mine)
                grad = contract(low_mid[:, place], grad_up[b], 0, 0).astype(LOW)
                for i in range(per):
                    z, a, s = spot_of(m * per + i, core)
                    parts["up"][b, z, a, s] = grad[i * tall : (i + 1) * tall]

            if fused:
                Job("up", b).start()

        def mid_part(here):
            return contract(grad_up[0, here, :], weight_up[0], 1, 1) + contract(
                grad_up[1, here, :], weight_up[1], 1, 1
            )

        @pl.loop(0, tiles)
        def _(i):
            part = mid_part(rows_of(lax.rem(other * 2 + i, tiles) * TILE, TILE))

            @pl.when(i < 2)
            def _():
                stage[tile_rows(i), :] = part.astype(LOW)
                mid_back(i).start()

            @pl.when(i >= 2)
            def _():
                grad_resid[tile_rows(i - 2), :] = part

            steps_when(i == 1, "up0 turn")

        @pl.loop(0, 2)
        def _(i):
            here = tile_rows(i)
            mid_back(i).wait_recv()
            grad = grad_resid[here, :] + catch_mid[here, :].astype(FULL)
            unit, inverse = layer_norm(resid[here, :])
            vec_sums[2:3, :] += jnp.sum(grad * unit, 0, keepdims=True)
            vec_sums[3:4, :] += jnp.sum(grad, 0, keepdims=True)
            scaled = grad * flat(gain_mid)
            total = grads_all[own_rows(i), :].astype(FULL) + inverse * (
                scaled
                - jnp.mean(scaled, -1, keepdims=True)
                - unit * jnp.mean(scaled * unit, -1, keepdims=True)
            )
            grad_resid[here, :] = total
            low_resid[own_rows(i), :] = total.astype(LOW)
            dz_far(i).start()

        for i in range(2):
            mid_back(i).wait_send()
            give_down(i).wait_send()
        if fused:
            down.turn_at(core * 2 + 1)

    vec_sums[...] = jnp.zeros_like(vec_sums)
    pl.run_scoped(
        forward,
        pltpu.VMEM((width, 3 * mine + 2 * PAIR), LOW),
        pltpu.VMEM((length, PAIR), LOW),
        pltpu.VMEM((length, PAIR), LOW),
        pltpu.VMEM((tiles * (tiles + 1) // 2, TILE, TILE), LOW),
        pltpu.VMEM((length, length), FULL),
        pltpu.VMEM((128, length), FULL),
        pltpu.VMEM((length, 128), FULL),
        pltpu.VMEM((length, 128), FULL),
        pltpu.VMEM((length, 128), FULL),
    )
    pl.run_scoped(
        feed_forward,
        pltpu.VMEM((2, width, block), LOW),
        pltpu.VMEM((2, length, block), LOW),
        pltpu.VMEM((2, wide, deep) + block_shapes(width, hidden)["down"][0], LOW),
    )

    def attention(slopes, fades, key_sum, value_sum, carry, grad_qkv, weight_in, grad_heads, stage_out):
        give_out = remote(
            stage_out,
            parts["out"].at[0, pl.ds(core * 2, 2)],
            po_sems.at[0],
            po_sems.at[1],
            partner,
        )

        slope_load = local(slope_hbm, slopes, 13)
        weight_loads = []
        for place, source in enumerate((w_query, w_key, w_value)):
            for p in range(pair_count):
                weight_loads.append(
                    local(
                        source.at[:, pl.ds(pl.multiple_of(core * mine + p * PAIR, 128), PAIR)],
                        weight_in.at[:, pl.ds(p * mine + place * PAIR, PAIR)],
                        17 + place * pair_count + p,
                    )
                )
        for one in [slope_load] + weight_loads:
            one.start()

        keep = lanes_below((TILE, PAIR), HEAD)
        def head_grads(here):
            result = contract(low_resid[here, :], weight_out[pl.ds(0, mine), :], 1, 1)
            for p in range(pair_count):
                scale = jnp.where(
                    keep, scales[here, 2 * p : 2 * p + 1], scales[here, 2 * p + 1 : 2 * p + 2]
                )
                grad_heads[p, here, :] = (result[:, p * PAIR : (p + 1) * PAIR] * scale).astype(LOW)

        @pl.loop(0, tiles)
        def _(i):
            @pl.when(i > 1)
            def _():
                dz_far(i - 2).wait_recv()

            head_grads(rows_of(lax.rem(core * 2 + i, tiles) * TILE, TILE))

        joined = jnp.concatenate([heads[p] for p in range(pair_count)], 1)
        grad = contract(joined, low_resid[...], 0, 0).astype(LOW)
        kept = jnp.where(core == 0, grad[:, :mine], grad[:, mine:])
        given = jnp.where(core == 0, grad[:, mine:], grad[:, :mine])
        tall = width // COUNT
        for i in range(mine // tall):
            rank = core * (COUNT // 2) + i
            z, a, s = spot_of(rank, core)
            parts["out"][0, z, a, s] = kept[i * tall : (i + 1) * tall]
            _, a, s = spot_of(rank, other)
            stage_out[i // (wide * deep), a, s] = given[i * tall : (i + 1) * tall]
        give_out.start()
        if fused:
            down.turn_at(other * 2 + 1)

        spots = (
            lax.broadcasted_iota(jnp.int32, (TILE, TILE), 0),
            lax.broadcasted_iota(jnp.int32, (TILE, TILE), 1),
        )
        after = jnp.where(spots[0] > spots[1], 1.0, 0.0).astype(LOW)

        def fade_send(t):
            part = pl.ds(t * (t + 1) // 2, t + 1)
            return remote(
                share.at[part],
                share.at[part],
                df_sems.at[0, t],
                df_sems.at[1, t],
                partner,
            )

        def pair_step(step, p):
            slot = lax.rem(step, 2)
            @pl.when(step == 1)
            def _():
                for t in range(tiles):
                    prob_load(t).start()

            @pl.when(step == 2)
            def _():
                for t in range(tiles):
                    prob_load(t).wait()

            for t in reversed(range(tiles)):
                count = (t + 1) * TILE
                span, rows = pl.ds(t * TILE, TILE), pl.ds(0, count)
                grad_tile = grad_heads[p, span, :]
                product = (grad_tile.astype(FULL) * heads[p, span, :].astype(FULL)).T
                query = queries[p, span, :]
                sides_q = jnp.concatenate(
                    [jnp.where(keep, query, LOW(0.0)), jnp.where(keep, LOW(0.0), query)], 0
                )
                sides_g = jnp.concatenate(
                    [jnp.where(keep, grad_tile, LOW(0.0)), jnp.where(keep, LOW(0.0), grad_tile)], 0
                )
                delta = jnp.concatenate(
                    [
                        jnp.sum(product[:HEAD, :], 0, keepdims=True),
                        jnp.sum(product[HEAD:, :], 0, keepdims=True),
                    ],
                    1,
                )
                change = probs[t][slot].astype(FULL) * (
                    contract(values[p, rows, :], sides_g, 1, 1) - delta
                )
                fade = change[:, :TILE] + change[:, TILE:]
                both = change.astype(LOW)
                fades[rows, span] = jnp.where(step == 0, 0.0, fades[rows, span]) + fade

                key_part = contract(both, sides_q, 1, 0)
                value_part = contract(probs[t][slot], sides_g, 1, 0)
                if t == tiles - 1:
                    key_sum[...] = key_part
                    value_sum[...] = value_part
                else:
                    key_sum[rows, :] += key_part
                    value_sum[rows, :] += value_part
                query_part = contract(keys[p, rows, :], both, 0, 0)
                query_part = jnp.concatenate(
                    [query_part[:HEAD, :TILE], query_part[HEAD:, TILE:]], 0
                )
                grad_qkv[p, span, pl.ds(0, PAIR)] = (query_part.T * 0.125).astype(LOW)

                if t == tiles - 1:
                    @pl.when(step == 0)
                    def _():
                        give_out.wait_recv()
                        steps("out start")

                    steps_when(step == 1, "up1 turn")
                    steps_when(step == 2, "attn2 turn", "up1 gather")

        def lead_head():
            @pl.when(core == 0)
            def _():
                carry[...] = jnp.zeros_like(carry)
                for t in reversed(range(tiles)):
                    count = (t + 1) * TILE
                    span, rows = pl.ds(t * TILE, TILE), pl.ds(0, count)
                    part = pl.ds(t * (t + 1) // 2, t + 1)
                    fade_send(t).wait_recv()
                    total = fades[rows, span] + share[part].astype(FULL).reshape(count, TILE)
                    later = contract(total.astype(LOW), after, 1, 0) + carry[rows, :]
                    if t:
                        carry[rows, :] += jnp.sum(total, -1, keepdims=True)
                    slope = slopes[part].astype(FULL).reshape(count, TILE)
                    extra = (-later * slope).astype(LOW)
                    query = jnp.where(keep, queries[0, span, :], LOW(0.0))
                    key_sum[rows, :] += contract(extra, query, 1, 0)
                    whole = contract(keys[0, rows, :], extra, 0, 0).T * 0.125
                    grad_qkv[0, span, pl.ds(0, PAIR)] = (
                        grad_qkv[0, span, pl.ds(0, PAIR)].astype(FULL)
                        + jnp.where(keep, whole, 0.0)
                    ).astype(LOW)

            @pl.when(core == 1)
            def _():
                for t in range(tiles):
                    fade_send(t).wait_send()

        def weights_into(kind, k, right):
            @pl.loop(0, 2)
            def _(m):
                place = pl.ds(pl.multiple_of(m * mine, 128), mine)
                grad = contract(low_in[:, place], right, 0, 0).astype(LOW)
                for i in range(mine // tall):
                    z, a, s = spot_of(m * (mine // tall) + i, core)
                    parts[kind][k, z, a, s] = grad[i * tall : (i + 1) * tall]

            if fused:
                Job(kind, k).start()

        @pl.loop(0, pair_count)
        def _(step):
            p = pair_count - 1 - step
            pair_step(step, p)
            grad_qkv[p, :, pl.ds(2 * PAIR, PAIR)] = value_sum[...].astype(LOW)

            @pl.when(p > 0)
            def _():
                grad_qkv[p, :, pl.ds(PAIR, PAIR)] = key_sum[...].astype(LOW)
                weights_into("attn", p - 1, grad_qkv[p])

            steps_when(step == 0, "up0 gather")


        @pl.when(core == 1)
        def _():
            for t in reversed(range(tiles)):
                count = (t + 1) * TILE
                share[pl.ds(t * (t + 1) // 2, t + 1)] = (
                    fades[pl.ds(0, count), pl.ds(t * TILE, TILE)]
                    .astype(LOW)
                    .reshape(t + 1, TILE, TILE)
                )
                fade_send(t).start()

        keep_all = lanes_below((length, PAIR), HEAD)
        second_head = jnp.where(
            keep_all,
            pltpu.roll(grad_qkv[0, :, pl.ds(0, PAIR)].astype(FULL), HEAD, 1),
            key_sum[...],
        )
        weights_into(
            "early",
            0,
            jnp.concatenate(
                [second_head.astype(LOW), grad_qkv[0, :, pl.ds(2 * PAIR, PAIR)]], 1
            ),
        )
        slope_load.wait()
        steps("down cross", "out turn", "attn2 gather", "attn1 turn", "up0 close")
        lead_head()
        grad_qkv[0, :, pl.ds(PAIR, PAIR)] = key_sum[...].astype(LOW)
        first_head = jnp.where(
            keep_all,
            grad_qkv[0, :, pl.ds(0, PAIR)].astype(FULL),
            pltpu.roll(key_sum[...], HEAD, 1),
        )
        weights_into("lead", 0, first_head.astype(LOW))

        for one in weight_loads:
            one.wait()

        def in_part(here):
            joined = jnp.concatenate([grad_qkv[p, here, :] for p in range(pair_count)], 1)
            return contract(joined, weight_in[...], 1, 1)

        @pl.loop(0, tiles)
        def _(i):
            part = in_part(rows_of(lax.rem(other * 2 + i, tiles) * TILE, TILE))

            @pl.when(i < 2)
            def _():
                stage[tile_rows(i), :] = part.astype(LOW)
                in_back(i).start()

            @pl.when(i >= 2)
            def _():
                fades[tile_rows(i - 2), pl.ds(0, width)] = part

            steps_when(i == 1, "out gather", "early turn", "attn1 gather")
            steps_when(i == 3, "lead turn")

        for i in range(2):
            mid_far(i).wait_send()

        @pl.loop(0, 2)
        def _(i):
            here = tile_rows(i)
            in_back(i).wait_recv()
            grad = fades[here, pl.ds(0, width)] + catch_mid[here, :].astype(FULL)
            unit, inverse = layer_norm(tokens[here, :].astype(FULL))
            vec_sums[0:1, :] += jnp.sum(grad * unit, 0, keepdims=True)
            vec_sums[1:2, :] += jnp.sum(grad, 0, keepdims=True)
            scaled = grad * flat(gain)
            low_mid[here, :] = (
                grad_resid[here, :]
                + inverse
                * (
                    scaled
                    - jnp.mean(scaled, -1, keepdims=True)
                    - unit * jnp.mean(scaled * unit, -1, keepdims=True)
                )
            ).astype(LOW)

        in_put.start()
        give_out.wait_send()
        for i in range(2):
            in_back(i).wait_send()

    pl.run_scoped(
        attention,
        pltpu.VMEM((tiles * (tiles + 1) // 2, TILE, TILE), LOW),
        pltpu.VMEM((length, length), FULL),
        pltpu.VMEM((length, PAIR), FULL),
        pltpu.VMEM((length, PAIR), FULL),
        pltpu.VMEM((length, 1), FULL),
        pltpu.VMEM((pair_count, length, mine), LOW),
        pltpu.VMEM((width, 3 * mine), LOW),
        pltpu.VMEM((pair_count, length, PAIR), LOW),
        pltpu.VMEM((2, wide, deep) + block_shapes(width, hidden)["out"][0], LOW),
    )

    if not fused:
        for kind in KINDS[:-1]:
            one = pltpu.make_async_copy(parts[kind], results[kind], load_sems.at[0])
            one.start()
            one.wait()
        one = pltpu.make_async_copy(vec_sums, results["vec"], load_sems.at[0])
        one.start()
        one.wait()
    else:
        sums = vec_sums[...]
        tall = width // COUNT
        for rank in range(COUNT):
            z, a, s = spot_of(rank, core)
            shifted = pltpu.roll(sums, width - rank * tall, 1) if rank else sums
            parts["vec"][0, z, a, s] = shifted[:, :128]
    steps("vec start", "early gather", "down close")

    def out_part(here):
        return contract(hidden_low[0, here, :], weight_down[0], 1, 0) + contract(
            hidden_low[1, here, :], weight_down[1], 1, 0
        )

    @pl.loop(0, tiles)
    def _(i):
        part = out_part(rows_of(lax.rem(other * 2 + i, tiles) * TILE, TILE))

        @pl.when(i < 2)
        def _():
            stage[tile_rows(i), :] = part.astype(LOW)
            out_back(i).start()

        @pl.when(i >= 2)
        def _():
            resid[tile_rows(i - 2), :] += part

        steps_when(i == 0, "lead gather", "up1 close", "attn2 close")
        steps_when(i == 1, "out close")
        steps_when(i == 2, "vec gather")
        steps_when(i == 3, "attn1 close")

    steps("down store", "up0 store", "up1 store")

    @pl.loop(0, 2)
    def _(i):
        here = tile_rows(i)
        out_back(i).wait_recv()
        low_mid[rows_of(half + i * TILE, TILE), :] = (
            resid[here, :] + catch_out[here, :].astype(FULL)
        ).astype(LOW)

    out_put.start()
    steps("early close", "lead close", "vec close")
    steps("out store", "attn2 store", "attn1 store", "early store", "vec store", "lead store")
    if fused:
        for job in jobs.values():
            job.drain()
    in_put.wait()
    out_put.wait()
    g_far.wait_send()
    for i in range(2):
        for one in (dz_far, out_back):
            one(i).wait_send()
    for p in range(pair_count):
        send_heads(p).wait_send()


def layer(fused, tokens, seg, cotangent, gain_in, shift_in, gain_mid, shift_mid, weights):
    half, width = tokens.shape
    length, mine = 2 * half, width // 2
    hidden = weights[-1].shape[0]
    pairs, tiles = mine // PAIR, length // TILE
    shapes = block_shapes(width, hidden)
    long, wide, deep = GRID
    anywhere = pl.BlockSpec(memory_space=pl.ANY)
    local = pl.BlockSpec(memory_space=pltpu.VMEM)
    outs = [jax.ShapeDtypeStruct((half, width), LOW)] * 2
    out_specs = [anywhere] * 2
    for kind in KINDS:
        shape, kept = shapes[kind]
        if fused:
            outs.append(jax.ShapeDtypeStruct((FAN[kind], 2) + shape, kept))
            out_specs.append(anywhere)
        elif kind == "vec":
            outs.append(jax.ShapeDtypeStruct((8, width), FULL))
            out_specs.append(anywhere)
        else:
            outs.append(jax.ShapeDtypeStruct((FAN[kind],) + GRID + shape, kept))
            out_specs.append(anywhere)
    spans = [(t + 1) * TILE for t in range(tiles)]
    outs += [jax.ShapeDtypeStruct((span, 2 * TILE), LOW) for span in spans]
    outs.append(jax.ShapeDtypeStruct((tiles * (tiles + 1) // 2, TILE, TILE), LOW))
    outs.append(jax.ShapeDtypeStruct((8, half), FULL))
    out_specs += [anywhere] * (tiles + 1) + [local]
    scratch = [
        pltpu.VMEM((length, width), LOW),
        pltpu.VMEM((width, width), LOW),
        pltpu.VMEM((pairs, length, PAIR), LOW),
        pltpu.VMEM((pairs, half, PAIR), LOW),
        pltpu.VMEM((half, width), FULL),
        pltpu.VMEM((length, width), LOW),
        pltpu.VMEM((half, width), FULL),
        pltpu.VMEM((length, width), LOW),
        pltpu.VMEM((length, width), LOW),
        pltpu.VMEM((pairs, length, PAIR), LOW),
        pltpu.VMEM((pairs, length, PAIR), LOW),
        pltpu.VMEM((pairs, length, PAIR), LOW),
        pltpu.VMEM((length, 128), FULL),
        pltpu.VMEM((half, width), LOW),
    ]
    scratch += [pltpu.VMEM((2, (t + 1) * TILE, 2 * TILE), LOW) for t in range(tiles)]
    corners = tiles * (tiles + 1) // 2
    scratch += [pltpu.VMEM((corners, TILE, TILE), LOW)]
    scratch += [pltpu.VMEM((half, width), LOW)] * 3
    block = hidden // 4
    scratch += [pltpu.VMEM((2, block, width), LOW), pltpu.VMEM((2, length, block), LOW)]
    scratch += [
        pltpu.VMEM((8, width), FULL),
    ]
    scratch += [pltpu.VMEM((FAN[kind],) + GRID + shapes[kind][0], shapes[kind][1]) for kind in KINDS]
    dma = pltpu.SemaphoreType.DMA
    if fused:
        leads = {kind: ((long, deep), (long,), (long - 1,), ()) for kind in KINDS}
        leads["down"] = ((long, deep), (long - 1, deep), (), ())
        leads["vec"] = ((3, long), (), (long - 1,), ())
        for step in range(4):
            scratch += [
                pltpu.VMEM((FAN[kind],) + leads[kind][step] + shapes[kind][0], shapes[kind][1])
                for kind in KINDS
            ]
        scratch += [dma((long, deep))] * 2 + [dma((long - 1,))] * 2 + [dma((1,))] * 4
        for kind in KINDS[1:]:
            fan = FAN[kind]
            count = 3 if kind == "vec" else fan
            scratch += [dma((count,))] * 4 + [dma((fan, long - 1))] * 2 + [dma((fan,))] * 2
        scratch += [dma((FAN[kind], 2)) for kind in KINDS]
    scratch += [dma((17 + 3 * pairs,)), dma((2,))]
    scratch += [dma((2, 2))] * 6
    scratch += [dma((2,)), dma((2, tiles)), dma((tiles, 2))]
    scratch += [dma((2,)), dma((2, pairs)), dma((7,))]
    return pl.pallas_call(
        functools.partial(layer_kernel, fused),
        out_shape=outs,
        in_specs=[anywhere, local, anywhere] + [local] * 4 + [anywhere] * 6,
        out_specs=out_specs,
        scratch_shapes=scratch,
        compiler_params=pltpu.CompilerParams(
            collective_id=0, has_side_effects=True, vmem_limit_bytes=VMEM_LIMIT
        ),
        name="layer",
    )(tokens, seg, cotangent, gain_in, shift_in, gain_mid, shift_mid, *weights)


def deliver_kernel(count, *refs):
    refs, (load_sems, put_sems) = refs[:-2], refs[-2:]
    targets = refs[count : (len(refs) - 2 * count + 2) // 2 + count]
    sources, held = refs[:count], refs[count + len(targets) : 2 * count + len(targets)]
    made = refs[2 * count + len(targets) :]
    loads = [
        pltpu.make_async_copy(source, target, load_sems.at[i])
        for i, (source, target) in enumerate(zip(sources, held))
    ]
    for one in loads:
        one.start()
    puts = [
        pltpu.make_async_copy(source, target, put_sems.at[i])
        for i, (source, target) in enumerate(zip(held[:2] + made, targets))
    ]
    for i in range(2):
        loads[i].wait()
        puts[i].start()
    for one in loads[2:]:
        one.wait()
    share_in, down, up, out, attn, early, lead, vec = held[2:]
    share, g_query, g_key, g_value, g_out, g_up, g_down, *g_vecs = made
    tall, mine = out.shape[2:]
    for k in range(2):
        for b in range(2):
            g_up[:, (2 * k + b) * 2 * mine : (2 * k + b + 1) * 2 * mine] = up[b, k].astype(FULL)
    puts[7].start()
    for k in range(2):
        g_down[:, k * mine : (k + 1) * mine] = down[0, k].astype(FULL)
    puts[8].start()
    for k in range(2):
        start = k * mine
        g_out[:, start : start + mine] = out[0, k].astype(FULL)
        for p in range(attn.shape[0]):
            for place, target in enumerate((g_query, g_key, g_value)):
                target[:, start + (p + 1) * PAIR : start + (p + 2) * PAIR] = attn[
                    p, k, :, place * PAIR : (place + 1) * PAIR
                ].astype(FULL)
        ones, twos = lead[0, k].astype(FULL), early[0, k].astype(FULL)
        keep = lanes_below(ones.shape, HEAD)
        seconds = twos[:, :PAIR]
        g_query[:, start : start + PAIR] = jnp.where(keep, ones, pltpu.roll(seconds, HEAD, 1))
        g_key[:, start : start + PAIR] = jnp.where(keep, pltpu.roll(ones, HEAD, 1), seconds)
        g_value[:, start : start + PAIR] = twos[:, PAIR:]
    share[...] = share_in[0:1, :]
    sums = vec[0, 0] + vec[0, 1]
    for i, target in enumerate(g_vecs):
        target[...] = sums[i, :tall]
    for one in puts[2:7] + puts[9:]:
        one.start()
    for one in puts:
        one.wait()


def deliver(*arrays):
    output, _, shares, down, up, out = arrays[:6]
    tall, mine = out.shape[2:]
    width = 2 * mine
    shapes = [(1, shares.shape[1])] + [(tall, width)] * 4
    shapes += [(tall, 2 * up.shape[3] * 2), (down.shape[2], width)] + [(tall,)] * 4
    anywhere = pl.BlockSpec(memory_space=pl.ANY)
    return pl.pallas_call(
        functools.partial(deliver_kernel, len(arrays)),
        out_shape=[jax.ShapeDtypeStruct(output.shape, output.dtype)] * 2
        + [jax.ShapeDtypeStruct(shape, FULL) for shape in shapes],
        in_specs=[anywhere] * len(arrays),
        out_specs=[anywhere] * (2 + len(shapes)),
        scratch_shapes=[pltpu.VMEM(one.shape, one.dtype) for one in arrays]
        + [pltpu.VMEM(shape, FULL) for shape in shapes]
        + [pltpu.SemaphoreType.DMA((len(arrays),)), pltpu.SemaphoreType.DMA((2 + len(shapes),))],
        compiler_params=pltpu.CompilerParams(vmem_limit_bytes=VMEM_LIMIT),
        name="deliver",
    )(*arrays)


def reduce_plain(parts, rows):
    down, up, out, attn, early, lead, vec = parts
    width = vec.shape[1]

    def scattered(part):
        summed = lax.psum_scatter(part.astype(FULL), "rows", scatter_dimension=0, tiled=True)
        return summed.astype(LOW)

    def joined(part):
        return lax.all_gather(part, "keys", axis=1, tiled=True).astype(FULL)

    def flat_part(part):
        return part.reshape(-1, part.shape[-1])

    ones, twos = scattered(flat_part(lead[0])), scattered(flat_part(early[0]))
    first = [
        jnp.concatenate([ones[:, :HEAD], twos[:, :HEAD]], 1),
        jnp.concatenate([ones[:, HEAD:], twos[:, HEAD:PAIR]], 1),
        twos[:, PAIR:],
    ]
    rest = [scattered(flat_part(attn[p])) for p in range(attn.shape[0])]
    halves = [
        jnp.concatenate([first[i]] + [one[:, i * PAIR : (i + 1) * PAIR] for one in rest], 1)
        for i in range(3)
    ]
    halves.append(scattered(flat_part(out[0])))
    halves.append(jnp.concatenate([scattered(flat_part(up[b])) for b in range(2)], 1))
    halves.append(scattered(flat_part(down[0])))
    sums = lax.psum_scatter(
        lax.psum(vec[:4].T, "keys"), "rows", scatter_dimension=0, tiled=True
    )
    return [joined(one) for one in halves], [sums[:, i] for i in range(4)]


def body(
    rows,
    tokens,
    seg_ids,
    doc_starts,
    gain_in,
    shift_in,
    w_query,
    w_key,
    w_value,
    w_out,
    gain_mid,
    shift_mid,
    w_up,
    w_down,
    out_grad,
):
    fused = rows == COUNT
    own_tokens, own_grad = tokens[0], out_grad[0]
    output, input_grad, *parts = layer(
        fused,
        own_tokens,
        seg_ids,
        own_grad,
        gain_in,
        shift_in,
        gain_mid,
        shift_mid,
        (w_query, w_key, w_value, w_out, w_up, w_down),
    )
    parts, shares = parts[: len(KINDS)], parts[-1]
    if fused:
        output, input_grad, shares, *grads = deliver(output, input_grad, shares, *parts)
        grads, vectors = grads[:6], grads[6:]
    else:
        grads, vectors = reduce_plain(parts, rows)
    g_query, g_key, g_value, g_out, g_up, g_down = grads
    return (
        output[None],
        input_grad[None],
        shares[:1],
        vectors[0],
        vectors[1],
        g_query,
        g_key,
        g_value,
        g_out,
        vectors[2],
        vectors[3],
        g_up,
        g_down,
    )


def solution(mesh):
    in_specs = (
        P("rows", "keys", None),
        P("rows", None),
        P("rows", "keys"),
        P(),
        P(),
        P(),
        P(),
        P(),
        P(),
        P(),
        P(),
        P(),
        P(),
        P("rows", "keys", None),
    )
    out_specs = (
        P("rows", "keys", None),
        P("rows", "keys", None),
        P("rows", "keys"),
        P("rows"),
        P("rows"),
        P("rows", None),
        P("rows", None),
        P("rows", None),
        P("rows", None),
        P("rows"),
        P("rows"),
        P("rows", None),
        P("rows", None),
    )
    return jax.shard_map(
        functools.partial(body, mesh.shape["rows"]),
        mesh=mesh,
        in_specs=in_specs,
        out_specs=out_specs,
        check_vma=False,
    )
```

```python
import functools

import jax
import jax.numpy as jnp
from jax import lax
from jax.experimental import pallas as pl
from jax.experimental.pallas import tpu as pltpu
from jax.sharding import PartitionSpec as P

HEAD = 64
PAIR = 2 * HEAD
TILE = 256
EPS = 1e-05
MASKED = 1e30
SELECT_SHIFT = 4.0
LOW = jnp.bfloat16
FULL = jnp.float32
MESH = pl.DeviceIdType.MESH
VMEM_LIMIT = 67_000_000


def contract(left, right, left_dim, right_dim):
    return lax.dot_general(
        left, right, (((left_dim,), (right_dim,)), ((), ())), preferred_element_type=FULL
    )


def layer_norm(field):
    center = field - jnp.mean(field, -1, keepdims=True)
    inverse = lax.rsqrt(jnp.mean(center * center, -1, keepdims=True) + EPS)
    return center * inverse, inverse


def remote(source, target, send, recv, device):
    return pltpu.make_async_remote_copy(
        src_ref=source,
        dst_ref=target,
        send_sem=send,
        recv_sem=recv,
        device_id=device,
        device_id_type=MESH,
    )


def lanes_below(shape, bound):
    return lax.broadcasted_iota(jnp.int32, shape, len(shape) - 1) < bound


def flat(ref):
    return ref[...].reshape(1, ref.shape[0])


def corner(step, tiles):
    t = sum((step >= n * (n + 1) // 2).astype(jnp.int32) for n in range(1, tiles))
    return t, step - t * (t + 1) // 2


def rows_of(start, size):
    return pl.ds(pl.multiple_of(start, size), size)


def gelu_parts(field):
    scale = 0.7978845608028654
    square = field * field
    inner = jnp.tanh(scale * field * (1.0 + 0.044715 * square))
    half_sum = 0.5 * (1.0 + inner)
    slope = half_sum + 0.5 * field * (1.0 - inner * inner) * (
        scale * (1.0 + 3.0 * 0.044715 * square)
    )
    return field * half_sum, slope


GRID = (4, 2, 2)
COUNT = GRID[0] * GRID[1] * GRID[2]
KINDS = ("down", "up", "out", "attn", "early", "lead", "vec")
FAN = {"down": 1, "up": 2, "out": 1, "attn": 2, "early": 1, "lead": 1, "vec": 1}


def block_shapes(width, hidden):
    mine = width // 2
    tall = width // COUNT
    return {
        "down": ((hidden // COUNT, mine), LOW),
        "up": ((tall, mine * 2), LOW),
        "out": ((tall, mine), LOW),
        "attn": ((tall, mine), LOW),
        "early": ((tall, 2 * PAIR), LOW),
        "lead": ((tall, PAIR), LOW),
        "vec": ((8, 128), FULL),
    }


def layer_kernel(fused, *refs):
    refs = list(refs)

    def take(count):
        taken = refs[:count]
        del refs[:count]
        return taken if count > 1 else taken[0]

    tokens_hbm, seg, cotangent, gain, shift, gain_mid, shift_mid = take(7)
    w_query, w_key, w_value, w_out, w_up, w_down = take(6)
    output, input_grad = take(2)
    results = dict(zip(KINDS, take(len(KINDS))))
    prob_hbm, slope_hbm, share_out = take(4), take(1), take(1)
    (
        grads_all,
        weight_out,
        heads,
        heads_far,
        resid,
        low_mid,
        grad_resid,
        low_resid,
        low_in,
        queries,
        keys,
        values,
        scales,
        tokens,
    ) = take(14)
    probs = take(4)
    share = take(1)
    stage, catch_mid, catch_out = take(3)
    weight_down, hidden_low = take(2)
    vec_sums = take(1)
    parts = dict(zip(KINDS, take(len(KINDS))))
    if fused:
        got1 = dict(zip(KINDS, take(len(KINDS))))
        got2 = dict(zip(KINDS, take(len(KINDS))))
        got3 = dict(zip(KINDS, take(len(KINDS))))
        pair = dict(zip(KINDS, take(len(KINDS))))
        sems = {
            name: take(2) for name in ("down1", "down2", "down3", "down4")
        }
        for kind in KINDS[1:]:
            for stage_name in "1234":
                sems[kind + stage_name] = take(2)
        for kind in KINDS:
            sems[kind + "5"] = take(1)
    (load_sems, g_sems, mid_sems, dz_sems, a_sems, b_sems, c_sems, pd_sems, po_sems, df_sems, prob_sems) = take(11)
    far_sems, head_sems, weight_sems = take(3)

    long, wide, deep = GRID
    core = lax.axis_index("keys")
    row = lax.axis_index("rows")
    other = 1 - core
    partner = (row, other)
    half, width = tokens.shape
    length, mine = 2 * half, width // 2
    pair_count = mine // PAIR
    tiles = length // TILE
    hidden = w_down.shape[0]
    block = hidden // 4
    own_start, far_start = core * half, other * half

    if fused:
        slow, mid, fast = row // (wide * deep), (row // deep) % wide, row % deep
    else:
        slow, mid, fast = 0, 0, 0

    def spot_of(rank, whose):
        z, y, x = rank // (wide * deep), (rank // deep) % wide, rank % deep
        if not fused:
            return z, y, x
        return z, x + whose * (y - x), y + whose * (x - y)

    first, second = fast + core * (mid - fast), mid + core * (fast - mid)
    near, next_ = 1 - first, 1 - second

    def rank_of(z, a, b):
        y, x = b + core * (a - b), a + core * (b - a)
        return (z * wide + y) * deep + x

    near_device = (rank_of(slow, near, second), core)
    next_device = (rank_of(slow, first, next_), core)
    far_places = [lax.rem(slow + step, long) for step in range(1, long)]

    def add_into(target, index, terms):
        total = target[index].astype(FULL)
        for term in terms:
            total = total + term.astype(FULL)
        target[index] = total.astype(target.dtype)

    class Job:
        def __init__(self, kind, k):
            self.kind, self.k = kind, k

        def first_copy(self):
            kind, k = self.kind, self.k
            part, got = parts[kind].at[k], got1[kind].at[k]
            send, recv = sems[kind + "1"]
            return remote(part.at[:, near], got, send.at[k], recv.at[k], near_device)

        def second_copy(self):
            kind, k = self.kind, self.k
            part, got = parts[kind].at[k], got2[kind].at[k]
            send, recv = sems[kind + "2"]
            return remote(part.at[:, first, next_], got, send.at[k], recv.at[k], next_device)

        def third_copies(self):
            kind, k = self.kind, self.k
            send, recv = sems[kind + "3"]
            return [
                remote(
                    parts[kind].at[k, z, first, second],
                    got3[kind].at[k, step],
                    send.at[k, step],
                    recv.at[k, step],
                    (rank_of(z, first, second), core),
                )
                for step, z in enumerate(far_places)
            ]

        def last_copy(self):
            kind, k = self.kind, self.k
            send, recv = sems[kind + "4"]
            return remote(
                parts[kind].at[k, slow, first, second],
                pair[kind].at[k],
                send.at[k],
                recv.at[k],
                partner,
            )

        def start(self):
            self.first_copy().start()

        def turn(self):
            self.first_copy().wait_recv()
            kind, k = self.kind, self.k

            @pl.loop(0, long * deep)
            def _(step):
                z, b = step // deep, lax.rem(step, deep)
                add_into(parts[kind], (k, z, first, b), [got1[kind][k, z, b]])

            self.second_copy().start()

        def gather(self):
            self.second_copy().wait_recv()
            kind, k = self.kind, self.k

            @pl.loop(0, long)
            def _(z):
                add_into(parts[kind], (k, z, first, second), [got2[kind][k, z]])

            for one in self.third_copies():
                one.start()

        def close(self):
            for one in self.third_copies():
                one.wait_recv()
            kind, k = self.kind, self.k
            add_into(
                parts[kind],
                (k, slow, first, second),
                [got3[kind][k, step] for step in range(long - 1)],
            )
            self.last_copy().start()

        def puts(self):
            kind, k = self.kind, self.k
            own_part = parts[kind].at[k, slow, first, second]
            sem = sems[kind + "5"]
            return [
                pltpu.make_async_copy(own_part, results[kind].at[k, core], sem.at[k, 0]),
                pltpu.make_async_copy(pair[kind].at[k], results[kind].at[k, other], sem.at[k, 1]),
            ]

        def store(self):
            self.last_copy().wait_recv()
            for one in self.puts():
                one.start()

        def drain(self):
            self.first_copy().wait_send()
            self.second_copy().wait_send()
            for one in self.third_copies():
                one.wait_send()
            self.last_copy().wait_send()
            for one in self.puts():
                one.wait()

    class Down(Job):
        def near_copy(self, z, s):
            send, recv = sems["down1"]
            return remote(
                parts["down"].at[0, z, near, s],
                got1["down"].at[0, z, s],
                send.at[z, s],
                recv.at[z, s],
                near_device,
            )

        def slow_copy(self, step):
            z = lax.rem(slow + step, long)
            send, recv = sems["down2"]
            return remote(
                parts["down"].at[0, z, first],
                got2["down"].at[0, step - 1],
                send.at[step - 1],
                recv.at[step - 1],
                (rank_of(z, first, second), core),
            )

        def next_copy(self):
            send, recv = sems["down3"]
            return remote(
                parts["down"].at[0, slow, first, next_],
                got3["down"].at[0],
                send.at[0],
                recv.at[0],
                next_device,
            )

        def start_at(self, z):
            for s in range(deep):
                self.near_copy(z, s).start()

        def start_part(self, z, m):
            @pl.when(core == 0)
            def _():
                self.near_copy(z, m).start()

            @pl.when((core == 1) & (m == near))
            def _():
                self.start_at(z)

        def turn_at(self, z):
            for s in range(deep):
                self.near_copy(z, s).wait_recv()

            @pl.loop(0, deep)
            def _(b):
                add_into(parts["down"], (0, z, first, b), [got1["down"][0, z, b]])

            step = lax.rem(z - slow + long, long)

            @pl.when(step > 0)
            def _():
                self.slow_copy(step).start()

        def cross(self):
            for step in range(1, long):
                self.slow_copy(step).wait_recv()

            @pl.loop(0, deep)
            def _(b):
                add_into(
                    parts["down"],
                    (0, slow, first, b),
                    [got2["down"][0, step, b] for step in range(long - 1)],
                )

            self.next_copy().start()

        def close(self):
            self.next_copy().wait_recv()
            add_into(parts["down"], (0, slow, first, second), [got3["down"][0]])
            self.last_copy().start()

        def drain(self):
            for z in range(long):
                for s in range(deep):
                    self.near_copy(z, s).wait_send()
            for step in range(1, long):
                self.slow_copy(step).wait_send()
            self.next_copy().wait_send()
            self.last_copy().wait_send()
            for one in self.puts():
                one.wait()

    class Vectors(Job):
        def first_copies(self):
            send, recv = sems["vec1"]
            places = ((near, second), (first, next_), (near, next_))
            return [
                remote(
                    parts["vec"].at[0, :, a, b],
                    got1["vec"].at[0, i],
                    send.at[i],
                    recv.at[i],
                    (rank_of(slow, a, b), core),
                )
                for i, (a, b) in enumerate(places)
            ]

        def start(self):
            for one in self.first_copies():
                one.start()

        def gather(self):
            for one in self.first_copies():
                one.wait_recv()

            @pl.loop(0, long)
            def _(z):
                add_into(
                    parts["vec"], (0, z, first, second), [got1["vec"][0, i, z] for i in range(3)]
                )

            for one in self.third_copies():
                one.start()

        def drain(self):
            for one in self.first_copies() + self.third_copies():
                one.wait_send()
            self.last_copy().wait_send()
            for one in self.puts():
                one.wait()

    def steps(*names):
        if fused:
            for name in names:
                job, step = name.split()
                getattr(jobs[job], step)()

    def steps_when(condition, *names):
        if fused:
            pl.when(condition)(lambda: steps(*names))

    down = Down("down", 0)
    jobs = {"down": down, "vec": Vectors("vec", 0)}
    jobs |= {kind: Job(kind, 0) for kind in ("out", "early", "lead")}
    jobs |= {f"up{k}": Job("up", k) for k in range(2)}
    jobs |= {f"attn{k + 1}": Job("attn", k) for k in range(pair_count - 1)}

    def local(source, target, index):
        return pltpu.make_async_copy(source, target, load_sems.at[index])

    own = rows_of(own_start, half)
    in_put = local(low_mid.at[pl.ds(0, half)], input_grad, 0)
    out_put = local(low_mid.at[pl.ds(half, half)], output, 1)
    g_load = local(cotangent, grads_all.at[own], 0)
    out_loads = [
        local(tokens_hbm, tokens, 15),
        local(w_out.at[rows_of(core * mine, mine)], weight_out.at[pl.ds(0, mine)], 1),
        local(w_out.at[rows_of(other * mine, mine)], weight_out.at[pl.ds(mine, mine)], 2),
    ]
    down_loads = [
        local(w_down.at[rows_of((core * 2 + b) * block, block)], weight_down.at[b], 11 + b)
        for b in range(2)
    ]

    peers = [partner]
    if fused:
        peers += [near_device, next_device, (rank_of(slow, near, next_), core)]
        peers += [(rank_of(z, first, second), core) for z in far_places]
    barrier = pltpu.get_barrier_semaphore()
    for peer in peers:
        pl.semaphore_signal(barrier, inc=1, device_id=peer, device_id_type=MESH)

    exchange = remote(tokens_hbm, low_resid.at[own], far_sems.at[0], far_sems.at[1], partner)

    def send_heads(p):
        return remote(
            heads.at[p, rows_of(far_start, half)],
            heads_far.at[p],
            head_sems.at[0, p],
            head_sems.at[1, p],
            partner,
        )

    def prob_put(t):
        return pltpu.make_async_copy(probs[t].at[0], prob_hbm[t], prob_sems.at[t, 0])

    def prob_load(t):
        return pltpu.make_async_copy(prob_hbm[t], probs[t].at[0], prob_sems.at[t, 1])

    def own_rows(i):
        return rows_of(own_start + i * TILE, TILE)

    def far_rows(i):
        return rows_of(far_start + i * TILE, TILE)

    def tile_rows(i):
        return rows_of(i * TILE, TILE)

    def to_partner(source, target, pair_sems):
        def one(i):
            return remote(
                source(i), target(i), pair_sems.at[0, i], pair_sems.at[1, i], partner
            )

        return one

    g_far = remote(cotangent, grads_all.at[own], g_sems.at[0], g_sems.at[1], partner)
    mid_far = to_partner(
        lambda i: low_mid.at[own_rows(i)], lambda i: low_mid.at[own_rows(i)], mid_sems
    )
    dz_far = to_partner(
        lambda i: low_resid.at[own_rows(i)], lambda i: low_resid.at[own_rows(i)], dz_sems
    )
    mid_back = to_partner(
        lambda i: stage.at[tile_rows(i)], lambda i: catch_mid.at[tile_rows(i)], a_sems
    )
    in_back = to_partner(
        lambda i: stage.at[tile_rows(i)], lambda i: catch_mid.at[tile_rows(i)], b_sems
    )
    out_back = to_partner(
        lambda i: stage.at[tile_rows(i)], lambda i: catch_out.at[tile_rows(i)], c_sems
    )

    def forward(
        weights,
        lead_query,
        lead_key,
        slopes,
        penalty,
        scale_rows,
        seg_cols,
        free_cols,
        sums,
    ):
        def column(rows, i):
            return (rows, pl.ds(i, 1))

        columns = pl.ds(pl.multiple_of(core * mine, 128), mine)
        loads = []
        for place, source in enumerate((w_query, w_key, w_value)):
            loads.append((source.at[:, columns], weights.at[:, pl.ds(place * mine, mine)]))
        for place, source in enumerate((w_query, w_key)):
            loads.append(
                (source.at[:, pl.ds(0, PAIR)], weights.at[:, pl.ds(3 * mine + place * PAIR, PAIR)])
            )
        loads = [
            pltpu.make_async_copy(source, target, weight_sems.at[i])
            for i, (source, target) in enumerate(loads)
        ]
        own_load = pltpu.make_async_copy(tokens_hbm, low_resid.at[own], weight_sems.at[5])
        own_load.start()
        for one in loads:
            one.start()

        pl.semaphore_wait(barrier, len(peers))
        exchange.start()
        g_far.start()
        for one in out_loads + [g_load] + down_loads:
            one.start()

        own_load.wait()

        keep = lanes_below((TILE, PAIR), HEAD)
        keep_half = lanes_below((half, PAIR), HEAD)

        def normalize(whose):
            here = rows_of(whose * half, half)
            unit, _ = layer_norm(low_resid[here, :].astype(FULL))
            low_in[here, :] = (unit * flat(gain) + flat(shift)).astype(LOW)

        def project(whose):
            here = rows_of(whose * half, half)
            result = contract(low_in[here, :], weights[...], 1, 0).astype(LOW)
            for p in range(pair_count):
                queries[p, here, :] = result[:, p * PAIR : (p + 1) * PAIR] * LOW(0.125)
                keys[p, here, :] = result[:, mine + p * PAIR : mine + (p + 1) * PAIR]
                values[p, here, :] = result[:, 2 * mine + p * PAIR : 2 * mine + (p + 1) * PAIR]
            first = result[:, 3 * mine : 3 * mine + PAIR]
            lead_query[here, :] = jnp.where(keep_half, first, LOW(0.0)) * LOW(0.125)
            lead_key[here, :] = result[:, 3 * mine + PAIR :]

        spots = (
            lax.broadcasted_iota(jnp.int32, (2 * TILE, 2 * TILE), 0),
            lax.broadcasted_iota(jnp.int32, (2 * TILE, 2 * TILE), 1),
        )
        earlier = jnp.where(spots[0] < spots[1], 1.0, 0.0).astype(LOW)
        scale_rows[...] = jnp.zeros_like(scale_rows)
        sums[...] = jnp.zeros_like(sums)

        def select_block(wide, k, diagonal=False):
            rows, span = rows_of(k * 2 * TILE, 2 * TILE), rows_of(wide * 2 * TILE, 2 * TILE)
            scores = contract(lead_key[rows, :], lead_query[span, :], 1, 1)
            repeat = 2 * TILE // 128
            same = jnp.concatenate([seg_cols[rows, :]] * repeat, 1) == seg[:, span].astype(FULL)
            ahead = spots[1] - spots[0] + (wide - k) * 2 * TILE
            later = same & (ahead > 0)
            allowed = same & (ahead >= 0)
            select = jnp.where(later, jnp.concatenate([free_cols[rows, :]] * repeat, 1), 0.0)
            level = scores - SELECT_SHIFT
            chosen = select * (jnp.maximum(level, 0.0) + jnp.log(1.0 + jnp.exp(-jnp.abs(level))))
            slope = (select * (0.5 + 0.5 * jnp.tanh(0.5 * level))).astype(LOW)

            slopes[wide * (2 * wide + 1) + 2 * k] = slope[:TILE, :TILE]

            if not diagonal:

                @pl.when(k < wide)
                def _():
                    slopes[wide * (2 * wide + 1) + 2 * k + 1] = slope[TILE:, :TILE]

            slopes[(2 * wide + 1) * (wide + 1) + 2 * k] = slope[:TILE, TILE:]
            slopes[(2 * wide + 1) * (wide + 1) + 2 * k + 1] = slope[TILE:, TILE:]
            high = chosen.astype(LOW)
            rest = (chosen - high.astype(FULL)).astype(LOW)
            total = (
                sums[column(rows, 0)] + contract(high, earlier, 1, 0) + contract(rest, earlier, 1, 0)
            )
            penalty[rows, span] = jnp.where(allowed, total, MASKED)
            sums[column(rows, 0)] += jnp.sum(chosen, -1, keepdims=True)
            ratio = jnp.where(later, 0.5 + 0.5 * jnp.tanh(0.5 * total - 1.0), 0.0)
            sums[column(rows, 1)] += jnp.sum(ratio, -1, keepdims=True)
            sums[column(rows, 2)] += jnp.sum(jnp.where(later, 1.0, 0.0), -1, keepdims=True)

        normalize(core)
        seg_row = seg[...]
        seg_wide = jnp.broadcast_to(seg_row.astype(FULL), (128, length))
        spot = lax.broadcasted_iota(jnp.int32, (128, length), 1)
        before = pltpu.roll(seg_wide, 1, 1)
        free_wide = jnp.where((spot > 0) & (before == seg_wide), 1.0, 0.0)
        seg_cols[...] = seg_wide.T
        free_cols[...] = free_wide.T
        for one in loads:
            one.wait()
        project(core)
        exchange.wait_recv()
        select_block(core, core, True)
        normalize(other)
        project(other)

        @pl.loop(0, 2)
        def _(step):
            select_block(other + step * core, other * (1 - step))

        slope_put = pltpu.make_async_copy(slopes, slope_hbm, weight_sems.at[6])
        slope_put.start()

        shares = sums[column(own, 1)] / jnp.maximum(sums[column(own, 2)], 1.0)
        share_out[...] = jnp.broadcast_to(shares, (half, 128)).T[0:8, :]

        @pl.loop(0, pair_count)
        def _(p):
            slot = lax.rem(p, 2)

            @pl.when(p == 2)
            def _():
                for t in range(tiles):
                    prob_put(t).wait()

            for t in range(tiles):
                count = (t + 1) * TILE
                span = pl.ds(t * TILE, TILE)
                query = queries[p, span, :]
                both = jnp.concatenate(
                    [jnp.where(keep, query, LOW(0.0)), jnp.where(keep, LOW(0.0), query)], 0
                )
                fine = penalty[pl.ds(0, count), span]
                logits = contract(keys[p, pl.ds(0, count), :], both, 1, 1) - jnp.concatenate(
                    [fine, fine], 1
                )
                scaled = jnp.exp(logits - jnp.max(logits, 0, keepdims=True))
                prob = scaled.astype(LOW)
                probs[t][slot] = prob
                scale = 1.0 / jnp.sum(scaled, 0, keepdims=True)
                scale_rows[pl.ds(2 * p, 1), span] = scale[:, :TILE]
                scale_rows[pl.ds(2 * p + 1, 1), span] = scale[:, TILE:]
                out = contract(values[p, pl.ds(0, count), :], prob, 0, 0) * scale
                out = jnp.concatenate([out[:HEAD, :TILE], out[HEAD:, TILE:]], 0)
                heads[p, span, :] = out.T.astype(LOW)
            @pl.when(p == 0)
            def _():
                for t in range(tiles):
                    prob_put(t).start()

            send_heads(p).start()

        scales[...] = scale_rows[...].T
        slope_put.wait()
        exchange.wait_send()

    def feed_forward(weight_up, grad_up, stage_down):
        def give_down(b):
            return remote(
                stage_down.at[b],
                parts["down"].at[0, core * 2 + b],
                pd_sems.at[0, b],
                pd_sems.at[1, b],
                partner,
            )

        up_loads = [
            local(
                w_up.at[:, pl.ds(pl.multiple_of((core * 2 + b) * block, 128), block)],
                weight_up.at[b],
                9 + b,
            )
            for b in range(2)
        ]
        for one in up_loads:
            one.start()
        for one in out_loads:
            one.wait()
        for p in range(pair_count):
            send_heads(p).wait_recv()

        joined = jnp.concatenate(
            [heads[p, own, :] for p in range(pair_count)]
            + [heads_far[p] for p in range(pair_count)],
            1,
        )
        field = tokens[...].astype(FULL) + contract(joined, weight_out[...], 1, 0)
        resid[...] = field
        unit, _ = layer_norm(field)
        low_mid[own, :] = (unit * flat(gain_mid) + flat(shift_mid)).astype(LOW)
        for i in range(2):
            mid_far(i).start()

        for one in up_loads:
            one.wait()

        @pl.loop(0, 2)
        def _(b):
            @pl.loop(0, tiles)
            def _(i):
                @pl.when((b == 0) & (i >= 2))
                def _():
                    mid_far(i - 2).wait_recv()

                here = rows_of(lax.rem(core * 2 + i, tiles) * TILE, TILE)
                value, slope = gelu_parts(contract(low_mid[here, :], weight_up[b], 1, 0))
                hidden_low[b, here, :] = value.astype(LOW)
                grad_up[b, here, :] = slope.astype(LOW)
                if fused:

                    @pl.when((b == 1) & (i == 3))
                    def _():
                        down.turn_at(core * 2)

            @pl.when(b == 0)
            def _():
                for one in [g_load] + down_loads:
                    one.wait()
                g_far.wait_recv()

            tall = hidden // COUNT
            per = mine // tall
            @pl.loop(0, 2)
            def _(turn):
                m = lax.rem(turn + core * near, 2)
                place = pl.ds(pl.multiple_of(m * mine, 128), mine)
                grad = contract(hidden_low[b, :, place], grads_all[...], 0, 0).astype(LOW)
                kept = jnp.where(core == 0, grad[:, :mine], grad[:, mine:])
                given = jnp.where(core == 0, grad[:, mine:], grad[:, :mine])
                for i in range(per):
                    rank = (core * 2 + b) * (COUNT // 4) + m * per + i
                    z, a, s = spot_of(rank, core)
                    parts["down"][0, z, a, s] = kept[i * tall : (i + 1) * tall]
                    _, a, s = spot_of(rank, other)
                    stage_down[b, a, s] = given[i * tall : (i + 1) * tall]
                if fused:
                    down.start_part(core * 2 + b, m)

            give_down(b).start()

            @pl.loop(0, tiles)
            def _(i):
                here = rows_of(i * TILE, TILE)
                back = contract(grads_all[here, :], weight_down[b], 1, 1)
                grad_up[b, here, :] = (back * grad_up[b, here, :].astype(FULL)).astype(LOW)

                @pl.when(i == 3)
                def _():
                    give_down(b).wait_recv()
                    if fused:
                        down.start_at(other * 2 + b)

                if fused:

                    @pl.when((b == 1) & (i == 1))
                    def _():
                        down.turn_at(other * 2)

            @pl.loop(0, 2)
            def _(m):
                tall = width // COUNT
                per = mine // tall
                place = pl.ds(pl.multiple_of(m * mine, 128), mine)
                grad = contract(low_mid[:, place], grad_up[b], 0, 0).astype(LOW)
                for i in range(per):
                    z, a, s = spot_of(m * per + i, core)
                    parts["up"][b, z, a, s] = grad[i * tall : (i + 1) * tall]

            if fused:
                Job("up", b).start()

        def mid_part(here):
            return contract(grad_up[0, here, :], weight_up[0], 1, 1) + contract(
                grad_up[1, here, :], weight_up[1], 1, 1
            )

        @pl.loop(0, tiles)
        def _(i):
            part = mid_part(rows_of(lax.rem(other * 2 + i, tiles) * TILE, TILE))

            @pl.when(i < 2)
            def _():
                stage[tile_rows(i), :] = part.astype(LOW)
                mid_back(i).start()

            @pl.when(i >= 2)
            def _():
                grad_resid[tile_rows(i - 2), :] = part

            steps_when(i == 1, "up0 turn")

        @pl.loop(0, 2)
        def _(i):
            here = tile_rows(i)
            mid_back(i).wait_recv()
            grad = grad_resid[here, :] + catch_mid[here, :].astype(FULL)
            unit, inverse = layer_norm(resid[here, :])
            vec_sums[2:3, :] += jnp.sum(grad * unit, 0, keepdims=True)
            vec_sums[3:4, :] += jnp.sum(grad, 0, keepdims=True)
            scaled = grad * flat(gain_mid)
            total = grads_all[own_rows(i), :].astype(FULL) + inverse * (
                scaled
                - jnp.mean(scaled, -1, keepdims=True)
                - unit * jnp.mean(scaled * unit, -1, keepdims=True)
            )
            grad_resid[here, :] = total
            low_resid[own_rows(i), :] = total.astype(LOW)
            dz_far(i).start()

        for i in range(2):
            mid_back(i).wait_send()
            give_down(i).wait_send()
        if fused:
            down.turn_at(core * 2 + 1)

    vec_sums[...] = jnp.zeros_like(vec_sums)
    pl.run_scoped(
        forward,
        pltpu.VMEM((width, 3 * mine + 2 * PAIR), LOW),
        pltpu.VMEM((length, PAIR), LOW),
        pltpu.VMEM((length, PAIR), LOW),
        pltpu.VMEM((tiles * (tiles + 1) // 2, TILE, TILE), LOW),
        pltpu.VMEM((length, length), FULL),
        pltpu.VMEM((128, length), FULL),
        pltpu.VMEM((length, 128), FULL),
        pltpu.VMEM((length, 128), FULL),
        pltpu.VMEM((length, 128), FULL),
    )
    pl.run_scoped(
        feed_forward,
        pltpu.VMEM((2, width, block), LOW),
        pltpu.VMEM((2, length, block), LOW),
        pltpu.VMEM((2, wide, deep) + block_shapes(width, hidden)["down"][0], LOW),
    )

    def attention(slopes, fades, key_sum, value_sum, carry, grad_qkv, weight_in, grad_heads, stage_out):
        give_out = remote(
            stage_out,
            parts["out"].at[0, pl.ds(core * 2, 2)],
            po_sems.at[0],
            po_sems.at[1],
            partner,
        )

        slope_load = local(slope_hbm, slopes, 13)
        weight_loads = []
        for place, source in enumerate((w_query, w_key, w_value)):
            for p in range(pair_count):
                weight_loads.append(
                    local(
                        source.at[:, pl.ds(pl.multiple_of(core * mine + p * PAIR, 128), PAIR)],
                        weight_in.at[:, pl.ds(p * mine + place * PAIR, PAIR)],
                        17 + place * pair_count + p,
                    )
                )
        for one in [slope_load] + weight_loads:
            one.start()

        keep = lanes_below((TILE, PAIR), HEAD)
        def head_grads(here):
            result = contract(low_resid[here, :], weight_out[pl.ds(0, mine), :], 1, 1)
            for p in range(pair_count):
                scale = jnp.where(
                    keep, scales[here, 2 * p : 2 * p + 1], scales[here, 2 * p + 1 : 2 * p + 2]
                )
                grad_heads[p, here, :] = (result[:, p * PAIR : (p + 1) * PAIR] * scale).astype(LOW)

        @pl.loop(0, tiles)
        def _(i):
            @pl.when(i > 1)
            def _():
                dz_far(i - 2).wait_recv()

            head_grads(rows_of(lax.rem(core * 2 + i, tiles) * TILE, TILE))

        joined = jnp.concatenate([heads[p] for p in range(pair_count)], 1)
        grad = contract(joined, low_resid[...], 0, 0).astype(LOW)
        kept = jnp.where(core == 0, grad[:, :mine], grad[:, mine:])
        given = jnp.where(core == 0, grad[:, mine:], grad[:, :mine])
        tall = width // COUNT
        for i in range(mine // tall):
            rank = core * (COUNT // 2) + i
            z, a, s = spot_of(rank, core)
            parts["out"][0, z, a, s] = kept[i * tall : (i + 1) * tall]
            _, a, s = spot_of(rank, other)
            stage_out[i // (wide * deep), a, s] = given[i * tall : (i + 1) * tall]
        give_out.start()
        if fused:
            down.turn_at(other * 2 + 1)

        spots = (
            lax.broadcasted_iota(jnp.int32, (TILE, TILE), 0),
            lax.broadcasted_iota(jnp.int32, (TILE, TILE), 1),
        )
        after = jnp.where(spots[0] > spots[1], 1.0, 0.0).astype(LOW)

        def fade_send(t):
            part = pl.ds(t * (t + 1) // 2, t + 1)
            return remote(
                share.at[part],
                share.at[part],
                df_sems.at[0, t],
                df_sems.at[1, t],
                partner,
            )

        def pair_step(step, p):
            slot = lax.rem(step, 2)
            @pl.when(step == 1)
            def _():
                for t in range(tiles):
                    prob_load(t).start()

            @pl.when(step == 2)
            def _():
                for t in range(tiles):
                    prob_load(t).wait()

            for t in reversed(range(tiles)):
                count = (t + 1) * TILE
                span, rows = pl.ds(t * TILE, TILE), pl.ds(0, count)
                grad_tile = grad_heads[p, span, :]
                product = (grad_tile.astype(FULL) * heads[p, span, :].astype(FULL)).T
                query = queries[p, span, :]
                sides_q = jnp.concatenate(
                    [jnp.where(keep, query, LOW(0.0)), jnp.where(keep, LOW(0.0), query)], 0
                )
                sides_g = jnp.concatenate(
                    [jnp.where(keep, grad_tile, LOW(0.0)), jnp.where(keep, LOW(0.0), grad_tile)], 0
                )
                delta = jnp.concatenate(
                    [
                        jnp.sum(product[:HEAD, :], 0, keepdims=True),
                        jnp.sum(product[HEAD:, :], 0, keepdims=True),
                    ],
                    1,
                )
                change = probs[t][slot].astype(FULL) * (
                    contract(values[p, rows, :], sides_g, 1, 1) - delta
                )
                fade = change[:, :TILE] + change[:, TILE:]
                both = change.astype(LOW)
                fades[rows, span] = jnp.where(step == 0, 0.0, fades[rows, span]) + fade

                key_part = contract(both, sides_q, 1, 0)
                value_part = contract(probs[t][slot], sides_g, 1, 0)
                if t == tiles - 1:
                    key_sum[...] = key_part
                    value_sum[...] = value_part
                else:
                    key_sum[rows, :] += key_part
                    value_sum[rows, :] += value_part
                query_part = contract(keys[p, rows, :], both, 0, 0)
                query_part = jnp.concatenate(
                    [query_part[:HEAD, :TILE], query_part[HEAD:, TILE:]], 0
                )
                grad_qkv[p, span, pl.ds(0, PAIR)] = (query_part.T * 0.125).astype(LOW)

                if t == tiles - 1:
                    @pl.when(step == 0)
                    def _():
                        give_out.wait_recv()
                        steps("out start")

                    steps_when(step == 1, "up1 turn")
                    steps_when(step == 2, "attn2 turn", "up1 gather")

        def lead_head():
            @pl.when(core == 0)
            def _():
                carry[...] = jnp.zeros_like(carry)
                for t in reversed(range(tiles)):
                    count = (t + 1) * TILE
                    span, rows = pl.ds(t * TILE, TILE), pl.ds(0, count)
                    part = pl.ds(t * (t + 1) // 2, t + 1)
                    fade_send(t).wait_recv()
                    total = fades[rows, span] + share[part].astype(FULL).reshape(count, TILE)
                    later = contract(total.astype(LOW), after, 1, 0) + carry[rows, :]
                    if t:
                        carry[rows, :] += jnp.sum(total, -1, keepdims=True)
                    slope = slopes[part].astype(FULL).reshape(count, TILE)
                    extra = (-later * slope).astype(LOW)
                    query = jnp.where(keep, queries[0, span, :], LOW(0.0))
                    key_sum[rows, :] += contract(extra, query, 1, 0)
                    whole = contract(keys[0, rows, :], extra, 0, 0).T * 0.125
                    grad_qkv[0, span, pl.ds(0, PAIR)] = (
                        grad_qkv[0, span, pl.ds(0, PAIR)].astype(FULL)
                        + jnp.where(keep, whole, 0.0)
                    ).astype(LOW)

            @pl.when(core == 1)
            def _():
                for t in range(tiles):
                    fade_send(t).wait_send()

        def weights_into(kind, k, right):
            @pl.loop(0, 2)
            def _(m):
                place = pl.ds(pl.multiple_of(m * mine, 128), mine)
                grad = contract(low_in[:, place], right, 0, 0).astype(LOW)
                for i in range(mine // tall):
                    z, a, s = spot_of(m * (mine // tall) + i, core)
                    parts[kind][k, z, a, s] = grad[i * tall : (i + 1) * tall]

            if fused:
                Job(kind, k).start()

        @pl.loop(0, pair_count)
        def _(step):
            p = pair_count - 1 - step
            pair_step(step, p)
            grad_qkv[p, :, pl.ds(2 * PAIR, PAIR)] = value_sum[...].astype(LOW)

            @pl.when(p > 0)
            def _():
                grad_qkv[p, :, pl.ds(PAIR, PAIR)] = key_sum[...].astype(LOW)
                weights_into("attn", p - 1, grad_qkv[p])

            steps_when(step == 0, "up0 gather")


        @pl.when(core == 1)
        def _():
            for t in reversed(range(tiles)):
                count = (t + 1) * TILE
                share[pl.ds(t * (t + 1) // 2, t + 1)] = (
                    fades[pl.ds(0, count), pl.ds(t * TILE, TILE)]
                    .astype(LOW)
                    .reshape(t + 1, TILE, TILE)
                )
                fade_send(t).start()

        keep_all = lanes_below((length, PAIR), HEAD)
        second_head = jnp.where(
            keep_all,
            pltpu.roll(grad_qkv[0, :, pl.ds(0, PAIR)].astype(FULL), HEAD, 1),
            key_sum[...],
        )
        weights_into(
            "early",
            0,
            jnp.concatenate(
                [second_head.astype(LOW), grad_qkv[0, :, pl.ds(2 * PAIR, PAIR)]], 1
            ),
        )
        slope_load.wait()
        steps("down cross", "out turn", "attn2 gather", "attn1 turn", "up0 close")
        lead_head()
        grad_qkv[0, :, pl.ds(PAIR, PAIR)] = key_sum[...].astype(LOW)
        first_head = jnp.where(
            keep_all,
            grad_qkv[0, :, pl.ds(0, PAIR)].astype(FULL),
            pltpu.roll(key_sum[...], HEAD, 1),
        )
        weights_into("lead", 0, first_head.astype(LOW))

        for one in weight_loads:
            one.wait()

        def in_part(here):
            joined = jnp.concatenate([grad_qkv[p, here, :] for p in range(pair_count)], 1)
            return contract(joined, weight_in[...], 1, 1)

        @pl.loop(0, tiles)
        def _(i):
            part = in_part(rows_of(lax.rem(other * 2 + i, tiles) * TILE, TILE))

            @pl.when(i < 2)
            def _():
                stage[tile_rows(i), :] = part.astype(LOW)
                in_back(i).start()

            @pl.when(i >= 2)
            def _():
                fades[tile_rows(i - 2), pl.ds(0, width)] = part

            steps_when(i == 0, "out gather")
            steps_when(i == 1, "early turn")
            steps_when(i == 2, "attn1 gather")
            steps_when(i == 3, "lead turn")

        for i in range(2):
            mid_far(i).wait_send()

        @pl.loop(0, 2)
        def _(i):
            here = tile_rows(i)
            in_back(i).wait_recv()
            grad = fades[here, pl.ds(0, width)] + catch_mid[here, :].astype(FULL)
            unit, inverse = layer_norm(tokens[here, :].astype(FULL))
            vec_sums[0:1, :] += jnp.sum(grad * unit, 0, keepdims=True)
            vec_sums[1:2, :] += jnp.sum(grad, 0, keepdims=True)
            scaled = grad * flat(gain)
            low_mid[here, :] = (
                grad_resid[here, :]
                + inverse
                * (
                    scaled
                    - jnp.mean(scaled, -1, keepdims=True)
                    - unit * jnp.mean(scaled * unit, -1, keepdims=True)
                )
            ).astype(LOW)

        in_put.start()
        give_out.wait_send()
        for i in range(2):
            in_back(i).wait_send()

    pl.run_scoped(
        attention,
        pltpu.VMEM((tiles * (tiles + 1) // 2, TILE, TILE), LOW),
        pltpu.VMEM((length, length), FULL),
        pltpu.VMEM((length, PAIR), FULL),
        pltpu.VMEM((length, PAIR), FULL),
        pltpu.VMEM((length, 1), FULL),
        pltpu.VMEM((pair_count, length, mine), LOW),
        pltpu.VMEM((width, 3 * mine), LOW),
        pltpu.VMEM((pair_count, length, PAIR), LOW),
        pltpu.VMEM((2, wide, deep) + block_shapes(width, hidden)["out"][0], LOW),
    )

    if not fused:
        for kind in KINDS[:-1]:
            one = pltpu.make_async_copy(parts[kind], results[kind], load_sems.at[0])
            one.start()
            one.wait()
        one = pltpu.make_async_copy(vec_sums, results["vec"], load_sems.at[0])
        one.start()
        one.wait()
    else:
        sums = vec_sums[...]
        tall = width // COUNT
        for rank in range(COUNT):
            z, a, s = spot_of(rank, core)
            shifted = pltpu.roll(sums, width - rank * tall, 1) if rank else sums
            parts["vec"][0, z, a, s] = shifted[:, :128]
    steps("vec start", "early gather", "down close")

    def out_part(here):
        return contract(hidden_low[0, here, :], weight_down[0], 1, 0) + contract(
            hidden_low[1, here, :], weight_down[1], 1, 0
        )

    @pl.loop(0, tiles)
    def _(i):
        part = out_part(rows_of(lax.rem(other * 2 + i, tiles) * TILE, TILE))

        @pl.when(i < 2)
        def _():
            stage[tile_rows(i), :] = part.astype(LOW)
            out_back(i).start()

        @pl.when(i >= 2)
        def _():
            resid[tile_rows(i - 2), :] += part

        steps_when(i == 0, "lead gather", "up1 close", "attn2 close")
        steps_when(i == 1, "out close")
        steps_when(i == 2, "vec gather")
        steps_when(i == 3, "attn1 close")

    steps("down store", "up0 store", "up1 store")

    @pl.loop(0, 2)
    def _(i):
        here = tile_rows(i)
        out_back(i).wait_recv()
        low_mid[rows_of(half + i * TILE, TILE), :] = (
            resid[here, :] + catch_out[here, :].astype(FULL)
        ).astype(LOW)

    out_put.start()
    steps("early close", "lead close", "vec close")
    steps("out store", "attn2 store", "attn1 store", "early store", "vec store", "lead store")
    if fused:
        for job in jobs.values():
            job.drain()
    in_put.wait()
    out_put.wait()
    g_far.wait_send()
    for i in range(2):
        for one in (dz_far, out_back):
            one(i).wait_send()
    for p in range(pair_count):
        send_heads(p).wait_send()


def layer(fused, tokens, seg, cotangent, gain_in, shift_in, gain_mid, shift_mid, weights):
    half, width = tokens.shape
    length, mine = 2 * half, width // 2
    hidden = weights[-1].shape[0]
    pairs, tiles = mine // PAIR, length // TILE
    shapes = block_shapes(width, hidden)
    long, wide, deep = GRID
    anywhere = pl.BlockSpec(memory_space=pl.ANY)
    local = pl.BlockSpec(memory_space=pltpu.VMEM)
    outs = [jax.ShapeDtypeStruct((half, width), LOW)] * 2
    out_specs = [anywhere] * 2
    for kind in KINDS:
        shape, kept = shapes[kind]
        if fused:
            outs.append(jax.ShapeDtypeStruct((FAN[kind], 2) + shape, kept))
            out_specs.append(anywhere)
        elif kind == "vec":
            outs.append(jax.ShapeDtypeStruct((8, width), FULL))
            out_specs.append(anywhere)
        else:
            outs.append(jax.ShapeDtypeStruct((FAN[kind],) + GRID + shape, kept))
            out_specs.append(anywhere)
    spans = [(t + 1) * TILE for t in range(tiles)]
    outs += [jax.ShapeDtypeStruct((span, 2 * TILE), LOW) for span in spans]
    outs.append(jax.ShapeDtypeStruct((tiles * (tiles + 1) // 2, TILE, TILE), LOW))
    outs.append(jax.ShapeDtypeStruct((8, half), FULL))
    out_specs += [anywhere] * (tiles + 1) + [local]
    scratch = [
        pltpu.VMEM((length, width), LOW),
        pltpu.VMEM((width, width), LOW),
        pltpu.VMEM((pairs, length, PAIR), LOW),
        pltpu.VMEM((pairs, half, PAIR), LOW),
        pltpu.VMEM((half, width), FULL),
        pltpu.VMEM((length, width), LOW),
        pltpu.VMEM((half, width), FULL),
        pltpu.VMEM((length, width), LOW),
        pltpu.VMEM((length, width), LOW),
        pltpu.VMEM((pairs, length, PAIR), LOW),
        pltpu.VMEM((pairs, length, PAIR), LOW),
        pltpu.VMEM((pairs, length, PAIR), LOW),
        pltpu.VMEM((length, 128), FULL),
        pltpu.VMEM((half, width), LOW),
    ]
    scratch += [pltpu.VMEM((2, (t + 1) * TILE, 2 * TILE), LOW) for t in range(tiles)]
    corners = tiles * (tiles + 1) // 2
    scratch += [pltpu.VMEM((corners, TILE, TILE), LOW)]
    scratch += [pltpu.VMEM((half, width), LOW)] * 3
    block = hidden // 4
    scratch += [pltpu.VMEM((2, block, width), LOW), pltpu.VMEM((2, length, block), LOW)]
    scratch += [
        pltpu.VMEM((8, width), FULL),
    ]
    scratch += [pltpu.VMEM((FAN[kind],) + GRID + shapes[kind][0], shapes[kind][1]) for kind in KINDS]
    dma = pltpu.SemaphoreType.DMA
    if fused:
        leads = {kind: ((long, deep), (long,), (long - 1,), ()) for kind in KINDS}
        leads["down"] = ((long, deep), (long - 1, deep), (), ())
        leads["vec"] = ((3, long), (), (long - 1,), ())
        for step in range(4):
            scratch += [
                pltpu.VMEM((FAN[kind],) + leads[kind][step] + shapes[kind][0], shapes[kind][1])
                for kind in KINDS
            ]
        scratch += [dma((long, deep))] * 2 + [dma((long - 1,))] * 2 + [dma((1,))] * 4
        for kind in KINDS[1:]:
            fan = FAN[kind]
            count = 3 if kind == "vec" else fan
            scratch += [dma((count,))] * 4 + [dma((fan, long - 1))] * 2 + [dma((fan,))] * 2
        scratch += [dma((FAN[kind], 2)) for kind in KINDS]
    scratch += [dma((17 + 3 * pairs,)), dma((2,))]
    scratch += [dma((2, 2))] * 6
    scratch += [dma((2,)), dma((2, tiles)), dma((tiles, 2))]
    scratch += [dma((2,)), dma((2, pairs)), dma((7,))]
    return pl.pallas_call(
        functools.partial(layer_kernel, fused),
        out_shape=outs,
        in_specs=[anywhere, local, anywhere] + [local] * 4 + [anywhere] * 6,
        out_specs=out_specs,
        scratch_shapes=scratch,
        compiler_params=pltpu.CompilerParams(
            collective_id=0, has_side_effects=True, vmem_limit_bytes=VMEM_LIMIT
        ),
        name="layer",
    )(tokens, seg, cotangent, gain_in, shift_in, gain_mid, shift_mid, *weights)


def deliver_kernel(count, *refs):
    refs, (load_sems, put_sems) = refs[:-2], refs[-2:]
    targets = refs[count : (len(refs) - 2 * count + 2) // 2 + count]
    sources, held = refs[:count], refs[count + len(targets) : 2 * count + len(targets)]
    made = refs[2 * count + len(targets) :]
    loads = [
        pltpu.make_async_copy(source, target, load_sems.at[i])
        for i, (source, target) in enumerate(zip(sources, held))
    ]
    for one in loads:
        one.start()
    puts = [
        pltpu.make_async_copy(source, target, put_sems.at[i])
        for i, (source, target) in enumerate(zip(held[:2] + made, targets))
    ]
    for i in range(2):
        loads[i].wait()
        puts[i].start()
    for one in loads[2:]:
        one.wait()
    share_in, down, up, out, attn, early, lead, vec = held[2:]
    share, g_query, g_key, g_value, g_out, g_up, g_down, *g_vecs = made
    tall, mine = out.shape[2:]
    for k in range(2):
        for b in range(2):
            g_up[:, (2 * k + b) * 2 * mine : (2 * k + b + 1) * 2 * mine] = up[b, k].astype(FULL)
    puts[7].start()
    for k in range(2):
        g_down[:, k * mine : (k + 1) * mine] = down[0, k].astype(FULL)
    puts[8].start()
    for k in range(2):
        start = k * mine
        g_out[:, start : start + mine] = out[0, k].astype(FULL)
        for p in range(attn.shape[0]):
            for place, target in enumerate((g_query, g_key, g_value)):
                target[:, start + (p + 1) * PAIR : start + (p + 2) * PAIR] = attn[
                    p, k, :, place * PAIR : (place + 1) * PAIR
                ].astype(FULL)
        ones, twos = lead[0, k].astype(FULL), early[0, k].astype(FULL)
        keep = lanes_below(ones.shape, HEAD)
        seconds = twos[:, :PAIR]
        g_query[:, start : start + PAIR] = jnp.where(keep, ones, pltpu.roll(seconds, HEAD, 1))
        g_key[:, start : start + PAIR] = jnp.where(keep, pltpu.roll(ones, HEAD, 1), seconds)
        g_value[:, start : start + PAIR] = twos[:, PAIR:]
    share[...] = share_in[0:1, :]
    sums = vec[0, 0] + vec[0, 1]
    for i, target in enumerate(g_vecs):
        target[...] = sums[i, :tall]
    for one in puts[2:7] + puts[9:]:
        one.start()
    for one in puts:
        one.wait()


def deliver(*arrays):
    output, _, shares, down, up, out = arrays[:6]
    tall, mine = out.shape[2:]
    width = 2 * mine
    shapes = [(1, shares.shape[1])] + [(tall, width)] * 4
    shapes += [(tall, 2 * up.shape[3] * 2), (down.shape[2], width)] + [(tall,)] * 4
    anywhere = pl.BlockSpec(memory_space=pl.ANY)
    return pl.pallas_call(
        functools.partial(deliver_kernel, len(arrays)),
        out_shape=[jax.ShapeDtypeStruct(output.shape, output.dtype)] * 2
        + [jax.ShapeDtypeStruct(shape, FULL) for shape in shapes],
        in_specs=[anywhere] * len(arrays),
        out_specs=[anywhere] * (2 + len(shapes)),
        scratch_shapes=[pltpu.VMEM(one.shape, one.dtype) for one in arrays]
        + [pltpu.VMEM(shape, FULL) for shape in shapes]
        + [pltpu.SemaphoreType.DMA((len(arrays),)), pltpu.SemaphoreType.DMA((2 + len(shapes),))],
        compiler_params=pltpu.CompilerParams(vmem_limit_bytes=VMEM_LIMIT),
        name="deliver",
    )(*arrays)


def reduce_plain(parts, rows):
    down, up, out, attn, early, lead, vec = parts
    width = vec.shape[1]

    def scattered(part):
        summed = lax.psum_scatter(part.astype(FULL), "rows", scatter_dimension=0, tiled=True)
        return summed.astype(LOW)

    def joined(part):
        return lax.all_gather(part, "keys", axis=1, tiled=True).astype(FULL)

    def flat_part(part):
        return part.reshape(-1, part.shape[-1])

    ones, twos = scattered(flat_part(lead[0])), scattered(flat_part(early[0]))
    first = [
        jnp.concatenate([ones[:, :HEAD], twos[:, :HEAD]], 1),
        jnp.concatenate([ones[:, HEAD:], twos[:, HEAD:PAIR]], 1),
        twos[:, PAIR:],
    ]
    rest = [scattered(flat_part(attn[p])) for p in range(attn.shape[0])]
    halves = [
        jnp.concatenate([first[i]] + [one[:, i * PAIR : (i + 1) * PAIR] for one in rest], 1)
        for i in range(3)
    ]
    halves.append(scattered(flat_part(out[0])))
    halves.append(jnp.concatenate([scattered(flat_part(up[b])) for b in range(2)], 1))
    halves.append(scattered(flat_part(down[0])))
    sums = lax.psum_scatter(
        lax.psum(vec[:4].T, "keys"), "rows", scatter_dimension=0, tiled=True
    )
    return [joined(one) for one in halves], [sums[:, i] for i in range(4)]


def body(
    rows,
    tokens,
    seg_ids,
    doc_starts,
    gain_in,
    shift_in,
    w_query,
    w_key,
    w_value,
    w_out,
    gain_mid,
    shift_mid,
    w_up,
    w_down,
    out_grad,
):
    fused = rows == COUNT
    own_tokens, own_grad = tokens[0], out_grad[0]
    output, input_grad, *parts = layer(
        fused,
        own_tokens,
        seg_ids,
        own_grad,
        gain_in,
        shift_in,
        gain_mid,
        shift_mid,
        (w_query, w_key, w_value, w_out, w_up, w_down),
    )
    parts, shares = parts[: len(KINDS)], parts[-1]
    if fused:
        output, input_grad, shares, *grads = deliver(output, input_grad, shares, *parts)
        grads, vectors = grads[:6], grads[6:]
    else:
        grads, vectors = reduce_plain(parts, rows)
    g_query, g_key, g_value, g_out, g_up, g_down = grads
    return (
        output[None],
        input_grad[None],
        shares[:1],
        vectors[0],
        vectors[1],
        g_query,
        g_key,
        g_value,
        g_out,
        vectors[2],
        vectors[3],
        g_up,
        g_down,
    )


def solution(mesh):
    in_specs = (
        P("rows", "keys", None),
        P("rows", None),
        P("rows", "keys"),
        P(),
        P(),
        P(),
        P(),
        P(),
        P(),
        P(),
        P(),
        P(),
        P(),
        P("rows", "keys", None),
    )
    out_specs = (
        P("rows", "keys", None),
        P("rows", "keys", None),
        P("rows", "keys"),
        P("rows"),
        P("rows"),
        P("rows", None),
        P("rows", None),
        P("rows", None),
        P("rows", None),
        P("rows"),
        P("rows"),
        P("rows", None),
        P("rows", None),
    )
    return jax.shard_map(
        functools.partial(body, mesh.shape["rows"]),
        mesh=mesh,
        in_specs=in_specs,
        out_specs=out_specs,
        check_vma=False,
    )
```
